512 devices in a mesh: lon: 128 (over y, z, x_hi), lat: 4 (over x_lo, core).
Axes of the slice: x: 4 (x_hi: 2, x_lo: 2; x = x_hi * 2 + x_lo), y: 4, z: 16, core: 2. Of those that a mesh axis runs over, the one named last changes fastest.
Arguments:
- features: bfloat16 [128, 4, 16, 16, 128], P('lon', 'lat'), may hold values from -12 to 12
- conv_first: bfloat16 [3, 3, 128, 256], replicated, may hold values from -0.1875 to 0.1875
- conv_second: bfloat16 [3, 3, 256, 256], replicated, may hold values from -0.125 to 0.125
- cotangent: bfloat16 [128, 4, 8, 8, 256], P('lon', 'lat'), may hold values from -60 to 60
- edge_pick: int32 [128, 4, 2], P('lon', 'lat'), may hold values from 0 to 3
- edge_flip: int32 [128, 4, 2], P('lon', 'lat'), may hold values from 0 to 1
- corner_rule: int32 [128, 4, 4], P('lon', 'lat'), may hold values from 0 to 1
Outputs:
- pooled: bfloat16 [128, 4, 8, 8, 256], P('lon', 'lat')
- input_grad: bfloat16 [128, 4, 16, 16, 128], P('lon', 'lat')
- scaled_first: bfloat16 [3, 3, 128, 256], replicated
- scaled_second: bfloat16 [3, 3, 256, 256], replicated
The draws below stay inside these ranges and needn't reach their ends.
All inputs are finite; a program needn't handle non-finite values.
Results may differ from the reference program's by a relative error of at most 0.015.
Values may be sent and summed in bfloat16 or wider, within the bound.
A program may use at most 64 MiB of HBM per device.

```python
import math
import jax
import jax.numpy as jnp
from jax import lax

C_IN = 128
C_OUT = 256
TILE = 16
TILES_LON = 128
TILES_LAT = 4
HALF = 8


def draw_features(key, part):
    scale_key, value_key = jax.random.split(key, 2)
    full_shape = (TILES_LON, TILES_LAT, TILE, TILE, C_IN)
    channel_scale = jnp.exp(jax.random.uniform(scale_key, (C_IN,), jnp.float32, math.log(0.3), math.log(3.0)))
    values = jax.random.truncated_normal(value_key, -4.0, 4.0, full_shape, jnp.float32)
    return (values * channel_scale).astype(jnp.bfloat16)


def draw_cotangent(key, part):
    scale_key, value_key = jax.random.split(key, 2)
    full_shape = (TILES_LON, TILES_LAT, HALF, HALF, C_OUT)
    channel_scale = jnp.exp(jax.random.uniform(scale_key, (C_OUT,), jnp.float32, math.log(0.3), math.log(3.0)))
    position = jnp.arange(TILES_LON).astype(jnp.float32) / (TILES_LON - 1)
    ramp_up = 1.0 + 2.0 * position
    values = jax.random.truncated_normal(value_key, -4.0, 4.0, full_shape, jnp.float32)
    values = values * channel_scale * ramp_up[:, None, None, None, None]
    return values.astype(jnp.bfloat16)


def set_ends(result, stream_key, smallest, top_value):
    extent = result.shape
    index_at = [jax.random.randint(jax.random.fold_in(stream_key, axis), (), 0, extent[axis]) for axis in range(len(extent))]
    result = result.at[tuple(index_at)].set(smallest)
    longest = extent.index(max(extent))
    index_at[longest] = (index_at[longest] + 1) % extent[longest]
    return result.at[tuple(index_at)].set(top_value)


def scatter_about(rng, dims, scale, reach, kind=jnp.bfloat16):
    values = scale * jax.random.normal(rng, dims, jnp.float32)
    return jnp.clip(values, min=-reach, max=reach).astype(kind)


def setup_inputs(seed: int = 0) -> dict:
    streams_of = jax.random.split(jax.random.key(seed), 8)
    return {
        "features": draw_features(jax.random.fold_in(streams_of[7], 71), 0),
        "conv_first": scatter_about(streams_of[1], (3, 3, C_IN, C_OUT), (9 * C_IN) ** -0.5, 0.1875),
        "conv_second": scatter_about(streams_of[2], (3, 3, C_OUT, C_OUT), (9 * C_OUT) ** -0.5, 0.125),
        "cotangent": draw_cotangent(jax.random.fold_in(streams_of[7], 71), 0),
        "edge_pick": set_ends(jax.random.randint(streams_of[4], (TILES_LON, TILES_LAT, 2), 0, 4), jax.random.fold_in(streams_of[4], 1), 0, 3).astype(jnp.int32),
        "edge_flip": set_ends(jax.random.randint(streams_of[5], (TILES_LON, TILES_LAT, 2), 0, 2), jax.random.fold_in(streams_of[5], 1), 0, 1).astype(jnp.int32),
        "corner_rule": set_ends(jax.random.randint(streams_of[6], (TILES_LON, TILES_LAT, 4), 0, 2), jax.random.fold_in(streams_of[6], 1), 0, 1).astype(jnp.int32),
    }


def normal_cdf(values):
    return 0.5 * (1.0 + lax.erf(values * (1.0 / math.sqrt(2.0))))

def gelu_value(values):
    return values * normal_cdf(values)

def gelu_slope(values):
    return normal_cdf(values) + values * jnp.exp(-0.5 * values * values) * (1.0 / math.sqrt(2.0 * math.pi))

def edge_pack(square):
    return jnp.stack([square[0], square[-1], square[:, 0], square[:, -1]])

def pick_row(bundle, choose_edge, reverse_flag):
    chosen = jnp.zeros_like(bundle[0])
    for edge_id in range(4):
        chosen = jnp.where(choose_edge == edge_id, bundle[edge_id], chosen)
    return jnp.where(reverse_flag == 1, chosen[::-1], chosen)

def extend_rows(square, from_north, from_south, edge_picks, edge_flips):
    south_row = pick_row(from_south, edge_picks[0], edge_flips[0])
    north_row = pick_row(from_north, edge_picks[1], edge_flips[1])
    return jnp.concatenate([south_row[None], square, north_row[None]], axis=0)

def extend_cols(extended, west_column, east_column, corner_rules):
    padded = jnp.concatenate([west_column[:, None], extended, east_column[:, None]], axis=1)
    far_edge = padded.shape[0] - 1
    corner_spots = ((0, 0, 0, 1, 1, 0), (0, far_edge, 0, far_edge - 1, 1, far_edge), (far_edge, 0, far_edge, 1, far_edge - 1, 0), (far_edge, far_edge, far_edge, far_edge - 1, far_edge - 1, far_edge))
    for corner_id, corner_spot in enumerate(corner_spots):
        row_at, col_at, first_row, first_col, second_row, second_col = corner_spot
        blended = 0.5 * (padded[first_row, first_col] + padded[second_row, second_col])
        padded = padded.at[row_at, col_at].set(jnp.where(corner_rules[corner_id] == 1, blended, padded[row_at, col_at]))
    return padded

def twice_mapped(func):
    return jax.vmap(jax.vmap(func))

def halo_field(values, edge_pick, edge_flip, corner_rule):
    lon_count, lat_count = (values.shape[0], values.shape[1])
    bundles = twice_mapped(edge_pack)(values)
    blank_rows = jnp.zeros_like(bundles[:, :1])
    north_band = jnp.concatenate([bundles[:, 1:], blank_rows], axis=1)
    south_band = jnp.concatenate([blank_rows, bundles[:, :-1]], axis=1)
    across_pole = jnp.roll(bundles, lon_count // 2, axis=0)
    band_index = jnp.arange(lat_count)[None, :, None, None, None]
    from_north = jnp.where(band_index == lat_count - 1, across_pole, north_band)
    from_south = jnp.where(band_index == 0, across_pole, south_band)
    extended = twice_mapped(extend_rows)(values, from_north, from_south, edge_pick, edge_flip)
    west_column = jnp.roll(extended[:, :, :, -1], 1, axis=0)
    east_column = jnp.roll(extended[:, :, :, 0], -1, axis=0)
    return twice_mapped(extend_cols)(extended, west_column, east_column, corner_rule)

def halo_back(grad_pad, edge_pick, edge_flip, corner_rule):
    lon_count, lat_count, side_cells = (grad_pad.shape[0], grad_pad.shape[1], grad_pad.shape[2] - 2)
    blank_field = jnp.zeros((lon_count, lat_count, side_cells, side_cells, grad_pad.shape[4]), jnp.float32)
    _, pullback = jax.vjp(lambda field_in: halo_field(field_in, edge_pick, edge_flip, corner_rule), blank_field)
    return pullback(grad_pad)[0]

def convolve(padded, weight):
    tile_count, tile_width = (padded.shape[0], padded.shape[1] - 2)
    summed = jnp.zeros((tile_count * tile_width * tile_width, weight.shape[3]), jnp.float32)
    for shift_row in range(3):
        for shift_col in range(3):
            window = padded[:, shift_row:shift_row + tile_width, shift_col:shift_col + tile_width].reshape(tile_count * tile_width * tile_width, -1)
            summed = summed + jnp.dot(window, weight[shift_row, shift_col], preferred_element_type=jnp.float32)
    return summed.reshape(tile_count, tile_width, tile_width, -1)

def weight_grad(padded, gradient):
    tile_count, tile_width = (gradient.shape[0], gradient.shape[1])
    flat_grad = gradient.reshape(tile_count * tile_width * tile_width, -1)
    blocks = []
    for shift_row in range(3):
        for shift_col in range(3):
            window = padded[:, shift_row:shift_row + tile_width, shift_col:shift_col + tile_width].reshape(tile_count * tile_width * tile_width, -1)
            blocks.append(lax.dot_general(window, flat_grad, (((0,), (0,)), ((), ())), preferred_element_type=jnp.float32))
    return jnp.stack(blocks).reshape(3, 3, padded.shape[3], gradient.shape[3])

def input_side_grad(gradient, weight):
    tile_count, tile_width = (gradient.shape[0], gradient.shape[1])
    flat_grad = gradient.reshape(tile_count * tile_width * tile_width, -1)
    summed = jnp.zeros((tile_count, tile_width + 2, tile_width + 2, weight.shape[2]), jnp.float32)
    for shift_row in range(3):
        for shift_col in range(3):
            product = lax.dot_general(flat_grad, weight[shift_row, shift_col], (((1,), (1,)), ((), ())), preferred_element_type=jnp.float32)
            product = product.reshape(tile_count, tile_width, tile_width, -1)
            summed = summed + jnp.pad(product, ((0, 0), (shift_row, 2 - shift_row), (shift_col, 2 - shift_col), (0, 0)))
    return summed

def pool_cells(values):
    tile_count, tile_width, channels = (values.shape[0], values.shape[1], values.shape[3])
    grouped = values.reshape(tile_count, tile_width // 2, 2, tile_width // 2, 2, channels)
    return lax.optimization_barrier(jnp.sum(grouped, axis=(2, 4))) * 0.25

def expand_grad(values):
    tile_count, half_width, channels = (values.shape[0], values.shape[1], values.shape[3])
    spread = jnp.broadcast_to(values[:, :, None, :, None, :], (tile_count, half_width, 2, half_width, 2, channels))
    return spread.reshape(tile_count, 2 * half_width, 2 * half_width, channels) * 0.25

def reference(features, conv_first, conv_second, cotangent, edge_pick, edge_flip, corner_rule):
    features_pad = halo_field(features, edge_pick, edge_flip, corner_rule)
    first_pre = lax.map(lambda padded: convolve(padded, conv_first), features_pad)
    first_act = gelu_value(first_pre).astype(jnp.bfloat16)
    first_pad = halo_field(first_act, edge_pick, edge_flip, corner_rule)

    def second_step(running, inputs):
        padded, cot_rows = inputs
        second_pre = convolve(padded, conv_second)
        pooled_rows = pool_cells(gelu_value(second_pre)).astype(jnp.bfloat16)
        second_grad = (expand_grad(cot_rows.astype(jnp.float32)) * gelu_slope(second_pre)).astype(jnp.bfloat16)
        running = running + weight_grad(padded, second_grad)
        pad_grad = input_side_grad(second_grad, conv_second).astype(jnp.bfloat16)
        return (running, (pooled_rows, pad_grad))
    grad_second, (pooled, first_pad_grad) = lax.scan(second_step, jnp.zeros(conv_second.shape, jnp.float32), (first_pad, cotangent))
    first_grad = halo_back(first_pad_grad.astype(jnp.float32), edge_pick, edge_flip, corner_rule)

    def first_step(running, inputs):
        padded, upstream, pre_act = inputs
        pre_grad = (upstream * gelu_slope(pre_act)).astype(jnp.bfloat16)
        running = running + weight_grad(padded, pre_grad)
        return (running, input_side_grad(pre_grad, conv_first).astype(jnp.bfloat16))
    grad_first, features_pad_grad = lax.scan(first_step, jnp.zeros(conv_first.shape, jnp.float32), (features_pad, first_grad, first_pre))
    input_grad = halo_back(features_pad_grad.astype(jnp.float32), edge_pick, edge_flip, corner_rule).astype(jnp.bfloat16)
    squared = jnp.sum(grad_first * grad_first) + jnp.sum(grad_second * grad_second)
    norm_target = math.sqrt(9.0 * (conv_first.shape[2] + conv_first.shape[3]) * conv_first.shape[3])
    grad_norm = jnp.sqrt(squared + 1e-06)
    norm_scale = norm_target / grad_norm
    return (pooled, input_grad, (grad_first * norm_scale).astype(jnp.bfloat16), (grad_second * norm_scale).astype(jnp.bfloat16))
```

```python
import math

import jax
import jax.numpy as jnp
from jax import lax
from jax.experimental import pallas as pl
from jax.experimental.pallas import tpu as pltpu
from jax.sharding import PartitionSpec as P

MESH = pl.DeviceIdType.MESH
BF = jnp.bfloat16
F32 = jnp.float32
NX, NY, NZ = 4, 4, 16
LON, LAT = 2 * NY * NZ, 4
C1, C2 = 128, 256


def normal_cdf(values):
    return 0.5 * (1.0 + lax.erf(values * (1.0 / math.sqrt(2.0))))


def gelu_slope(values, cdf):
    return cdf + values * jnp.exp(-0.5 * values * values) * (1.0 / math.sqrt(2.0 * math.pi))


def iota(shape, dim):
    return lax.broadcasted_iota(jnp.int32, shape, dim)


def hot(cond, value=1.0):
    return jnp.where(cond, jnp.float32(value), jnp.float32(0.0))


def mm(a, b):
    return jnp.dot(a, b, preferred_element_type=F32)


def mm_nt(a, b):
    return lax.dot_general(a, b, (((1,), (1,)), ((), ())), preferred_element_type=F32)


def mm_tn(a, b):
    return lax.dot_general(a, b, (((0,), (0,)), ((), ())), preferred_element_type=F32)


def remote(src, dst, send_sem, recv_sem, device):
    return pltpu.make_async_remote_copy(
        src_ref=src, dst_ref=dst, send_sem=send_sem, recv_sem=recv_sem,
        device_id=device, device_id_type=MESH,
    )


def corner_slot(edge, at_end):
    return jnp.where(
        edge == 0, at_end, jnp.where(edge == 1, 2 + at_end, jnp.where(edge == 2, 2 * at_end, 1 + 2 * at_end))
    )


class Reduce:
    def __init__(self, m, z_base, refs, place):
        self.m = m
        self.z_base = z_base
        self.total = m[0] + m[1]
        self.start = (0, 16 * m[0])
        (self.halves, self.r0, self.a1, self.r1a, self.r1b, self.a2a, self.a2b, self.r2a, self.r2b,
         self.a3, self.r3, self.out, self.s_send, self.s_recv, self.z_recv, self.g_send, self.g_recv,
         self.gz_send) = refs
        self.place = place
        self.x, self.y, self.z, self.core, self.device = place
        self.pending = []

    def peer(self, axis, d):
        x, y = self.x, self.y
        if axis == "x":
            x = lax.rem(x + d, NX)
        else:
            y = lax.rem(y + d, NY)
        return x, y

    def axes(self, part):
        return ("x", "y") if part == 0 else ("y", "x")

    def coords(self, part):
        return (self.x, self.y) if part == 0 else (self.y, self.x)

    def send(self, copy):
        copy.start()
        self.pending.append(copy)

    def finish(self):
        for copy in self.pending:
            copy.wait_send()
        self.pending = []

    def core_send(self):
        self.send(remote(self.halves.at[1 - self.core], self.r0, self.s_send.at[0], self.s_recv.at[0],
                         self.device(self.x, self.y, self.z, 1 - self.core)))

    def core_add(self):
        remote(self.halves.at[0], self.r0, self.s_send.at[0], self.s_recv.at[0],
               self.device(self.x, self.y, self.z, 1 - self.core)).wait_recv()
        units = 16 * self.total

        step = 8

        def body(i, carry):
            at = pl.ds(i * step, step)
            self.a1[at] = (self.halves[self.core, at].astype(F32) + self.r0[at].astype(F32)).astype(BF)
            return carry

        lax.fori_loop(0, units // step, body, 0)

    def first_send(self):
        for part in range(2):
            n = 4 * self.m[part]
            r1 = (self.r1a, self.r1b)[part]
            mine = self.coords(part)[0]
            for d in (2, 1, 3):
                x, y = self.peer(self.axes(part)[0], d)
                block = lax.rem(mine + d, 4)
                k = 1 + part * 3 + d - 1
                self.send(remote(self.a1.at[pl.ds(self.start[part] + block * n, n)], r1.at[d - 1],
                                 self.s_send.at[k], self.s_recv.at[k], self.device(x, y, self.z, self.core)))

    def first_add(self):
        for part in range(2):
            n = 4 * self.m[part]
            r1 = (self.r1a, self.r1b)[part]
            a2 = (self.a2a, self.a2b)[part]
            mine = self.coords(part)[0]
            for d in (1, 2, 3):
                k = 1 + part * 3 + d - 1
                remote(r1.at[d - 1], r1.at[d - 1], self.s_send.at[k], self.s_recv.at[k],
                       self.device(self.x, self.y, self.z, 1 - self.core)).wait_recv()
            step = self.m[part]

            def body(i, carry):
                at = pl.ds(i * step, step)
                total = self.a1[pl.ds(self.start[part] + mine * n + i * step, step)].astype(F32)
                for d in range(3):
                    total = total + r1[d, at].astype(F32)
                a2[at] = total.astype(BF)
                return carry

            lax.fori_loop(0, 4, body, 0)

    def second_send(self):
        for part in range(2):
            m = self.m[part]
            a2 = (self.a2a, self.a2b)[part]
            r2 = (self.r2a, self.r2b)[part]
            mine = self.coords(part)[1]
            for d in (2, 1, 3):
                x, y = self.peer(self.axes(part)[1], d)
                block = lax.rem(mine + d, 4)
                k = 7 + part * 3 + d - 1
                self.send(remote(a2.at[pl.ds(block * m, m)], r2.at[d - 1],
                                 self.s_send.at[k], self.s_recv.at[k], self.device(x, y, self.z, self.core)))

    def second_add(self):
        for part in range(2):
            m = self.m[part]
            a2 = (self.a2a, self.a2b)[part]
            r2 = (self.r2a, self.r2b)[part]
            mine = self.coords(part)[1]
            for d in (1, 2, 3):
                k = 7 + part * 3 + d - 1
                remote(r2.at[d - 1], r2.at[d - 1], self.s_send.at[k], self.s_recv.at[k],
                       self.device(self.x, self.y, self.z, 1 - self.core)).wait_recv()
            total = a2[pl.ds(mine * m, m)].astype(F32)
            for d in range(3):
                total = total + r2[d].astype(F32)
            self.a3[pl.ds(part * self.m[0], m)] = total.astype(BF)

    def z_send(self):
        for u in range(self.total):
            owner = self.z_base + u
            away = lax.rem(self.z - owner + NZ, NZ)

            @pl.when(away != 0)
            def _():
                remote(self.a3.at[u], self.r3.at[away - 1], self.s_send.at[13 + u], self.z_recv.at[away - 1],
                       self.device(self.x, self.y, owner, self.core)).start()

    def z_send_done(self):
        for u in range(self.total):
            @pl.when(self.z != self.z_base + u)
            def _():
                remote(self.a3.at[u], self.r3.at[0], self.s_send.at[13 + u], self.z_recv.at[0],
                       self.device(self.x, self.y, self.z_base + u, self.core)).wait_send()

    def unit_at(self, u):
        ma, mb = self.m
        first = (self.x * 4 + self.y) * ma + u
        second = self.start[1] + (self.y * 4 + self.x) * mb + u - ma
        if isinstance(u, int):
            return first if u < ma else second
        return jnp.where(u < ma, first, second)

    def owner(self):
        return jnp.logical_and(self.z >= self.z_base, self.z < self.z_base + self.total)

    def z_add_and_gather(self):
        mine = self.z - self.z_base

        @pl.when(self.owner())
        def _():
            for d in range(1, NZ):
                remote(self.r3.at[d - 1], self.r3.at[d - 1], self.s_send.at[13], self.z_recv.at[d - 1],
                       self.device(self.x, self.y, self.z, 1 - self.core)).wait_recv()
            total = self.a3[mine].astype(F32)
            for d in range(NZ - 1):
                total = total + self.r3[d].astype(F32)
            at = self.unit_at(mine)
            self.out[self.core, at] = total.astype(BF)
            for d in (8, 7, 9, 6, 10, 5, 11, 4, 12, 3, 13, 2, 14, 1, 15):
                remote(self.out.at[self.core, at], self.out.at[self.core, at], self.gz_send.at[d - 1],
                       self.g_recv.at[mine],
                       self.device(self.x, self.y, lax.rem(self.z + d, NZ), self.core)).start()

    def z_gather_sent(self):
        mine = self.z - self.z_base

        @pl.when(self.owner())
        def _():
            at = self.unit_at(mine)
            for d in range(1, NZ):
                remote(self.out.at[self.core, at], self.out.at[self.core, at], self.gz_send.at[d - 1],
                       self.g_recv.at[mine],
                       self.device(self.x, self.y, lax.rem(self.z + d, NZ), self.core)).wait_send()

    def gather_second(self):
        for u in range(self.total):
            at = self.unit_at(u)

            @pl.when(self.z != self.z_base + u)
            def _():
                remote(self.out.at[self.core, at], self.out.at[self.core, at], self.gz_send.at[0],
                       self.g_recv.at[u], self.device(self.x, self.y, self.z, 1 - self.core)).wait_recv()
        for part in range(2):
            m = self.m[part]
            ca, cb = self.coords(part)
            at = pl.ds(self.start[part] + (ca * 4 + cb) * m, m)
            for d in (2, 1, 3):
                x, y = self.peer(self.axes(part)[1], d)
                k = part * 3 + d - 1
                self.send(remote(self.out.at[self.core, at], self.out.at[self.core, at], self.g_send.at[k],
                                 self.g_recv.at[9 + k], self.device(x, y, self.z, self.core)))

    def gather_first(self):
        for part in range(2):
            m = self.m[part]
            ca, cb = self.coords(part)
            for d in (1, 3, 2):
                k = part * 3 + d - 1
                there = lax.rem(cb + 4 - d, 4)
                at = pl.ds(self.start[part] + (ca * 4 + there) * m, m)
                remote(self.out.at[self.core, at], self.out.at[self.core, at], self.g_send.at[k],
                       self.g_recv.at[9 + k], self.device(self.x, self.y, self.z, 1 - self.core)).wait_recv()
            at = pl.ds(self.start[part] + ca * 4 * m, 4 * m)
            for d in (2, 1, 3):
                x, y = self.peer(self.axes(part)[0], d)
                k = 6 + part * 3 + d - 1
                self.send(remote(self.out.at[self.core, at], self.out.at[self.core, at], self.g_send.at[k],
                                 self.g_recv.at[9 + k], self.device(x, y, self.z, self.core)))
            self.to_core(part, 0, at)

    def to_core(self, part, d, at):
        k = 12 + part * 4 + d
        self.send(remote(self.out.at[self.core, at], self.out.at[self.core, at], self.g_send.at[k],
                         self.g_recv.at[9 + k], self.device(self.x, self.y, self.z, 1 - self.core)))

    def gather_core(self):
        for d in (1, 3, 2):
            for part in range(2):
                n = 4 * self.m[part]
                ca = self.coords(part)[0]
                k = 6 + part * 3 + d - 1
                at = pl.ds(self.start[part] + lax.rem(ca + 4 - d, 4) * n, n)
                remote(self.out.at[self.core, at], self.out.at[self.core, at], self.g_send.at[k],
                       self.g_recv.at[9 + k], self.device(self.x, self.y, self.z, 1 - self.core)).wait_recv()
                self.to_core(part, d, at)

    def gather_done(self):
        for part in range(2):
            n = 4 * self.m[part]
            ca = self.coords(part)[0]
            for d in range(4):
                k = 12 + part * 4 + d
                at = pl.ds(self.start[part] + lax.rem(ca + 4 - d, 4) * n, n)
                remote(self.out.at[1 - self.core, at], self.out.at[1 - self.core, at], self.g_send.at[k],
                       self.g_recv.at[9 + k], self.device(self.x, self.y, self.z, 1 - self.core)).wait_recv()


def reduce_scratch(ma, mb):
    units = 16 * (ma + mb)
    total = ma + mb
    return [
        pltpu.VMEM((2, units, 16, 128), BF),
        pltpu.VMEM((units, 16, 128), BF),
        pltpu.VMEM((units, 16, 128), BF),
        pltpu.VMEM((3, 4 * ma, 16, 128), BF),
        pltpu.VMEM((3, 4 * mb, 16, 128), BF),
        pltpu.VMEM((4 * ma, 16, 128), BF),
        pltpu.VMEM((4 * mb, 16, 128), BF),
        pltpu.VMEM((3, ma, 16, 128), BF),
        pltpu.VMEM((3, mb, 16, 128), BF),
        pltpu.VMEM((total, 16, 128), BF),
        pltpu.VMEM((NZ - 1, 16, 128), BF),
        pltpu.VMEM((2, units, 16, 128), BF),
        pltpu.SemaphoreType.DMA((13 + total,)),
        pltpu.SemaphoreType.DMA((13,)),
        pltpu.SemaphoreType.DMA((NZ - 1,)),
        pltpu.SemaphoreType.DMA((20,)),
        pltpu.SemaphoreType.DMA((9 + 20,)),
        pltpu.SemaphoreType.DMA((NZ - 1,)),
    ]


N_REDUCE = 18
M2 = (5, 4)
M1 = (3, 2)
FIRST_ROWS = ((0, 0, 40), (48, 40, 32))


def halo_scratch(channels):
    return [
        pltpu.VMEM((80, channels), BF),
        pltpu.VMEM((256, channels), BF),
        pltpu.SemaphoreType.DMA((8,)),
        pltpu.SemaphoreType.DMA((8,)),
        pltpu.VMEM((304, channels), F32),
        pltpu.VMEM((288, 3 * channels), BF),
        pltpu.VMEM((416, C2), BF),
        pltpu.VMEM((304, 3 * channels), F32),
        pltpu.VMEM((384, channels), BF),
        pltpu.VMEM((128, channels), BF),
        pltpu.VMEM((128, channels), BF),
        pltpu.SemaphoreType.DMA((8,)),
        pltpu.SemaphoreType.DMA((8,)),
    ]


N_HALO = 13


def step_kernel(*refs):
    (feat_ref, w1_hbm, w2_hbm, cot_ref, pick_ref, flip_ref, rule_ref,
     pooled_ref, grad_ref, first_ref, second_ref) = refs[:11]
    refs = refs[11:]
    halo1, refs = refs[:N_HALO], refs[N_HALO:]
    halo2, refs = refs[:N_HALO], refs[N_HALO:]
    red2_refs, refs = refs[:N_REDUCE], refs[N_REDUCE:]
    red1_refs, refs = refs[:N_REDUCE], refs[N_REDUCE:]
    (w1, w2, w_sem, rules_out, rules_in, rule_send, rule_recv, q_fwd, q_back, slope1, pre2) = refs

    lon, lat = lax.axis_index("lon"), lax.axis_index("lat")
    y = lax.div(lon, 2 * NZ)
    z = lax.div(lax.rem(lon, 2 * NZ), 2)
    x = lax.rem(lon, 2) * 2 + lax.div(lat, 2)
    core = lax.rem(lat, 2)

    def device(x_at, y_at, z_at, core_at):
        return (y_at * (2 * NZ) + z_at * 2 + lax.div(x_at, 2), lax.rem(x_at, 2) * 2 + core_at)

    across = lax.rem(lon + LON // 2, LON)
    below, above = lat == 0, lat == LAT - 1
    vert = (
        (jnp.where(below, across, lon), jnp.where(below, lat, lat - 1)),
        (jnp.where(above, across, lon), jnp.where(above, lat, lat + 1)),
    )
    seen = (jnp.where(below, 0, 1), jnp.where(above, 1, 0))

    def west_of(at):
        return (lax.rem(at[0] + LON - 1, LON), at[1])

    def east_of(at):
        return (lax.rem(at[0] + 1, LON), at[1])

    here = (lon, lat)
    west, east = west_of(here), east_of(here)
    diagonal = [
        (west_of(vert[0]), 2 * seen[0] + 1),
        (east_of(vert[0]), 2 * seen[0]),
        (west_of(vert[1]), 2 * seen[1] + 1),
        (east_of(vert[1]), 2 * seen[1]),
    ]

    load1 = pltpu.make_async_copy(w1_hbm, w1, w_sem.at[0])
    load2 = pltpu.make_async_copy(w2_hbm, w2, w_sem.at[1])
    load1.start()
    load2.start()

    barrier = pltpu.get_barrier_semaphore()
    partners = [vert[0], vert[1], west, east] + [d[0] for d in diagonal]
    partners.append(device(x, y, z, 1 - core))
    for d in (1, 2, 3):
        partners.append(device(lax.rem(x + d, NX), y, z, core))
        partners.append(device(x, lax.rem(y + d, NY), z, core))
    for d in range(1, NZ):
        partners.append(device(x, y, lax.rem(z + d, NZ), core))
    for partner in partners:
        pl.semaphore_signal(barrier, inc=1, device_id=partner, device_id_type=MESH)

    picks = [pick_ref[0, 0, s] for s in range(2)]
    flips = [flip_ref[0, 0, s] for s in range(2)]
    rules = [rule_ref[0, 0, k] for k in range(4)]

    row8 = iota((8, 256), 0)
    rules_out[...] = jnp.where(
        row8 == 0, picks[0], jnp.where(row8 == 1, flips[0], jnp.where(row8 == 2, picks[1], flips[1]))
    )

    p, cell = iota((80, 256), 0), iota((80, 256), 1)
    k = p & 15
    want = jnp.where(
        p < 16, k, jnp.where(p < 32, 240 + k, jnp.where(p < 48, 16 * k, jnp.where(p < 64, 16 * k + 15, (
            jnp.where(k == 0, 0, jnp.where(k == 1, 15, jnp.where(k == 2, 240, jnp.where(k == 3, 255, -1))))
        ))))
    )
    take_edges = hot(cell == want).astype(BF)

    halo1[0][...] = mm(take_edges, feat_ref[...]).astype(BF)
    halo1[1][224:256, :] = jnp.zeros((32, C1), BF)
    halo2[1][224:256, :] = jnp.zeros((32, C2), BF)

    pl.semaphore_wait(barrier, len(partners))

    def halo_sends(halo):
        out, got, send, recv = halo[:4]
        copies = []
        for side in range(2):
            copies.append(remote(out.at[0:64], got.at[pl.ds(pl.multiple_of(64 * seen[side], 64), 64)],
                                 send.at[side], recv.at[seen[side]], vert[side]))
        copies.append(remote(out.at[32:48], got.at[144:160], send.at[2], recv.at[3], west))
        copies.append(remote(out.at[48:64], got.at[128:144], send.at[3], recv.at[2], east))
        for i, (target, slot) in enumerate(diagonal):
            copies.append(remote(out.at[64:80], got.at[pl.ds(pl.multiple_of(160 + 16 * slot, 16), 16)],
                                 send.at[4 + i], recv.at[4 + slot], target))
        for copy in copies:
            copy.start()
        return copies

    def halo_waits(halo):
        out, got, send, recv = halo[:4]
        spots = [(0, 64), (64, 64), (128, 16), (144, 16), (160, 16), (176, 16), (192, 16), (208, 16)]
        for i, (at, size) in enumerate(spots):
            remote(out.at[0:size], got.at[at:at + size], send.at[i], recv.at[i], west).wait_recv()

    rule_copies = []
    for i, (target, slot) in enumerate(((vert[0], seen[0]), (vert[1], seen[1]), (west, 3), (east, 2))):
        rule_copies.append(remote(rules_out, rules_in.at[slot], rule_send.at[i], rule_recv.at[slot], target))
    for copy in rule_copies:
        copy.start()
    sent = halo_sends(halo1)

    r, c = iota((288, 256), 0), iota((288, 256), 1)
    j, i = r & 15, r >> 4
    want = jnp.where(j == 0, 127 + i, jnp.where(j == 15, 143 + i, -1))
    q_fwd[0:288, :] = hot(c == want).astype(BF)
    r, c = iota((32, 256), 0), iota((32, 256), 1)
    k, north = r & 15, r >= 16
    flip = jnp.where(north, flips[1], flips[0])
    pick = jnp.where(north, picks[1], picks[0])
    want = jnp.where(north, 64, 0) + 16 * pick + jnp.where(flip == 1, 15 - k, k)
    q_fwd[288:320, :] = hot(c == want).astype(BF)

    p, q = iota((128, 384), 0), iota((128, 384), 1)
    block, k = p >> 4, p & 15
    low, high = k == 0, k == 15
    corner_at = (0, 15, 272, 287)
    want = jnp.where(block == 0, 288 + k, jnp.where(block == 1, 304 + k, jnp.where(
        block == 2, 16 * k + 16, jnp.where(block == 3, 16 * k + 31, -1))))
    half = jnp.full_like(want, -1)
    ends = ((0, 1), (2, 3), (0, 2), (1, 3))
    for b in range(4):
        first, second = ends[b]
        half = jnp.where((block == b) & low & (rules[first] == 1), corner_at[first], half)
        half = jnp.where((block == b) & high & (rules[second] == 1), corner_at[second], half)
        want = jnp.where((block == 4 + b) & low & (rules[b] != 1), corner_at[b], want)
    q_back[...] = (hot(q == want) + hot(q == half, 0.5)).astype(BF)

    for halo in (halo1, halo2):
        g_pad = halo[6]
        g_pad[0:32, :] = jnp.zeros((32, C2), BF)
        g_pad[288:416, :] = jnp.zeros((128, C2), BF)
        halo[8][320:384, :] = jnp.zeros((64, halo[8].shape[1]), BF)

    red2 = Reduce(M2, 0, red2_refs, (x, y, z, core, device))
    red1 = Reduce(M1, 9, red1_refs, (x, y, z, core, device))
    red1.halves[:, 40:48] = jnp.zeros((2, 8, 16, 128), BF)

    for slot in range(4):
        remote(rules_out, rules_in.at[slot], rule_send.at[slot], rule_recv.at[slot], west).wait_recv()

    r, c = iota((16, 256), 0), iota((16, 256), 1)
    for side in range(2):
        def source(position):
            return 64 * side + 16 * picks[side] + jnp.where(flips[side] == 1, 15 - position, position)

        rows = 2 * side
        w_pick, w_flip = rules_in[2, rows:rows + 1, :], rules_in[2, rows + 1:rows + 2, :]
        e_pick, e_flip = rules_in[3, rows:rows + 1, :], rules_in[3, rows + 1:rows + 2, :]
        w_at = 160 + 32 * side + corner_slot(w_pick, jnp.where(w_flip == 1, 0, 1))
        e_at = 176 + 32 * side + corner_slot(e_pick, jnp.where(e_flip == 1, 1, 0))
        w_rule, e_rule = rules[2 * side] == 1, rules[2 * side + 1] == 1
        shape = (16, 256)
        w_main = jnp.where(w_rule, jnp.full(shape, -1), jnp.broadcast_to(w_at, shape))
        e_main = jnp.where(e_rule, jnp.full(shape, -1), jnp.broadcast_to(e_at, shape))
        w_a, w_c = jnp.where(w_rule, source(0), -1), jnp.where(w_rule, 128 + 15 * side, -1)
        e_a, e_c = jnp.where(e_rule, source(15), -1), jnp.where(e_rule, 144 + 15 * side, -1)
        w_row = hot(c == w_main) + hot(c == w_a, 0.5) + hot(c == w_c, 0.5)
        e_row = hot(c == e_main) + hot(c == e_a, 0.5) + hot(c == e_c, 0.5)
        values = jnp.where(r == 0, w_row, jnp.where(r == 15, e_row, 0.0))
        q_fwd[272 * side:272 * side + 16, :] = values.astype(BF)

    face = (jnp.where(below, 0, 1), jnp.where(above, 1, 0))
    facing = []
    for side in range(2):
        south = face[side] == 0
        facing.append((
            jnp.where(south, rules_in[side, 0:1, 0:128], rules_in[side, 2:3, 0:128]),
            jnp.where(south, rules_in[side, 1:2, 0:128], rules_in[side, 3:4, 0:128]),
        ))
    p = iota((1, 128), 1)
    block, k = p >> 4, p & 15
    on_north = (block == 1) | (block >= 6)
    pick = jnp.where(on_north, facing[1][0], facing[0][0])
    flip = jnp.where(on_north, facing[1][1], facing[0][1])
    position = jnp.where(block < 2, k, jnp.where((block & 1) == 1, 15, 0))
    position = jnp.where(flip == 1, 15 - position, position)
    target = jnp.where(pick == 0, position, jnp.where(pick == 1, 240 + position, jnp.where(
        pick == 2, 16 * position, 16 * position + 15)))
    target = jnp.where(block == 2, 16 * k + 15, jnp.where(block == 3, 16 * k, target))
    target = jnp.where((block >= 4) & (k != 0), -1, target)
    place_grads = hot(iota((256, 128), 0) == target).astype(BF)

    def pad_tile(halo, tile, channels):
        got, ext, padded = halo[1], halo[4], halo[5]
        cells = mm(q_fwd[...], got[...])
        south, north = cells[288:304], cells[304:320]
        ext[8:24, :] = south
        ext[24:280, :] = tile.astype(F32)
        ext[280:296, :] = north
        j = iota((288, channels), 0) & 15
        padded[:, 0:channels] = jnp.where(j == 0, cells[0:288], ext[7:295, :]).astype(BF)
        padded[:, channels:2 * channels] = ext[8:296, :].astype(BF)
        padded[:, 2 * channels:] = jnp.where(j == 15, cells[0:288], ext[9:297, :]).astype(BF)

    def convolve(halo, weight):
        padded = halo[5]
        total = mm(padded[0:256, :], weight[0])
        for dh in (1, 2):
            total = total + mm(padded[16 * dh:16 * dh + 256, :], weight[dh])
        return total

    def input_side(halo, weight, channels):
        g_pad, by_shift, leaving, out = halo[6], halo[7], halo[8], halo[9]
        total = mm_nt(g_pad[32:320, :], weight[0])
        for dh in (1, 2):
            at = 32 - 16 * dh
            total = total + mm_nt(g_pad[at:at + 288, :], weight[dh])
        by_shift[8:296, :] = total
        j = iota((288, channels), 0) & 15
        centre = by_shift[8:296, channels:2 * channels]
        centre = centre + jnp.where(j == 15, 0.0, by_shift[9:297, 0:channels])
        centre = centre + jnp.where(j == 0, 0.0, by_shift[7:295, 2 * channels:])
        centre = centre.astype(BF)
        sides = jnp.where(j == 0, by_shift[8:296, 0:channels], by_shift[8:296, 2 * channels:])
        sides = jnp.where((j == 0) | (j == 15), sides, 0.0)
        leaving[0:288, :] = sides.astype(BF)
        leaving[288:304, :] = centre[0:16]
        leaving[304:320, :] = centre[272:288]
        out[...] = mm(q_back[...], leaving[...]).astype(BF)
        return centre[16:272]

    def grad_sends(halo):
        out, got, send, recv = halo[9:13]
        copies = []
        for side in range(2):
            copies.append(remote(out.at[16 * side:16 * side + 16],
                                 got.at[pl.ds(pl.multiple_of(16 * seen[side], 16), 16)],
                                 send.at[side], recv.at[seen[side]], vert[side]))
        copies.append(remote(out.at[32:48], got.at[32:48], send.at[2], recv.at[2], west))
        copies.append(remote(out.at[48:64], got.at[48:64], send.at[3], recv.at[3], east))
        for i, (target_at, slot) in enumerate(diagonal):
            copies.append(remote(out.at[64 + 16 * i:80 + 16 * i],
                                 got.at[pl.ds(pl.multiple_of(64 + 16 * slot, 16), 16)],
                                 send.at[4 + i], recv.at[4 + slot], target_at))
        for copy in copies:
            copy.start()
        return copies

    def grad_waits(halo):
        out, got, send, recv = halo[9:13]
        for i in range(8):
            remote(out.at[0:16], got.at[16 * i:16 * i + 16], send.at[i], recv.at[i], west).wait_recv()

    def weight_grads(halo, halves, channels, starts):
        padded, g_pad = halo[5], halo[6]
        units = channels // 16
        gradient = g_pad[32:288, :]
        for dh in range(3):
            for dw in range(3):
                tap = 3 * dh + dw
                block = mm_tn(padded[16 * dh:16 * dh + 256, dw * channels:(dw + 1) * channels], gradient)
                block = block.astype(BF)
                for h in range(2):
                    halves[h, starts[tap]:starts[tap] + units] = (
                        block[:, 128 * h:128 * h + 128].reshape(units, 16, 128)
                    )

    halo_waits(halo1)
    pad_tile(halo1, feat_ref[...], C1)
    load1.wait()
    pre1 = convolve(halo1, w1)
    cdf1 = normal_cdf(pre1)
    act1 = (pre1 * cdf1).astype(BF)
    halo2[0][...] = mm(take_edges, act1).astype(BF)
    sent += halo_sends(halo2)
    slope1[...] = gelu_slope(pre1, cdf1)
    r, c = iota((256, 64), 0), iota((256, 64), 1)
    spread = hot(c == 8 * (r >> 5) + ((r & 15) >> 1), 0.25).astype(BF)
    cot = mm(spread, cot_ref[...])
    load2.wait()

    halo_waits(halo2)
    pad_tile(halo2, act1, C2)
    second_pre = convolve(halo2, w2)
    cdf2 = normal_cdf(second_pre)
    halo2[6][32:288, :] = (cot * gelu_slope(second_pre, cdf2)).astype(BF)
    centre2 = input_side(halo2, w2, C2)
    sent += grad_sends(halo2)
    pre2[...] = second_pre * cdf2
    weight_grads(halo2, red2.halves, C2, [16 * tap for tap in range(9)])
    red2.core_send()

    grad_waits(halo2)
    first_grad = centre2.astype(F32) + mm(place_grads, halo2[10][...])
    halo1[6][32:288, :] = (first_grad * slope1[...]).astype(BF)
    weight_grads(halo1, red1.halves, C1, [8 * tap + (8 if tap >= 5 else 0) for tap in range(9)])
    red1.core_send()
    red2.core_add()
    red2.first_send()
    centre1 = input_side(halo1, w1, C1)
    sent += grad_sends(halo1)
    red1.core_add()
    red1.first_send()
    red2.first_add()
    red2.second_send()
    red1.first_add()
    red1.second_send()
    red2.second_add()
    red2.z_send()
    red1.second_add()
    red1.z_send()

    r, c = iota((64, 256), 0), iota((64, 256), 1)
    gather_cells = hot(r == 8 * (c >> 5) + ((c & 15) >> 1), 0.25).astype(BF)
    act2 = pre2[...]
    high = act2.astype(BF)
    low = (act2 - high.astype(F32)).astype(BF)
    pooled_ref[...] = (mm(gather_cells, high) + mm(gather_cells, low)).astype(BF)

    grad_waits(halo1)
    grad_ref[...] = (centre1.astype(F32) + mm(place_grads, halo1[10][...])).astype(BF)

    red2.z_add_and_gather()
    red1.z_add_and_gather()
    red2.gather_second()
    red1.gather_second()
    red2.gather_first()
    red1.gather_first()
    red2.gather_core()
    red1.gather_core()
    red2.gather_done()
    red1.gather_done()

    def squares(ref, at, count, total):
        def body(i, total):
            values = ref[:, pl.ds(at + i * 8, 8)].astype(F32)
            return total + jnp.sum(values * values, axis=(0, 1))

        return lax.fori_loop(0, count // 8, body, total)

    total = jnp.zeros((16, 128), F32)
    total = squares(red2.out, 0, 144, total)
    for at, _, count in FIRST_ROWS:
        total = squares(red1.out, at, count, total)
    squared = jnp.sum(jnp.sum(total, axis=0, keepdims=True), axis=1, keepdims=True)
    target_norm = math.sqrt(9.0 * (C1 + C2) * C2)
    scale = jnp.broadcast_to(target_norm / jnp.sqrt(squared + 1e-06), (16, 128))

    def write(ref, at, to, count, out):
        def body(i, carry):
            for h in range(2):
                values = ref[h, pl.ds(at + i * 8, 8)].astype(F32) * scale
                rows = pl.ds(pl.multiple_of((to + i * 8) * 16, 128), 128)
                out[rows, 128 * h:128 * h + 128] = values.astype(BF).reshape(128, 128)
            return carry

        lax.fori_loop(0, count // 8, body, 0)

    write(red2.out, 0, 0, 144, second_ref)
    for at, to, count in FIRST_ROWS:
        write(red1.out, at, to, count, first_ref)

    for copy in sent + rule_copies:
        copy.wait_send()
    for red in (red2, red1):
        red.finish()
        red.z_send_done()
        red.z_gather_sent()


def on_device(features, conv_first, conv_second, cotangent, edge_pick, edge_flip, corner_rule):
    vmem = pl.BlockSpec(memory_space=pltpu.VMEM)
    smem = pl.BlockSpec(memory_space=pltpu.SMEM)
    hbm = pl.BlockSpec(memory_space=pl.ANY)
    pooled, input_grad, first, second = pl.pallas_call(
        step_kernel,
        out_shape=(
            jax.ShapeDtypeStruct((64, C2), BF),
            jax.ShapeDtypeStruct((256, C1), BF),
            jax.ShapeDtypeStruct((9 * C1, C2), BF),
            jax.ShapeDtypeStruct((9 * C2, C2), BF),
        ),
        in_specs=[vmem, hbm, hbm, vmem, smem, smem, smem],
        out_specs=[vmem, vmem, vmem, vmem],
        scratch_shapes=(
            halo_scratch(C1)
            + halo_scratch(C2)
            + reduce_scratch(*M2)
            + reduce_scratch(*M1)
            + [
                pltpu.VMEM((3, 3 * C1, C2), BF),
                pltpu.VMEM((3, 3 * C2, C2), BF),
                pltpu.SemaphoreType.DMA((2,)),
                pltpu.VMEM((8, 256), jnp.int32),
                pltpu.VMEM((4, 8, 256), jnp.int32),
                pltpu.SemaphoreType.DMA((4,)),
                pltpu.SemaphoreType.DMA((4,)),
                pltpu.VMEM((320, 256), BF),
                pltpu.VMEM((128, 384), BF),
                pltpu.VMEM((256, C2), F32),
                pltpu.VMEM((256, C2), F32),
            ]
        ),
        compiler_params=pltpu.CompilerParams(
            collective_id=0, has_side_effects=True, vmem_limit_bytes=40 * 1024 * 1024
        ),
        name="level_step",
    )(
        features.reshape(256, C1),
        conv_first.reshape(3, 3 * C1, C2),
        conv_second.reshape(3, 3 * C2, C2),
        cotangent.reshape(64, C2),
        edge_pick,
        edge_flip,
        corner_rule,
    )
    return (
        pooled.reshape(1, 1, 8, 8, C2),
        input_grad.reshape(1, 1, 16, 16, C1),
        first.reshape(3, 3, C1, C2),
        second.reshape(3, 3, C2, C2),
    )


def solution(mesh):
    return jax.shard_map(
        on_device,
        mesh=mesh,
        in_specs=(
            P("lon", "lat", None, None, None),
            P(),
            P(),
            P("lon", "lat", None, None, None),
            P("lon", "lat", None),
            P("lon", "lat", None),
            P("lon", "lat", None),
        ),
        out_specs=(P("lon", "lat", None, None, None), P("lon", "lat", None, None, None), P(), P()),
        check_vma=False,
    )
```

```python
import math

import jax
import jax.numpy as jnp
from jax import lax
from jax.experimental import pallas as pl
from jax.experimental.pallas import tpu as pltpu
from jax.sharding import PartitionSpec as P

MESH = pl.DeviceIdType.MESH
BF = jnp.bfloat16
F32 = jnp.float32
NX, NY, NZ = 4, 4, 16
LON, LAT = 2 * NY * NZ, 4
C1, C2 = 128, 256


def normal_cdf(values):
    return 0.5 * (1.0 + lax.erf(values * (1.0 / math.sqrt(2.0))))


def gelu_slope(values, cdf):
    return cdf + values * jnp.exp(-0.5 * values * values) * (1.0 / math.sqrt(2.0 * math.pi))


def iota(shape, dim):
    return lax.broadcasted_iota(jnp.int32, shape, dim)


def hot(cond, value=1.0):
    return jnp.where(cond, jnp.float32(value), jnp.float32(0.0))


def mm(a, b):
    return jnp.dot(a, b, preferred_element_type=F32)


def mm_nt(a, b):
    return lax.dot_general(a, b, (((1,), (1,)), ((), ())), preferred_element_type=F32)


def mm_tn(a, b):
    return lax.dot_general(a, b, (((0,), (0,)), ((), ())), preferred_element_type=F32)


def remote(src, dst, send_sem, recv_sem, device):
    return pltpu.make_async_remote_copy(
        src_ref=src, dst_ref=dst, send_sem=send_sem, recv_sem=recv_sem,
        device_id=device, device_id_type=MESH,
    )


def corner_slot(edge, at_end):
    return jnp.where(
        edge == 0, at_end, jnp.where(edge == 1, 2 + at_end, jnp.where(edge == 2, 2 * at_end, 1 + 2 * at_end))
    )


class Reduce:
    def __init__(self, m, z_base, refs, place):
        self.m = m
        self.z_base = z_base
        self.total = m[0] + m[1]
        self.start = (0, 16 * m[0])
        (self.halves, self.r0, self.a1, self.r1a, self.r1b, self.a2a, self.a2b, self.r2a, self.r2b,
         self.a3, self.r3, self.out, self.s_send, self.s_recv, self.z_recv, self.g_send, self.g_recv,
         self.gz_send) = refs
        self.place = place
        self.x, self.y, self.z, self.core, self.device = place
        self.pending = []

    def peer(self, axis, d):
        x, y = self.x, self.y
        if axis == "x":
            x = lax.rem(x + d, NX)
        else:
            y = lax.rem(y + d, NY)
        return x, y

    def axes(self, part):
        return ("x", "y") if part == 0 else ("y", "x")

    def coords(self, part):
        return (self.x, self.y) if part == 0 else (self.y, self.x)

    def send(self, copy):
        copy.start()
        self.pending.append(copy)

    def finish(self):
        for copy in self.pending:
            copy.wait_send()
        self.pending = []

    def core_send(self):
        self.send(remote(self.halves.at[1 - self.core], self.r0, self.s_send.at[0], self.s_recv.at[0],
                         self.device(self.x, self.y, self.z, 1 - self.core)))

    def core_add(self):
        remote(self.halves.at[0], self.r0, self.s_send.at[0], self.s_recv.at[0],
               self.device(self.x, self.y, self.z, 1 - self.core)).wait_recv()
        units = 16 * self.total

        step = 8

        def body(i, carry):
            at = pl.ds(i * step, step)
            self.a1[at] = (self.halves[self.core, at].astype(F32) + self.r0[at].astype(F32)).astype(BF)
            return carry

        lax.fori_loop(0, units // step, body, 0)

    def first_send(self):
        for part in range(2):
            n = 4 * self.m[part]
            r1 = (self.r1a, self.r1b)[part]
            mine = self.coords(part)[0]
            for d in (2, 1, 3):
                x, y = self.peer(self.axes(part)[0], d)
                block = lax.rem(mine + d, 4)
                k = 1 + part * 3 + d - 1
                self.send(remote(self.a1.at[pl.ds(self.start[part] + block * n, n)], r1.at[d - 1],
                                 self.s_send.at[k], self.s_recv.at[k], self.device(x, y, self.z, self.core)))

    def first_add(self):
        for part in range(2):
            n = 4 * self.m[part]
            r1 = (self.r1a, self.r1b)[part]
            a2 = (self.a2a, self.a2b)[part]
            mine = self.coords(part)[0]
            for d in (1, 2, 3):
                k = 1 + part * 3 + d - 1
                remote(r1.at[d - 1], r1.at[d - 1], self.s_send.at[k], self.s_recv.at[k],
                       self.device(self.x, self.y, self.z, 1 - self.core)).wait_recv()
            step = self.m[part]

            def body(i, carry):
                at = pl.ds(i * step, step)
                total = self.a1[pl.ds(self.start[part] + mine * n + i * step, step)].astype(F32)
                for d in range(3):
                    total = total + r1[d, at].astype(F32)
                a2[at] = total.astype(BF)
                return carry

            lax.fori_loop(0, 4, body, 0)

    def second_send(self):
        for part in range(2):
            m = self.m[part]
            a2 = (self.a2a, self.a2b)[part]
            r2 = (self.r2a, self.r2b)[part]
            mine = self.coords(part)[1]
            for d in (2, 1, 3):
                x, y = self.peer(self.axes(part)[1], d)
                block = lax.rem(mine + d, 4)
                k = 7 + part * 3 + d - 1
                self.send(remote(a2.at[pl.ds(block * m, m)], r2.at[d - 1],
                                 self.s_send.at[k], self.s_recv.at[k], self.device(x, y, self.z, self.core)))

    def second_add(self):
        for part in range(2):
            m = self.m[part]
            a2 = (self.a2a, self.a2b)[part]
            r2 = (self.r2a, self.r2b)[part]
            mine = self.coords(part)[1]
            for d in (1, 2, 3):
                k = 7 + part * 3 + d - 1
                remote(r2.at[d - 1], r2.at[d - 1], self.s_send.at[k], self.s_recv.at[k],
                       self.device(self.x, self.y, self.z, 1 - self.core)).wait_recv()
            total = a2[pl.ds(mine * m, m)].astype(F32)
            for d in range(3):
                total = total + r2[d].astype(F32)
            self.a3[pl.ds(part * self.m[0], m)] = total.astype(BF)

    def z_send(self):
        for u in range(self.total):
            owner = self.z_base + u
            away = lax.rem(self.z - owner + NZ, NZ)

            @pl.when(away != 0)
            def _():
                remote(self.a3.at[u], self.r3.at[away - 1], self.s_send.at[13 + u], self.z_recv.at[away - 1],
                       self.device(self.x, self.y, owner, self.core)).start()

    def z_send_done(self):
        for u in range(self.total):
            @pl.when(self.z != self.z_base + u)
            def _():
                remote(self.a3.at[u], self.r3.at[0], self.s_send.at[13 + u], self.z_recv.at[0],
                       self.device(self.x, self.y, self.z_base + u, self.core)).wait_send()

    def unit_at(self, u):
        ma, mb = self.m
        first = (self.x * 4 + self.y) * ma + u
        second = self.start[1] + (self.y * 4 + self.x) * mb + u - ma
        if isinstance(u, int):
            return first if u < ma else second
        return jnp.where(u < ma, first, second)

    def owner(self):
        return jnp.logical_and(self.z >= self.z_base, self.z < self.z_base + self.total)

    def z_add_and_gather(self):
        mine = self.z - self.z_base

        @pl.when(self.owner())
        def _():
            for d in range(1, NZ):
                remote(self.r3.at[d - 1], self.r3.at[d - 1], self.s_send.at[13], self.z_recv.at[d - 1],
                       self.device(self.x, self.y, self.z, 1 - self.core)).wait_recv()
            total = self.a3[mine].astype(F32)
            for d in range(NZ - 1):
                total = total + self.r3[d].astype(F32)
            at = self.unit_at(mine)
            self.out[self.core, at] = total.astype(BF)
            for d in (8, 7, 9, 6, 10, 5, 11, 4, 12, 3, 13, 2, 14, 1, 15):
                remote(self.out.at[self.core, at], self.out.at[self.core, at], self.gz_send.at[d - 1],
                       self.g_recv.at[mine],
                       self.device(self.x, self.y, lax.rem(self.z + d, NZ), self.core)).start()

    def z_gather_sent(self):
        mine = self.z - self.z_base

        @pl.when(self.owner())
        def _():
            at = self.unit_at(mine)
            for d in range(1, NZ):
                remote(self.out.at[self.core, at], self.out.at[self.core, at], self.gz_send.at[d - 1],
                       self.g_recv.at[mine],
                       self.device(self.x, self.y, lax.rem(self.z + d, NZ), self.core)).wait_send()

    def gather_second(self):
        for u in range(self.total):
            at = self.unit_at(u)

            @pl.when(self.z != self.z_base + u)
            def _():
                remote(self.out.at[self.core, at], self.out.at[self.core, at], self.gz_send.at[0],
                       self.g_recv.at[u], self.device(self.x, self.y, self.z, 1 - self.core)).wait_recv()
        for part in range(2):
            m = self.m[part]
            ca, cb = self.coords(part)
            at = pl.ds(self.start[part] + (ca * 4 + cb) * m, m)
            for d in (2, 1, 3):
                x, y = self.peer(self.axes(part)[1], d)
                k = part * 3 + d - 1
                self.send(remote(self.out.at[self.core, at], self.out.at[self.core, at], self.g_send.at[k],
                                 self.g_recv.at[9 + k], self.device(x, y, self.z, self.core)))

    def gather_first(self):
        for part in range(2):
            m = self.m[part]
            ca, cb = self.coords(part)
            for d in (1, 3, 2):
                k = part * 3 + d - 1
                there = lax.rem(cb + 4 - d, 4)
                at = pl.ds(self.start[part] + (ca * 4 + there) * m, m)
                remote(self.out.at[self.core, at], self.out.at[self.core, at], self.g_send.at[k],
                       self.g_recv.at[9 + k], self.device(self.x, self.y, self.z, 1 - self.core)).wait_recv()
            at = pl.ds(self.start[part] + ca * 4 * m, 4 * m)
            for d in (2, 1, 3):
                x, y = self.peer(self.axes(part)[0], d)
                k = 6 + part * 3 + d - 1
                self.send(remote(self.out.at[self.core, at], self.out.at[self.core, at], self.g_send.at[k],
                                 self.g_recv.at[9 + k], self.device(x, y, self.z, self.core)))
            self.to_core(part, 0, at)

    def to_core(self, part, d, at):
        k = 12 + part * 4 + d
        self.send(remote(self.out.at[self.core, at], self.out.at[self.core, at], self.g_send.at[k],
                         self.g_recv.at[9 + k], self.device(self.x, self.y, self.z, 1 - self.core)))

    def gather_core(self):
        for d in (1, 3, 2):
            for part in range(2):
                n = 4 * self.m[part]
                ca = self.coords(part)[0]
                k = 6 + part * 3 + d - 1
                at = pl.ds(self.start[part] + lax.rem(ca + 4 - d, 4) * n, n)
                remote(self.out.at[self.core, at], self.out.at[self.core, at], self.g_send.at[k],
                       self.g_recv.at[9 + k], self.device(self.x, self.y, self.z, 1 - self.core)).wait_recv()
                self.to_core(part, d, at)

    def gather_done(self):
        for part in range(2):
            n = 4 * self.m[part]
            ca = self.coords(part)[0]
            for d in range(4):
                k = 12 + part * 4 + d
                at = pl.ds(self.start[part] + lax.rem(ca + 4 - d, 4) * n, n)
                remote(self.out.at[1 - self.core, at], self.out.at[1 - self.core, at], self.g_send.at[k],
                       self.g_recv.at[9 + k], self.device(self.x, self.y, self.z, 1 - self.core)).wait_recv()


def reduce_scratch(ma, mb):
    units = 16 * (ma + mb)
    total = ma + mb
    return [
        pltpu.VMEM((2, units, 16, 128), BF),
        pltpu.VMEM((units, 16, 128), BF),
        pltpu.VMEM((units, 16, 128), BF),
        pltpu.VMEM((3, 4 * ma, 16, 128), BF),
        pltpu.VMEM((3, 4 * mb, 16, 128), BF),
        pltpu.VMEM((4 * ma, 16, 128), BF),
        pltpu.VMEM((4 * mb, 16, 128), BF),
        pltpu.VMEM((3, ma, 16, 128), BF),
        pltpu.VMEM((3, mb, 16, 128), BF),
        pltpu.VMEM((total, 16, 128), BF),
        pltpu.VMEM((NZ - 1, 16, 128), BF),
        pltpu.SemaphoreType.DMA((13 + total,)),
        pltpu.SemaphoreType.DMA((13,)),
        pltpu.SemaphoreType.DMA((NZ - 1,)),
        pltpu.SemaphoreType.DMA((20,)),
        pltpu.SemaphoreType.DMA((9 + 20,)),
        pltpu.SemaphoreType.DMA((NZ - 1,)),
    ]


N_REDUCE = 17
M2 = (5, 4)
M1 = (3, 2)
FIRST_ROWS = ((0, 0, 40), (48, 40, 32))


def halo_scratch(channels):
    return [
        pltpu.VMEM((80, channels), BF),
        pltpu.VMEM((256, channels), BF),
        pltpu.SemaphoreType.DMA((8,)),
        pltpu.SemaphoreType.DMA((8,)),
        pltpu.VMEM((304, channels), F32),
        pltpu.VMEM((288, 3 * channels), BF),
        pltpu.VMEM((416, C2), BF),
        pltpu.VMEM((304, 3 * channels), F32),
        pltpu.VMEM((384, channels), BF),
        pltpu.VMEM((128, channels), BF),
        pltpu.VMEM((128, channels), BF),
        pltpu.SemaphoreType.DMA((8,)),
        pltpu.SemaphoreType.DMA((8,)),
    ]


N_HALO = 13


def step_kernel(*refs):
    (feat_hbm, w1_hbm, w2_hbm, cot_hbm, pick_hbm, flip_hbm, rule_hbm,
     pooled_ref, grad_ref, first_out, second_out) = refs[:11]
    refs = refs[11:]
    halo1, refs = refs[:N_HALO], refs[N_HALO:]
    halo2, refs = refs[:N_HALO], refs[N_HALO:]
    red2_refs, refs = refs[:N_REDUCE], refs[N_REDUCE:]
    red1_refs, refs = refs[:N_REDUCE], refs[N_REDUCE:]
    (feat_ref, w1, w2, cot_ref, pick_ref, flip_ref, rule_ref, load_sem,
     rules_out, rules_in, rule_send, rule_recv, q_fwd, q_back, slope1, pre2) = refs
    red2_refs = red2_refs[:11] + (second_out,) + red2_refs[11:]
    red1_refs = red1_refs[:11] + (first_out,) + red1_refs[11:]

    lon, lat = lax.axis_index("lon"), lax.axis_index("lat")
    y = lax.div(lon, 2 * NZ)
    z = lax.div(lax.rem(lon, 2 * NZ), 2)
    x = lax.rem(lon, 2) * 2 + lax.div(lat, 2)
    core = lax.rem(lat, 2)

    def device(x_at, y_at, z_at, core_at):
        return (y_at * (2 * NZ) + z_at * 2 + lax.div(x_at, 2), lax.rem(x_at, 2) * 2 + core_at)

    across = lax.rem(lon + LON // 2, LON)
    below, above = lat == 0, lat == LAT - 1
    vert = (
        (jnp.where(below, across, lon), jnp.where(below, lat, lat - 1)),
        (jnp.where(above, across, lon), jnp.where(above, lat, lat + 1)),
    )
    seen = (jnp.where(below, 0, 1), jnp.where(above, 1, 0))

    def west_of(at):
        return (lax.rem(at[0] + LON - 1, LON), at[1])

    def east_of(at):
        return (lax.rem(at[0] + 1, LON), at[1])

    here = (lon, lat)
    west, east = west_of(here), east_of(here)
    diagonal = [
        (west_of(vert[0]), 2 * seen[0] + 1),
        (east_of(vert[0]), 2 * seen[0]),
        (west_of(vert[1]), 2 * seen[1] + 1),
        (east_of(vert[1]), 2 * seen[1]),
    ]

    loads = [
        pltpu.make_async_copy(src, dst, load_sem.at[n])
        for n, (src, dst) in enumerate((
            (pick_hbm, pick_ref), (flip_hbm, flip_ref), (rule_hbm, rule_ref), (feat_hbm, feat_ref),
            (w1_hbm, w1), (cot_hbm, cot_ref), (w2_hbm, w2),
        ))
    ]
    for load in loads:
        load.start()

    barrier = pltpu.get_barrier_semaphore()
    partners = [vert[0], vert[1], west, east] + [d[0] for d in diagonal]
    partners.append(device(x, y, z, 1 - core))
    for d in (1, 2, 3):
        partners.append(device(lax.rem(x + d, NX), y, z, core))
        partners.append(device(x, lax.rem(y + d, NY), z, core))
    for d in range(1, NZ):
        partners.append(device(x, y, lax.rem(z + d, NZ), core))
    for partner in partners:
        pl.semaphore_signal(barrier, inc=1, device_id=partner, device_id_type=MESH)

    for load in loads[:3]:
        load.wait()
    picks = [pick_ref[0, 0, s] for s in range(2)]
    flips = [flip_ref[0, 0, s] for s in range(2)]
    rules = [rule_ref[0, 0, k] for k in range(4)]

    row8 = iota((8, 256), 0)
    rules_out[...] = jnp.where(
        row8 == 0, picks[0], jnp.where(row8 == 1, flips[0], jnp.where(row8 == 2, picks[1], flips[1]))
    )

    p, cell = iota((80, 256), 0), iota((80, 256), 1)
    k = p & 15
    want = jnp.where(
        p < 16, k, jnp.where(p < 32, 240 + k, jnp.where(p < 48, 16 * k, jnp.where(p < 64, 16 * k + 15, (
            jnp.where(k == 0, 0, jnp.where(k == 1, 15, jnp.where(k == 2, 240, jnp.where(k == 3, 255, -1))))
        ))))
    )
    take_edges = hot(cell == want).astype(BF)

    loads[3].wait()
    halo1[0][...] = mm(take_edges, feat_ref[...]).astype(BF)
    halo1[1][224:256, :] = jnp.zeros((32, C1), BF)
    halo2[1][224:256, :] = jnp.zeros((32, C2), BF)

    pl.semaphore_wait(barrier, len(partners))

    def halo_sends(halo):
        out, got, send, recv = halo[:4]
        copies = []
        for side in range(2):
            copies.append(remote(out.at[0:64], got.at[pl.ds(pl.multiple_of(64 * seen[side], 64), 64)],
                                 send.at[side], recv.at[seen[side]], vert[side]))
        copies.append(remote(out.at[32:48], got.at[144:160], send.at[2], recv.at[3], west))
        copies.append(remote(out.at[48:64], got.at[128:144], send.at[3], recv.at[2], east))
        for i, (target, slot) in enumerate(diagonal):
            copies.append(remote(out.at[64:80], got.at[pl.ds(pl.multiple_of(160 + 16 * slot, 16), 16)],
                                 send.at[4 + i], recv.at[4 + slot], target))
        for copy in copies:
            copy.start()
        return copies

    def halo_waits(halo):
        out, got, send, recv = halo[:4]
        spots = [(0, 64), (64, 64), (128, 16), (144, 16), (160, 16), (176, 16), (192, 16), (208, 16)]
        for i, (at, size) in enumerate(spots):
            remote(out.at[0:size], got.at[at:at + size], send.at[i], recv.at[i], west).wait_recv()

    rule_copies = []
    for i, (target, slot) in enumerate(((vert[0], seen[0]), (vert[1], seen[1]), (west, 3), (east, 2))):
        rule_copies.append(remote(rules_out, rules_in.at[slot], rule_send.at[i], rule_recv.at[slot], target))
    for copy in rule_copies:
        copy.start()
    sent = halo_sends(halo1)

    r, c = iota((288, 256), 0), iota((288, 256), 1)
    j, i = r & 15, r >> 4
    want = jnp.where(j == 0, 127 + i, jnp.where(j == 15, 143 + i, -1))
    q_fwd[0:288, :] = hot(c == want).astype(BF)
    r, c = iota((32, 256), 0), iota((32, 256), 1)
    k, north = r & 15, r >= 16
    flip = jnp.where(north, flips[1], flips[0])
    pick = jnp.where(north, picks[1], picks[0])
    want = jnp.where(north, 64, 0) + 16 * pick + jnp.where(flip == 1, 15 - k, k)
    q_fwd[288:320, :] = hot(c == want).astype(BF)

    p, q = iota((128, 384), 0), iota((128, 384), 1)
    block, k = p >> 4, p & 15
    low, high = k == 0, k == 15
    corner_at = (0, 15, 272, 287)
    want = jnp.where(block == 0, 288 + k, jnp.where(block == 1, 304 + k, jnp.where(
        block == 2, 16 * k + 16, jnp.where(block == 3, 16 * k + 31, -1))))
    half = jnp.full_like(want, -1)
    ends = ((0, 1), (2, 3), (0, 2), (1, 3))
    for b in range(4):
        first, second = ends[b]
        half = jnp.where((block == b) & low & (rules[first] == 1), corner_at[first], half)
        half = jnp.where((block == b) & high & (rules[second] == 1), corner_at[second], half)
        want = jnp.where((block == 4 + b) & low & (rules[b] != 1), corner_at[b], want)
    q_back[...] = (hot(q == want) + hot(q == half, 0.5)).astype(BF)

    for halo in (halo1, halo2):
        g_pad = halo[6]
        g_pad[0:32, :] = jnp.zeros((32, C2), BF)
        g_pad[288:416, :] = jnp.zeros((128, C2), BF)
        halo[8][320:384, :] = jnp.zeros((64, halo[8].shape[1]), BF)

    red2 = Reduce(M2, 0, red2_refs, (x, y, z, core, device))
    red1 = Reduce(M1, 9, red1_refs, (x, y, z, core, device))
    red1.halves[:, 40:48] = jnp.zeros((2, 8, 16, 128), BF)

    for slot in range(4):
        remote(rules_out, rules_in.at[slot], rule_send.at[slot], rule_recv.at[slot], west).wait_recv()

    r, c = iota((16, 256), 0), iota((16, 256), 1)
    for side in range(2):
        def source(position):
            return 64 * side + 16 * picks[side] + jnp.where(flips[side] == 1, 15 - position, position)

        rows = 2 * side
        w_pick, w_flip = rules_in[2, rows:rows + 1, :], rules_in[2, rows + 1:rows + 2, :]
        e_pick, e_flip = rules_in[3, rows:rows + 1, :], rules_in[3, rows + 1:rows + 2, :]
        w_at = 160 + 32 * side + corner_slot(w_pick, jnp.where(w_flip == 1, 0, 1))
        e_at = 176 + 32 * side + corner_slot(e_pick, jnp.where(e_flip == 1, 1, 0))
        w_rule, e_rule = rules[2 * side] == 1, rules[2 * side + 1] == 1
        shape = (16, 256)
        w_main = jnp.where(w_rule, jnp.full(shape, -1), jnp.broadcast_to(w_at, shape))
        e_main = jnp.where(e_rule, jnp.full(shape, -1), jnp.broadcast_to(e_at, shape))
        w_a, w_c = jnp.where(w_rule, source(0), -1), jnp.where(w_rule, 128 + 15 * side, -1)
        e_a, e_c = jnp.where(e_rule, source(15), -1), jnp.where(e_rule, 144 + 15 * side, -1)
        w_row = hot(c == w_main) + hot(c == w_a, 0.5) + hot(c == w_c, 0.5)
        e_row = hot(c == e_main) + hot(c == e_a, 0.5) + hot(c == e_c, 0.5)
        values = jnp.where(r == 0, w_row, jnp.where(r == 15, e_row, 0.0))
        q_fwd[272 * side:272 * side + 16, :] = values.astype(BF)

    face = (jnp.where(below, 0, 1), jnp.where(above, 1, 0))
    facing = []
    for side in range(2):
        south = face[side] == 0
        facing.append((
            jnp.where(south, rules_in[side, 0:1, 0:128], rules_in[side, 2:3, 0:128]),
            jnp.where(south, rules_in[side, 1:2, 0:128], rules_in[side, 3:4, 0:128]),
        ))
    p = iota((1, 128), 1)
    block, k = p >> 4, p & 15
    on_north = (block == 1) | (block >= 6)
    pick = jnp.where(on_north, facing[1][0], facing[0][0])
    flip = jnp.where(on_north, facing[1][1], facing[0][1])
    position = jnp.where(block < 2, k, jnp.where((block & 1) == 1, 15, 0))
    position = jnp.where(flip == 1, 15 - position, position)
    target = jnp.where(pick == 0, position, jnp.where(pick == 1, 240 + position, jnp.where(
        pick == 2, 16 * position, 16 * position + 15)))
    target = jnp.where(block == 2, 16 * k + 15, jnp.where(block == 3, 16 * k, target))
    target = jnp.where((block >= 4) & (k != 0), -1, target)
    place_grads = hot(iota((256, 128), 0) == target).astype(BF)

    def pad_tile(halo, tile, channels):
        got, ext, padded = halo[1], halo[4], halo[5]
        cells = mm(q_fwd[...], got[...])
        south, north = cells[288:304], cells[304:320]
        ext[8:24, :] = south
        ext[24:280, :] = tile.astype(F32)
        ext[280:296, :] = north
        j = iota((288, channels), 0) & 15
        padded[:, 0:channels] = jnp.where(j == 0, cells[0:288], ext[7:295, :]).astype(BF)
        padded[:, channels:2 * channels] = ext[8:296, :].astype(BF)
        padded[:, 2 * channels:] = jnp.where(j == 15, cells[0:288], ext[9:297, :]).astype(BF)

    def convolve(halo, weight):
        padded = halo[5]
        total = mm(padded[0:256, :], weight[0])
        for dh in (1, 2):
            total = total + mm(padded[16 * dh:16 * dh + 256, :], weight[dh])
        return total

    def input_side(halo, weight, channels):
        g_pad, by_shift, leaving, out = halo[6], halo[7], halo[8], halo[9]
        total = mm_nt(g_pad[32:320, :], weight[0])
        for dh in (1, 2):
            at = 32 - 16 * dh
            total = total + mm_nt(g_pad[at:at + 288, :], weight[dh])
        by_shift[8:296, :] = total
        j = iota((288, channels), 0) & 15
        centre = by_shift[8:296, channels:2 * channels]
        centre = centre + jnp.where(j == 15, 0.0, by_shift[9:297, 0:channels])
        centre = centre + jnp.where(j == 0, 0.0, by_shift[7:295, 2 * channels:])
        centre = centre.astype(BF)
        sides = jnp.where(j == 0, by_shift[8:296, 0:channels], by_shift[8:296, 2 * channels:])
        sides = jnp.where((j == 0) | (j == 15), sides, 0.0)
        leaving[0:288, :] = sides.astype(BF)
        leaving[288:304, :] = centre[0:16]
        leaving[304:320, :] = centre[272:288]
        out[...] = mm(q_back[...], leaving[...]).astype(BF)
        return centre[16:272]

    def grad_sends(halo):
        out, got, send, recv = halo[9:13]
        copies = []
        for side in range(2):
            copies.append(remote(out.at[16 * side:16 * side + 16],
                                 got.at[pl.ds(pl.multiple_of(16 * seen[side], 16), 16)],
                                 send.at[side], recv.at[seen[side]], vert[side]))
        copies.append(remote(out.at[32:48], got.at[32:48], send.at[2], recv.at[2], west))
        copies.append(remote(out.at[48:64], got.at[48:64], send.at[3], recv.at[3], east))
        for i, (target_at, slot) in enumerate(diagonal):
            copies.append(remote(out.at[64 + 16 * i:80 + 16 * i],
                                 got.at[pl.ds(pl.multiple_of(64 + 16 * slot, 16), 16)],
                                 send.at[4 + i], recv.at[4 + slot], target_at))
        for copy in copies:
            copy.start()
        return copies

    def grad_waits(halo):
        out, got, send, recv = halo[9:13]
        for i in range(8):
            remote(out.at[0:16], got.at[16 * i:16 * i + 16], send.at[i], recv.at[i], west).wait_recv()

    def weight_grads(halo, halves, channels, starts):
        padded, g_pad = halo[5], halo[6]
        units = channels // 16
        gradient = g_pad[32:288, :]
        for dh in range(3):
            for dw in range(3):
                tap = 3 * dh + dw
                block = mm_tn(padded[16 * dh:16 * dh + 256, dw * channels:(dw + 1) * channels], gradient)
                block = block.astype(BF)
                for h in range(2):
                    halves[h, starts[tap]:starts[tap] + units] = (
                        block[:, 128 * h:128 * h + 128].reshape(units, 16, 128)
                    )

    halo_waits(halo1)
    pad_tile(halo1, feat_ref[...], C1)
    loads[4].wait()
    pre1 = convolve(halo1, w1)
    cdf1 = normal_cdf(pre1)
    act1 = (pre1 * cdf1).astype(BF)
    halo2[0][...] = mm(take_edges, act1).astype(BF)
    sent += halo_sends(halo2)
    slope1[...] = gelu_slope(pre1, cdf1)
    r, c = iota((256, 64), 0), iota((256, 64), 1)
    spread = hot(c == 8 * (r >> 5) + ((r & 15) >> 1), 0.25).astype(BF)
    loads[5].wait()
    cot = mm(spread, cot_ref[...])
    loads[6].wait()

    halo_waits(halo2)
    pad_tile(halo2, act1, C2)
    second_pre = convolve(halo2, w2)
    cdf2 = normal_cdf(second_pre)
    halo2[6][32:288, :] = (cot * gelu_slope(second_pre, cdf2)).astype(BF)
    centre2 = input_side(halo2, w2, C2)
    sent += grad_sends(halo2)
    pre2[...] = second_pre * cdf2
    weight_grads(halo2, red2.halves, C2, [16 * tap for tap in range(9)])
    red2.core_send()

    grad_waits(halo2)
    first_grad = centre2.astype(F32) + mm(place_grads, halo2[10][...])
    halo1[6][32:288, :] = (first_grad * slope1[...]).astype(BF)
    weight_grads(halo1, red1.halves, C1, [8 * tap + (8 if tap >= 5 else 0) for tap in range(9)])
    red1.core_send()
    red2.core_add()
    red2.first_send()
    centre1 = input_side(halo1, w1, C1)
    sent += grad_sends(halo1)
    red1.core_add()
    red1.first_send()
    red2.first_add()
    red2.second_send()
    red1.first_add()
    red1.second_send()
    red2.second_add()
    red2.z_send()
    red1.second_add()
    red1.z_send()

    r, c = iota((64, 256), 0), iota((64, 256), 1)
    gather_cells = hot(r == 8 * (c >> 5) + ((c & 15) >> 1), 0.25).astype(BF)
    act2 = pre2[...]
    high = act2.astype(BF)
    low = (act2 - high.astype(F32)).astype(BF)
    pooled_ref[...] = (mm(gather_cells, high) + mm(gather_cells, low)).astype(BF)

    grad_waits(halo1)
    grad_ref[...] = (centre1.astype(F32) + mm(place_grads, halo1[10][...])).astype(BF)

    red2.z_add_and_gather()
    red1.z_add_and_gather()
    red2.gather_second()
    red1.gather_second()
    red2.gather_first()
    red1.gather_first()
    red2.gather_core()
    red1.gather_core()
    red2.gather_done()
    red1.gather_done()

    for copy in sent + rule_copies:
        copy.wait_send()
    for red in (red2, red1):
        red.finish()
        red.z_send_done()
        red.z_gather_sent()


def finish_kernel(pooled_ref, grad_ref, first_ref, second_ref, pooled_out, grad_out, first_out, second_out,
                  first_rows, second_rows, sems):
    copies = [pltpu.make_async_copy(pooled_ref, pooled_out, sems.at[0]),
              pltpu.make_async_copy(grad_ref, grad_out, sems.at[1])]
    for copy in copies:
        copy.start()

    def squares(ref, at, count, total):
        def body(i, total):
            values = ref[:, pl.ds(at + i * 8, 8)].astype(F32)
            return total + jnp.sum(values * values, axis=(0, 1))

        return lax.fori_loop(0, count // 8, body, total)

    total = squares(second_ref, 0, 144, jnp.zeros((16, 128), F32))
    for at, _, count in FIRST_ROWS:
        total = squares(first_ref, at, count, total)
    squared = jnp.sum(jnp.sum(total, axis=0, keepdims=True), axis=1, keepdims=True)
    target_norm = math.sqrt(9.0 * (C1 + C2) * C2)
    scale = jnp.broadcast_to(target_norm / jnp.sqrt(squared + 1e-06), (16, 128))

    def write(ref, at, to, count, out):
        def body(i, carry):
            for h in range(2):
                values = ref[h, pl.ds(at + i * 8, 8)].astype(F32) * scale
                rows = pl.ds(pl.multiple_of((to + i * 8) * 16, 128), 128)
                out[rows, 128 * h:128 * h + 128] = values.astype(BF).reshape(128, 128)
            return carry

        lax.fori_loop(0, count // 8, body, 0)

    jobs = [(second_ref, n * 48, n * 48, 48, second_rows, second_out) for n in range(3)]
    jobs += [(first_ref, at, to, count, first_rows, first_out) for at, to, count in FIRST_ROWS]
    for n, (ref, at, to, count, rows, out) in enumerate(jobs):
        write(ref, at, to, count, rows)
        span = pl.ds(16 * to, 16 * count)
        copies.append(pltpu.make_async_copy(rows.at[span], out.at[span], sems.at[2 + n]))
        copies[-1].start()
    for copy in copies:
        copy.wait()


def on_device(features, conv_first, conv_second, cotangent, edge_pick, edge_flip, corner_rule):
    vmem = pl.BlockSpec(memory_space=pltpu.VMEM)
    hbm = pl.BlockSpec(memory_space=pltpu.HBM)
    pooled, input_grad, first, second = pl.pallas_call(
        step_kernel,
        out_shape=(
            jax.ShapeDtypeStruct((64, C2), BF),
            jax.ShapeDtypeStruct((256, C1), BF),
            jax.ShapeDtypeStruct((2, 16 * sum(M1), 16, 128), BF),
            jax.ShapeDtypeStruct((2, 16 * sum(M2), 16, 128), BF),
        ),
        in_specs=[hbm] * 7,
        out_specs=[vmem] * 4,
        scratch_shapes=(
            halo_scratch(C1)
            + halo_scratch(C2)
            + reduce_scratch(*M2)
            + reduce_scratch(*M1)
            + [
                pltpu.VMEM((256, C1), BF),
                pltpu.VMEM((3, 3 * C1, C2), BF),
                pltpu.VMEM((3, 3 * C2, C2), BF),
                pltpu.VMEM((64, C2), BF),
                pltpu.SMEM((1, 1, 2), jnp.int32),
                pltpu.SMEM((1, 1, 2), jnp.int32),
                pltpu.SMEM((1, 1, 4), jnp.int32),
                pltpu.SemaphoreType.DMA((7,)),
                pltpu.VMEM((8, 256), jnp.int32),
                pltpu.VMEM((4, 8, 256), jnp.int32),
                pltpu.SemaphoreType.DMA((4,)),
                pltpu.SemaphoreType.DMA((4,)),
                pltpu.VMEM((320, 256), BF),
                pltpu.VMEM((128, 384), BF),
                pltpu.VMEM((256, C2), F32),
                pltpu.VMEM((256, C2), F32),
            ]
        ),
        compiler_params=pltpu.CompilerParams(
            collective_id=0, has_side_effects=True, vmem_limit_bytes=32 * 1024 * 1024
        ),
        name="level_step",
    )(*(
        pltpu.with_memory_space_constraint(value, pltpu.HBM)
        for value in (
            features.reshape(256, C1),
            conv_first.reshape(3, 3 * C1, C2),
            conv_second.reshape(3, 3 * C2, C2),
            cotangent.reshape(64, C2),
            edge_pick,
            edge_flip,
            corner_rule,
        )
    ))
    pooled, input_grad, first, second = pl.pallas_call(
        finish_kernel,
        out_shape=(
            jax.ShapeDtypeStruct((64, C2), BF),
            jax.ShapeDtypeStruct((256, C1), BF),
            jax.ShapeDtypeStruct((9 * C1, C2), BF),
            jax.ShapeDtypeStruct((9 * C2, C2), BF),
        ),
        in_specs=[vmem] * 4,
        out_specs=[hbm] * 4,
        scratch_shapes=[
            pltpu.VMEM((9 * C1, C2), BF),
            pltpu.VMEM((9 * C2, C2), BF),
            pltpu.SemaphoreType.DMA((7,)),
        ],
        compiler_params=pltpu.CompilerParams(vmem_limit_bytes=16 * 1024 * 1024),
        name="scale_outputs",
    )(pooled, input_grad, first, second)
    return (
        pooled.reshape(1, 1, 8, 8, C2),
        input_grad.reshape(1, 1, 16, 16, C1),
        first.reshape(3, 3, C1, C2),
        second.reshape(3, 3, C2, C2),
    )


def solution(mesh):
    return jax.shard_map(
        on_device,
        mesh=mesh,
        in_specs=(
            P("lon", "lat", None, None, None),
            P(),
            P(),
            P("lon", "lat", None, None, None),
            P("lon", "lat", None),
            P("lon", "lat", None),
            P("lon", "lat", None),
        ),
        out_specs=(P("lon", "lat", None, None, None), P("lon", "lat", None, None, None), P(), P()),
        check_vma=False,
    )
```

```python
import math

import jax
import jax.numpy as jnp
from jax import lax
from jax.experimental import pallas as pl
from jax.experimental.pallas import tpu as pltpu
from jax.sharding import PartitionSpec as P

MESH = pl.DeviceIdType.MESH
BF = jnp.bfloat16
F32 = jnp.float32
NX, NY, NZ = 4, 4, 16
LON, LAT = 2 * NY * NZ, 4
C1, C2 = 128, 256


def normal_cdf(values):
    return 0.5 * (1.0 + lax.erf(values * (1.0 / math.sqrt(2.0))))


def gelu_slope(values, cdf):
    return cdf + values * jnp.exp(-0.5 * values * values) * (1.0 / math.sqrt(2.0 * math.pi))


def iota(shape, dim):
    return lax.broadcasted_iota(jnp.int32, shape, dim)


def hot(cond, value=1.0):
    return jnp.where(cond, jnp.float32(value), jnp.float32(0.0))


def wide(row, count):
    return jnp.concatenate([row] * count, axis=1)


def edge_cell(edge, flip, position):
    at = jnp.where(flip == 1, 15 - position, position)
    return jnp.where(edge == 0, at, jnp.where(edge == 1, 240 + at, jnp.where(edge == 2, 16 * at, 16 * at + 15)))


def mm(a, b):
    return jnp.dot(a, b, preferred_element_type=F32)


def mm_nt(a, b):
    return lax.dot_general(a, b, (((1,), (1,)), ((), ())), preferred_element_type=F32)


def mm_tn(a, b):
    return lax.dot_general(a, b, (((0,), (0,)), ((), ())), preferred_element_type=F32)


def remote(src, dst, send_sem, recv_sem, device):
    return pltpu.make_async_remote_copy(
        src_ref=src, dst_ref=dst, send_sem=send_sem, recv_sem=recv_sem,
        device_id=device, device_id_type=MESH,
    )


def corner_slot(edge, at_end):
    return jnp.where(
        edge == 0, at_end, jnp.where(edge == 1, 2 + at_end, jnp.where(edge == 2, 2 * at_end, 1 + 2 * at_end))
    )


class Reduce:
    def __init__(self, m, z_base, refs, place):
        self.m = m
        self.z_base = z_base
        self.total = m[0] + m[1]
        self.start = (0, 16 * m[0])
        (self.halves, self.r0, self.a1, self.r1a, self.r1b, self.a2a, self.a2b, self.r2a, self.r2b,
         self.a3, self.r3, self.out, self.s_send, self.s_recv, self.z_recv, self.g_send, self.g_recv,
         self.gz_send) = refs
        self.place = place
        self.x, self.y, self.z, self.core, self.device = place
        self.pending = []

    def peer(self, axis, d):
        x, y = self.x, self.y
        if axis == "x":
            x = lax.rem(x + d, NX)
        else:
            y = lax.rem(y + d, NY)
        return x, y

    def axes(self, part):
        return ("x", "y") if part == 0 else ("y", "x")

    def coords(self, part):
        return (self.x, self.y) if part == 0 else (self.y, self.x)

    def send(self, copy):
        copy.start()
        self.pending.append(copy)

    def finish(self):
        for copy in self.pending:
            copy.wait_send()
        self.pending = []

    def core_send(self):
        self.send(remote(self.halves.at[1 - self.core], self.r0, self.s_send.at[0], self.s_recv.at[0],
                         self.device(self.x, self.y, self.z, 1 - self.core)))

    def core_add(self):
        remote(self.halves.at[0], self.r0, self.s_send.at[0], self.s_recv.at[0],
               self.device(self.x, self.y, self.z, 1 - self.core)).wait_recv()
        units = 16 * self.total

        step = 8

        def body(i, carry):
            at = pl.ds(i * step, step)
            self.a1[at] = (self.halves[self.core, at].astype(F32) + self.r0[at].astype(F32)).astype(BF)
            return carry

        lax.fori_loop(0, units // step, body, 0)

    def first_send(self):
        for part in range(2):
            n = 4 * self.m[part]
            r1 = (self.r1a, self.r1b)[part]
            mine = self.coords(part)[0]
            for d in (2, 1, 3):
                x, y = self.peer(self.axes(part)[0], d)
                block = lax.rem(mine + d, 4)
                k = 1 + part * 3 + d - 1
                self.send(remote(self.a1.at[pl.ds(self.start[part] + block * n, n)], r1.at[d - 1],
                                 self.s_send.at[k], self.s_recv.at[k], self.device(x, y, self.z, self.core)))

    def first_add(self):
        for part in range(2):
            n = 4 * self.m[part]
            r1 = (self.r1a, self.r1b)[part]
            a2 = (self.a2a, self.a2b)[part]
            mine = self.coords(part)[0]
            for d in (1, 2, 3):
                k = 1 + part * 3 + d - 1
                remote(r1.at[d - 1], r1.at[d - 1], self.s_send.at[k], self.s_recv.at[k],
                       self.device(self.x, self.y, self.z, 1 - self.core)).wait_recv()
            step = self.m[part]

            def body(i, carry):
                at = pl.ds(i * step, step)
                total = self.a1[pl.ds(self.start[part] + mine * n + i * step, step)].astype(F32)
                for d in range(3):
                    total = total + r1[d, at].astype(F32)
                a2[at] = total.astype(BF)
                return carry

            lax.fori_loop(0, 4, body, 0)

    def second_send(self):
        for part in range(2):
            m = self.m[part]
            a2 = (self.a2a, self.a2b)[part]
            r2 = (self.r2a, self.r2b)[part]
            mine = self.coords(part)[1]
            for d in (2, 1, 3):
                x, y = self.peer(self.axes(part)[1], d)
                block = lax.rem(mine + d, 4)
                k = 7 + part * 3 + d - 1
                self.send(remote(a2.at[pl.ds(block * m, m)], r2.at[d - 1],
                                 self.s_send.at[k], self.s_recv.at[k], self.device(x, y, self.z, self.core)))

    def second_add(self):
        for part in range(2):
            m = self.m[part]
            a2 = (self.a2a, self.a2b)[part]
            r2 = (self.r2a, self.r2b)[part]
            mine = self.coords(part)[1]
            for d in (1, 2, 3):
                k = 7 + part * 3 + d - 1
                remote(r2.at[d - 1], r2.at[d - 1], self.s_send.at[k], self.s_recv.at[k],
                       self.device(self.x, self.y, self.z, 1 - self.core)).wait_recv()
            total = a2[pl.ds(mine * m, m)].astype(F32)
            for d in range(3):
                total = total + r2[d].astype(F32)
            self.a3[pl.ds(part * self.m[0], m)] = total.astype(BF)

    def z_send(self):
        for u in range(self.total):
            owner = self.z_base + u
            away = lax.rem(self.z - owner + NZ, NZ)

            @pl.when(away != 0)
            def _():
                remote(self.a3.at[u], self.r3.at[away - 1], self.s_send.at[13 + u], self.z_recv.at[away - 1],
                       self.device(self.x, self.y, owner, self.core)).start()

    def z_send_done(self):
        for u in range(self.total):
            @pl.when(self.z != self.z_base + u)
            def _():
                remote(self.a3.at[u], self.r3.at[0], self.s_send.at[13 + u], self.z_recv.at[0],
                       self.device(self.x, self.y, self.z_base + u, self.core)).wait_send()

    def unit_at(self, u):
        ma, mb = self.m
        first = (self.x * 4 + self.y) * ma + u
        second = self.start[1] + (self.y * 4 + self.x) * mb + u - ma
        if isinstance(u, int):
            return first if u < ma else second
        return jnp.where(u < ma, first, second)

    def owner(self):
        return jnp.logical_and(self.z >= self.z_base, self.z < self.z_base + self.total)

    def z_add_and_gather(self):
        mine = self.z - self.z_base

        @pl.when(self.owner())
        def _():
            for d in range(1, NZ):
                remote(self.r3.at[d - 1], self.r3.at[d - 1], self.s_send.at[13], self.z_recv.at[d - 1],
                       self.device(self.x, self.y, self.z, 1 - self.core)).wait_recv()
            total = self.a3[mine].astype(F32)
            for d in range(NZ - 1):
                total = total + self.r3[d].astype(F32)
            at = self.unit_at(mine)
            self.out[self.core, at] = total.astype(BF)
            for d in (8, 7, 9, 6, 10, 5, 11, 4, 12, 3, 13, 2, 14, 1, 15):
                remote(self.out.at[self.core, at], self.out.at[self.core, at], self.gz_send.at[d - 1],
                       self.g_recv.at[mine],
                       self.device(self.x, self.y, lax.rem(self.z + d, NZ), self.core)).start()

    def z_gather_sent(self):
        mine = self.z - self.z_base

        @pl.when(self.owner())
        def _():
            at = self.unit_at(mine)
            for d in range(1, NZ):
                remote(self.out.at[self.core, at], self.out.at[self.core, at], self.gz_send.at[d - 1],
                       self.g_recv.at[mine],
                       self.device(self.x, self.y, lax.rem(self.z + d, NZ), self.core)).wait_send()

    def gather_second(self):
        for u in range(self.total):
            at = self.unit_at(u)

            @pl.when(self.z != self.z_base + u)
            def _():
                remote(self.out.at[self.core, at], self.out.at[self.core, at], self.gz_send.at[0],
                       self.g_recv.at[u], self.device(self.x, self.y, self.z, 1 - self.core)).wait_recv()
        for part in range(2):
            m = self.m[part]
            ca, cb = self.coords(part)
            at = pl.ds(self.start[part] + (ca * 4 + cb) * m, m)
            for d in (2, 1, 3):
                x, y = self.peer(self.axes(part)[1], d)
                k = part * 3 + d - 1
                self.send(remote(self.out.at[self.core, at], self.out.at[self.core, at], self.g_send.at[k],
                                 self.g_recv.at[9 + k], self.device(x, y, self.z, self.core)))

    def gather_first(self):
        for part in range(2):
            m = self.m[part]
            ca, cb = self.coords(part)
            for d in (1, 3, 2):
                k = part * 3 + d - 1
                there = lax.rem(cb + 4 - d, 4)
                at = pl.ds(self.start[part] + (ca * 4 + there) * m, m)
                remote(self.out.at[self.core, at], self.out.at[self.core, at], self.g_send.at[k],
                       self.g_recv.at[9 + k], self.device(self.x, self.y, self.z, 1 - self.core)).wait_recv()
            at = pl.ds(self.start[part] + ca * 4 * m, 4 * m)
            for d in (2, 1, 3):
                x, y = self.peer(self.axes(part)[0], d)
                k = 6 + part * 3 + d - 1
                self.send(remote(self.out.at[self.core, at], self.out.at[self.core, at], self.g_send.at[k],
                                 self.g_recv.at[9 + k], self.device(x, y, self.z, self.core)))
            self.to_core(part, 0, at)

    def to_core(self, part, d, at):
        k = 12 + part * 4 + d
        self.send(remote(self.out.at[self.core, at], self.out.at[self.core, at], self.g_send.at[k],
                         self.g_recv.at[9 + k], self.device(self.x, self.y, self.z, 1 - self.core)))

    def gather_core(self):
        for d in (1, 3, 2):
            for part in range(2):
                n = 4 * self.m[part]
                ca = self.coords(part)[0]
                k = 6 + part * 3 + d - 1
                at = pl.ds(self.start[part] + lax.rem(ca + 4 - d, 4) * n, n)
                remote(self.out.at[self.core, at], self.out.at[self.core, at], self.g_send.at[k],
                       self.g_recv.at[9 + k], self.device(self.x, self.y, self.z, 1 - self.core)).wait_recv()
                self.to_core(part, d, at)

    def gather_done(self):
        for part in range(2):
            n = 4 * self.m[part]
            ca = self.coords(part)[0]
            for d in range(4):
                k = 12 + part * 4 + d
                at = pl.ds(self.start[part] + lax.rem(ca + 4 - d, 4) * n, n)
                remote(self.out.at[1 - self.core, at], self.out.at[1 - self.core, at], self.g_send.at[k],
                       self.g_recv.at[9 + k], self.device(self.x, self.y, self.z, 1 - self.core)).wait_recv()


def reduce_scratch(ma, mb):
    units = 16 * (ma + mb)
    total = ma + mb
    return [
        pltpu.VMEM((2, units, 16, 128), BF),
        pltpu.VMEM((units, 16, 128), BF),
        pltpu.VMEM((units, 16, 128), BF),
        pltpu.VMEM((3, 4 * ma, 16, 128), BF),
        pltpu.VMEM((3, 4 * mb, 16, 128), BF),
        pltpu.VMEM((4 * ma, 16, 128), BF),
        pltpu.VMEM((4 * mb, 16, 128), BF),
        pltpu.VMEM((3, ma, 16, 128), BF),
        pltpu.VMEM((3, mb, 16, 128), BF),
        pltpu.VMEM((total, 16, 128), BF),
        pltpu.VMEM((NZ - 1, 16, 128), BF),
        pltpu.SemaphoreType.DMA((13 + total,)),
        pltpu.SemaphoreType.DMA((13,)),
        pltpu.SemaphoreType.DMA((NZ - 1,)),
        pltpu.SemaphoreType.DMA((20,)),
        pltpu.SemaphoreType.DMA((9 + 20,)),
        pltpu.SemaphoreType.DMA((NZ - 1,)),
    ]


N_REDUCE = 17
M2 = (5, 4)
M1 = (3, 2)
FIRST_ROWS = ((0, 0, 40), (48, 40, 32))


def edge_scratch(channels):
    return [
        pltpu.VMEM((80, channels), BF),
        pltpu.VMEM((256, channels), BF),
        pltpu.SemaphoreType.DMA((8,)),
        pltpu.SemaphoreType.DMA((8,)),
    ]


def patch_scratch():
    return [
        pltpu.VMEM((32, 9 * C1), BF),
        pltpu.VMEM((2, 32, 3 * C1), BF),
        pltpu.VMEM((4, 16, C1), BF),
        pltpu.VMEM((128, 9 * C1), BF),
        pltpu.VMEM((2, 32, 3 * C1), BF),
        pltpu.VMEM((4, 16, C1), BF),
        pltpu.SemaphoreType.DMA((8,)),
        pltpu.SemaphoreType.DMA((8,)),
    ]


def layer_scratch(channels):
    return [
        pltpu.VMEM((304, channels), F32),
        pltpu.VMEM((384, 3 * channels), BF),
        pltpu.VMEM((416, C2), BF),
        pltpu.VMEM((304, 3 * channels), F32),
        pltpu.VMEM((384, channels), BF),
        pltpu.VMEM((128, channels), BF),
        pltpu.VMEM((128, channels), BF),
        pltpu.SemaphoreType.DMA((8,)),
        pltpu.SemaphoreType.DMA((8,)),
    ]


N_EDGE, N_PATCH, N_LAYER = 4, 8, 9


def step_kernel(*refs):
    (feat_hbm, w1_hbm, w2_hbm, cot_hbm, pick_hbm, flip_hbm, rule_hbm,
     pooled_ref, grad_ref, first_out, second_out) = refs[:11]
    refs = refs[11:]
    edges, refs = refs[:N_EDGE], refs[N_EDGE:]
    patch_refs, refs = refs[:N_PATCH], refs[N_PATCH:]
    layer1, refs = refs[:N_LAYER], refs[N_LAYER:]
    layer2, refs = refs[:N_LAYER], refs[N_LAYER:]
    red2_refs, refs = refs[:N_REDUCE], refs[N_REDUCE:]
    red1_refs, refs = refs[:N_REDUCE], refs[N_REDUCE:]
    (feat_ref, w1, w2, cot_ref, pick_ref, flip_ref, rule_ref, load_sem,
     rules_out, rules_in, rule_send, rule_recv, q_fwd, q_back, q_act, slope1, pre2) = refs
    red2_refs = red2_refs[:11] + (second_out,) + red2_refs[11:]
    red1_refs = red1_refs[:11] + (first_out,) + red1_refs[11:]

    lon, lat = lax.axis_index("lon"), lax.axis_index("lat")
    y = lax.div(lon, 2 * NZ)
    z = lax.div(lax.rem(lon, 2 * NZ), 2)
    x = lax.rem(lon, 2) * 2 + lax.div(lat, 2)
    core = lax.rem(lat, 2)

    def device(x_at, y_at, z_at, core_at):
        return (y_at * (2 * NZ) + z_at * 2 + lax.div(x_at, 2), lax.rem(x_at, 2) * 2 + core_at)

    across = lax.rem(lon + LON // 2, LON)
    below, above = lat == 0, lat == LAT - 1
    vert = (
        (jnp.where(below, across, lon), jnp.where(below, lat, lat - 1)),
        (jnp.where(above, across, lon), jnp.where(above, lat, lat + 1)),
    )
    seen = (jnp.where(below, 0, 1), jnp.where(above, 1, 0))

    def west_of(at):
        return (lax.rem(at[0] + LON - 1, LON), at[1])

    def east_of(at):
        return (lax.rem(at[0] + 1, LON), at[1])

    here = (lon, lat)
    west, east = west_of(here), east_of(here)
    diagonal = [
        (west_of(vert[0]), 2 * seen[0] + 1),
        (east_of(vert[0]), 2 * seen[0]),
        (west_of(vert[1]), 2 * seen[1] + 1),
        (east_of(vert[1]), 2 * seen[1]),
    ]

    loads = [
        pltpu.make_async_copy(src, dst, load_sem.at[n])
        for n, (src, dst) in enumerate((
            (pick_hbm, pick_ref), (flip_hbm, flip_ref), (rule_hbm, rule_ref), (feat_hbm, feat_ref),
            (w1_hbm, w1), (cot_hbm, cot_ref), (w2_hbm, w2),
        ))
    ]
    for load in loads:
        load.start()

    barrier = pltpu.get_barrier_semaphore()
    partners = [vert[0], vert[1], west, east] + [d[0] for d in diagonal]
    partners.append(device(x, y, z, 1 - core))
    for d in (1, 2, 3):
        partners.append(device(lax.rem(x + d, NX), y, z, core))
        partners.append(device(x, lax.rem(y + d, NY), z, core))
    for d in range(1, NZ):
        partners.append(device(x, y, lax.rem(z + d, NZ), core))
    for partner in partners:
        pl.semaphore_signal(barrier, inc=1, device_id=partner, device_id_type=MESH)

    for load in loads[:3]:
        load.wait()
    picks = [pick_ref[0, 0, s] for s in range(2)]
    flips = [flip_ref[0, 0, s] for s in range(2)]
    rules = [rule_ref[0, 0, k] for k in range(4)]

    row8 = iota((8, 128), 0)
    rules_out[...] = jnp.where(
        row8 == 0, picks[0], jnp.where(row8 == 1, flips[0], jnp.where(row8 == 2, picks[1], flips[1]))
    )

    p, cell = iota((80, 256), 0), iota((80, 256), 1)
    k = p & 15
    want = jnp.where(
        p < 16, k, jnp.where(p < 32, 240 + k, jnp.where(p < 48, 16 * k, jnp.where(p < 64, 16 * k + 15, (
            jnp.where(k == 0, 0, jnp.where(k == 1, 15, jnp.where(k == 2, 240, jnp.where(k == 3, 255, -1))))
        ))))
    )
    take_edges = hot(cell == want).astype(BF)

    loads[3].wait()
    edges[0][...] = mm(take_edges, feat_ref[...]).astype(BF)
    edges[1][224:256, :] = jnp.zeros((32, C1), BF)
    layer1[1][288:384, :] = jnp.zeros((96, 3 * C1), BF)

    pl.semaphore_wait(barrier, len(partners))

    def edge_sends():
        out, got, send, recv = edges
        copies = []
        for side in range(2):
            copies.append(remote(out.at[0:64], got.at[pl.ds(pl.multiple_of(64 * seen[side], 64), 64)],
                                 send.at[side], recv.at[seen[side]], vert[side]))
        copies.append(remote(out.at[32:48], got.at[144:160], send.at[2], recv.at[3], west))
        copies.append(remote(out.at[48:64], got.at[128:144], send.at[3], recv.at[2], east))
        for i, (target, slot) in enumerate(diagonal):
            copies.append(remote(out.at[64:80], got.at[pl.ds(pl.multiple_of(160 + 16 * slot, 16), 16)],
                                 send.at[4 + i], recv.at[4 + slot], target))
        for copy in copies:
            copy.start()
        return copies

    def edge_waits():
        out, got, send, recv = edges
        spots = [(0, 64), (64, 64), (128, 16), (144, 16), (160, 16), (176, 16), (192, 16), (208, 16)]
        for i, (at, size) in enumerate(spots):
            remote(out.at[0:size], got.at[at:at + size], send.at[i], recv.at[i], west).wait_recv()

    rule_copies = []
    for i, (target, slot) in enumerate(((vert[0], seen[0]), (vert[1], seen[1]), (west, 3), (east, 2))):
        rule_copies.append(remote(rules_out, rules_in.at[slot], rule_send.at[i], rule_recv.at[slot], target))
    for copy in rule_copies:
        copy.start()
    sent = edge_sends()

    r, c = iota((288, 256), 0), iota((288, 256), 1)
    j, i = r & 15, r >> 4
    want = jnp.where(j == 0, 127 + i, jnp.where(j == 15, 143 + i, -1))
    q_fwd[0:288, :] = hot(c == want).astype(BF)
    r, c = iota((32, 256), 0), iota((32, 256), 1)
    k, north = r & 15, r >= 16
    flip = jnp.where(north, flips[1], flips[0])
    pick = jnp.where(north, picks[1], picks[0])
    want = jnp.where(north, 64, 0) + 16 * pick + jnp.where(flip == 1, 15 - k, k)
    q_fwd[288:320, :] = hot(c == want).astype(BF)

    def halo_cells(p, q):
        block, k = p >> 4, p & 15
        low, high = k == 0, k == 15
        corner_at = (0, 15, 272, 287)
        want = jnp.where(block == 0, 288 + k, jnp.where(block == 1, 304 + k, jnp.where(
            block == 2, 16 * k + 16, jnp.where(block == 3, 16 * k + 31, -1))))
        half = jnp.full_like(want, -1)
        ends = ((0, 1), (2, 3), (0, 2), (1, 3))
        for b in range(4):
            first, second = ends[b]
            half = jnp.where((block == b) & low & (rules[first] == 1), corner_at[first], half)
            half = jnp.where((block == b) & high & (rules[second] == 1), corner_at[second], half)
            want = jnp.where((block == 4 + b) & low & (rules[b] != 1), corner_at[b], want)
        return (hot(q == want) + hot(q == half, 0.5)).astype(BF)

    q_back[...] = halo_cells(iota((128, 384), 0), iota((128, 384), 1))
    q_act[...] = halo_cells(iota((320, 128), 1), iota((320, 128), 0))

    for layer in (layer1, layer2):
        g_pad = layer[2]
        g_pad[0:32, :] = jnp.zeros((32, C2), BF)
        g_pad[288:416, :] = jnp.zeros((128, C2), BF)
        layer[4][320:384, :] = jnp.zeros((64, layer[4].shape[1]), BF)

    red2 = Reduce(M2, 0, red2_refs, (x, y, z, core, device))
    red1 = Reduce(M1, 9, red1_refs, (x, y, z, core, device))
    red1.halves[:, 40:48] = jnp.zeros((2, 8, 16, 128), BF)

    for slot in range(4):
        remote(rules_out, rules_in.at[slot], rule_send.at[slot], rule_recv.at[slot], west).wait_recv()

    r, c = iota((16, 256), 0), iota((16, 256), 1)
    for side in range(2):
        def source(position):
            return 64 * side + 16 * picks[side] + jnp.where(flips[side] == 1, 15 - position, position)

        rows = 2 * side
        w_pick, w_flip = wide(rules_in[2, rows:rows + 1, :], 2), wide(rules_in[2, rows + 1:rows + 2, :], 2)
        e_pick, e_flip = wide(rules_in[3, rows:rows + 1, :], 2), wide(rules_in[3, rows + 1:rows + 2, :], 2)
        w_at = 160 + 32 * side + corner_slot(w_pick, jnp.where(w_flip == 1, 0, 1))
        e_at = 176 + 32 * side + corner_slot(e_pick, jnp.where(e_flip == 1, 1, 0))
        w_rule, e_rule = rules[2 * side] == 1, rules[2 * side + 1] == 1
        shape = (16, 256)
        w_main = jnp.where(w_rule, jnp.full(shape, -1), jnp.broadcast_to(w_at, shape))
        e_main = jnp.where(e_rule, jnp.full(shape, -1), jnp.broadcast_to(e_at, shape))
        w_a, w_c = jnp.where(w_rule, source(0), -1), jnp.where(w_rule, 128 + 15 * side, -1)
        e_a, e_c = jnp.where(e_rule, source(15), -1), jnp.where(e_rule, 144 + 15 * side, -1)
        w_row = hot(c == w_main) + hot(c == w_a, 0.5) + hot(c == w_c, 0.5)
        e_row = hot(c == e_main) + hot(c == e_a, 0.5) + hot(c == e_c, 0.5)
        values = jnp.where(r == 0, w_row, jnp.where(r == 15, e_row, 0.0))
        q_fwd[272 * side:272 * side + 16, :] = values.astype(BF)

    face = (jnp.where(below, 0, 1), jnp.where(above, 1, 0))
    facing = []
    for side in range(2):
        south = face[side] == 0
        facing.append((
            jnp.where(south, rules_in[side, 0:1, 0:128], rules_in[side, 2:3, 0:128]),
            jnp.where(south, rules_in[side, 1:2, 0:128], rules_in[side, 3:4, 0:128]),
        ))
    p = iota((1, 128), 1)
    block, k = p >> 4, p & 15
    on_north = (block == 1) | (block >= 6)
    pick = jnp.where(on_north, facing[1][0], facing[0][0])
    flip = jnp.where(on_north, facing[1][1], facing[0][1])
    position = jnp.where(block < 2, k, jnp.where((block & 1) == 1, 15, 0))
    target = edge_cell(pick, flip, position)
    target = jnp.where(block == 2, 16 * k + 15, jnp.where(block == 3, 16 * k, target))
    target = jnp.where((block >= 4) & (k != 0), -1, target)
    place_grads = hot(iota((256, 128), 0) == target).astype(BF)

    r, c = iota((32, 256), 0), iota((32, 256), 1)
    pick = jnp.where(r < 16, wide(facing[0][0], 2), wide(facing[1][0], 2))
    flip = jnp.where(r < 16, wide(facing[0][1], 2), wide(facing[1][1], 2))
    take_cells = hot(c == edge_cell(pick, flip, r & 15)).astype(BF)
    r, c = iota((64, 384), 0), iota((64, 384), 1)
    row = r & 31
    take_strips = hot((row < 18) & (c == 16 * row + jnp.where(r < 32, 15, 0))).astype(BF)
    tap, which = r & 15, r >> 4
    tap_row = (tap * 11) >> 5
    pick = jnp.where(which < 2, wide(facing[0][0], 3), wide(facing[1][0], 3))
    flip = jnp.where(which < 2, wide(facing[0][1], 3), wide(facing[1][1], 3))
    at = 16 * tap_row + edge_cell(pick, flip, jnp.where((which & 1) == 1, 15, 0))
    take_corners = [
        hot((tap < 9) & (tap - 3 * tap_row == dw) & (c == at)).astype(BF) for dw in range(3)
    ]

    def patch_sends():
        cells, strips, corners, got_cells, got_strips, got_corners, send, recv = patch_refs
        padded = layer1[1]
        for dh in range(3):
            cells[:, 384 * dh:384 * dh + 384] = mm(take_cells, padded[16 * dh:16 * dh + 256, :]).astype(BF)
        strips[...] = mm(take_strips, padded[...]).astype(BF).reshape(2, 32, 3 * C1)
        values = mm(take_corners[0], padded[:, 0:C1])
        for dw in (1, 2):
            values = values + mm(take_corners[dw], padded[:, dw * C1:(dw + 1) * C1])
        corners[...] = values.astype(BF).reshape(4, 16, C1)
        copies = []
        for side in range(2):
            copies.append(remote(cells.at[16 * side:16 * side + 16],
                                 got_cells.at[pl.ds(pl.multiple_of(16 * seen[side], 16), 16)],
                                 send.at[side], recv.at[seen[side]], vert[side]))
        copies.append(remote(strips.at[0], got_strips.at[0], send.at[2], recv.at[2], east))
        copies.append(remote(strips.at[1], got_strips.at[1], send.at[3], recv.at[3], west))
        for i, (target_at, slot) in enumerate(diagonal):
            copies.append(remote(corners.at[i], got_corners.at[slot], send.at[4 + i], recv.at[4 + slot], target_at))
        for copy in copies:
            copy.start()
        return copies

    def patch_waits():
        cells, strips, corners, got_cells, got_strips, got_corners, send, recv = patch_refs
        for i in range(2):
            remote(cells.at[0:16], got_cells.at[16 * i:16 * i + 16], send.at[i], recv.at[i], west).wait_recv()
            remote(strips.at[i], got_strips.at[i], send.at[2 + i], recv.at[2 + i], west).wait_recv()
        r, c = iota((32, 64), 0), iota((32, 64), 1)
        both = got_strips[...].reshape(64, 3 * C1)
        for dh in range(3):
            spread_rows = hot(c == jnp.where(r < 16, r, r + 16) + dh).astype(BF)
            got_cells[32:64, 384 * dh:384 * dh + 384] = mm(spread_rows, both).astype(BF)
        for i in range(4):
            remote(corners.at[i], got_corners.at[i], send.at[4 + i], recv.at[4 + i], west).wait_recv()
        r, c = iota((64, 64), 0), iota((64, 64), 1)
        taps = got_corners[...].reshape(64, C1)
        for tap in range(9):
            first_row = hot(((r & 15) == 0) & (c == r + tap)).astype(BF)
            got_cells[64:128, C1 * tap:C1 * tap + C1] = mm(first_row, taps).astype(BF)

    def pad_tile(layer, tile, cells, channels):
        ext, padded = layer[:2]
        south, north = cells[288:304], cells[304:320]
        ext[8:24, :] = south
        ext[24:280, :] = tile.astype(F32)
        ext[280:296, :] = north
        j = iota((288, channels), 0) & 15
        padded[0:288, 0:channels] = jnp.where(j == 0, cells[0:288], ext[7:295, :]).astype(BF)
        padded[0:288, channels:2 * channels] = ext[8:296, :].astype(BF)
        padded[0:288, 2 * channels:] = jnp.where(j == 15, cells[0:288], ext[9:297, :]).astype(BF)

    def convolve(layer, weight):
        padded = layer[1]
        total = mm(padded[0:256, :], weight[0])
        for dh in (1, 2):
            total = total + mm(padded[16 * dh:16 * dh + 256, :], weight[dh])
        return total

    def input_side(layer, weight, channels):
        g_pad, by_shift, leaving, out = layer[2:6]
        total = mm_nt(g_pad[32:320, :], weight[0])
        for dh in (1, 2):
            at = 32 - 16 * dh
            total = total + mm_nt(g_pad[at:at + 288, :], weight[dh])
        by_shift[8:296, :] = total
        j = iota((288, channels), 0) & 15
        centre = by_shift[8:296, channels:2 * channels]
        centre = centre + jnp.where(j == 15, 0.0, by_shift[9:297, 0:channels])
        centre = centre + jnp.where(j == 0, 0.0, by_shift[7:295, 2 * channels:])
        centre = centre.astype(BF)
        sides = jnp.where(j == 0, by_shift[8:296, 0:channels], by_shift[8:296, 2 * channels:])
        sides = jnp.where((j == 0) | (j == 15), sides, 0.0)
        leaving[0:288, :] = sides.astype(BF)
        leaving[288:304, :] = centre[0:16]
        leaving[304:320, :] = centre[272:288]
        out[...] = mm(q_back[...], leaving[...]).astype(BF)
        return centre[16:272]

    def grad_sends(layer):
        out, got, send, recv = layer[5:9]
        copies = []
        for side in range(2):
            copies.append(remote(out.at[16 * side:16 * side + 16],
                                 got.at[pl.ds(pl.multiple_of(16 * seen[side], 16), 16)],
                                 send.at[side], recv.at[seen[side]], vert[side]))
        copies.append(remote(out.at[32:48], got.at[32:48], send.at[2], recv.at[2], west))
        copies.append(remote(out.at[48:64], got.at[48:64], send.at[3], recv.at[3], east))
        for i, (target_at, slot) in enumerate(diagonal):
            copies.append(remote(out.at[64 + 16 * i:80 + 16 * i],
                                 got.at[pl.ds(pl.multiple_of(64 + 16 * slot, 16), 16)],
                                 send.at[4 + i], recv.at[4 + slot], target_at))
        for copy in copies:
            copy.start()
        return copies

    def grad_waits(layer):
        out, got, send, recv = layer[5:9]
        for i in range(8):
            remote(out.at[0:16], got.at[16 * i:16 * i + 16], send.at[i], recv.at[i], west).wait_recv()

    def weight_grads(halves, channels, spots, pairs):
        units = 3 * channels // 16
        for dh in range(3):
            block = None
            for cells, gradient in pairs(dh):
                part = mm_tn(cells, gradient)
                block = part if block is None else block + part
            block = block.astype(BF)
            for h in range(2):
                values = block[:, 128 * h:128 * h + 128].reshape(units, 16, 128)
                for first, count, to in spots[dh]:
                    halves[h, to:to + count] = values[first:first + count]

    edge_waits()
    pad_tile(layer1, feat_ref[...], mm(q_fwd[...], edges[1][...]), C1)
    sent += patch_sends()
    loads[4].wait()
    pre1 = convolve(layer1, w1)
    cdf1 = normal_cdf(pre1)
    act1 = (pre1 * cdf1).astype(BF)
    slope1[...] = gelu_slope(pre1, cdf1)
    r, c = iota((256, 64), 0), iota((256, 64), 1)
    spread = hot(c == 8 * (r >> 5) + ((r & 15) >> 1), 0.25).astype(BF)
    loads[5].wait()
    cot = mm(spread, cot_ref[...])
    loads[6].wait()

    patch_waits()
    patches = patch_refs[3]
    halo_pre = mm(patches[:, 0:384], w1[0])
    for dh in (1, 2):
        halo_pre = halo_pre + mm(patches[:, 384 * dh:384 * dh + 384], w1[dh])
    halo_cdf = normal_cdf(halo_pre)
    halo_act = (halo_pre * halo_cdf).astype(BF)
    pad_tile(layer2, act1, mm(q_act[...], halo_act), C2)
    second_pre = convolve(layer2, w2)
    cdf2 = normal_cdf(second_pre)
    grad2 = (cot * gelu_slope(second_pre, cdf2)).astype(BF)
    layer2[2][32:288, :] = grad2
    pre2[...] = second_pre * cdf2
    weight_grads(red2.halves, C2, [[(0, 48, 48 * dh)] for dh in range(3)],
                 lambda dh: [(layer2[1][16 * dh:16 * dh + 256, :], grad2)])
    red2.core_send()
    centre2 = input_side(layer2, w2, C2)
    sent += grad_sends(layer2)

    own = (centre2.astype(F32) * slope1[...]).astype(BF)
    leaving = (layer2[5][...].astype(F32) * gelu_slope(halo_pre, halo_cdf)).astype(BF)
    weight_grads(red1.halves, C1, [[(0, 24, 0)], [(0, 16, 24), (16, 8, 48)], [(0, 24, 56)]],
                 lambda dh: [(layer1[1][16 * dh:16 * dh + 256, :], own),
                             (patches[:, 384 * dh:384 * dh + 384], leaving)])
    red1.core_send()
    red2.core_add()
    red2.first_send()
    red1.core_add()
    red1.first_send()

    r, c = iota((64, 256), 0), iota((64, 256), 1)
    gather_cells = hot(r == 8 * (c >> 5) + ((c & 15) >> 1), 0.25).astype(BF)
    act2 = pre2[...]
    high = act2.astype(BF)
    low = (act2 - high.astype(F32)).astype(BF)
    pooled_ref[...] = (mm(gather_cells, high) + mm(gather_cells, low)).astype(BF)

    red2.first_add()
    red2.second_send()
    red1.first_add()
    red1.second_send()

    grad_waits(layer2)
    first_grad = centre2.astype(F32) + mm(place_grads, layer2[6][...])
    layer1[2][32:288, :] = (first_grad * slope1[...]).astype(BF)
    centre1 = input_side(layer1, w1, C1)
    sent += grad_sends(layer1)

    red2.second_add()
    red2.z_send()
    red1.second_add()
    red1.z_send()

    grad_waits(layer1)
    grad_ref[...] = (centre1.astype(F32) + mm(place_grads, layer1[6][...])).astype(BF)

    red2.z_add_and_gather()
    red1.z_add_and_gather()
    red2.gather_second()
    red1.gather_second()
    red2.gather_first()
    red1.gather_first()
    red2.gather_core()
    red1.gather_core()
    red2.gather_done()
    red1.gather_done()

    for copy in sent + rule_copies:
        copy.wait_send()
    for red in (red2, red1):
        red.finish()
        red.z_send_done()
        red.z_gather_sent()


def finish_kernel(pooled_ref, grad_ref, first_ref, second_ref, pooled_out, grad_out, first_out, second_out,
                  first_rows, second_rows, sems):
    copies = [pltpu.make_async_copy(pooled_ref, pooled_out, sems.at[0]),
              pltpu.make_async_copy(grad_ref, grad_out, sems.at[1])]
    for copy in copies:
        copy.start()

    def squares(ref, at, count, total):
        def body(i, total):
            values = ref[:, pl.ds(at + i * 8, 8)].astype(F32)
            return total + jnp.sum(values * values, axis=(0, 1))

        return lax.fori_loop(0, count // 8, body, total)

    total = squares(second_ref, 0, 144, jnp.zeros((16, 128), F32))
    for at, _, count in FIRST_ROWS:
        total = squares(first_ref, at, count, total)
    squared = jnp.sum(jnp.sum(total, axis=0, keepdims=True), axis=1, keepdims=True)
    target_norm = math.sqrt(9.0 * (C1 + C2) * C2)
    scale = jnp.broadcast_to(target_norm / jnp.sqrt(squared + 1e-06), (16, 128))

    def write(ref, at, to, count, out):
        def body(i, carry):
            for h in range(2):
                values = ref[h, pl.ds(at + i * 8, 8)].astype(F32) * scale
                rows = pl.ds(pl.multiple_of((to + i * 8) * 16, 128), 128)
                out[rows, 128 * h:128 * h + 128] = values.astype(BF).reshape(128, 128)
            return carry

        lax.fori_loop(0, count // 8, body, 0)

    jobs = [(second_ref, n * 48, n * 48, 48, second_rows, second_out) for n in range(3)]
    jobs += [(first_ref, at, to, count, first_rows, first_out) for at, to, count in FIRST_ROWS]
    for n, (ref, at, to, count, rows, out) in enumerate(jobs):
        write(ref, at, to, count, rows)
        span = pl.ds(16 * to, 16 * count)
        copies.append(pltpu.make_async_copy(rows.at[span], out.at[span], sems.at[2 + n]))
        copies[-1].start()
    for copy in copies:
        copy.wait()


def on_device(features, conv_first, conv_second, cotangent, edge_pick, edge_flip, corner_rule):
    vmem = pl.BlockSpec(memory_space=pltpu.VMEM)
    hbm = pl.BlockSpec(memory_space=pltpu.HBM)
    pooled, input_grad, first, second = pl.pallas_call(
        step_kernel,
        out_shape=(
            jax.ShapeDtypeStruct((64, C2), BF),
            jax.ShapeDtypeStruct((256, C1), BF),
            jax.ShapeDtypeStruct((2, 16 * sum(M1), 16, 128), BF),
            jax.ShapeDtypeStruct((2, 16 * sum(M2), 16, 128), BF),
        ),
        in_specs=[hbm] * 7,
        out_specs=[vmem] * 4,
        scratch_shapes=(
            edge_scratch(C1)
            + patch_scratch()
            + layer_scratch(C1)
            + layer_scratch(C2)
            + reduce_scratch(*M2)
            + reduce_scratch(*M1)
            + [
                pltpu.VMEM((256, C1), BF),
                pltpu.VMEM((3, 3 * C1, C2), BF),
                pltpu.VMEM((3, 3 * C2, C2), BF),
                pltpu.VMEM((64, C2), BF),
                pltpu.SMEM((1, 1, 2), jnp.int32),
                pltpu.SMEM((1, 1, 2), jnp.int32),
                pltpu.SMEM((1, 1, 4), jnp.int32),
                pltpu.SemaphoreType.DMA((7,)),
                pltpu.VMEM((8, 128), jnp.int32),
                pltpu.VMEM((4, 8, 128), jnp.int32),
                pltpu.SemaphoreType.DMA((4,)),
                pltpu.SemaphoreType.DMA((4,)),
                pltpu.VMEM((320, 256), BF),
                pltpu.VMEM((128, 384), BF),
                pltpu.VMEM((320, 128), BF),
                pltpu.VMEM((256, C2), F32),
                pltpu.VMEM((256, C2), F32),
            ]
        ),
        compiler_params=pltpu.CompilerParams(
            collective_id=0, has_side_effects=True, vmem_limit_bytes=32 * 1024 * 1024
        ),
        name="level_step",
    )(*(
        pltpu.with_memory_space_constraint(value, pltpu.HBM)
        for value in (
            features.reshape(256, C1),
            conv_first.reshape(3, 3 * C1, C2),
            conv_second.reshape(3, 3 * C2, C2),
            cotangent.reshape(64, C2),
            edge_pick,
            edge_flip,
            corner_rule,
        )
    ))
    pooled, input_grad, first, second = pl.pallas_call(
        finish_kernel,
        out_shape=(
            jax.ShapeDtypeStruct((64, C2), BF),
            jax.ShapeDtypeStruct((256, C1), BF),
            jax.ShapeDtypeStruct((9 * C1, C2), BF),
            jax.ShapeDtypeStruct((9 * C2, C2), BF),
        ),
        in_specs=[vmem] * 4,
        out_specs=[hbm] * 4,
        scratch_shapes=[
            pltpu.VMEM((9 * C1, C2), BF),
            pltpu.VMEM((9 * C2, C2), BF),
            pltpu.SemaphoreType.DMA((7,)),
        ],
        compiler_params=pltpu.CompilerParams(vmem_limit_bytes=16 * 1024 * 1024),
        name="scale_outputs",
    )(pooled, input_grad, first, second)
    return (
        pooled.reshape(1, 1, 8, 8, C2),
        input_grad.reshape(1, 1, 16, 16, C1),
        first.reshape(3, 3, C1, C2),
        second.reshape(3, 3, C2, C2),
    )


def solution(mesh):
    return jax.shard_map(
        on_device,
        mesh=mesh,
        in_specs=(
            P("lon", "lat", None, None, None),
            P(),
            P(),
            P("lon", "lat", None, None, None),
            P("lon", "lat", None),
            P("lon", "lat", None),
            P("lon", "lat", None),
        ),
        out_specs=(P("lon", "lat", None, None, None), P("lon", "lat", None, None, None), P(), P()),
        check_vma=False,
    )
```

```python
import math

import jax
import jax.numpy as jnp
from jax import lax
from jax.experimental import pallas as pl
from jax.experimental.pallas import tpu as pltpu
from jax.sharding import PartitionSpec as P

MESH = pl.DeviceIdType.MESH
BF = jnp.bfloat16
F32 = jnp.float32
NX, NY, NZ = 4, 4, 16
LON, LAT = 2 * NY * NZ, 4
C1, C2 = 128, 256


def normal_cdf(values):
    return 0.5 * (1.0 + lax.erf(values * (1.0 / math.sqrt(2.0))))


def gelu_slope(values, cdf):
    return cdf + values * jnp.exp(-0.5 * values * values) * (1.0 / math.sqrt(2.0 * math.pi))


def iota(shape, dim):
    return lax.broadcasted_iota(jnp.int32, shape, dim)


def hot(cond, value=1.0):
    return jnp.where(cond, jnp.float32(value), jnp.float32(0.0))


def wide(row, count):
    return jnp.concatenate([row] * count, axis=1)


def edge_cell(edge, flip, position):
    at = jnp.where(flip == 1, 15 - position, position)
    return jnp.where(edge == 0, at, jnp.where(edge == 1, 240 + at, jnp.where(edge == 2, 16 * at, 16 * at + 15)))


def mm(a, b):
    return jnp.dot(a, b, preferred_element_type=F32)


def mm_nt(a, b):
    return lax.dot_general(a, b, (((1,), (1,)), ((), ())), preferred_element_type=F32)


def mm_tn(a, b):
    return lax.dot_general(a, b, (((0,), (0,)), ((), ())), preferred_element_type=F32)


def remote(src, dst, send_sem, recv_sem, device):
    return pltpu.make_async_remote_copy(
        src_ref=src, dst_ref=dst, send_sem=send_sem, recv_sem=recv_sem,
        device_id=device, device_id_type=MESH,
    )


def corner_slot(edge, at_end):
    return jnp.where(
        edge == 0, at_end, jnp.where(edge == 1, 2 + at_end, jnp.where(edge == 2, 2 * at_end, 1 + 2 * at_end))
    )


class Reduce:
    def __init__(self, m, refs, place):
        self.m = m
        self.total = m[0] + m[1]
        self.start = (0, 16 * m[0])
        (self.halves, self.r0, self.a1, r1a, r1b, a2a, a2b, r2a, r2b, self.a3, self.n3, self.f3, self.out,
         self.s_send, self.s_recv, self.g_send, self.g_recv) = refs
        self.r1, self.a2, self.r2 = (r1a, r1b), (a2a, a2b), (r2a, r2b)
        self.x, self.y, self.z, self.core, self.device = place
        self.near, self.far = lax.rem(self.z, 4), lax.div(self.z, 4)
        self.pending = []
        self.pieces = []
        self.waited = 0

    def other_core(self):
        return self.device(self.x, self.y, self.z, 1 - self.core)

    def peer(self, axis, d):
        x = lax.rem(self.x + d, NX) if axis == "x" else self.x
        y = lax.rem(self.y + d, NY) if axis == "y" else self.y
        return self.device(x, y, self.z, self.core)

    def axes(self, part):
        return ("x", "y") if part == 0 else ("y", "x")

    def coords(self, part):
        return (self.x, self.y) if part == 0 else (self.y, self.x)

    def send(self, copy):
        copy.start()
        self.pending.append(copy)

    def received(self, ref, sem):
        remote(ref, ref, self.s_send.at[0], sem, self.other_core()).wait_recv()

    def finish(self):
        for copy in self.pending:
            copy.wait_send()

        @pl.when(self.near < self.total // 2)
        def _():
            for copy in self.near_copies():
                copy.wait_send()

    def core_send(self, at, count):
        k = len(self.pieces)
        self.pieces.append((at, count))
        self.send(remote(self.halves.at[1 - self.core, at:at + count], self.r0.at[at:at + count],
                         self.s_send.at[k], self.s_recv.at[k], self.other_core()))

    def core_add(self):
        for part in range(2):
            n = 4 * self.m[part]
            mine = self.coords(part)[0]
            while self.waited < len(self.pieces) and self.pieces[self.waited][0] < self.start[part] + 4 * n:
                at, count = self.pieces[self.waited]
                self.received(self.r0.at[at:at + count], self.s_recv.at[self.waited])
                self.waited += 1
            for d in (2, 1, 3, 0):
                at = pl.ds(self.start[part] + lax.rem(mine + d, 4) * n, n)
                self.a1[at] = (self.halves[self.core, at].astype(F32) + self.r0[at].astype(F32)).astype(BF)
                if d:
                    k = 3 + part * 3 + d - 1
                    self.send(remote(self.a1.at[at], self.r1[part].at[d - 1], self.s_send.at[k], self.s_recv.at[k],
                                     self.peer(self.axes(part)[0], d)))

    def first_add(self):
        for part in range(2):
            m = self.m[part]
            r1, a2, r2 = self.r1[part], self.a2[part], self.r2[part]
            ca, cb = self.coords(part)
            for d in (1, 3, 2):
                self.received(r1.at[d - 1], self.s_recv.at[3 + part * 3 + d - 1])
            for d in (2, 1, 3, 0):
                block = lax.rem(cb + d, 4)
                at = pl.ds(block * m, m)
                total = self.a1[pl.ds(self.start[part] + (ca * 4 + block) * m, m)].astype(F32)
                for e in range(3):
                    total = total + r1[e, at].astype(F32)
                a2[at] = total.astype(BF)
                if d:
                    k = 9 + part * 3 + d - 1
                    self.send(remote(a2.at[at], r2.at[d - 1], self.s_send.at[k], self.s_recv.at[k],
                                     self.peer(self.axes(part)[1], d)))

    def second_add(self):
        for part in range(2):
            m = self.m[part]
            a2, r2 = self.a2[part], self.r2[part]
            cb = self.coords(part)[1]
            for d in (1, 3, 2):
                self.received(r2.at[d - 1], self.s_recv.at[9 + part * 3 + d - 1])
            total = a2[pl.ds(cb * m, m)].astype(F32)
            for e in range(3):
                total = total + r2[e].astype(F32)
            self.a3[part * self.m[0]:part * self.m[0] + m] = total.astype(BF)
        for d in (2, 1, 3):
            owner = lax.rem(self.near + d, 4)
            self.send(remote(self.a3.at[pl.ds(2 * owner, 2)], self.n3.at[d - 1], self.s_send.at[14 + d],
                             self.s_recv.at[14 + d], self.device(self.x, self.y, 4 * self.far + owner, self.core)))

    def near_add(self):
        for d in (1, 3, 2):
            self.received(self.n3.at[d - 1], self.s_recv.at[14 + d])
        total = self.a3[pl.ds(2 * self.near, 2)].astype(F32)
        for e in range(3):
            total = total + self.n3[e].astype(F32)
        self.f3[self.far] = total.astype(BF)
        for d in (2, 1, 3):
            self.send(remote(self.f3.at[self.far], self.f3.at[self.far], self.s_send.at[17 + d], self.s_recv.at[17 + d],
                             self.device(self.x, self.y, 4 * lax.rem(self.far + d, 4) + self.near, self.core)))

    def unit_at(self, u):
        ma, mb = self.m
        first = (self.x * 4 + self.y) * ma + u
        second = self.start[1] + (self.y * 4 + self.x) * mb + u - ma
        return jnp.where(u < ma, first, second)

    def near_copies(self):
        at = pl.ds(self.unit_at(2 * self.near), 2)
        return [
            remote(self.out.at[self.core, at], self.out.at[self.core, at], self.g_send.at[19 + d], self.g_recv.at[19 + d],
                   self.device(self.x, self.y, 4 * self.far + lax.rem(self.near + d, 4), self.core))
            for d in (2, 1, 3)
        ]

    def far_add(self):
        for d in (1, 3, 2):
            self.received(self.f3.at[lax.rem(self.far + 4 - d, 4)], self.s_recv.at[17 + d])

        @pl.when(self.near < self.total // 2)
        def _():
            total = self.f3[0].astype(F32)
            for e in range(1, 4):
                total = total + self.f3[e].astype(F32)
            self.out[self.core, pl.ds(self.unit_at(2 * self.near), 2)] = total.astype(BF)
            for copy in self.near_copies():
                copy.start()

    def gather_second(self):
        for d in (1, 3, 2):
            owner = lax.rem(self.near + 4 - d, 4)

            @pl.when(owner < self.total // 2)
            def _():
                self.received(self.out.at[self.core, pl.ds(self.unit_at(2 * owner), 2)], self.g_recv.at[19 + d])

        for part in range(2):
            m = self.m[part]
            ca, cb = self.coords(part)
            at = pl.ds(self.start[part] + (ca * 4 + cb) * m, m)
            for d in (2, 1, 3):
                k = part * 3 + d - 1
                self.send(remote(self.out.at[self.core, at], self.out.at[self.core, at], self.g_send.at[k],
                                 self.g_recv.at[k], self.peer(self.axes(part)[1], d)))

    def gather_first(self):
        for part in range(2):
            m = self.m[part]
            ca, cb = self.coords(part)
            for d in (1, 3, 2):
                at = pl.ds(self.start[part] + (ca * 4 + lax.rem(cb + 4 - d, 4)) * m, m)
                self.received(self.out.at[self.core, at], self.g_recv.at[part * 3 + d - 1])
            at = pl.ds(self.start[part] + ca * 4 * m, 4 * m)
            for d in (2, 1, 3):
                k = 6 + part * 3 + d - 1
                self.send(remote(self.out.at[self.core, at], self.out.at[self.core, at], self.g_send.at[k],
                                 self.g_recv.at[k], self.peer(self.axes(part)[0], d)))
            self.to_core(part, 0, at)

    def to_core(self, part, d, at):
        k = 12 + part * 4 + d
        self.send(remote(self.out.at[self.core, at], self.out.at[self.core, at], self.g_send.at[k],
                         self.g_recv.at[k], self.other_core()))

    def block_of(self, part, d):
        n = 4 * self.m[part]
        return pl.ds(self.start[part] + lax.rem(self.coords(part)[0] + 4 - d, 4) * n, n)

    def gather_core(self):
        for d in (1, 3, 2):
            for part in range(2):
                at = self.block_of(part, d)
                self.received(self.out.at[self.core, at], self.g_recv.at[6 + part * 3 + d - 1])
                self.to_core(part, d, at)

    def gather_done(self):
        for d in (0, 1, 3, 2):
            for part in range(2):
                at = self.block_of(part, d)
                self.received(self.out.at[1 - self.core, at], self.g_recv.at[12 + part * 4 + d])


def reduce_scratch(ma, mb):
    units = 16 * (ma + mb)
    return [
        pltpu.VMEM((2, units, 16, 128), BF),
        pltpu.VMEM((units, 16, 128), BF),
        pltpu.VMEM((units, 16, 128), BF),
        pltpu.VMEM((3, 4 * ma, 16, 128), BF),
        pltpu.VMEM((3, 4 * mb, 16, 128), BF),
        pltpu.VMEM((4 * ma, 16, 128), BF),
        pltpu.VMEM((4 * mb, 16, 128), BF),
        pltpu.VMEM((3, ma, 16, 128), BF),
        pltpu.VMEM((3, mb, 16, 128), BF),
        pltpu.VMEM((8, 16, 128), BF),
        pltpu.VMEM((3, 2, 16, 128), BF),
        pltpu.VMEM((4, 2, 16, 128), BF),
        pltpu.SemaphoreType.DMA((21,)),
        pltpu.SemaphoreType.DMA((21,)),
        pltpu.SemaphoreType.DMA((23,)),
        pltpu.SemaphoreType.DMA((23,)),
    ]


N_REDUCE = 16
MA, MB = (4, 4), (4, 2)
A_UNITS, B_UNITS, FIRST_UNITS, LAST_UNITS = 128, 96, 72, 16


def edge_scratch(channels):
    return [
        pltpu.VMEM((80, channels), BF),
        pltpu.VMEM((256, channels), BF),
        pltpu.SemaphoreType.DMA((8,)),
        pltpu.SemaphoreType.DMA((8,)),
    ]


def patch_scratch():
    return [
        pltpu.VMEM((32, 9 * C1), BF),
        pltpu.VMEM((2, 32, 3 * C1), BF),
        pltpu.VMEM((4, 16, C1), BF),
        pltpu.VMEM((128, 9 * C1), BF),
        pltpu.VMEM((2, 32, 3 * C1), BF),
        pltpu.VMEM((4, 16, C1), BF),
        pltpu.SemaphoreType.DMA((8,)),
        pltpu.SemaphoreType.DMA((8,)),
    ]


def layer_scratch(channels):
    return [
        pltpu.VMEM((304, channels), F32),
        pltpu.VMEM((384, 3 * channels), BF),
        pltpu.VMEM((416, C2), BF),
        pltpu.VMEM((304, 3 * channels), F32),
        pltpu.VMEM((384, channels), BF),
        pltpu.VMEM((128, channels), BF),
        pltpu.VMEM((128, channels), BF),
        pltpu.SemaphoreType.DMA((8,)),
        pltpu.SemaphoreType.DMA((8,)),
    ]


N_EDGE, N_PATCH, N_LAYER = 4, 8, 9


def step_kernel(*refs):
    (feat_hbm, w1_hbm, w2_hbm, cot_hbm, pick_hbm, flip_hbm, rule_hbm,
     pooled_ref, grad_ref, first_out, second_out) = refs[:11]
    refs = refs[11:]
    edges, refs = refs[:N_EDGE], refs[N_EDGE:]
    patch_refs, refs = refs[:N_PATCH], refs[N_PATCH:]
    layer1, refs = refs[:N_LAYER], refs[N_LAYER:]
    layer2, refs = refs[:N_LAYER], refs[N_LAYER:]
    red2_refs, refs = refs[:N_REDUCE], refs[N_REDUCE:]
    red1_refs, refs = refs[:N_REDUCE], refs[N_REDUCE:]
    (feat_ref, w1, w2, cot_ref, pick_ref, flip_ref, rule_ref, load_sem,
     rules_out, rules_in, rule_send, rule_recv, q_fwd, q_back, q_act, slope1, pre2) = refs
    red2_refs = red2_refs[:12] + (second_out,) + red2_refs[12:]
    red1_refs = red1_refs[:12] + (first_out,) + red1_refs[12:]

    lon, lat = lax.axis_index("lon"), lax.axis_index("lat")
    y = lax.div(lon, 2 * NZ)
    z = lax.div(lax.rem(lon, 2 * NZ), 2)
    x = lax.rem(lon, 2) * 2 + lax.div(lat, 2)
    core = lax.rem(lat, 2)

    def device(x_at, y_at, z_at, core_at):
        return (y_at * (2 * NZ) + z_at * 2 + lax.div(x_at, 2), lax.rem(x_at, 2) * 2 + core_at)

    across = lax.rem(lon + LON // 2, LON)
    below, above = lat == 0, lat == LAT - 1
    vert = (
        (jnp.where(below, across, lon), jnp.where(below, lat, lat - 1)),
        (jnp.where(above, across, lon), jnp.where(above, lat, lat + 1)),
    )
    seen = (jnp.where(below, 0, 1), jnp.where(above, 1, 0))

    def west_of(at):
        return (lax.rem(at[0] + LON - 1, LON), at[1])

    def east_of(at):
        return (lax.rem(at[0] + 1, LON), at[1])

    here = (lon, lat)
    west, east = west_of(here), east_of(here)
    diagonal = [
        (west_of(vert[0]), 2 * seen[0] + 1),
        (east_of(vert[0]), 2 * seen[0]),
        (west_of(vert[1]), 2 * seen[1] + 1),
        (east_of(vert[1]), 2 * seen[1]),
    ]

    loads = [
        pltpu.make_async_copy(src, dst, load_sem.at[n])
        for n, (src, dst) in enumerate((
            (pick_hbm, pick_ref), (flip_hbm, flip_ref), (rule_hbm, rule_ref), (feat_hbm, feat_ref),
            (w1_hbm, w1), (cot_hbm, cot_ref), (w2_hbm, w2),
        ))
    ]
    for load in loads:
        load.start()

    barrier = pltpu.get_barrier_semaphore()
    partners = [vert[0], vert[1], west, east] + [d[0] for d in diagonal]
    partners.append(device(x, y, z, 1 - core))
    for d in (1, 2, 3):
        partners.append(device(lax.rem(x + d, NX), y, z, core))
        partners.append(device(x, lax.rem(y + d, NY), z, core))
        partners.append(device(x, y, 4 * lax.div(z, 4) + lax.rem(z + d, 4), core))
        partners.append(device(x, y, lax.rem(z + 4 * d, NZ), core))
    for partner in partners:
        pl.semaphore_signal(barrier, inc=1, device_id=partner, device_id_type=MESH)

    for load in loads[:3]:
        load.wait()
    picks = [pick_ref[0, 0, s] for s in range(2)]
    flips = [flip_ref[0, 0, s] for s in range(2)]
    rules = [rule_ref[0, 0, k] for k in range(4)]

    row8 = iota((8, 128), 0)
    rules_out[...] = jnp.where(
        row8 == 0, picks[0], jnp.where(row8 == 1, flips[0], jnp.where(row8 == 2, picks[1], flips[1]))
    )

    p, cell = iota((80, 256), 0), iota((80, 256), 1)
    k = p & 15
    want = jnp.where(
        p < 16, k, jnp.where(p < 32, 240 + k, jnp.where(p < 48, 16 * k, jnp.where(p < 64, 16 * k + 15, (
            jnp.where(k == 0, 0, jnp.where(k == 1, 15, jnp.where(k == 2, 240, jnp.where(k == 3, 255, -1))))
        ))))
    )
    take_edges = hot(cell == want).astype(BF)

    loads[3].wait()
    edges[0][...] = mm(take_edges, feat_ref[...]).astype(BF)
    edges[1][224:256, :] = jnp.zeros((32, C1), BF)
    layer1[1][288:384, :] = jnp.zeros((96, 3 * C1), BF)

    pl.semaphore_wait(barrier, len(partners))

    def edge_sends():
        out, got, send, recv = edges
        copies = []
        for side in range(2):
            copies.append(remote(out.at[0:64], got.at[pl.ds(pl.multiple_of(64 * seen[side], 64), 64)],
                                 send.at[side], recv.at[seen[side]], vert[side]))
        copies.append(remote(out.at[32:48], got.at[144:160], send.at[2], recv.at[3], west))
        copies.append(remote(out.at[48:64], got.at[128:144], send.at[3], recv.at[2], east))
        for i, (target, slot) in enumerate(diagonal):
            copies.append(remote(out.at[64:80], got.at[pl.ds(pl.multiple_of(160 + 16 * slot, 16), 16)],
                                 send.at[4 + i], recv.at[4 + slot], target))
        for copy in copies:
            copy.start()
        return copies

    def edge_waits():
        out, got, send, recv = edges
        spots = [(0, 64), (64, 64), (128, 16), (144, 16), (160, 16), (176, 16), (192, 16), (208, 16)]
        for i, (at, size) in enumerate(spots):
            remote(out.at[0:size], got.at[at:at + size], send.at[i], recv.at[i], west).wait_recv()

    rule_copies = []
    for i, (target, slot) in enumerate(((vert[0], seen[0]), (vert[1], seen[1]), (west, 3), (east, 2))):
        rule_copies.append(remote(rules_out, rules_in.at[slot], rule_send.at[i], rule_recv.at[slot], target))
    for copy in rule_copies:
        copy.start()
    sent = edge_sends()

    r, c = iota((288, 256), 0), iota((288, 256), 1)
    j, i = r & 15, r >> 4
    want = jnp.where(j == 0, 127 + i, jnp.where(j == 15, 143 + i, -1))
    q_fwd[0:288, :] = hot(c == want).astype(BF)
    r, c = iota((32, 256), 0), iota((32, 256), 1)
    k, north = r & 15, r >= 16
    flip = jnp.where(north, flips[1], flips[0])
    pick = jnp.where(north, picks[1], picks[0])
    want = jnp.where(north, 64, 0) + 16 * pick + jnp.where(flip == 1, 15 - k, k)
    q_fwd[288:320, :] = hot(c == want).astype(BF)

    def halo_cells(p, q):
        block, k = p >> 4, p & 15
        low, high = k == 0, k == 15
        corner_at = (0, 15, 272, 287)
        want = jnp.where(block == 0, 288 + k, jnp.where(block == 1, 304 + k, jnp.where(
            block == 2, 16 * k + 16, jnp.where(block == 3, 16 * k + 31, -1))))
        half = jnp.full_like(want, -1)
        ends = ((0, 1), (2, 3), (0, 2), (1, 3))
        for b in range(4):
            first, second = ends[b]
            half = jnp.where((block == b) & low & (rules[first] == 1), corner_at[first], half)
            half = jnp.where((block == b) & high & (rules[second] == 1), corner_at[second], half)
            want = jnp.where((block == 4 + b) & low & (rules[b] != 1), corner_at[b], want)
        return (hot(q == want) + hot(q == half, 0.5)).astype(BF)

    q_back[...] = halo_cells(iota((128, 384), 0), iota((128, 384), 1))
    q_act[...] = halo_cells(iota((320, 128), 1), iota((320, 128), 0))

    for layer in (layer1, layer2):
        g_pad = layer[2]
        g_pad[0:32, :] = jnp.zeros((32, C2), BF)
        g_pad[288:416, :] = jnp.zeros((128, C2), BF)
        layer[4][320:384, :] = jnp.zeros((64, layer[4].shape[1]), BF)

    red2 = Reduce(MA, red2_refs, (x, y, z, core, device))
    red1 = Reduce(MB, red1_refs, (x, y, z, core, device))
    used = FIRST_UNITS + LAST_UNITS
    red1.halves[:, used:B_UNITS] = jnp.zeros((2, B_UNITS - used, 16, 128), BF)
    red1.a3[6:8] = jnp.zeros((2, 16, 128), BF)

    for slot in range(4):
        remote(rules_out, rules_in.at[slot], rule_send.at[slot], rule_recv.at[slot], west).wait_recv()

    r, c = iota((16, 256), 0), iota((16, 256), 1)
    for side in range(2):
        def source(position):
            return 64 * side + 16 * picks[side] + jnp.where(flips[side] == 1, 15 - position, position)

        rows = 2 * side
        w_pick, w_flip = wide(rules_in[2, rows:rows + 1, :], 2), wide(rules_in[2, rows + 1:rows + 2, :], 2)
        e_pick, e_flip = wide(rules_in[3, rows:rows + 1, :], 2), wide(rules_in[3, rows + 1:rows + 2, :], 2)
        w_at = 160 + 32 * side + corner_slot(w_pick, jnp.where(w_flip == 1, 0, 1))
        e_at = 176 + 32 * side + corner_slot(e_pick, jnp.where(e_flip == 1, 1, 0))
        w_rule, e_rule = rules[2 * side] == 1, rules[2 * side + 1] == 1
        shape = (16, 256)
        w_main = jnp.where(w_rule, jnp.full(shape, -1), jnp.broadcast_to(w_at, shape))
        e_main = jnp.where(e_rule, jnp.full(shape, -1), jnp.broadcast_to(e_at, shape))
        w_a, w_c = jnp.where(w_rule, source(0), -1), jnp.where(w_rule, 128 + 15 * side, -1)
        e_a, e_c = jnp.where(e_rule, source(15), -1), jnp.where(e_rule, 144 + 15 * side, -1)
        w_row = hot(c == w_main) + hot(c == w_a, 0.5) + hot(c == w_c, 0.5)
        e_row = hot(c == e_main) + hot(c == e_a, 0.5) + hot(c == e_c, 0.5)
        values = jnp.where(r == 0, w_row, jnp.where(r == 15, e_row, 0.0))
        q_fwd[272 * side:272 * side + 16, :] = values.astype(BF)

    face = (jnp.where(below, 0, 1), jnp.where(above, 1, 0))
    facing = []
    for side in range(2):
        south = face[side] == 0
        facing.append((
            jnp.where(south, rules_in[side, 0:1, 0:128], rules_in[side, 2:3, 0:128]),
            jnp.where(south, rules_in[side, 1:2, 0:128], rules_in[side, 3:4, 0:128]),
        ))
    p = iota((1, 128), 1)
    block, k = p >> 4, p & 15
    on_north = (block == 1) | (block >= 6)
    pick = jnp.where(on_north, facing[1][0], facing[0][0])
    flip = jnp.where(on_north, facing[1][1], facing[0][1])
    position = jnp.where(block < 2, k, jnp.where((block & 1) == 1, 15, 0))
    target = edge_cell(pick, flip, position)
    target = jnp.where(block == 2, 16 * k + 15, jnp.where(block == 3, 16 * k, target))
    target = jnp.where((block >= 4) & (k != 0), -1, target)
    place_grads = hot(iota((256, 128), 0) == target).astype(BF)

    r, c = iota((32, 256), 0), iota((32, 256), 1)
    pick = jnp.where(r < 16, wide(facing[0][0], 2), wide(facing[1][0], 2))
    flip = jnp.where(r < 16, wide(facing[0][1], 2), wide(facing[1][1], 2))
    take_cells = hot(c == edge_cell(pick, flip, r & 15)).astype(BF)
    r, c = iota((64, 384), 0), iota((64, 384), 1)
    row = r & 31
    take_strips = hot((row < 18) & (c == 16 * row + jnp.where(r < 32, 15, 0))).astype(BF)
    tap, which = r & 15, r >> 4
    tap_row = (tap * 11) >> 5
    pick = jnp.where(which < 2, wide(facing[0][0], 3), wide(facing[1][0], 3))
    flip = jnp.where(which < 2, wide(facing[0][1], 3), wide(facing[1][1], 3))
    at = 16 * tap_row + edge_cell(pick, flip, jnp.where((which & 1) == 1, 15, 0))
    take_corners = [
        hot((tap < 9) & (tap - 3 * tap_row == dw) & (c == at)).astype(BF) for dw in range(3)
    ]

    def patch_sends():
        cells, strips, corners, got_cells, got_strips, got_corners, send, recv = patch_refs
        padded = layer1[1]
        for dh in range(3):
            cells[:, 384 * dh:384 * dh + 384] = mm(take_cells, padded[16 * dh:16 * dh + 256, :]).astype(BF)
        strips[...] = mm(take_strips, padded[...]).astype(BF).reshape(2, 32, 3 * C1)
        values = mm(take_corners[0], padded[:, 0:C1])
        for dw in (1, 2):
            values = values + mm(take_corners[dw], padded[:, dw * C1:(dw + 1) * C1])
        corners[...] = values.astype(BF).reshape(4, 16, C1)
        copies = []
        for side in range(2):
            copies.append(remote(cells.at[16 * side:16 * side + 16],
                                 got_cells.at[pl.ds(pl.multiple_of(16 * seen[side], 16), 16)],
                                 send.at[side], recv.at[seen[side]], vert[side]))
        copies.append(remote(strips.at[0], got_strips.at[0], send.at[2], recv.at[2], east))
        copies.append(remote(strips.at[1], got_strips.at[1], send.at[3], recv.at[3], west))
        for i, (target_at, slot) in enumerate(diagonal):
            copies.append(remote(corners.at[i], got_corners.at[slot], send.at[4 + i], recv.at[4 + slot], target_at))
        for copy in copies:
            copy.start()
        return copies

    def patch_waits():
        cells, strips, corners, got_cells, got_strips, got_corners, send, recv = patch_refs
        for i in range(2):
            remote(cells.at[0:16], got_cells.at[16 * i:16 * i + 16], send.at[i], recv.at[i], west).wait_recv()
            remote(strips.at[i], got_strips.at[i], send.at[2 + i], recv.at[2 + i], west).wait_recv()
        r, c = iota((32, 64), 0), iota((32, 64), 1)
        both = got_strips[...].reshape(64, 3 * C1)
        for dh in range(3):
            spread_rows = hot(c == jnp.where(r < 16, r, r + 16) + dh).astype(BF)
            got_cells[32:64, 384 * dh:384 * dh + 384] = mm(spread_rows, both).astype(BF)
        for i in range(4):
            remote(corners.at[i], got_corners.at[i], send.at[4 + i], recv.at[4 + i], west).wait_recv()
        r, c = iota((64, 64), 0), iota((64, 64), 1)
        taps = got_corners[...].reshape(64, C1)
        for tap in range(9):
            first_row = hot(((r & 15) == 0) & (c == r + tap)).astype(BF)
            got_cells[64:128, C1 * tap:C1 * tap + C1] = mm(first_row, taps).astype(BF)

    def pad_tile(layer, tile, cells, channels):
        ext, padded = layer[:2]
        south, north = cells[288:304], cells[304:320]
        ext[8:24, :] = south
        ext[24:280, :] = tile.astype(F32)
        ext[280:296, :] = north
        j = iota((288, channels), 0) & 15
        padded[0:288, 0:channels] = jnp.where(j == 0, cells[0:288], ext[7:295, :]).astype(BF)
        padded[0:288, channels:2 * channels] = ext[8:296, :].astype(BF)
        padded[0:288, 2 * channels:] = jnp.where(j == 15, cells[0:288], ext[9:297, :]).astype(BF)

    def convolve(layer, weight):
        padded = layer[1]
        total = mm(padded[0:256, :], weight[0])
        for dh in (1, 2):
            total = total + mm(padded[16 * dh:16 * dh + 256, :], weight[dh])
        return total

    def input_side(layer, weight, channels):
        g_pad, by_shift, leaving, out = layer[2:6]
        total = mm_nt(g_pad[32:320, :], weight[0])
        for dh in (1, 2):
            at = 32 - 16 * dh
            total = total + mm_nt(g_pad[at:at + 288, :], weight[dh])
        by_shift[8:296, :] = total
        j = iota((288, channels), 0) & 15
        centre = by_shift[8:296, channels:2 * channels]
        centre = centre + jnp.where(j == 15, 0.0, by_shift[9:297, 0:channels])
        centre = centre + jnp.where(j == 0, 0.0, by_shift[7:295, 2 * channels:])
        centre = centre.astype(BF)
        sides = jnp.where(j == 0, by_shift[8:296, 0:channels], by_shift[8:296, 2 * channels:])
        sides = jnp.where((j == 0) | (j == 15), sides, 0.0)
        leaving[0:288, :] = sides.astype(BF)
        leaving[288:304, :] = centre[0:16]
        leaving[304:320, :] = centre[272:288]
        out[...] = mm(q_back[...], leaving[...]).astype(BF)
        return centre[16:272]

    def grad_sends(layer):
        out, got, send, recv = layer[5:9]
        copies = []
        for side in range(2):
            copies.append(remote(out.at[16 * side:16 * side + 16],
                                 got.at[pl.ds(pl.multiple_of(16 * seen[side], 16), 16)],
                                 send.at[side], recv.at[seen[side]], vert[side]))
        copies.append(remote(out.at[32:48], got.at[32:48], send.at[2], recv.at[2], west))
        copies.append(remote(out.at[48:64], got.at[48:64], send.at[3], recv.at[3], east))
        for i, (target_at, slot) in enumerate(diagonal):
            copies.append(remote(out.at[64 + 16 * i:80 + 16 * i],
                                 got.at[pl.ds(pl.multiple_of(64 + 16 * slot, 16), 16)],
                                 send.at[4 + i], recv.at[4 + slot], target_at))
        for copy in copies:
            copy.start()
        return copies

    def grad_waits(layer):
        out, got, send, recv = layer[5:9]
        for i in range(8):
            remote(out.at[0:16], got.at[16 * i:16 * i + 16], send.at[i], recv.at[i], west).wait_recv()

    def weight_grad(pairs, spots):
        block = None
        for cells, gradient in pairs:
            part = mm_tn(cells, gradient)
            block = part if block is None else block + part
        block = block.astype(BF)
        units = block.shape[0] // 16
        for h in range(2):
            values = block[:, 128 * h:128 * h + 128].reshape(units, 16, 128)
            for first, count, red, to in spots:
                red.halves[h, to:to + count] = values[first:first + count]

    edge_waits()
    pad_tile(layer1, feat_ref[...], mm(q_fwd[...], edges[1][...]), C1)
    sent += patch_sends()
    loads[4].wait()
    pre1 = convolve(layer1, w1)
    cdf1 = normal_cdf(pre1)
    act1 = (pre1 * cdf1).astype(BF)
    slope1[...] = gelu_slope(pre1, cdf1)
    r, c = iota((256, 64), 0), iota((256, 64), 1)
    spread = hot(c == 8 * (r >> 5) + ((r & 15) >> 1), 0.25).astype(BF)
    loads[5].wait()
    cot = mm(spread, cot_ref[...])
    loads[6].wait()

    patch_waits()
    patches = patch_refs[3]
    halo_pre = mm(patches[:, 0:384], w1[0])
    for dh in (1, 2):
        halo_pre = halo_pre + mm(patches[:, 384 * dh:384 * dh + 384], w1[dh])
    halo_cdf = normal_cdf(halo_pre)
    halo_act = (halo_pre * halo_cdf).astype(BF)
    pad_tile(layer2, act1, mm(q_act[...], halo_act), C2)
    second_pre = convolve(layer2, w2)
    cdf2 = normal_cdf(second_pre)
    grad2 = (cot * gelu_slope(second_pre, cdf2)).astype(BF)
    layer2[2][32:288, :] = grad2
    pre2[...] = second_pre * cdf2
    for dh in range(3):
        spots = [(0, 48, red2, 48 * dh)] if dh < 2 else [(0, 32, red2, 96), (32, 16, red1, FIRST_UNITS)]
        weight_grad([(layer2[1][16 * dh:16 * dh + 256, :], grad2)], spots)
        red2.core_send(48 * dh, spots[0][1])
    centre2 = input_side(layer2, w2, C2)
    sent += grad_sends(layer2)

    own = (centre2.astype(F32) * slope1[...]).astype(BF)
    leaving = (layer2[5][...].astype(F32) * gelu_slope(halo_pre, halo_cdf)).astype(BF)
    for dh in range(3):
        weight_grad([(layer1[1][16 * dh:16 * dh + 256, :], own),
                     (patches[:, 384 * dh:384 * dh + 384], leaving)], [(0, 24, red1, 24 * dh)])
    red1.core_send(0, B_UNITS)
    red2.core_add()
    red1.core_add()

    r, c = iota((64, 256), 0), iota((64, 256), 1)
    gather_cells = hot(r == 8 * (c >> 5) + ((c & 15) >> 1), 0.25).astype(BF)
    act2 = pre2[...]
    high = act2.astype(BF)
    low = (act2 - high.astype(F32)).astype(BF)
    pooled_ref[...] = (mm(gather_cells, high) + mm(gather_cells, low)).astype(BF)

    red2.first_add()
    red1.first_add()

    grad_waits(layer2)
    first_grad = centre2.astype(F32) + mm(place_grads, layer2[6][...])
    layer1[2][32:288, :] = (first_grad * slope1[...]).astype(BF)
    centre1 = input_side(layer1, w1, C1)
    sent += grad_sends(layer1)

    red2.second_add()
    red1.second_add()
    red2.near_add()
    red1.near_add()

    grad_waits(layer1)
    grad_ref[...] = (centre1.astype(F32) + mm(place_grads, layer1[6][...])).astype(BF)

    red2.far_add()
    red1.far_add()
    red2.gather_second()
    red1.gather_second()
    red2.gather_first()
    red1.gather_first()
    red2.gather_core()
    red1.gather_core()
    red2.gather_done()
    red1.gather_done()

    for copy in sent + rule_copies:
        copy.wait_send()
    for red in (red2, red1):
        red.finish()


def finish_kernel(pooled_ref, grad_ref, first_ref, second_ref, pooled_out, grad_out, first_out, second_out,
                  first_rows, second_rows, sems):
    copies = [pltpu.make_async_copy(pooled_ref, pooled_out, sems.at[0]),
              pltpu.make_async_copy(grad_ref, grad_out, sems.at[1])]
    for copy in copies:
        copy.start()

    def squares(ref, at, count, total):
        def body(i, total):
            values = ref[:, pl.ds(at + i * 8, 8)].astype(F32)
            return total + jnp.sum(values * values, axis=(0, 1))

        return lax.fori_loop(0, count // 8, body, total)

    total = squares(second_ref, 0, A_UNITS, jnp.zeros((16, 128), F32))
    total = squares(first_ref, 0, FIRST_UNITS + LAST_UNITS, total)
    squared = jnp.sum(jnp.sum(total, axis=0, keepdims=True), axis=1, keepdims=True)
    target_norm = math.sqrt(9.0 * (C1 + C2) * C2)
    scale = jnp.broadcast_to(target_norm / jnp.sqrt(squared + 1e-06), (16, 128))

    def write(ref, at, to, count, out):
        def body(i, carry):
            for h in range(2):
                values = ref[h, pl.ds(at + i * 8, 8)].astype(F32) * scale
                rows = pl.ds(pl.multiple_of((to + i * 8) * 16, 128), 128)
                out[rows, 128 * h:128 * h + 128] = values.astype(BF).reshape(128, 128)
            return carry

        lax.fori_loop(0, count // 8, body, 0)

    jobs = [(second_ref, n * 64, n * 64, 64, second_rows, second_out) for n in range(2)]
    jobs.append((first_ref, 0, 0, FIRST_UNITS, first_rows, first_out))
    jobs.append((first_ref, FIRST_UNITS, A_UNITS, LAST_UNITS, second_rows, second_out))
    for n, (ref, at, to, count, rows, out) in enumerate(jobs):
        write(ref, at, to, count, rows)
        span = pl.ds(16 * to, 16 * count)
        copies.append(pltpu.make_async_copy(rows.at[span], out.at[span], sems.at[2 + n]))
        copies[-1].start()
    for copy in copies:
        copy.wait()


def on_device(features, conv_first, conv_second, cotangent, edge_pick, edge_flip, corner_rule):
    vmem = pl.BlockSpec(memory_space=pltpu.VMEM)
    hbm = pl.BlockSpec(memory_space=pltpu.HBM)
    pooled, input_grad, first, second = pl.pallas_call(
        step_kernel,
        out_shape=(
            jax.ShapeDtypeStruct((64, C2), BF),
            jax.ShapeDtypeStruct((256, C1), BF),
            jax.ShapeDtypeStruct((2, B_UNITS, 16, 128), BF),
            jax.ShapeDtypeStruct((2, A_UNITS, 16, 128), BF),
        ),
        in_specs=[hbm] * 7,
        out_specs=[vmem] * 4,
        scratch_shapes=(
            edge_scratch(C1)
            + patch_scratch()
            + layer_scratch(C1)
            + layer_scratch(C2)
            + reduce_scratch(*MA)
            + reduce_scratch(*MB)
            + [
                pltpu.VMEM((256, C1), BF),
                pltpu.VMEM((3, 3 * C1, C2), BF),
                pltpu.VMEM((3, 3 * C2, C2), BF),
                pltpu.VMEM((64, C2), BF),
                pltpu.SMEM((1, 1, 2), jnp.int32),
                pltpu.SMEM((1, 1, 2), jnp.int32),
                pltpu.SMEM((1, 1, 4), jnp.int32),
                pltpu.SemaphoreType.DMA((7,)),
                pltpu.VMEM((8, 128), jnp.int32),
                pltpu.VMEM((4, 8, 128), jnp.int32),
                pltpu.SemaphoreType.DMA((4,)),
                pltpu.SemaphoreType.DMA((4,)),
                pltpu.VMEM((320, 256), BF),
                pltpu.VMEM((128, 384), BF),
                pltpu.VMEM((320, 128), BF),
                pltpu.VMEM((256, C2), F32),
                pltpu.VMEM((256, C2), F32),
            ]
        ),
        compiler_params=pltpu.CompilerParams(
            collective_id=0, has_side_effects=True, vmem_limit_bytes=32 * 1024 * 1024
        ),
        name="level_step",
    )(*(
        pltpu.with_memory_space_constraint(value, pltpu.HBM)
        for value in (
            features.reshape(256, C1),
            conv_first.reshape(3, 3 * C1, C2),
            conv_second.reshape(3, 3 * C2, C2),
            cotangent.reshape(64, C2),
            edge_pick,
            edge_flip,
            corner_rule,
        )
    ))
    pooled, input_grad, first, second = pl.pallas_call(
        finish_kernel,
        out_shape=(
            jax.ShapeDtypeStruct((64, C2), BF),
            jax.ShapeDtypeStruct((256, C1), BF),
            jax.ShapeDtypeStruct((9 * C1, C2), BF),
            jax.ShapeDtypeStruct((9 * C2, C2), BF),
        ),
        in_specs=[vmem] * 4,
        out_specs=[hbm] * 4,
        scratch_shapes=[
            pltpu.VMEM((9 * C1, C2), BF),
            pltpu.VMEM((9 * C2, C2), BF),
            pltpu.SemaphoreType.DMA((6,)),
        ],
        compiler_params=pltpu.CompilerParams(vmem_limit_bytes=16 * 1024 * 1024),
        name="scale_outputs",
    )(pooled, input_grad, first, second)
    return (
        pooled.reshape(1, 1, 8, 8, C2),
        input_grad.reshape(1, 1, 16, 16, C1),
        first.reshape(3, 3, C1, C2),
        second.reshape(3, 3, C2, C2),
    )


def solution(mesh):
    return jax.shard_map(
        on_device,
        mesh=mesh,
        in_specs=(
            P("lon", "lat", None, None, None),
            P(),
            P(),
            P("lon", "lat", None, None, None),
            P("lon", "lat", None),
            P("lon", "lat", None),
            P("lon", "lat", None),
        ),
        out_specs=(P("lon", "lat", None, None, None), P("lon", "lat", None, None, None), P(), P()),
        check_vma=False,
    )
```

```python
import math

import jax
import jax.numpy as jnp
from jax import lax
from jax.experimental import pallas as pl
from jax.experimental.pallas import tpu as pltpu
from jax.sharding import PartitionSpec as P

MESH = pl.DeviceIdType.MESH
BF = jnp.bfloat16
F32 = jnp.float32
NX, NY, NZ = 4, 4, 16
LON, LAT = 2 * NY * NZ, 4
C1, C2 = 128, 256


def normal_cdf(values):
    return 0.5 * (1.0 + lax.erf(values * (1.0 / math.sqrt(2.0))))


def gelu_slope(values, cdf):
    return cdf + values * jnp.exp(-0.5 * values * values) * (1.0 / math.sqrt(2.0 * math.pi))


def iota(shape, dim):
    return lax.broadcasted_iota(jnp.int32, shape, dim)


def hot(cond, value=1.0):
    return jnp.where(cond, jnp.float32(value), jnp.float32(0.0))


def wide(row, count):
    return jnp.concatenate([row] * count, axis=1)


def edge_cell(edge, flip, position):
    at = jnp.where(flip == 1, 15 - position, position)
    return jnp.where(edge == 0, at, jnp.where(edge == 1, 240 + at, jnp.where(edge == 2, 16 * at, 16 * at + 15)))


def mm(a, b):
    return jnp.dot(a, b, preferred_element_type=F32)


def mm_nt(a, b):
    return lax.dot_general(a, b, (((1,), (1,)), ((), ())), preferred_element_type=F32)


def mm_tn(a, b):
    return lax.dot_general(a, b, (((0,), (0,)), ((), ())), preferred_element_type=F32)


def remote(src, dst, send_sem, recv_sem, device):
    return pltpu.make_async_remote_copy(
        src_ref=src, dst_ref=dst, send_sem=send_sem, recv_sem=recv_sem,
        device_id=device, device_id_type=MESH,
    )


def corner_slot(edge, at_end):
    return jnp.where(
        edge == 0, at_end, jnp.where(edge == 1, 2 + at_end, jnp.where(edge == 2, 2 * at_end, 1 + 2 * at_end))
    )


class Reduce:
    def __init__(self, m, refs, place):
        self.m = m
        self.total = m[0] + m[1]
        self.start = (0, 16 * m[0])
        (self.halves, self.r0, self.a1, r1a, r1b, a2a, a2b, r2a, r2b, self.a3, self.n3, self.f3, self.out,
         self.s_send, self.s_recv, self.g_send, self.g_recv) = refs
        self.r1, self.a2, self.r2 = (r1a, r1b), (a2a, a2b), (r2a, r2b)
        self.x, self.y, self.z, self.core, self.device = place
        self.near, self.far = lax.rem(self.z, 4), lax.div(self.z, 4)
        self.pending = []
        self.pieces = []
        self.waited = 0

    def other_core(self):
        return self.device(self.x, self.y, self.z, 1 - self.core)

    def peer(self, axis, d):
        x = lax.rem(self.x + d, NX) if axis == "x" else self.x
        y = lax.rem(self.y + d, NY) if axis == "y" else self.y
        return self.device(x, y, self.z, self.core)

    def axes(self, part):
        return ("x", "y") if part == 0 else ("y", "x")

    def coords(self, part):
        return (self.x, self.y) if part == 0 else (self.y, self.x)

    def send(self, copy):
        copy.start()
        self.pending.append(copy)

    def received(self, ref, sem):
        remote(ref, ref, self.s_send.at[0], sem, self.other_core()).wait_recv()

    def flush(self):
        for copy in self.pending:
            copy.wait_send()
        self.pending = []

    def near_flush(self):
        @pl.when(self.near < self.total // 2)
        def _():
            for copy in self.near_copies():
                copy.wait_send()

    def core_send(self, at, count):
        k = len(self.pieces)
        self.pieces.append((at, count))
        self.send(remote(self.halves.at[1 - self.core, at:at + count], self.r0.at[at:at + count],
                         self.s_send.at[k], self.s_recv.at[k], self.other_core()))

    def core_add(self):
        for part in range(2):
            n = 4 * self.m[part]
            mine = self.coords(part)[0]
            while self.waited < len(self.pieces) and self.pieces[self.waited][0] < self.start[part] + 4 * n:
                at, count = self.pieces[self.waited]
                self.received(self.r0.at[at:at + count], self.s_recv.at[self.waited])
                self.waited += 1
            for d in (2, 1, 3, 0):
                at = pl.ds(self.start[part] + lax.rem(mine + d, 4) * n, n)
                self.a1[at] = (self.halves[self.core, at].astype(F32) + self.r0[at].astype(F32)).astype(BF)
                if d:
                    k = 3 + part * 3 + d - 1
                    self.send(remote(self.a1.at[at], self.r1[part].at[d - 1], self.s_send.at[k], self.s_recv.at[k],
                                     self.peer(self.axes(part)[0], d)))

    def first_add(self):
        for part in range(2):
            m = self.m[part]
            r1, a2, r2 = self.r1[part], self.a2[part], self.r2[part]
            ca, cb = self.coords(part)
            for d in (1, 3, 2):
                self.received(r1.at[d - 1], self.s_recv.at[3 + part * 3 + d - 1])
            for d in (2, 1, 3, 0):
                block = lax.rem(cb + d, 4)
                at = pl.ds(block * m, m)
                total = self.a1[pl.ds(self.start[part] + (ca * 4 + block) * m, m)].astype(F32)
                for e in range(3):
                    total = total + r1[e, at].astype(F32)
                a2[at] = total.astype(BF)
                if d:
                    k = 9 + part * 3 + d - 1
                    self.send(remote(a2.at[at], r2.at[d - 1], self.s_send.at[k], self.s_recv.at[k],
                                     self.peer(self.axes(part)[1], d)))

    def second_add(self):
        for part in range(2):
            m = self.m[part]
            a2, r2 = self.a2[part], self.r2[part]
            cb = self.coords(part)[1]
            for d in (1, 3, 2):
                self.received(r2.at[d - 1], self.s_recv.at[9 + part * 3 + d - 1])
            total = a2[pl.ds(cb * m, m)].astype(F32)
            for e in range(3):
                total = total + r2[e].astype(F32)
            self.a3[part * self.m[0]:part * self.m[0] + m] = total.astype(BF)
        for d in (2, 1, 3):
            owner = lax.rem(self.near + d, 4)
            self.send(remote(self.a3.at[pl.ds(2 * owner, 2)], self.n3.at[d - 1], self.s_send.at[14 + d],
                             self.s_recv.at[14 + d], self.device(self.x, self.y, 4 * self.far + owner, self.core)))

    def near_add(self):
        for d in (1, 3, 2):
            self.received(self.n3.at[d - 1], self.s_recv.at[14 + d])
        total = self.a3[pl.ds(2 * self.near, 2)].astype(F32)
        for e in range(3):
            total = total + self.n3[e].astype(F32)
        self.f3[self.far] = total.astype(BF)
        for d in (2, 1, 3):
            self.send(remote(self.f3.at[self.far], self.f3.at[self.far], self.s_send.at[17 + d], self.s_recv.at[17 + d],
                             self.device(self.x, self.y, 4 * lax.rem(self.far + d, 4) + self.near, self.core)))

    def unit_at(self, u):
        ma, mb = self.m
        first = (self.x * 4 + self.y) * ma + u
        second = self.start[1] + (self.y * 4 + self.x) * mb + u - ma
        return jnp.where(u < ma, first, second)

    def near_copies(self):
        at = pl.ds(self.unit_at(2 * self.near), 2)
        return [
            remote(self.out.at[self.core, at], self.out.at[self.core, at], self.g_send.at[19 + d], self.g_recv.at[19 + d],
                   self.device(self.x, self.y, 4 * self.far + lax.rem(self.near + d, 4), self.core))
            for d in (2, 1, 3)
        ]

    def far_add(self):
        for d in (1, 3, 2):
            self.received(self.f3.at[lax.rem(self.far + 4 - d, 4)], self.s_recv.at[17 + d])

        @pl.when(self.near < self.total // 2)
        def _():
            total = self.f3[0].astype(F32)
            for e in range(1, 4):
                total = total + self.f3[e].astype(F32)
            self.out[self.core, pl.ds(self.unit_at(2 * self.near), 2)] = total.astype(BF)
            for copy in self.near_copies():
                copy.start()

    def gather_second(self):
        for d in (1, 3, 2):
            owner = lax.rem(self.near + 4 - d, 4)

            @pl.when(owner < self.total // 2)
            def _():
                self.received(self.out.at[self.core, pl.ds(self.unit_at(2 * owner), 2)], self.g_recv.at[19 + d])

        for part in range(2):
            m = self.m[part]
            ca, cb = self.coords(part)
            at = pl.ds(self.start[part] + (ca * 4 + cb) * m, m)
            for d in (2, 1, 3):
                k = part * 3 + d - 1
                self.send(remote(self.out.at[self.core, at], self.out.at[self.core, at], self.g_send.at[k],
                                 self.g_recv.at[k], self.peer(self.axes(part)[1], d)))

    def gather_first(self):
        for part in range(2):
            m = self.m[part]
            ca, cb = self.coords(part)
            for d in (1, 3, 2):
                at = pl.ds(self.start[part] + (ca * 4 + lax.rem(cb + 4 - d, 4)) * m, m)
                self.received(self.out.at[self.core, at], self.g_recv.at[part * 3 + d - 1])
            at = pl.ds(self.start[part] + ca * 4 * m, 4 * m)
            for d in (2, 1, 3):
                k = 6 + part * 3 + d - 1
                self.send(remote(self.out.at[self.core, at], self.out.at[self.core, at], self.g_send.at[k],
                                 self.g_recv.at[k], self.peer(self.axes(part)[0], d)))
            self.to_core(part, 0, at)

    def to_core(self, part, d, at):
        k = 12 + part * 4 + d
        self.send(remote(self.out.at[self.core, at], self.out.at[self.core, at], self.g_send.at[k],
                         self.g_recv.at[k], self.other_core()))

    def block_of(self, part, d):
        n = 4 * self.m[part]
        return pl.ds(self.start[part] + lax.rem(self.coords(part)[0] + 4 - d, 4) * n, n)

    def gather_core(self):
        for d in (1, 3, 2):
            for part in range(2):
                at = self.block_of(part, d)
                self.received(self.out.at[self.core, at], self.g_recv.at[6 + part * 3 + d - 1])
                self.to_core(part, d, at)

    def gather_done(self):
        for d in (0, 1, 3, 2):
            for part in range(2):
                at = self.block_of(part, d)
                self.received(self.out.at[1 - self.core, at], self.g_recv.at[12 + part * 4 + d])


def reduce_scratch(ma, mb):
    units = 16 * (ma + mb)
    return [
        pltpu.VMEM((2, units, 16, 128), BF),
        pltpu.VMEM((units, 16, 128), BF),
        pltpu.VMEM((units, 16, 128), BF),
        pltpu.VMEM((3, 4 * ma, 16, 128), BF),
        pltpu.VMEM((3, 4 * mb, 16, 128), BF),
        pltpu.VMEM((4 * ma, 16, 128), BF),
        pltpu.VMEM((4 * mb, 16, 128), BF),
        pltpu.VMEM((3, ma, 16, 128), BF),
        pltpu.VMEM((3, mb, 16, 128), BF),
        pltpu.VMEM((8, 16, 128), BF),
        pltpu.VMEM((3, 2, 16, 128), BF),
        pltpu.VMEM((4, 2, 16, 128), BF),
        pltpu.SemaphoreType.DMA((21,)),
        pltpu.SemaphoreType.DMA((21,)),
        pltpu.SemaphoreType.DMA((23,)),
        pltpu.SemaphoreType.DMA((23,)),
    ]


N_REDUCE = 16
MA, MB = (4, 4), (4, 2)
A_UNITS, B_UNITS, FIRST_UNITS, LAST_UNITS = 128, 96, 72, 16


def edge_scratch(channels):
    return [
        pltpu.VMEM((80, channels), BF),
        pltpu.VMEM((256, channels), BF),
        pltpu.SemaphoreType.DMA((8,)),
        pltpu.SemaphoreType.DMA((8,)),
    ]


def patch_scratch():
    return [
        pltpu.VMEM((32, 9 * C1), BF),
        pltpu.VMEM((2, 32, 3 * C1), BF),
        pltpu.VMEM((4, 16, C1), BF),
        pltpu.VMEM((128, 9 * C1), BF),
        pltpu.VMEM((2, 32, 3 * C1), BF),
        pltpu.VMEM((4, 16, C1), BF),
        pltpu.SemaphoreType.DMA((8,)),
        pltpu.SemaphoreType.DMA((8,)),
    ]


def layer_scratch(channels):
    return [
        pltpu.VMEM((304, channels), F32),
        pltpu.VMEM((384, 3 * channels), BF),
        pltpu.VMEM((416, C2), BF),
        pltpu.VMEM((304, 3 * channels), F32),
        pltpu.VMEM((384, channels), BF),
        pltpu.VMEM((128, channels), BF),
        pltpu.VMEM((128, channels), BF),
        pltpu.SemaphoreType.DMA((8,)),
        pltpu.SemaphoreType.DMA((8,)),
    ]


N_EDGE, N_PATCH, N_LAYER = 4, 8, 9


def step_kernel(*refs):
    (feat_hbm, w1_hbm, w2_hbm, cot_hbm, pick_hbm, flip_hbm, rule_hbm,
     pooled_ref, grad_ref, first_out, second_out, square_ref) = refs[:12]
    refs = refs[12:]
    edges, refs = refs[:N_EDGE], refs[N_EDGE:]
    patch_refs, refs = refs[:N_PATCH], refs[N_PATCH:]
    layer1, refs = refs[:N_LAYER], refs[N_LAYER:]
    layer2, refs = refs[:N_LAYER], refs[N_LAYER:]
    red2_refs, refs = refs[:N_REDUCE], refs[N_REDUCE:]
    red1_refs, refs = refs[:N_REDUCE], refs[N_REDUCE:]
    (feat_ref, w1, w2, cot_ref, pick_ref, flip_ref, rule_ref, load_sem,
     rules_out, rules_in, rule_send, rule_recv, q_fwd, q_back, q_act, slope1, pre2,
     windows) = refs
    red2_refs = red2_refs[:12] + (second_out,) + red2_refs[12:]
    red1_refs = red1_refs[:12] + (first_out,) + red1_refs[12:]

    lon, lat = lax.axis_index("lon"), lax.axis_index("lat")
    y = lax.div(lon, 2 * NZ)
    z = lax.div(lax.rem(lon, 2 * NZ), 2)
    x = lax.rem(lon, 2) * 2 + lax.div(lat, 2)
    core = lax.rem(lat, 2)

    def device(x_at, y_at, z_at, core_at):
        return (y_at * (2 * NZ) + z_at * 2 + lax.div(x_at, 2), lax.rem(x_at, 2) * 2 + core_at)

    across = lax.rem(lon + LON // 2, LON)
    below, above = lat == 0, lat == LAT - 1
    vert = (
        (jnp.where(below, across, lon), jnp.where(below, lat, lat - 1)),
        (jnp.where(above, across, lon), jnp.where(above, lat, lat + 1)),
    )
    seen = (jnp.where(below, 0, 1), jnp.where(above, 1, 0))

    def west_of(at):
        return (lax.rem(at[0] + LON - 1, LON), at[1])

    def east_of(at):
        return (lax.rem(at[0] + 1, LON), at[1])

    here = (lon, lat)
    west, east = west_of(here), east_of(here)
    diagonal = [
        (west_of(vert[0]), 2 * seen[0] + 1),
        (east_of(vert[0]), 2 * seen[0]),
        (west_of(vert[1]), 2 * seen[1] + 1),
        (east_of(vert[1]), 2 * seen[1]),
    ]

    loads = [
        pltpu.make_async_copy(src, dst, load_sem.at[n])
        for n, (src, dst) in enumerate((
            (pick_hbm, pick_ref), (flip_hbm, flip_ref), (rule_hbm, rule_ref), (feat_hbm, feat_ref),
            (w1_hbm, w1), (cot_hbm, cot_ref), (w2_hbm, w2),
        ))
    ]
    for load in loads:
        load.start()

    barrier = pltpu.get_barrier_semaphore()
    partners = [vert[0], vert[1], west, east] + [d[0] for d in diagonal]
    partners.append(device(x, y, z, 1 - core))
    for d in (1, 2, 3):
        partners.append(device(lax.rem(x + d, NX), y, z, core))
        partners.append(device(x, lax.rem(y + d, NY), z, core))
        partners.append(device(x, y, 4 * lax.div(z, 4) + lax.rem(z + d, 4), core))
        partners.append(device(x, y, lax.rem(z + 4 * d, NZ), core))
    for partner in partners:
        pl.semaphore_signal(barrier, inc=1, device_id=partner, device_id_type=MESH)

    for load in loads[:3]:
        load.wait()
    picks = [pick_ref[0, 0, s] for s in range(2)]
    flips = [flip_ref[0, 0, s] for s in range(2)]
    rules = [rule_ref[0, 0, k] for k in range(4)]

    row8 = iota((8, 128), 0)
    rules_out[...] = jnp.where(
        row8 == 0, picks[0], jnp.where(row8 == 1, flips[0], jnp.where(row8 == 2, picks[1], flips[1]))
    )

    p, cell = iota((80, 256), 0), iota((80, 256), 1)
    k = p & 15
    want = jnp.where(
        p < 16, k, jnp.where(p < 32, 240 + k, jnp.where(p < 48, 16 * k, jnp.where(p < 64, 16 * k + 15, (
            jnp.where(k == 0, 0, jnp.where(k == 1, 15, jnp.where(k == 2, 240, jnp.where(k == 3, 255, -1))))
        ))))
    )
    take_edges = hot(cell == want).astype(BF)

    loads[3].wait()
    edges[0][...] = mm(take_edges, feat_ref[...]).astype(BF)
    edges[1][224:256, :] = jnp.zeros((32, C1), BF)
    layer1[1][288:384, :] = jnp.zeros((96, 3 * C1), BF)

    pl.semaphore_wait(barrier, len(partners))

    def edge_sends():
        out, got, send, recv = edges
        copies = []
        for side in range(2):
            copies.append(remote(out.at[0:64], got.at[pl.ds(pl.multiple_of(64 * seen[side], 64), 64)],
                                 send.at[side], recv.at[seen[side]], vert[side]))
        copies.append(remote(out.at[32:48], got.at[144:160], send.at[2], recv.at[3], west))
        copies.append(remote(out.at[48:64], got.at[128:144], send.at[3], recv.at[2], east))
        for i, (target, slot) in enumerate(diagonal):
            copies.append(remote(out.at[64:80], got.at[pl.ds(pl.multiple_of(160 + 16 * slot, 16), 16)],
                                 send.at[4 + i], recv.at[4 + slot], target))
        for copy in copies:
            copy.start()
        return copies

    def edge_waits():
        out, got, send, recv = edges
        spots = [(0, 64), (64, 64), (128, 16), (144, 16), (160, 16), (176, 16), (192, 16), (208, 16)]
        for i, (at, size) in enumerate(spots):
            remote(out.at[0:size], got.at[at:at + size], send.at[i], recv.at[i], west).wait_recv()

    rule_copies = []
    for i, (target, slot) in enumerate(((vert[0], seen[0]), (vert[1], seen[1]), (west, 3), (east, 2))):
        rule_copies.append(remote(rules_out, rules_in.at[slot], rule_send.at[i], rule_recv.at[slot], target))
    for copy in rule_copies:
        copy.start()
    sent = edge_sends()

    r, c = iota((288, 256), 0), iota((288, 256), 1)
    j, i = r & 15, r >> 4
    want = jnp.where(j == 0, 127 + i, jnp.where(j == 15, 143 + i, -1))
    q_fwd[0:288, :] = hot(c == want).astype(BF)
    r, c = iota((32, 256), 0), iota((32, 256), 1)
    k, north = r & 15, r >= 16
    flip = jnp.where(north, flips[1], flips[0])
    pick = jnp.where(north, picks[1], picks[0])
    want = jnp.where(north, 64, 0) + 16 * pick + jnp.where(flip == 1, 15 - k, k)
    q_fwd[288:320, :] = hot(c == want).astype(BF)

    def halo_cells(p, q):
        block, k = p >> 4, p & 15
        low, high = k == 0, k == 15
        corner_at = (0, 15, 272, 287)
        want = jnp.where(block == 0, 288 + k, jnp.where(block == 1, 304 + k, jnp.where(
            block == 2, 16 * k + 16, jnp.where(block == 3, 16 * k + 31, -1))))
        half = jnp.full_like(want, -1)
        ends = ((0, 1), (2, 3), (0, 2), (1, 3))
        for b in range(4):
            first, second = ends[b]
            half = jnp.where((block == b) & low & (rules[first] == 1), corner_at[first], half)
            half = jnp.where((block == b) & high & (rules[second] == 1), corner_at[second], half)
            want = jnp.where((block == 4 + b) & low & (rules[b] != 1), corner_at[b], want)
        return (hot(q == want) + hot(q == half, 0.5)).astype(BF)

    q_back[...] = halo_cells(iota((128, 384), 0), iota((128, 384), 1))
    q_act[...] = halo_cells(iota((320, 128), 1), iota((320, 128), 0))

    for layer in (layer1, layer2):
        g_pad = layer[2]
        g_pad[0:32, :] = jnp.zeros((32, C2), BF)
        g_pad[288:416, :] = jnp.zeros((128, C2), BF)
        layer[4][320:384, :] = jnp.zeros((64, layer[4].shape[1]), BF)

    red2 = Reduce(MA, red2_refs, (x, y, z, core, device))
    red1 = Reduce(MB, red1_refs, (x, y, z, core, device))
    used = FIRST_UNITS + LAST_UNITS
    red1.halves[:, used:B_UNITS] = jnp.zeros((2, B_UNITS - used, 16, 128), BF)
    red1.a3[6:8] = jnp.zeros((2, 16, 128), BF)

    for slot in range(4):
        remote(rules_out, rules_in.at[slot], rule_send.at[slot], rule_recv.at[slot], west).wait_recv()

    r, c = iota((16, 256), 0), iota((16, 256), 1)
    for side in range(2):
        def source(position):
            return 64 * side + 16 * picks[side] + jnp.where(flips[side] == 1, 15 - position, position)

        rows = 2 * side
        w_pick, w_flip = wide(rules_in[2, rows:rows + 1, :], 2), wide(rules_in[2, rows + 1:rows + 2, :], 2)
        e_pick, e_flip = wide(rules_in[3, rows:rows + 1, :], 2), wide(rules_in[3, rows + 1:rows + 2, :], 2)
        w_at = 160 + 32 * side + corner_slot(w_pick, jnp.where(w_flip == 1, 0, 1))
        e_at = 176 + 32 * side + corner_slot(e_pick, jnp.where(e_flip == 1, 1, 0))
        w_rule, e_rule = rules[2 * side] == 1, rules[2 * side + 1] == 1
        shape = (16, 256)
        w_main = jnp.where(w_rule, jnp.full(shape, -1), jnp.broadcast_to(w_at, shape))
        e_main = jnp.where(e_rule, jnp.full(shape, -1), jnp.broadcast_to(e_at, shape))
        w_a, w_c = jnp.where(w_rule, source(0), -1), jnp.where(w_rule, 128 + 15 * side, -1)
        e_a, e_c = jnp.where(e_rule, source(15), -1), jnp.where(e_rule, 144 + 15 * side, -1)
        w_row = hot(c == w_main) + hot(c == w_a, 0.5) + hot(c == w_c, 0.5)
        e_row = hot(c == e_main) + hot(c == e_a, 0.5) + hot(c == e_c, 0.5)
        values = jnp.where(r == 0, w_row, jnp.where(r == 15, e_row, 0.0))
        q_fwd[272 * side:272 * side + 16, :] = values.astype(BF)

    face = (jnp.where(below, 0, 1), jnp.where(above, 1, 0))
    facing = []
    for side in range(2):
        south = face[side] == 0
        facing.append((
            jnp.where(south, rules_in[side, 0:1, 0:128], rules_in[side, 2:3, 0:128]),
            jnp.where(south, rules_in[side, 1:2, 0:128], rules_in[side, 3:4, 0:128]),
        ))
    p = iota((1, 128), 1)
    block, k = p >> 4, p & 15
    on_north = (block == 1) | (block >= 6)
    pick = jnp.where(on_north, facing[1][0], facing[0][0])
    flip = jnp.where(on_north, facing[1][1], facing[0][1])
    position = jnp.where(block < 2, k, jnp.where((block & 1) == 1, 15, 0))
    target = edge_cell(pick, flip, position)
    target = jnp.where(block == 2, 16 * k + 15, jnp.where(block == 3, 16 * k, target))
    target = jnp.where((block >= 4) & (k != 0), -1, target)
    place_grads = hot(iota((256, 128), 0) == target).astype(BF)

    r, c = iota((32, 256), 0), iota((32, 256), 1)
    pick = jnp.where(r < 16, wide(facing[0][0], 2), wide(facing[1][0], 2))
    flip = jnp.where(r < 16, wide(facing[0][1], 2), wide(facing[1][1], 2))
    take_cells = hot(c == edge_cell(pick, flip, r & 15)).astype(BF)
    r, c = iota((64, 384), 0), iota((64, 384), 1)
    row = r & 31
    take_strips = hot((row < 18) & (c == 16 * row + jnp.where(r < 32, 15, 0))).astype(BF)
    tap, which = r & 15, r >> 4
    tap_row = (tap * 11) >> 5
    pick = jnp.where(which < 2, wide(facing[0][0], 3), wide(facing[1][0], 3))
    flip = jnp.where(which < 2, wide(facing[0][1], 3), wide(facing[1][1], 3))
    at = 16 * tap_row + edge_cell(pick, flip, jnp.where((which & 1) == 1, 15, 0))
    take_corners = [
        hot((tap < 9) & (tap - 3 * tap_row == dw) & (c == at)).astype(BF) for dw in range(3)
    ]

    def patch_sends():
        cells, strips, corners, got_cells, got_strips, got_corners, send, recv = patch_refs
        padded = layer1[1]
        for dh in range(3):
            cells[:, 384 * dh:384 * dh + 384] = mm(take_cells, padded[16 * dh:16 * dh + 256, :]).astype(BF)
        strips[...] = mm(take_strips, padded[...]).astype(BF).reshape(2, 32, 3 * C1)
        values = mm(take_corners[0], padded[:, 0:C1])
        for dw in (1, 2):
            values = values + mm(take_corners[dw], padded[:, dw * C1:(dw + 1) * C1])
        corners[...] = values.astype(BF).reshape(4, 16, C1)
        copies = []
        for side in range(2):
            copies.append(remote(cells.at[16 * side:16 * side + 16],
                                 got_cells.at[pl.ds(pl.multiple_of(16 * seen[side], 16), 16)],
                                 send.at[side], recv.at[seen[side]], vert[side]))
        copies.append(remote(strips.at[0], got_strips.at[0], send.at[2], recv.at[2], east))
        copies.append(remote(strips.at[1], got_strips.at[1], send.at[3], recv.at[3], west))
        for i, (target_at, slot) in enumerate(diagonal):
            copies.append(remote(corners.at[i], got_corners.at[slot], send.at[4 + i], recv.at[4 + slot], target_at))
        for copy in copies:
            copy.start()
        return copies

    def patch_waits():
        cells, strips, corners, got_cells, got_strips, got_corners, send, recv = patch_refs
        for i in range(2):
            remote(cells.at[0:16], got_cells.at[16 * i:16 * i + 16], send.at[i], recv.at[i], west).wait_recv()
            remote(strips.at[i], got_strips.at[i], send.at[2 + i], recv.at[2 + i], west).wait_recv()
        r, c = iota((32, 64), 0), iota((32, 64), 1)
        both = got_strips[...].reshape(64, 3 * C1)
        for dh in range(3):
            spread_rows = hot(c == jnp.where(r < 16, r, r + 16) + dh).astype(BF)
            got_cells[32:64, 384 * dh:384 * dh + 384] = mm(spread_rows, both).astype(BF)
        for i in range(4):
            remote(corners.at[i], got_corners.at[i], send.at[4 + i], recv.at[4 + i], west).wait_recv()
        r, c = iota((64, 64), 0), iota((64, 64), 1)
        taps = got_corners[...].reshape(64, C1)
        for tap in range(9):
            first_row = hot(((r & 15) == 0) & (c == r + tap)).astype(BF)
            got_cells[64:128, C1 * tap:C1 * tap + C1] = mm(first_row, taps).astype(BF)

    def pad_tile(layer, tile, cells, channels):
        ext, padded = layer[:2]
        south, north = cells[288:304], cells[304:320]
        ext[8:24, :] = south
        ext[24:280, :] = tile.astype(F32)
        ext[280:296, :] = north
        j = iota((288, channels), 0) & 15
        padded[0:288, 0:channels] = jnp.where(j == 0, cells[0:288], ext[7:295, :]).astype(BF)
        padded[0:288, channels:2 * channels] = ext[8:296, :].astype(BF)
        padded[0:288, 2 * channels:] = jnp.where(j == 15, cells[0:288], ext[9:297, :]).astype(BF)

    def convolve(layer, weight):
        padded = layer[1]
        total = mm(padded[0:256, :], weight[0])
        for dh in (1, 2):
            total = total + mm(padded[16 * dh:16 * dh + 256, :], weight[dh])
        return total

    def input_side(layer, weight, channels):
        g_pad, by_shift, leaving, out = layer[2:6]
        total = mm_nt(g_pad[32:320, :], weight[0])
        for dh in (1, 2):
            at = 32 - 16 * dh
            total = total + mm_nt(g_pad[at:at + 288, :], weight[dh])
        by_shift[8:296, :] = total
        j = iota((288, channels), 0) & 15
        centre = by_shift[8:296, channels:2 * channels]
        centre = centre + jnp.where(j == 15, 0.0, by_shift[9:297, 0:channels])
        centre = centre + jnp.where(j == 0, 0.0, by_shift[7:295, 2 * channels:])
        centre = centre.astype(BF)
        sides = jnp.where(j == 0, by_shift[8:296, 0:channels], by_shift[8:296, 2 * channels:])
        sides = jnp.where((j == 0) | (j == 15), sides, 0.0)
        leaving[0:288, :] = sides.astype(BF)
        leaving[288:304, :] = centre[0:16]
        leaving[304:320, :] = centre[272:288]
        out[...] = mm(q_back[...], leaving[...]).astype(BF)
        return centre[16:272]

    def grad_sends(layer):
        out, got, send, recv = layer[5:9]
        copies = []
        for side in range(2):
            copies.append(remote(out.at[16 * side:16 * side + 16],
                                 got.at[pl.ds(pl.multiple_of(16 * seen[side], 16), 16)],
                                 send.at[side], recv.at[seen[side]], vert[side]))
        copies.append(remote(out.at[32:48], got.at[32:48], send.at[2], recv.at[2], west))
        copies.append(remote(out.at[48:64], got.at[48:64], send.at[3], recv.at[3], east))
        for i, (target_at, slot) in enumerate(diagonal):
            copies.append(remote(out.at[64 + 16 * i:80 + 16 * i],
                                 got.at[pl.ds(pl.multiple_of(64 + 16 * slot, 16), 16)],
                                 send.at[4 + i], recv.at[4 + slot], target_at))
        for copy in copies:
            copy.start()
        return copies

    def grad_waits(layer):
        out, got, send, recv = layer[5:9]
        for i in range(8):
            remote(out.at[0:16], got.at[16 * i:16 * i + 16], send.at[i], recv.at[i], west).wait_recv()

    def weight_grad(block, spots):
        block = block.astype(BF)
        units = block.shape[0] // 16
        for h in range(2):
            values = block[:, 128 * h:128 * h + 128].reshape(units, 16, 128)
            for first, count, red, to in spots:
                red.halves[h, to:to + count] = values[first:first + count]

    edge_waits()
    pad_tile(layer1, feat_ref[...], mm(q_fwd[...], edges[1][...]), C1)
    sent += patch_sends()
    loads[4].wait()
    pre1 = convolve(layer1, w1)
    cdf1 = normal_cdf(pre1)
    act1 = (pre1 * cdf1).astype(BF)
    slope1[...] = gelu_slope(pre1, cdf1)
    for dh in range(3):
        windows[dh] = layer1[1][16 * dh:16 * dh + 256, :].T
    r, c = iota((256, 64), 0), iota((256, 64), 1)
    spread = hot(c == 8 * (r >> 5) + ((r & 15) >> 1), 0.25).astype(BF)
    loads[5].wait()
    cot = mm(spread, cot_ref[...])
    loads[6].wait()

    patch_waits()
    patches = patch_refs[3]
    halo_pre = mm(patches[:, 0:384], w1[0])
    for dh in (1, 2):
        halo_pre = halo_pre + mm(patches[:, 384 * dh:384 * dh + 384], w1[dh])
    halo_cdf = normal_cdf(halo_pre)
    halo_act = (halo_pre * halo_cdf).astype(BF)
    pad_tile(layer2, act1, mm(q_act[...], halo_act), C2)
    second_pre = convolve(layer2, w2)
    cdf2 = normal_cdf(second_pre)
    grad2 = (cot * gelu_slope(second_pre, cdf2)).astype(BF)
    layer2[2][32:288, :] = grad2
    for dh in range(3):
        spots = [(0, 48, red2, 48 * dh)] if dh < 2 else [(0, 32, red2, 96), (32, 16, red1, FIRST_UNITS)]
        weight_grad(mm_tn(layer2[1][16 * dh:16 * dh + 256, :], grad2), spots)
        red2.core_send(48 * dh, spots[0][1])
    centre2 = input_side(layer2, w2, C2)
    sent += grad_sends(layer2)

    own = (centre2.astype(F32) * slope1[...]).astype(BF)
    leaving = (layer2[5][...].astype(F32) * gelu_slope(halo_pre, halo_cdf)).astype(BF)
    for dh in range(3):
        block = mm(windows[dh], own) + mm_tn(patches[:, 384 * dh:384 * dh + 384], leaving)
        weight_grad(block, [(0, 24, red1, 24 * dh)])
    red1.core_send(0, B_UNITS)
    red2.core_add()
    red1.core_add()
    pre2[...] = second_pre * cdf2

    r, c = iota((64, 256), 0), iota((64, 256), 1)
    gather_cells = hot(r == 8 * (c >> 5) + ((c & 15) >> 1), 0.25).astype(BF)
    act2 = pre2[...]
    high = act2.astype(BF)
    low = (act2 - high.astype(F32)).astype(BF)
    pooled_ref[...] = (mm(gather_cells, high) + mm(gather_cells, low)).astype(BF)

    red2.first_add()
    red1.first_add()

    grad_waits(layer2)
    first_grad = centre2.astype(F32) + mm(place_grads, layer2[6][...])
    layer1[2][32:288, :] = (first_grad * slope1[...]).astype(BF)
    centre1 = input_side(layer1, w1, C1)
    sent += grad_sends(layer1)

    red2.second_add()
    red1.second_add()
    red2.near_add()
    red1.near_add()

    grad_waits(layer1)
    grad_ref[...] = (centre1.astype(F32) + mm(place_grads, layer1[6][...])).astype(BF)

    for copy in sent + rule_copies:
        copy.wait_send()
    red2.flush()
    red1.flush()
    red2.far_add()
    red1.far_add()
    red2.gather_second()
    red1.gather_second()
    red2.near_flush()
    red1.near_flush()
    red2.gather_first()
    red1.gather_first()
    red2.gather_core()
    red1.gather_core()
    red2.gather_done()
    red2.flush()
    square_ref[...] = sum_squares(second_out, 0, A_UNITS, jnp.zeros((16, 128), F32))
    red1.gather_done()
    red1.flush()


def sum_squares(ref, at, count, total):
    def body(i, total):
        values = ref[:, pl.ds(at + i * 8, 8)].astype(F32)
        return total + jnp.sum(values * values, axis=(0, 1))

    return lax.fori_loop(0, count // 8, body, total)


def finish_kernel(pooled_ref, grad_ref, first_ref, second_ref, square_ref, pooled_out, grad_out, first_out, second_out,
                  first_rows, second_rows, sems):
    copies = [pltpu.make_async_copy(pooled_ref, pooled_out, sems.at[0]),
              pltpu.make_async_copy(grad_ref, grad_out, sems.at[1])]
    for copy in copies:
        copy.start()

    total = sum_squares(first_ref, 0, FIRST_UNITS + LAST_UNITS, square_ref[...])
    squared = jnp.sum(jnp.sum(total, axis=0, keepdims=True), axis=1, keepdims=True)
    target_norm = math.sqrt(9.0 * (C1 + C2) * C2)
    scale = jnp.broadcast_to(target_norm / jnp.sqrt(squared + 1e-06), (16, 128))

    def write(ref, at, to, count, out):
        def body(i, carry):
            for h in range(2):
                values = ref[h, pl.ds(at + i * 8, 8)].astype(F32) * scale
                rows = pl.ds(pl.multiple_of((to + i * 8) * 16, 128), 128)
                out[rows, 128 * h:128 * h + 128] = values.astype(BF).reshape(128, 128)
            return carry

        lax.fori_loop(0, count // 8, body, 0)

    jobs = [(second_ref, n * 64, n * 64, 64, second_rows, second_out) for n in range(2)]
    jobs.append((first_ref, 0, 0, FIRST_UNITS, first_rows, first_out))
    jobs.append((first_ref, FIRST_UNITS, A_UNITS, LAST_UNITS, second_rows, second_out))
    for n, (ref, at, to, count, rows, out) in enumerate(jobs):
        write(ref, at, to, count, rows)
        span = pl.ds(16 * to, 16 * count)
        copies.append(pltpu.make_async_copy(rows.at[span], out.at[span], sems.at[2 + n]))
        copies[-1].start()
    for copy in copies:
        copy.wait()


def on_device(features, conv_first, conv_second, cotangent, edge_pick, edge_flip, corner_rule):
    vmem = pl.BlockSpec(memory_space=pltpu.VMEM)
    hbm = pl.BlockSpec(memory_space=pltpu.HBM)
    pooled, input_grad, first, second, square = pl.pallas_call(
        step_kernel,
        out_shape=(
            jax.ShapeDtypeStruct((64, C2), BF),
            jax.ShapeDtypeStruct((256, C1), BF),
            jax.ShapeDtypeStruct((2, B_UNITS, 16, 128), BF),
            jax.ShapeDtypeStruct((2, A_UNITS, 16, 128), BF),
            jax.ShapeDtypeStruct((16, 128), F32),
        ),
        in_specs=[hbm] * 7,
        out_specs=[vmem] * 5,
        scratch_shapes=(
            edge_scratch(C1)
            + patch_scratch()
            + layer_scratch(C1)
            + layer_scratch(C2)
            + reduce_scratch(*MA)
            + reduce_scratch(*MB)
            + [
                pltpu.VMEM((256, C1), BF),
                pltpu.VMEM((3, 3 * C1, C2), BF),
                pltpu.VMEM((3, 3 * C2, C2), BF),
                pltpu.VMEM((64, C2), BF),
                pltpu.SMEM((1, 1, 2), jnp.int32),
                pltpu.SMEM((1, 1, 2), jnp.int32),
                pltpu.SMEM((1, 1, 4), jnp.int32),
                pltpu.SemaphoreType.DMA((7,)),
                pltpu.VMEM((8, 128), jnp.int32),
                pltpu.VMEM((4, 8, 128), jnp.int32),
                pltpu.SemaphoreType.DMA((4,)),
                pltpu.SemaphoreType.DMA((4,)),
                pltpu.VMEM((320, 256), BF),
                pltpu.VMEM((128, 384), BF),
                pltpu.VMEM((320, 128), BF),
                pltpu.VMEM((256, C2), F32),
                pltpu.VMEM((256, C2), F32),
                pltpu.VMEM((3, 3 * C1, 256), BF),
            ]
        ),
        compiler_params=pltpu.CompilerParams(
            collective_id=0, has_side_effects=True, vmem_limit_bytes=32 * 1024 * 1024
        ),
        name="level_step",
    )(*(
        pltpu.with_memory_space_constraint(value, pltpu.HBM)
        for value in (
            features.reshape(256, C1),
            conv_first.reshape(3, 3 * C1, C2),
            conv_second.reshape(3, 3 * C2, C2),
            cotangent.reshape(64, C2),
            edge_pick,
            edge_flip,
            corner_rule,
        )
    ))
    pooled, input_grad, first, second = pl.pallas_call(
        finish_kernel,
        out_shape=(
            jax.ShapeDtypeStruct((64, C2), BF),
            jax.ShapeDtypeStruct((256, C1), BF),
            jax.ShapeDtypeStruct((9 * C1, C2), BF),
            jax.ShapeDtypeStruct((9 * C2, C2), BF),
        ),
        in_specs=[vmem] * 5,
        out_specs=[hbm] * 4,
        scratch_shapes=[
            pltpu.VMEM((9 * C1, C2), BF),
            pltpu.VMEM((9 * C2, C2), BF),
            pltpu.SemaphoreType.DMA((6,)),
        ],
        compiler_params=pltpu.CompilerParams(vmem_limit_bytes=16 * 1024 * 1024),
        name="scale_outputs",
    )(pooled, input_grad, first, second, square)
    return (
        pooled.reshape(1, 1, 8, 8, C2),
        input_grad.reshape(1, 1, 16, 16, C1),
        first.reshape(3, 3, C1, C2),
        second.reshape(3, 3, C2, C2),
    )


def solution(mesh):
    return jax.shard_map(
        on_device,
        mesh=mesh,
        in_specs=(
            P("lon", "lat", None, None, None),
            P(),
            P(),
            P("lon", "lat", None, None, None),
            P("lon", "lat", None),
            P("lon", "lat", None),
            P("lon", "lat", None),
        ),
        out_specs=(P("lon", "lat", None, None, None), P("lon", "lat", None, None, None), P(), P()),
        check_vma=False,
    )
```

```python
import math

import jax
import jax.numpy as jnp
from jax import lax
from jax.experimental import pallas as pl
from jax.experimental.pallas import tpu as pltpu
from jax.sharding import PartitionSpec as P

MESH = pl.DeviceIdType.MESH
BF = jnp.bfloat16
F32 = jnp.float32
NX, NY, NZ = 4, 4, 16
LON, LAT = 2 * NY * NZ, 4
C1, C2 = 128, 256


def normal_cdf(values):
    return 0.5 * (1.0 + lax.erf(values * (1.0 / math.sqrt(2.0))))


def gelu_slope(values, cdf):
    return cdf + values * jnp.exp(-0.5 * values * values) * (1.0 / math.sqrt(2.0 * math.pi))


def iota(shape, dim):
    return lax.broadcasted_iota(jnp.int32, shape, dim)


def hot(cond, value=1.0):
    return jnp.where(cond, jnp.float32(value), jnp.float32(0.0))


def wide(row, count):
    return jnp.concatenate([row] * count, axis=1)


def edge_cell(edge, flip, position):
    at = jnp.where(flip == 1, 15 - position, position)
    return jnp.where(edge == 0, at, jnp.where(edge == 1, 240 + at, jnp.where(edge == 2, 16 * at, 16 * at + 15)))


def mm(a, b):
    return jnp.dot(a, b, preferred_element_type=F32)


def mm_nt(a, b):
    return lax.dot_general(a, b, (((1,), (1,)), ((), ())), preferred_element_type=F32)


def mm_tn(a, b):
    return lax.dot_general(a, b, (((0,), (0,)), ((), ())), preferred_element_type=F32)


def remote(src, dst, send_sem, recv_sem, device):
    return pltpu.make_async_remote_copy(
        src_ref=src, dst_ref=dst, send_sem=send_sem, recv_sem=recv_sem,
        device_id=device, device_id_type=MESH,
    )


def corner_slot(edge, at_end):
    return jnp.where(
        edge == 0, at_end, jnp.where(edge == 1, 2 + at_end, jnp.where(edge == 2, 2 * at_end, 1 + 2 * at_end))
    )


class Reduce:
    def __init__(self, m, refs, place):
        self.m = m
        self.total = m[0] + m[1]
        self.start = (0, 16 * m[0])
        (self.halves, self.r0, self.a1, r1a, r1b, a2a, a2b, r2a, r2b, self.a3, self.n3, self.f3, self.out,
         self.s_send, self.s_recv, self.g_send, self.g_recv) = refs
        self.r1, self.a2, self.r2 = (r1a, r1b), (a2a, a2b), (r2a, r2b)
        self.x, self.y, self.z, self.core, self.device = place
        self.near, self.far = lax.rem(self.z, 4), lax.div(self.z, 4)
        self.pending = []
        self.pieces = []
        self.waited = 0

    def other_core(self):
        return self.device(self.x, self.y, self.z, 1 - self.core)

    def peer(self, axis, d):
        x = lax.rem(self.x + d, NX) if axis == "x" else self.x
        y = lax.rem(self.y + d, NY) if axis == "y" else self.y
        return self.device(x, y, self.z, self.core)

    def axes(self, part):
        return ("x", "y") if part == 0 else ("y", "x")

    def coords(self, part):
        return (self.x, self.y) if part == 0 else (self.y, self.x)

    def send(self, copy):
        copy.start()
        self.pending.append(copy)

    def received(self, ref, sem):
        remote(ref, ref, self.s_send.at[0], sem, self.other_core()).wait_recv()

    def flush(self):
        for copy in self.pending:
            copy.wait_send()
        self.pending = []

    def near_flush(self):
        @pl.when(self.near < self.total // 2)
        def _():
            for copy in self.near_copies():
                copy.wait_send()

    def core_send(self, at, count):
        k = len(self.pieces)
        self.pieces.append((at, count))
        self.send(remote(self.halves.at[1 - self.core, at:at + count], self.r0.at[at:at + count],
                         self.s_send.at[k], self.s_recv.at[k], self.other_core()))

    def core_add(self):
        for part in range(2):
            n = 4 * self.m[part]
            mine = self.coords(part)[0]
            while self.waited < len(self.pieces) and self.pieces[self.waited][0] < self.start[part] + 4 * n:
                at, count = self.pieces[self.waited]
                self.received(self.r0.at[at:at + count], self.s_recv.at[self.waited])
                self.waited += 1
            k = 3 + part
            for d in (2, 1, 3, 0):
                at = pl.ds(self.start[part] + lax.rem(mine + d, 4) * n, n)
                self.a1[at] = (self.halves[self.core, at].astype(F32) + self.r0[at].astype(F32)).astype(BF)
                if d:
                    self.send(remote(self.a1.at[at], self.r1[part].at[d - 1],
                                     self.s_send.at[3 * k - 7 + d], self.s_recv.at[k],
                                     self.peer(self.axes(part)[0], d)))

    def first_add(self):
        for part in range(2):
            m = self.m[part]
            r1, a2, r2 = self.r1[part], self.a2[part], self.r2[part]
            ca, cb = self.coords(part)
            self.received(r1, self.s_recv.at[3 + part])
            k = 5 + part
            for d in (2, 1, 3, 0):
                block = lax.rem(cb + d, 4)
                at = pl.ds(block * m, m)
                total = self.a1[pl.ds(self.start[part] + (ca * 4 + block) * m, m)].astype(F32)
                for e in range(3):
                    total = total + r1[e, at].astype(F32)
                a2[at] = total.astype(BF)
                if d:
                    self.send(remote(a2.at[at], r2.at[d - 1],
                                     self.s_send.at[3 * k - 7 + d], self.s_recv.at[k],
                                     self.peer(self.axes(part)[1], d)))

    def second_add(self):
        for part in range(2):
            m = self.m[part]
            a2, r2 = self.a2[part], self.r2[part]
            cb = self.coords(part)[1]
            self.received(r2, self.s_recv.at[5 + part])
            total = a2[pl.ds(cb * m, m)].astype(F32)
            for e in range(3):
                total = total + r2[e].astype(F32)
            self.a3[part * self.m[0]:part * self.m[0] + m] = total.astype(BF)
        for d in (2, 1, 3):
            owner = lax.rem(self.near + d, 4)
            self.send(remote(self.a3.at[pl.ds(2 * owner, 2)], self.n3.at[d - 1], self.s_send.at[14 + d],
                             self.s_recv.at[7], self.device(self.x, self.y, 4 * self.far + owner, self.core)))

    def near_add(self):
        self.received(self.n3, self.s_recv.at[7])
        total = self.a3[pl.ds(2 * self.near, 2)].astype(F32)
        for e in range(3):
            total = total + self.n3[e].astype(F32)
        self.f3[self.far] = total.astype(BF)
        for d in (2, 1, 3):
            self.send(remote(self.f3.at[self.far], self.f3.at[self.far], self.s_send.at[17 + d], self.s_recv.at[8],
                             self.device(self.x, self.y, 4 * lax.rem(self.far + d, 4) + self.near, self.core)))

    def unit_at(self, u):
        ma, mb = self.m
        first = (self.x * 4 + self.y) * ma + u
        second = self.start[1] + (self.y * 4 + self.x) * mb + u - ma
        return jnp.where(u < ma, first, second)

    def near_copies(self):
        at = pl.ds(self.unit_at(2 * self.near), 2)
        return [
            remote(self.out.at[self.core, at], self.out.at[self.core, at], self.g_send.at[19 + d], self.g_recv.at[19 + d],
                   self.device(self.x, self.y, 4 * self.far + lax.rem(self.near + d, 4), self.core))
            for d in (2, 1, 3)
        ]

    def far_add(self):
        self.received(self.f3.at[0:3], self.s_recv.at[8])

        @pl.when(self.near < self.total // 2)
        def _():
            total = self.f3[0].astype(F32)
            for e in range(1, 4):
                total = total + self.f3[e].astype(F32)
            self.out[self.core, pl.ds(self.unit_at(2 * self.near), 2)] = total.astype(BF)
            for copy in self.near_copies():
                copy.start()

    def gather_second(self):
        for d in (1, 3, 2):
            owner = lax.rem(self.near + 4 - d, 4)

            @pl.when(owner < self.total // 2)
            def _():
                self.received(self.out.at[self.core, pl.ds(self.unit_at(2 * owner), 2)], self.g_recv.at[19 + d])

        for part in range(2):
            m = self.m[part]
            ca, cb = self.coords(part)
            at = pl.ds(self.start[part] + (ca * 4 + cb) * m, m)
            for d in (2, 1, 3):
                self.send(remote(self.out.at[self.core, at], self.out.at[self.core, at], self.g_send.at[part * 3 + d - 1],
                                 self.g_recv.at[part], self.peer(self.axes(part)[1], d)))

    def gather_first(self):
        for part in range(2):
            m = self.m[part]
            ca = self.coords(part)[0]
            self.received(self.r2[part], self.g_recv.at[part])
            at = pl.ds(self.start[part] + ca * 4 * m, 4 * m)
            for d in (2, 1, 3):
                k = 6 + part * 3 + d - 1
                self.send(remote(self.out.at[self.core, at], self.out.at[self.core, at], self.g_send.at[k],
                                 self.g_recv.at[k], self.peer(self.axes(part)[0], d)))
            self.to_core(part, 0, at)

    def to_core(self, part, d, at):
        k = 12 + part * 4 + d
        self.send(remote(self.out.at[self.core, at], self.out.at[self.core, at], self.g_send.at[k],
                         self.g_recv.at[k], self.other_core()))

    def block_of(self, part, d):
        n = 4 * self.m[part]
        return pl.ds(self.start[part] + lax.rem(self.coords(part)[0] + 4 - d, 4) * n, n)

    def gather_core(self):
        for d in (1, 3, 2):
            for part in range(2):
                at = self.block_of(part, d)
                self.received(self.out.at[self.core, at], self.g_recv.at[6 + part * 3 + d - 1])
                self.to_core(part, d, at)

    def gather_done(self):
        for d in (0, 1, 3, 2):
            for part in range(2):
                at = self.block_of(part, d)
                self.received(self.out.at[1 - self.core, at], self.g_recv.at[12 + part * 4 + d])


def reduce_scratch(ma, mb):
    units = 16 * (ma + mb)
    return [
        pltpu.VMEM((2, units, 16, 128), BF),
        pltpu.VMEM((units, 16, 128), BF),
        pltpu.VMEM((units, 16, 128), BF),
        pltpu.VMEM((3, 4 * ma, 16, 128), BF),
        pltpu.VMEM((3, 4 * mb, 16, 128), BF),
        pltpu.VMEM((4 * ma, 16, 128), BF),
        pltpu.VMEM((4 * mb, 16, 128), BF),
        pltpu.VMEM((3, ma, 16, 128), BF),
        pltpu.VMEM((3, mb, 16, 128), BF),
        pltpu.VMEM((8, 16, 128), BF),
        pltpu.VMEM((3, 2, 16, 128), BF),
        pltpu.VMEM((4, 2, 16, 128), BF),
        pltpu.SemaphoreType.DMA((21,)),
        pltpu.SemaphoreType.DMA((21,)),
        pltpu.SemaphoreType.DMA((23,)),
        pltpu.SemaphoreType.DMA((23,)),
    ]


N_REDUCE = 16
MA, MB = (4, 4), (4, 2)
A_UNITS, B_UNITS, FIRST_UNITS, LAST_UNITS = 128, 96, 72, 16


def edge_scratch(channels):
    return [
        pltpu.VMEM((80, channels), BF),
        pltpu.VMEM((256, channels), BF),
        pltpu.SemaphoreType.DMA((8,)),
        pltpu.SemaphoreType.DMA((8,)),
    ]


def patch_scratch():
    return [
        pltpu.VMEM((32, 9 * C1), BF),
        pltpu.VMEM((2, 32, 3 * C1), BF),
        pltpu.VMEM((4, 16, C1), BF),
        pltpu.VMEM((128, 9 * C1), BF),
        pltpu.VMEM((2, 32, 3 * C1), BF),
        pltpu.VMEM((4, 16, C1), BF),
        pltpu.SemaphoreType.DMA((8,)),
        pltpu.SemaphoreType.DMA((8,)),
    ]


def layer_scratch(channels):
    return [
        pltpu.VMEM((304, channels), F32),
        pltpu.VMEM((384, 3 * channels), BF),
        pltpu.VMEM((416, C2), BF),
        pltpu.VMEM((304, 3 * channels), F32),
        pltpu.VMEM((384, channels), BF),
        pltpu.VMEM((128, channels), BF),
        pltpu.VMEM((128, channels), BF),
        pltpu.SemaphoreType.DMA((8,)),
        pltpu.SemaphoreType.DMA((8,)),
    ]


N_EDGE, N_PATCH, N_LAYER = 4, 8, 9


def step_kernel(*refs):
    (feat_hbm, w1_hbm, w2_hbm, cot_hbm, pick_hbm, flip_hbm, rule_hbm,
     pooled_ref, grad_ref, first_out, second_out, square_ref) = refs[:12]
    refs = refs[12:]
    edges, refs = refs[:N_EDGE], refs[N_EDGE:]
    patch_refs, refs = refs[:N_PATCH], refs[N_PATCH:]
    layer1, refs = refs[:N_LAYER], refs[N_LAYER:]
    layer2, refs = refs[:N_LAYER], refs[N_LAYER:]
    red2_refs, refs = refs[:N_REDUCE], refs[N_REDUCE:]
    red1_refs, refs = refs[:N_REDUCE], refs[N_REDUCE:]
    (feat_ref, w1, w2, cot_ref, pick_ref, flip_ref, rule_ref, load_sem,
     rules_out, rules_in, rule_send, rule_recv, q_fwd, q_back, q_act, slope1, pre2,
     windows) = refs
    red2_refs = red2_refs[:12] + (second_out,) + red2_refs[12:]
    red1_refs = red1_refs[:12] + (first_out,) + red1_refs[12:]

    lon, lat = lax.axis_index("lon"), lax.axis_index("lat")
    y = lax.div(lon, 2 * NZ)
    z = lax.div(lax.rem(lon, 2 * NZ), 2)
    x = lax.rem(lon, 2) * 2 + lax.div(lat, 2)
    core = lax.rem(lat, 2)

    def device(x_at, y_at, z_at, core_at):
        return (y_at * (2 * NZ) + z_at * 2 + lax.div(x_at, 2), lax.rem(x_at, 2) * 2 + core_at)

    across = lax.rem(lon + LON // 2, LON)
    below, above = lat == 0, lat == LAT - 1
    vert = (
        (jnp.where(below, across, lon), jnp.where(below, lat, lat - 1)),
        (jnp.where(above, across, lon), jnp.where(above, lat, lat + 1)),
    )
    seen = (jnp.where(below, 0, 1), jnp.where(above, 1, 0))

    def west_of(at):
        return (lax.rem(at[0] + LON - 1, LON), at[1])

    def east_of(at):
        return (lax.rem(at[0] + 1, LON), at[1])

    here = (lon, lat)
    west, east = west_of(here), east_of(here)
    diagonal = [
        (west_of(vert[0]), 2 * seen[0] + 1),
        (east_of(vert[0]), 2 * seen[0]),
        (west_of(vert[1]), 2 * seen[1] + 1),
        (east_of(vert[1]), 2 * seen[1]),
    ]

    barrier = pltpu.get_barrier_semaphore()
    partners = [device(x, y, lax.rem(z + 4 * d, NZ), core) for d in (2, 1, 3)]
    partners += [d[0] for d in diagonal] + [west, east, vert[0], vert[1]]
    for d in (2, 1, 3):
        partners.append(device(x, y, 4 * lax.div(z, 4) + lax.rem(z + d, 4), core))
        partners.append(device(lax.rem(x + d, NX), y, z, core))
        partners.append(device(x, lax.rem(y + d, NY), z, core))
    partners.append(device(x, y, z, 1 - core))
    for partner in partners:
        pl.semaphore_signal(barrier, inc=1, device_id=partner, device_id_type=MESH)

    loads = [
        pltpu.make_async_copy(src, dst, load_sem.at[n])
        for n, (src, dst) in enumerate((
            (pick_hbm, pick_ref), (flip_hbm, flip_ref), (rule_hbm, rule_ref), (feat_hbm, feat_ref),
            (w1_hbm, w1), (cot_hbm, cot_ref), (w2_hbm, w2),
        ))
    ]
    for load in loads:
        load.start()

    for load in loads[:3]:
        load.wait()
    picks = [pick_ref[0, 0, s] for s in range(2)]
    flips = [flip_ref[0, 0, s] for s in range(2)]
    rules = [rule_ref[0, 0, k] for k in range(4)]

    row8 = iota((8, 128), 0)
    rules_out[...] = jnp.where(
        row8 == 0, picks[0], jnp.where(row8 == 1, flips[0], jnp.where(row8 == 2, picks[1], flips[1]))
    )

    p, cell = iota((80, 256), 0), iota((80, 256), 1)
    k = p & 15
    want = jnp.where(
        p < 16, k, jnp.where(p < 32, 240 + k, jnp.where(p < 48, 16 * k, jnp.where(p < 64, 16 * k + 15, (
            jnp.where(k == 0, 0, jnp.where(k == 1, 15, jnp.where(k == 2, 240, jnp.where(k == 3, 255, -1))))
        ))))
    )
    take_edges = hot(cell == want).astype(BF)

    loads[3].wait()
    edges[0][...] = mm(take_edges, feat_ref[...]).astype(BF)
    edges[1][224:256, :] = jnp.zeros((32, C1), BF)
    layer1[1][288:384, :] = jnp.zeros((96, 3 * C1), BF)

    pl.semaphore_wait(barrier, len(partners))

    def edge_sends():
        out, got, send, recv = edges
        copies = []
        for i, (target, slot) in enumerate(diagonal):
            copies.append(remote(out.at[64:80], got.at[pl.ds(pl.multiple_of(160 + 16 * slot, 16), 16)],
                                 send.at[4 + i], recv.at[4 + slot], target))
        for side in range(2):
            copies.append(remote(out.at[0:64], got.at[pl.ds(pl.multiple_of(64 * seen[side], 64), 64)],
                                 send.at[side], recv.at[seen[side]], vert[side]))
        copies.append(remote(out.at[32:48], got.at[144:160], send.at[2], recv.at[3], west))
        copies.append(remote(out.at[48:64], got.at[128:144], send.at[3], recv.at[2], east))
        for copy in copies:
            copy.start()
        return copies

    def edge_waits():
        out, got, send, recv = edges
        spots = [(0, 64), (64, 64), (128, 16), (144, 16), (160, 16), (176, 16), (192, 16), (208, 16)]
        for i, (at, size) in enumerate(spots):
            remote(out.at[0:size], got.at[at:at + size], send.at[i], recv.at[i], west).wait_recv()

    sent = edge_sends()
    rule_copies = []
    for i, (target, slot) in enumerate(((vert[0], seen[0]), (vert[1], seen[1]), (west, 3), (east, 2))):
        rule_copies.append(remote(rules_out, rules_in.at[slot], rule_send.at[i], rule_recv.at[slot], target))
    for copy in rule_copies:
        copy.start()

    r, c = iota((288, 256), 0), iota((288, 256), 1)
    j, i = r & 15, r >> 4
    want = jnp.where(j == 0, 127 + i, jnp.where(j == 15, 143 + i, -1))
    q_fwd[0:288, :] = hot(c == want).astype(BF)
    r, c = iota((32, 256), 0), iota((32, 256), 1)
    k, north = r & 15, r >= 16
    flip = jnp.where(north, flips[1], flips[0])
    pick = jnp.where(north, picks[1], picks[0])
    want = jnp.where(north, 64, 0) + 16 * pick + jnp.where(flip == 1, 15 - k, k)
    q_fwd[288:320, :] = hot(c == want).astype(BF)

    def halo_cells(p, q):
        block, k = p >> 4, p & 15
        low, high = k == 0, k == 15
        corner_at = (0, 15, 272, 287)
        want = jnp.where(block == 0, 288 + k, jnp.where(block == 1, 304 + k, jnp.where(
            block == 2, 16 * k + 16, jnp.where(block == 3, 16 * k + 31, -1))))
        half = jnp.full_like(want, -1)
        ends = ((0, 1), (2, 3), (0, 2), (1, 3))
        for b in range(4):
            first, second = ends[b]
            half = jnp.where((block == b) & low & (rules[first] == 1), corner_at[first], half)
            half = jnp.where((block == b) & high & (rules[second] == 1), corner_at[second], half)
            want = jnp.where((block == 4 + b) & low & (rules[b] != 1), corner_at[b], want)
        return (hot(q == want) + hot(q == half, 0.5)).astype(BF)

    q_back[...] = halo_cells(iota((128, 384), 0), iota((128, 384), 1))
    q_act[...] = halo_cells(iota((320, 128), 1), iota((320, 128), 0))

    for layer in (layer1, layer2):
        g_pad = layer[2]
        g_pad[0:32, :] = jnp.zeros((32, C2), BF)
        g_pad[288:416, :] = jnp.zeros((128, C2), BF)
        layer[4][320:384, :] = jnp.zeros((64, layer[4].shape[1]), BF)

    red2 = Reduce(MA, red2_refs, (x, y, z, core, device))
    red1 = Reduce(MB, red1_refs, (x, y, z, core, device))
    used = FIRST_UNITS + LAST_UNITS
    red1.halves[:, used:B_UNITS] = jnp.zeros((2, B_UNITS - used, 16, 128), BF)
    red1.a3[6:8] = jnp.zeros((2, 16, 128), BF)

    for slot in range(4):
        remote(rules_out, rules_in.at[slot], rule_send.at[slot], rule_recv.at[slot], west).wait_recv()

    r, c = iota((16, 256), 0), iota((16, 256), 1)
    for side in range(2):
        def source(position):
            return 64 * side + 16 * picks[side] + jnp.where(flips[side] == 1, 15 - position, position)

        rows = 2 * side
        w_pick, w_flip = wide(rules_in[2, rows:rows + 1, :], 2), wide(rules_in[2, rows + 1:rows + 2, :], 2)
        e_pick, e_flip = wide(rules_in[3, rows:rows + 1, :], 2), wide(rules_in[3, rows + 1:rows + 2, :], 2)
        w_at = 160 + 32 * side + corner_slot(w_pick, jnp.where(w_flip == 1, 0, 1))
        e_at = 176 + 32 * side + corner_slot(e_pick, jnp.where(e_flip == 1, 1, 0))
        w_rule, e_rule = rules[2 * side] == 1, rules[2 * side + 1] == 1
        shape = (16, 256)
        w_main = jnp.where(w_rule, jnp.full(shape, -1), jnp.broadcast_to(w_at, shape))
        e_main = jnp.where(e_rule, jnp.full(shape, -1), jnp.broadcast_to(e_at, shape))
        w_a, w_c = jnp.where(w_rule, source(0), -1), jnp.where(w_rule, 128 + 15 * side, -1)
        e_a, e_c = jnp.where(e_rule, source(15), -1), jnp.where(e_rule, 144 + 15 * side, -1)
        w_row = hot(c == w_main) + hot(c == w_a, 0.5) + hot(c == w_c, 0.5)
        e_row = hot(c == e_main) + hot(c == e_a, 0.5) + hot(c == e_c, 0.5)
        values = jnp.where(r == 0, w_row, jnp.where(r == 15, e_row, 0.0))
        q_fwd[272 * side:272 * side + 16, :] = values.astype(BF)

    face = (jnp.where(below, 0, 1), jnp.where(above, 1, 0))
    facing = []
    for side in range(2):
        south = face[side] == 0
        facing.append((
            jnp.where(south, rules_in[side, 0:1, 0:128], rules_in[side, 2:3, 0:128]),
            jnp.where(south, rules_in[side, 1:2, 0:128], rules_in[side, 3:4, 0:128]),
        ))
    p = iota((1, 128), 1)
    block, k = p >> 4, p & 15
    on_north = (block == 1) | (block >= 6)
    pick = jnp.where(on_north, facing[1][0], facing[0][0])
    flip = jnp.where(on_north, facing[1][1], facing[0][1])
    position = jnp.where(block < 2, k, jnp.where((block & 1) == 1, 15, 0))
    target = edge_cell(pick, flip, position)
    target = jnp.where(block == 2, 16 * k + 15, jnp.where(block == 3, 16 * k, target))
    target = jnp.where((block >= 4) & (k != 0), -1, target)
    place_grads = hot(iota((256, 128), 0) == target).astype(BF)

    r, c = iota((32, 256), 0), iota((32, 256), 1)
    pick = jnp.where(r < 16, wide(facing[0][0], 2), wide(facing[1][0], 2))
    flip = jnp.where(r < 16, wide(facing[0][1], 2), wide(facing[1][1], 2))
    take_cells = hot(c == edge_cell(pick, flip, r & 15)).astype(BF)
    r, c = iota((64, 384), 0), iota((64, 384), 1)
    row = r & 31
    take_strips = hot((row < 18) & (c == 16 * row + jnp.where(r < 32, 15, 0))).astype(BF)
    tap, which = r & 15, r >> 4
    tap_row = (tap * 11) >> 5
    pick = jnp.where(which < 2, wide(facing[0][0], 3), wide(facing[1][0], 3))
    flip = jnp.where(which < 2, wide(facing[0][1], 3), wide(facing[1][1], 3))
    at = 16 * tap_row + edge_cell(pick, flip, jnp.where((which & 1) == 1, 15, 0))
    take_corners = [
        hot((tap < 9) & (tap - 3 * tap_row == dw) & (c == at)).astype(BF) for dw in range(3)
    ]

    def patch_sends():
        cells, strips, corners, got_cells, got_strips, got_corners, send, recv = patch_refs
        padded = layer1[1]
        values = mm(take_corners[0], padded[:, 0:C1])
        for dw in (1, 2):
            values = values + mm(take_corners[dw], padded[:, dw * C1:(dw + 1) * C1])
        corners[...] = values.astype(BF).reshape(4, 16, C1)
        copies = []
        for i, (target_at, slot) in enumerate(diagonal):
            copies.append(remote(corners.at[i], got_corners.at[slot], send.at[4 + i], recv.at[4 + slot], target_at))
            copies[-1].start()
        strips[...] = mm(take_strips, padded[...]).astype(BF).reshape(2, 32, 3 * C1)
        copies.append(remote(strips.at[0], got_strips.at[0], send.at[2], recv.at[2], east))
        copies.append(remote(strips.at[1], got_strips.at[1], send.at[3], recv.at[3], west))
        for copy in copies[-2:]:
            copy.start()
        for dh in range(3):
            cells[:, 384 * dh:384 * dh + 384] = mm(take_cells, padded[16 * dh:16 * dh + 256, :]).astype(BF)
        for side in range(2):
            copies.append(remote(cells.at[16 * side:16 * side + 16],
                                 got_cells.at[pl.ds(pl.multiple_of(16 * seen[side], 16), 16)],
                                 send.at[side], recv.at[seen[side]], vert[side]))
            copies[-1].start()
        return copies

    def patch_waits():
        cells, strips, corners, got_cells, got_strips, got_corners, send, recv = patch_refs
        for i in range(2):
            remote(cells.at[0:16], got_cells.at[16 * i:16 * i + 16], send.at[i], recv.at[i], west).wait_recv()
            remote(strips.at[i], got_strips.at[i], send.at[2 + i], recv.at[2 + i], west).wait_recv()
        r, c = iota((32, 64), 0), iota((32, 64), 1)
        both = got_strips[...].reshape(64, 3 * C1)
        for dh in range(3):
            spread_rows = hot(c == jnp.where(r < 16, r, r + 16) + dh).astype(BF)
            got_cells[32:64, 384 * dh:384 * dh + 384] = mm(spread_rows, both).astype(BF)
        for i in range(4):
            remote(corners.at[i], got_corners.at[i], send.at[4 + i], recv.at[4 + i], west).wait_recv()
        r, c = iota((64, 64), 0), iota((64, 64), 1)
        taps = got_corners[...].reshape(64, C1)
        for tap in range(9):
            first_row = hot(((r & 15) == 0) & (c == r + tap)).astype(BF)
            got_cells[64:128, C1 * tap:C1 * tap + C1] = mm(first_row, taps).astype(BF)

    def pad_tile(layer, tile, cells, channels):
        ext, padded = layer[:2]
        south, north = cells[288:304], cells[304:320]
        ext[8:24, :] = south
        ext[24:280, :] = tile.astype(F32)
        ext[280:296, :] = north
        j = iota((288, channels), 0) & 15
        padded[0:288, 0:channels] = jnp.where(j == 0, cells[0:288], ext[7:295, :]).astype(BF)
        padded[0:288, channels:2 * channels] = ext[8:296, :].astype(BF)
        padded[0:288, 2 * channels:] = jnp.where(j == 15, cells[0:288], ext[9:297, :]).astype(BF)

    def convolve(layer, weight):
        padded = layer[1]
        total = mm(padded[0:256, :], weight[0])
        for dh in (1, 2):
            total = total + mm(padded[16 * dh:16 * dh + 256, :], weight[dh])
        return total

    def input_side(layer, weight, channels):
        g_pad, by_shift, leaving, out = layer[2:6]
        total = mm_nt(g_pad[32:320, :], weight[0])
        for dh in (1, 2):
            at = 32 - 16 * dh
            total = total + mm_nt(g_pad[at:at + 288, :], weight[dh])
        by_shift[8:296, :] = total
        j = iota((288, channels), 0) & 15
        centre = by_shift[8:296, channels:2 * channels]
        centre = centre + jnp.where(j == 15, 0.0, by_shift[9:297, 0:channels])
        centre = centre + jnp.where(j == 0, 0.0, by_shift[7:295, 2 * channels:])
        centre = centre.astype(BF)
        sides = jnp.where(j == 0, by_shift[8:296, 0:channels], by_shift[8:296, 2 * channels:])
        sides = jnp.where((j == 0) | (j == 15), sides, 0.0)
        leaving[0:288, :] = sides.astype(BF)
        leaving[288:304, :] = centre[0:16]
        leaving[304:320, :] = centre[272:288]
        out[...] = mm(q_back[...], leaving[...]).astype(BF)
        return centre[16:272]

    def grad_sends(layer):
        out, got, send, recv = layer[5:9]
        copies = []
        for side in range(2):
            copies.append(remote(out.at[16 * side:16 * side + 16],
                                 got.at[pl.ds(pl.multiple_of(16 * seen[side], 16), 16)],
                                 send.at[side], recv.at[seen[side]], vert[side]))
        copies.append(remote(out.at[32:48], got.at[32:48], send.at[2], recv.at[2], west))
        copies.append(remote(out.at[48:64], got.at[48:64], send.at[3], recv.at[3], east))
        for i, (target_at, slot) in enumerate(diagonal):
            copies.append(remote(out.at[64 + 16 * i:80 + 16 * i],
                                 got.at[pl.ds(pl.multiple_of(64 + 16 * slot, 16), 16)],
                                 send.at[4 + i], recv.at[4 + slot], target_at))
        for copy in copies:
            copy.start()
        return copies

    def grad_waits(layer):
        out, got, send, recv = layer[5:9]
        for i in range(8):
            remote(out.at[0:16], got.at[16 * i:16 * i + 16], send.at[i], recv.at[i], west).wait_recv()

    def weight_grad(block, spots):
        block = block.astype(BF)
        units = block.shape[0] // 16
        for h in range(2):
            values = block[:, 128 * h:128 * h + 128].reshape(units, 16, 128)
            for first, count, red, to in spots:
                red.halves[h, to:to + count] = values[first:first + count]

    edge_waits()
    pad_tile(layer1, feat_ref[...], mm(q_fwd[...], edges[1][...]), C1)
    sent += patch_sends()
    loads[4].wait()
    pre1 = convolve(layer1, w1)
    cdf1 = normal_cdf(pre1)
    act1 = (pre1 * cdf1).astype(BF)
    slope1[...] = gelu_slope(pre1, cdf1)
    for dh in range(3):
        windows[dh] = layer1[1][16 * dh:16 * dh + 256, :].T
    r, c = iota((256, 64), 0), iota((256, 64), 1)
    spread = hot(c == 8 * (r >> 5) + ((r & 15) >> 1), 0.25).astype(BF)
    loads[5].wait()
    cot = mm(spread, cot_ref[...])
    loads[6].wait()

    patch_waits()
    patches = patch_refs[3]
    halo_pre = mm(patches[:, 0:384], w1[0])
    for dh in (1, 2):
        halo_pre = halo_pre + mm(patches[:, 384 * dh:384 * dh + 384], w1[dh])
    halo_cdf = normal_cdf(halo_pre)
    halo_act = (halo_pre * halo_cdf).astype(BF)
    pad_tile(layer2, act1, mm(q_act[...], halo_act), C2)
    second_pre = convolve(layer2, w2)
    cdf2 = normal_cdf(second_pre)
    grad2 = (cot * gelu_slope(second_pre, cdf2)).astype(BF)
    layer2[2][32:288, :] = grad2
    for dh in range(3):
        spots = [(0, 48, red2, 48 * dh)] if dh < 2 else [(0, 32, red2, 96), (32, 16, red1, FIRST_UNITS)]
        weight_grad(mm_tn(layer2[1][16 * dh:16 * dh + 256, :], grad2), spots)
        red2.core_send(48 * dh, spots[0][1])
    centre2 = input_side(layer2, w2, C2)
    sent += grad_sends(layer2)

    own = (centre2.astype(F32) * slope1[...]).astype(BF)
    leaving = (layer2[5][...].astype(F32) * gelu_slope(halo_pre, halo_cdf)).astype(BF)
    for dh in range(3):
        block = mm(windows[dh], own) + mm_tn(patches[:, 384 * dh:384 * dh + 384], leaving)
        weight_grad(block, [(0, 24, red1, 24 * dh)])
    red1.core_send(0, B_UNITS)
    red2.core_add()
    red1.core_add()
    pre2[...] = second_pre * cdf2

    r, c = iota((64, 256), 0), iota((64, 256), 1)
    gather_cells = hot(r == 8 * (c >> 5) + ((c & 15) >> 1), 0.25).astype(BF)
    act2 = pre2[...]
    high = act2.astype(BF)
    low = (act2 - high.astype(F32)).astype(BF)
    pooled_ref[...] = (mm(gather_cells, high) + mm(gather_cells, low)).astype(BF)

    red2.first_add()
    red1.first_add()

    grad_waits(layer2)
    first_grad = centre2.astype(F32) + mm(place_grads, layer2[6][...])
    layer1[2][32:288, :] = (first_grad * slope1[...]).astype(BF)
    centre1 = input_side(layer1, w1, C1)
    sent += grad_sends(layer1)

    red2.second_add()
    red1.second_add()
    red2.near_add()
    red1.near_add()

    grad_waits(layer1)
    grad_ref[...] = (centre1.astype(F32) + mm(place_grads, layer1[6][...])).astype(BF)

    for copy in sent + rule_copies:
        copy.wait_send()
    red2.flush()
    red1.flush()
    red2.far_add()
    red1.far_add()
    red2.gather_second()
    red1.gather_second()
    red2.near_flush()
    red1.near_flush()
    red2.gather_first()
    red1.gather_first()
    red2.gather_core()
    red1.gather_core()
    red2.gather_done()
    red2.flush()
    square_ref[...] = sum_squares(second_out, 0, A_UNITS, jnp.zeros((16, 128), F32))
    red1.gather_done()
    red1.flush()


def sum_squares(ref, at, count, total):
    def body(i, total):
        values = ref[:, pl.ds(at + i * 8, 8)].astype(F32)
        return total + jnp.sum(values * values, axis=(0, 1))

    return lax.fori_loop(0, count // 8, body, total)


def finish_kernel(pooled_ref, grad_ref, first_ref, second_ref, square_ref, pooled_out, grad_out, first_out, second_out,
                  first_rows, second_rows, sems):
    copies = [pltpu.make_async_copy(pooled_ref, pooled_out, sems.at[0]),
              pltpu.make_async_copy(grad_ref, grad_out, sems.at[1])]
    for copy in copies:
        copy.start()

    total = sum_squares(first_ref, 0, FIRST_UNITS + LAST_UNITS, square_ref[...])
    squared = jnp.sum(jnp.sum(total, axis=0, keepdims=True), axis=1, keepdims=True)
    target_norm = math.sqrt(9.0 * (C1 + C2) * C2)
    scale = jnp.broadcast_to(target_norm / jnp.sqrt(squared + 1e-06), (16, 128))

    def write(ref, at, to, count, out):
        def body(i, carry):
            for h in range(2):
                values = ref[h, pl.ds(at + i * 8, 8)].astype(F32) * scale
                rows = pl.ds(pl.multiple_of((to + i * 8) * 16, 128), 128)
                out[rows, 128 * h:128 * h + 128] = values.astype(BF).reshape(128, 128)
            return carry

        lax.fori_loop(0, count // 8, body, 0)

    jobs = [(second_ref, n * 64, n * 64, 64, second_rows, second_out) for n in range(2)]
    jobs.append((first_ref, 0, 0, FIRST_UNITS, first_rows, first_out))
    jobs.append((first_ref, FIRST_UNITS, A_UNITS, LAST_UNITS, second_rows, second_out))
    for n, (ref, at, to, count, rows, out) in enumerate(jobs):
        write(ref, at, to, count, rows)
        span = pl.ds(16 * to, 16 * count)
        copies.append(pltpu.make_async_copy(rows.at[span], out.at[span], sems.at[2 + n]))
        copies[-1].start()
    for copy in copies:
        copy.wait()


def on_device(features, conv_first, conv_second, cotangent, edge_pick, edge_flip, corner_rule):
    vmem = pl.BlockSpec(memory_space=pltpu.VMEM)
    hbm = pl.BlockSpec(memory_space=pltpu.HBM)
    pooled, input_grad, first, second, square = pl.pallas_call(
        step_kernel,
        out_shape=(
            jax.ShapeDtypeStruct((64, C2), BF),
            jax.ShapeDtypeStruct((256, C1), BF),
            jax.ShapeDtypeStruct((2, B_UNITS, 16, 128), BF),
            jax.ShapeDtypeStruct((2, A_UNITS, 16, 128), BF),
            jax.ShapeDtypeStruct((16, 128), F32),
        ),
        in_specs=[hbm] * 7,
        out_specs=[vmem] * 5,
        scratch_shapes=(
            edge_scratch(C1)
            + patch_scratch()
            + layer_scratch(C1)
            + layer_scratch(C2)
            + reduce_scratch(*MA)
            + reduce_scratch(*MB)
            + [
                pltpu.VMEM((256, C1), BF),
                pltpu.VMEM((3, 3 * C1, C2), BF),
                pltpu.VMEM((3, 3 * C2, C2), BF),
                pltpu.VMEM((64, C2), BF),
                pltpu.SMEM((1, 1, 2), jnp.int32),
                pltpu.SMEM((1, 1, 2), jnp.int32),
                pltpu.SMEM((1, 1, 4), jnp.int32),
                pltpu.SemaphoreType.DMA((7,)),
                pltpu.VMEM((8, 128), jnp.int32),
                pltpu.VMEM((4, 8, 128), jnp.int32),
                pltpu.SemaphoreType.DMA((4,)),
                pltpu.SemaphoreType.DMA((4,)),
                pltpu.VMEM((320, 256), BF),
                pltpu.VMEM((128, 384), BF),
                pltpu.VMEM((320, 128), BF),
                pltpu.VMEM((256, C2), F32),
                pltpu.VMEM((256, C2), F32),
                pltpu.VMEM((3, 3 * C1, 256), BF),
            ]
        ),
        compiler_params=pltpu.CompilerParams(
            collective_id=0, has_side_effects=True, vmem_limit_bytes=32 * 1024 * 1024
        ),
        name="level_step",
    )(*(
        pltpu.with_memory_space_constraint(value, pltpu.HBM)
        for value in (
            features.reshape(256, C1),
            conv_first.reshape(3, 3 * C1, C2),
            conv_second.reshape(3, 3 * C2, C2),
            cotangent.reshape(64, C2),
            edge_pick,
            edge_flip,
            corner_rule,
        )
    ))
    pooled, input_grad, first, second = pl.pallas_call(
        finish_kernel,
        out_shape=(
            jax.ShapeDtypeStruct((64, C2), BF),
            jax.ShapeDtypeStruct((256, C1), BF),
            jax.ShapeDtypeStruct((9 * C1, C2), BF),
            jax.ShapeDtypeStruct((9 * C2, C2), BF),
        ),
        in_specs=[vmem] * 5,
        out_specs=[hbm] * 4,
        scratch_shapes=[
            pltpu.VMEM((9 * C1, C2), BF),
            pltpu.VMEM((9 * C2, C2), BF),
            pltpu.SemaphoreType.DMA((6,)),
        ],
        compiler_params=pltpu.CompilerParams(vmem_limit_bytes=16 * 1024 * 1024),
        name="scale_outputs",
    )(pooled, input_grad, first, second, square)
    return (
        pooled.reshape(1, 1, 8, 8, C2),
        input_grad.reshape(1, 1, 16, 16, C1),
        first.reshape(3, 3, C1, C2),
        second.reshape(3, 3, C2, C2),
    )


def solution(mesh):
    return jax.shard_map(
        on_device,
        mesh=mesh,
        in_specs=(
            P("lon", "lat", None, None, None),
            P(),
            P(),
            P("lon", "lat", None, None, None),
            P("lon", "lat", None),
            P("lon", "lat", None),
            P("lon", "lat", None),
        ),
        out_specs=(P("lon", "lat", None, None, None), P("lon", "lat", None, None, None), P(), P()),
        check_vma=False,
    )
```

```python
import math

import jax
import jax.numpy as jnp
from jax import lax
from jax.experimental import pallas as pl
from jax.experimental.pallas import tpu as pltpu
from jax.sharding import PartitionSpec as P

MESH = pl.DeviceIdType.MESH
BF = jnp.bfloat16
F32 = jnp.float32
NX, NY, NZ = 4, 4, 16
LON, LAT = 2 * NY * NZ, 4
C1, C2 = 128, 256


def normal_cdf(values):
    return 0.5 * (1.0 + lax.erf(values * (1.0 / math.sqrt(2.0))))


def gelu_slope(values, cdf):
    return cdf + values * jnp.exp(-0.5 * values * values) * (1.0 / math.sqrt(2.0 * math.pi))


def iota(shape, dim):
    return lax.broadcasted_iota(jnp.int32, shape, dim)


def hot(cond, value=1.0):
    return jnp.where(cond, jnp.float32(value), jnp.float32(0.0))


def wide(row, count):
    return jnp.concatenate([row] * count, axis=1)


def edge_cell(edge, flip, position):
    at = jnp.where(flip == 1, 15 - position, position)
    return jnp.where(edge == 0, at, jnp.where(edge == 1, 240 + at, jnp.where(edge == 2, 16 * at, 16 * at + 15)))


def mm(a, b):
    return jnp.dot(a, b, preferred_element_type=F32)


def mm_nt(a, b):
    return lax.dot_general(a, b, (((1,), (1,)), ((), ())), preferred_element_type=F32)


def mm_tn(a, b):
    return lax.dot_general(a, b, (((0,), (0,)), ((), ())), preferred_element_type=F32)


def remote(src, dst, send_sem, recv_sem, device):
    return pltpu.make_async_remote_copy(
        src_ref=src, dst_ref=dst, send_sem=send_sem, recv_sem=recv_sem,
        device_id=device, device_id_type=MESH,
    )


def corner_slot(edge, at_end):
    return jnp.where(
        edge == 0, at_end, jnp.where(edge == 1, 2 + at_end, jnp.where(edge == 2, 2 * at_end, 1 + 2 * at_end))
    )


class Reduce:
    def __init__(self, m, refs, place):
        self.m = m
        self.total = m[0] + m[1]
        self.start = (0, 16 * m[0])
        (self.halves, self.r0, self.a1, r1a, r1b, a2a, a2b, r2a, r2b, self.a3, self.n3, self.f3, self.out,
         self.s_send, self.s_recv, self.g_send, self.g_recv) = refs
        self.r1, self.a2, self.r2 = (r1a, r1b), (a2a, a2b), (r2a, r2b)
        self.x, self.y, self.z, self.core, self.device = place
        self.near, self.far = lax.rem(self.z, 4), lax.div(self.z, 4)
        self.pending = []
        self.pieces = []
        self.waited = 0

    def other_core(self):
        return self.device(self.x, self.y, self.z, 1 - self.core)

    def peer(self, axis, d):
        x = lax.rem(self.x + d, NX) if axis == "x" else self.x
        y = lax.rem(self.y + d, NY) if axis == "y" else self.y
        return self.device(x, y, self.z, self.core)

    def axes(self, part):
        return ("x", "y") if part == 0 else ("y", "x")

    def coords(self, part):
        return (self.x, self.y) if part == 0 else (self.y, self.x)

    def send(self, copy):
        copy.start()
        self.pending.append(copy)

    def received(self, ref, sem):
        remote(ref, ref, self.s_send.at[0], sem, self.other_core()).wait_recv()

    def flush(self):
        for copy in self.pending:
            copy.wait_send()
        self.pending = []

    def far_flush(self):
        @pl.when(self.near < self.total // 2)
        def _():
            for copy in self.far_copies():
                copy.wait_send()

    def near_flush(self):
        @pl.when(self.near < self.total // 2)
        def _():
            for copy in self.near_copies():
                copy.wait_send()

    def core_send(self, at, count):
        k = len(self.pieces)
        self.pieces.append((at, count))
        self.send(remote(self.halves.at[1 - self.core, at:at + count], self.r0.at[at:at + count],
                         self.s_send.at[k], self.s_recv.at[k], self.other_core()))

    def core_add(self):
        for part in range(2):
            n = 4 * self.m[part]
            mine = self.coords(part)[0]
            while self.waited < len(self.pieces) and self.pieces[self.waited][0] < self.start[part] + 4 * n:
                at, count = self.pieces[self.waited]
                self.received(self.r0.at[at:at + count], self.s_recv.at[self.waited])
                self.waited += 1
            k = 3 + part
            for d in (2, 1, 3, 0):
                at = pl.ds(self.start[part] + lax.rem(mine + d, 4) * n, n)
                self.a1[at] = (self.halves[self.core, at].astype(F32) + self.r0[at].astype(F32)).astype(BF)
                if d:
                    self.send(remote(self.a1.at[at], self.r1[part].at[d - 1],
                                     self.s_send.at[3 * k - 7 + d], self.s_recv.at[k],
                                     self.peer(self.axes(part)[0], d)))

    def first_add(self):
        for part in range(2):
            m = self.m[part]
            r1, a2, r2 = self.r1[part], self.a2[part], self.r2[part]
            ca, cb = self.coords(part)
            self.received(r1, self.s_recv.at[3 + part])
            k = 5 + part
            for d in (2, 1, 3, 0):
                block = lax.rem(cb + d, 4)
                at = pl.ds(block * m, m)
                total = self.a1[pl.ds(self.start[part] + (ca * 4 + block) * m, m)].astype(F32)
                for e in range(3):
                    total = total + r1[e, at].astype(F32)
                a2[at] = total.astype(BF)
                if d:
                    self.send(remote(a2.at[at], r2.at[d - 1],
                                     self.s_send.at[3 * k - 7 + d], self.s_recv.at[k],
                                     self.peer(self.axes(part)[1], d)))

    def second_add(self):
        for part in range(2):
            m = self.m[part]
            a2, r2 = self.a2[part], self.r2[part]
            cb = self.coords(part)[1]
            self.received(r2, self.s_recv.at[5 + part])
            total = a2[pl.ds(cb * m, m)].astype(F32)
            for e in range(3):
                total = total + r2[e].astype(F32)
            self.a3[part * self.m[0]:part * self.m[0] + m] = total.astype(BF)
        for d in (2, 1, 3):
            owner = lax.rem(self.near + d, 4)
            self.send(remote(self.a3.at[pl.ds(2 * owner, 2)], self.n3.at[d - 1], self.s_send.at[14 + d],
                             self.s_recv.at[7], self.device(self.x, self.y, 4 * self.far + owner, self.core)))

    def near_add(self):
        self.received(self.n3, self.s_recv.at[7])
        total = self.a3[pl.ds(2 * self.near, 2)].astype(F32)
        for e in range(3):
            total = total + self.n3[e].astype(F32)
        self.f3[self.far] = total.astype(BF)

        @pl.when(self.near < self.total // 2)
        def _():
            for copy in self.far_copies():
                copy.start()

    def far_copies(self):
        return [
            remote(self.f3.at[self.far], self.f3.at[self.far], self.s_send.at[17 + d], self.s_recv.at[8],
                   self.device(self.x, self.y, 4 * lax.rem(self.far + d, 4) + self.near, self.core))
            for d in (2, 1, 3)
        ]

    def unit_at(self, u):
        ma, mb = self.m
        first = (self.x * 4 + self.y) * ma + u
        second = self.start[1] + (self.y * 4 + self.x) * mb + u - ma
        return jnp.where(u < ma, first, second)

    def near_copies(self):
        at = pl.ds(self.unit_at(2 * self.near), 2)
        return [
            remote(self.out.at[self.core, at], self.out.at[self.core, at], self.g_send.at[19 + d], self.g_recv.at[19 + d],
                   self.device(self.x, self.y, 4 * self.far + lax.rem(self.near + d, 4), self.core))
            for d in (2, 1, 3)
        ]

    def far_add(self):
        @pl.when(self.near < self.total // 2)
        def _():
            self.received(self.f3.at[0:3], self.s_recv.at[8])
            total = self.f3[0].astype(F32)
            for e in range(1, 4):
                total = total + self.f3[e].astype(F32)
            self.out[self.core, pl.ds(self.unit_at(2 * self.near), 2)] = total.astype(BF)
            for copy in self.near_copies():
                copy.start()

    def gather_second(self):
        for d in (1, 3, 2):
            owner = lax.rem(self.near + 4 - d, 4)

            @pl.when(owner < self.total // 2)
            def _():
                self.received(self.out.at[self.core, pl.ds(self.unit_at(2 * owner), 2)], self.g_recv.at[19 + d])

        for part in range(2):
            m = self.m[part]
            ca, cb = self.coords(part)
            at = pl.ds(self.start[part] + (ca * 4 + cb) * m, m)
            for d in (2, 1, 3):
                self.send(remote(self.out.at[self.core, at], self.out.at[self.core, at], self.g_send.at[part * 3 + d - 1],
                                 self.g_recv.at[part], self.peer(self.axes(part)[1], d)))

    def gather_first(self):
        for part in range(2):
            m = self.m[part]
            ca = self.coords(part)[0]
            self.received(self.r2[part], self.g_recv.at[part])
            at = pl.ds(self.start[part] + ca * 4 * m, 4 * m)
            for d in (2, 1, 3):
                k = 6 + part * 3 + d - 1
                self.send(remote(self.out.at[self.core, at], self.out.at[self.core, at], self.g_send.at[k],
                                 self.g_recv.at[k], self.peer(self.axes(part)[0], d)))
            self.to_core(part, 0, at)

    def to_core(self, part, d, at):
        k = 12 + part * 4 + d
        self.send(remote(self.out.at[self.core, at], self.out.at[self.core, at], self.g_send.at[k],
                         self.g_recv.at[k], self.other_core()))

    def block_of(self, part, d):
        n = 4 * self.m[part]
        return pl.ds(self.start[part] + lax.rem(self.coords(part)[0] + 4 - d, 4) * n, n)

    def gather_core(self):
        for d in (1, 3, 2):
            for part in range(2):
                at = self.block_of(part, d)
                self.received(self.out.at[self.core, at], self.g_recv.at[6 + part * 3 + d - 1])
                self.to_core(part, d, at)

    def gather_done(self):
        for d in (0, 1, 3, 2):
            for part in range(2):
                at = self.block_of(part, d)
                self.received(self.out.at[1 - self.core, at], self.g_recv.at[12 + part * 4 + d])
                yield part, at.start


def reduce_scratch(ma, mb):
    units = 16 * (ma + mb)
    return [
        pltpu.VMEM((2, units, 16, 128), BF),
        pltpu.VMEM((units, 16, 128), BF),
        pltpu.VMEM((units, 16, 128), BF),
        pltpu.VMEM((3, 4 * ma, 16, 128), BF),
        pltpu.VMEM((3, 4 * mb, 16, 128), BF),
        pltpu.VMEM((4 * ma, 16, 128), BF),
        pltpu.VMEM((4 * mb, 16, 128), BF),
        pltpu.VMEM((3, ma, 16, 128), BF),
        pltpu.VMEM((3, mb, 16, 128), BF),
        pltpu.VMEM((8, 16, 128), BF),
        pltpu.VMEM((3, 2, 16, 128), BF),
        pltpu.VMEM((4, 2, 16, 128), BF),
        pltpu.SemaphoreType.DMA((21,)),
        pltpu.SemaphoreType.DMA((21,)),
        pltpu.SemaphoreType.DMA((23,)),
        pltpu.SemaphoreType.DMA((23,)),
    ]


N_REDUCE = 16
MA, MB = (4, 4), (4, 2)
A_UNITS, B_UNITS, FIRST_UNITS, LAST_UNITS = 128, 96, 72, 16


def edge_scratch(channels):
    return [
        pltpu.VMEM((80, channels), BF),
        pltpu.VMEM((256, channels), BF),
        pltpu.SemaphoreType.DMA((8,)),
        pltpu.SemaphoreType.DMA((8,)),
    ]


def patch_scratch():
    return [
        pltpu.VMEM((32, 9 * C1), BF),
        pltpu.VMEM((2, 32, 3 * C1), BF),
        pltpu.VMEM((4, 16, C1), BF),
        pltpu.VMEM((128, 9 * C1), BF),
        pltpu.VMEM((2, 32, 3 * C1), BF),
        pltpu.VMEM((4, 16, C1), BF),
        pltpu.SemaphoreType.DMA((8,)),
        pltpu.SemaphoreType.DMA((8,)),
    ]


def layer_scratch(channels):
    return [
        pltpu.VMEM((304, channels), F32),
        pltpu.VMEM((384, 3 * channels), BF),
        pltpu.VMEM((416, C2), BF),
        pltpu.VMEM((304, 3 * channels), F32),
        pltpu.VMEM((384, channels), BF),
        pltpu.VMEM((128, channels), BF),
        pltpu.VMEM((128, channels), BF),
        pltpu.SemaphoreType.DMA((8,)),
        pltpu.SemaphoreType.DMA((8,)),
    ]


N_EDGE, N_PATCH, N_LAYER = 4, 8, 9


def step_kernel(*refs):
    (feat_hbm, w1_hbm, w2_hbm, cot_hbm, pick_hbm, flip_hbm, rule_hbm,
     pooled_ref, grad_ref, first_out, second_out, square_ref) = refs[:12]
    refs = refs[12:]
    edges, refs = refs[:N_EDGE], refs[N_EDGE:]
    patch_refs, refs = refs[:N_PATCH], refs[N_PATCH:]
    layer1, refs = refs[:N_LAYER], refs[N_LAYER:]
    layer2, refs = refs[:N_LAYER], refs[N_LAYER:]
    red2_refs, refs = refs[:N_REDUCE], refs[N_REDUCE:]
    red1_refs, refs = refs[:N_REDUCE], refs[N_REDUCE:]
    (feat_ref, w1, w2, cot_ref, pick_ref, flip_ref, rule_ref, load_sem,
     rules_out, rules_in, rule_send, rule_recv, q_fwd, q_back, q_act, slope1, pre2,
     windows) = refs
    red2_refs = red2_refs[:12] + (second_out,) + red2_refs[12:]
    red1_refs = red1_refs[:12] + (first_out,) + red1_refs[12:]

    lon, lat = lax.axis_index("lon"), lax.axis_index("lat")
    y = lax.div(lon, 2 * NZ)
    z = lax.div(lax.rem(lon, 2 * NZ), 2)
    x = lax.rem(lon, 2) * 2 + lax.div(lat, 2)
    core = lax.rem(lat, 2)

    def device(x_at, y_at, z_at, core_at):
        return (y_at * (2 * NZ) + z_at * 2 + lax.div(x_at, 2), lax.rem(x_at, 2) * 2 + core_at)

    across = lax.rem(lon + LON // 2, LON)
    below, above = lat == 0, lat == LAT - 1
    vert = (
        (jnp.where(below, across, lon), jnp.where(below, lat, lat - 1)),
        (jnp.where(above, across, lon), jnp.where(above, lat, lat + 1)),
    )
    seen = (jnp.where(below, 0, 1), jnp.where(above, 1, 0))

    def west_of(at):
        return (lax.rem(at[0] + LON - 1, LON), at[1])

    def east_of(at):
        return (lax.rem(at[0] + 1, LON), at[1])

    here = (lon, lat)
    west, east = west_of(here), east_of(here)
    diagonal = [
        (west_of(vert[0]), 2 * seen[0] + 1),
        (east_of(vert[0]), 2 * seen[0]),
        (west_of(vert[1]), 2 * seen[1] + 1),
        (east_of(vert[1]), 2 * seen[1]),
    ]

    barrier = pltpu.get_barrier_semaphore()
    partners = [device(x, y, lax.rem(z + 4 * d, NZ), core) for d in (2, 1, 3)]
    partners += [d[0] for d in diagonal] + [west, east, vert[0], vert[1]]
    for d in (2, 1, 3):
        partners.append(device(x, y, 4 * lax.div(z, 4) + lax.rem(z + d, 4), core))
        partners.append(device(lax.rem(x + d, NX), y, z, core))
        partners.append(device(x, lax.rem(y + d, NY), z, core))
    partners.append(device(x, y, z, 1 - core))
    for partner in partners:
        pl.semaphore_signal(barrier, inc=1, device_id=partner, device_id_type=MESH)

    loads = [
        pltpu.make_async_copy(src, dst, load_sem.at[n])
        for n, (src, dst) in enumerate((
            (pick_hbm, pick_ref), (flip_hbm, flip_ref), (rule_hbm, rule_ref), (feat_hbm, feat_ref),
            (w1_hbm, w1), (cot_hbm, cot_ref), (w2_hbm, w2),
        ))
    ]
    for load in loads:
        load.start()

    for load in loads[:3]:
        load.wait()
    picks = [pick_ref[0, 0, s] for s in range(2)]
    flips = [flip_ref[0, 0, s] for s in range(2)]
    rules = [rule_ref[0, 0, k] for k in range(4)]

    row8 = iota((8, 128), 0)
    rules_out[...] = jnp.where(
        row8 == 0, picks[0], jnp.where(row8 == 1, flips[0], jnp.where(row8 == 2, picks[1], flips[1]))
    )

    p, cell = iota((80, 256), 0), iota((80, 256), 1)
    k = p & 15
    want = jnp.where(
        p < 16, k, jnp.where(p < 32, 240 + k, jnp.where(p < 48, 16 * k, jnp.where(p < 64, 16 * k + 15, (
            jnp.where(k == 0, 0, jnp.where(k == 1, 15, jnp.where(k == 2, 240, jnp.where(k == 3, 255, -1))))
        ))))
    )
    take_edges = hot(cell == want).astype(BF)

    loads[3].wait()
    edges[0][...] = mm(take_edges, feat_ref[...]).astype(BF)
    edges[1][224:256, :] = jnp.zeros((32, C1), BF)
    layer1[1][288:384, :] = jnp.zeros((96, 3 * C1), BF)

    pl.semaphore_wait(barrier, len(partners))

    def edge_sends():
        out, got, send, recv = edges
        copies = []
        for i, (target, slot) in enumerate(diagonal):
            copies.append(remote(out.at[64:80], got.at[pl.ds(pl.multiple_of(160 + 16 * slot, 16), 16)],
                                 send.at[4 + i], recv.at[4 + slot], target))
        for side in range(2):
            copies.append(remote(out.at[0:64], got.at[pl.ds(pl.multiple_of(64 * seen[side], 64), 64)],
                                 send.at[side], recv.at[seen[side]], vert[side]))
        copies.append(remote(out.at[32:48], got.at[144:160], send.at[2], recv.at[3], west))
        copies.append(remote(out.at[48:64], got.at[128:144], send.at[3], recv.at[2], east))
        for copy in copies:
            copy.start()
        return copies

    def edge_waits():
        out, got, send, recv = edges
        spots = [(0, 64), (64, 64), (128, 16), (144, 16), (160, 16), (176, 16), (192, 16), (208, 16)]
        for i, (at, size) in enumerate(spots):
            remote(out.at[0:size], got.at[at:at + size], send.at[i], recv.at[i], west).wait_recv()

    sent = edge_sends()
    rule_copies = []
    for i, (target, slot) in enumerate(((vert[0], seen[0]), (vert[1], seen[1]), (west, 3), (east, 2))):
        rule_copies.append(remote(rules_out, rules_in.at[slot], rule_send.at[i], rule_recv.at[slot], target))
    for copy in rule_copies:
        copy.start()

    r, c = iota((288, 256), 0), iota((288, 256), 1)
    j, i = r & 15, r >> 4
    want = jnp.where(j == 0, 127 + i, jnp.where(j == 15, 143 + i, -1))
    q_fwd[0:288, :] = hot(c == want).astype(BF)
    r, c = iota((32, 256), 0), iota((32, 256), 1)
    k, north = r & 15, r >= 16
    flip = jnp.where(north, flips[1], flips[0])
    pick = jnp.where(north, picks[1], picks[0])
    want = jnp.where(north, 64, 0) + 16 * pick + jnp.where(flip == 1, 15 - k, k)
    q_fwd[288:320, :] = hot(c == want).astype(BF)

    def halo_cells(p, q):
        block, k = p >> 4, p & 15
        low, high = k == 0, k == 15
        corner_at = (0, 15, 272, 287)
        want = jnp.where(block == 0, 288 + k, jnp.where(block == 1, 304 + k, jnp.where(
            block == 2, 16 * k + 16, jnp.where(block == 3, 16 * k + 31, -1))))
        half = jnp.full_like(want, -1)
        ends = ((0, 1), (2, 3), (0, 2), (1, 3))
        for b in range(4):
            first, second = ends[b]
            half = jnp.where((block == b) & low & (rules[first] == 1), corner_at[first], half)
            half = jnp.where((block == b) & high & (rules[second] == 1), corner_at[second], half)
            want = jnp.where((block == 4 + b) & low & (rules[b] != 1), corner_at[b], want)
        return (hot(q == want) + hot(q == half, 0.5)).astype(BF)

    q_back[...] = halo_cells(iota((128, 384), 0), iota((128, 384), 1))
    q_act[...] = halo_cells(iota((320, 128), 1), iota((320, 128), 0))

    for layer in (layer1, layer2):
        g_pad = layer[2]
        g_pad[0:32, :] = jnp.zeros((32, C2), BF)
        g_pad[288:416, :] = jnp.zeros((128, C2), BF)
        layer[4][320:384, :] = jnp.zeros((64, layer[4].shape[1]), BF)

    red2 = Reduce(MA, red2_refs, (x, y, z, core, device))
    red1 = Reduce(MB, red1_refs, (x, y, z, core, device))
    used = FIRST_UNITS + LAST_UNITS
    red1.halves[:, used:B_UNITS] = jnp.zeros((2, B_UNITS - used, 16, 128), BF)
    red1.a3[6:8] = jnp.zeros((2, 16, 128), BF)

    for slot in range(4):
        remote(rules_out, rules_in.at[slot], rule_send.at[slot], rule_recv.at[slot], west).wait_recv()

    r, c = iota((16, 256), 0), iota((16, 256), 1)
    for side in range(2):
        def source(position):
            return 64 * side + 16 * picks[side] + jnp.where(flips[side] == 1, 15 - position, position)

        rows = 2 * side
        w_pick, w_flip = wide(rules_in[2, rows:rows + 1, :], 2), wide(rules_in[2, rows + 1:rows + 2, :], 2)
        e_pick, e_flip = wide(rules_in[3, rows:rows + 1, :], 2), wide(rules_in[3, rows + 1:rows + 2, :], 2)
        w_at = 160 + 32 * side + corner_slot(w_pick, jnp.where(w_flip == 1, 0, 1))
        e_at = 176 + 32 * side + corner_slot(e_pick, jnp.where(e_flip == 1, 1, 0))
        w_rule, e_rule = rules[2 * side] == 1, rules[2 * side + 1] == 1
        shape = (16, 256)
        w_main = jnp.where(w_rule, jnp.full(shape, -1), jnp.broadcast_to(w_at, shape))
        e_main = jnp.where(e_rule, jnp.full(shape, -1), jnp.broadcast_to(e_at, shape))
        w_a, w_c = jnp.where(w_rule, source(0), -1), jnp.where(w_rule, 128 + 15 * side, -1)
        e_a, e_c = jnp.where(e_rule, source(15), -1), jnp.where(e_rule, 144 + 15 * side, -1)
        w_row = hot(c == w_main) + hot(c == w_a, 0.5) + hot(c == w_c, 0.5)
        e_row = hot(c == e_main) + hot(c == e_a, 0.5) + hot(c == e_c, 0.5)
        values = jnp.where(r == 0, w_row, jnp.where(r == 15, e_row, 0.0))
        q_fwd[272 * side:272 * side + 16, :] = values.astype(BF)

    face = (jnp.where(below, 0, 1), jnp.where(above, 1, 0))
    facing = []
    for side in range(2):
        south = face[side] == 0
        facing.append((
            jnp.where(south, rules_in[side, 0:1, 0:128], rules_in[side, 2:3, 0:128]),
            jnp.where(south, rules_in[side, 1:2, 0:128], rules_in[side, 3:4, 0:128]),
        ))
    p = iota((1, 128), 1)
    block, k = p >> 4, p & 15
    on_north = (block == 1) | (block >= 6)
    pick = jnp.where(on_north, facing[1][0], facing[0][0])
    flip = jnp.where(on_north, facing[1][1], facing[0][1])
    position = jnp.where(block < 2, k, jnp.where((block & 1) == 1, 15, 0))
    target = edge_cell(pick, flip, position)
    target = jnp.where(block == 2, 16 * k + 15, jnp.where(block == 3, 16 * k, target))
    target = jnp.where((block >= 4) & (k != 0), -1, target)
    place_grads = hot(iota((256, 128), 0) == target).astype(BF)

    r, c = iota((32, 256), 0), iota((32, 256), 1)
    pick = jnp.where(r < 16, wide(facing[0][0], 2), wide(facing[1][0], 2))
    flip = jnp.where(r < 16, wide(facing[0][1], 2), wide(facing[1][1], 2))
    take_cells = hot(c == edge_cell(pick, flip, r & 15)).astype(BF)
    r, c = iota((64, 384), 0), iota((64, 384), 1)
    row = r & 31
    take_strips = hot((row < 18) & (c == 16 * row + jnp.where(r < 32, 15, 0))).astype(BF)
    tap, which = r & 15, r >> 4
    tap_row = (tap * 11) >> 5
    pick = jnp.where(which < 2, wide(facing[0][0], 3), wide(facing[1][0], 3))
    flip = jnp.where(which < 2, wide(facing[0][1], 3), wide(facing[1][1], 3))
    at = 16 * tap_row + edge_cell(pick, flip, jnp.where((which & 1) == 1, 15, 0))
    take_corners = [
        hot((tap < 9) & (tap - 3 * tap_row == dw) & (c == at)).astype(BF) for dw in range(3)
    ]

    def patch_sends():
        cells, strips, corners, got_cells, got_strips, got_corners, send, recv = patch_refs
        padded = layer1[1]
        values = mm(take_corners[0], padded[:, 0:C1])
        for dw in (1, 2):
            values = values + mm(take_corners[dw], padded[:, dw * C1:(dw + 1) * C1])
        corners[...] = values.astype(BF).reshape(4, 16, C1)
        copies = []
        for i, (target_at, slot) in enumerate(diagonal):
            copies.append(remote(corners.at[i], got_corners.at[slot], send.at[4 + i], recv.at[4 + slot], target_at))
            copies[-1].start()
        strips[...] = mm(take_strips, padded[...]).astype(BF).reshape(2, 32, 3 * C1)
        copies.append(remote(strips.at[0], got_strips.at[0], send.at[2], recv.at[2], east))
        copies.append(remote(strips.at[1], got_strips.at[1], send.at[3], recv.at[3], west))
        for copy in copies[-2:]:
            copy.start()
        for dh in range(3):
            cells[:, 384 * dh:384 * dh + 384] = mm(take_cells, padded[16 * dh:16 * dh + 256, :]).astype(BF)
        for side in range(2):
            copies.append(remote(cells.at[16 * side:16 * side + 16],
                                 got_cells.at[pl.ds(pl.multiple_of(16 * seen[side], 16), 16)],
                                 send.at[side], recv.at[seen[side]], vert[side]))
            copies[-1].start()
        return copies

    def patch_waits():
        cells, strips, corners, got_cells, got_strips, got_corners, send, recv = patch_refs
        for i in range(2):
            remote(cells.at[0:16], got_cells.at[16 * i:16 * i + 16], send.at[i], recv.at[i], west).wait_recv()
            remote(strips.at[i], got_strips.at[i], send.at[2 + i], recv.at[2 + i], west).wait_recv()
        r, c = iota((32, 64), 0), iota((32, 64), 1)
        both = got_strips[...].reshape(64, 3 * C1)
        for dh in range(3):
            spread_rows = hot(c == jnp.where(r < 16, r, r + 16) + dh).astype(BF)
            got_cells[32:64, 384 * dh:384 * dh + 384] = mm(spread_rows, both).astype(BF)
        for i in range(4):
            remote(corners.at[i], got_corners.at[i], send.at[4 + i], recv.at[4 + i], west).wait_recv()
        r, c = iota((64, 64), 0), iota((64, 64), 1)
        taps = got_corners[...].reshape(64, C1)
        for tap in range(9):
            first_row = hot(((r & 15) == 0) & (c == r + tap)).astype(BF)
            got_cells[64:128, C1 * tap:C1 * tap + C1] = mm(first_row, taps).astype(BF)

    def pad_tile(layer, tile, cells, channels):
        ext, padded = layer[:2]
        south, north = cells[288:304], cells[304:320]
        ext[8:24, :] = south
        ext[24:280, :] = tile.astype(F32)
        ext[280:296, :] = north
        j = iota((288, channels), 0) & 15
        padded[0:288, 0:channels] = jnp.where(j == 0, cells[0:288], ext[7:295, :]).astype(BF)
        padded[0:288, channels:2 * channels] = ext[8:296, :].astype(BF)
        padded[0:288, 2 * channels:] = jnp.where(j == 15, cells[0:288], ext[9:297, :]).astype(BF)

    def convolve(layer, weight):
        padded = layer[1]
        total = mm(padded[0:256, :], weight[0])
        for dh in (1, 2):
            total = total + mm(padded[16 * dh:16 * dh + 256, :], weight[dh])
        return total

    def input_side(layer, weight, channels):
        g_pad, by_shift, leaving, out = layer[2:6]
        total = mm_nt(g_pad[32:320, :], weight[0])
        for dh in (1, 2):
            at = 32 - 16 * dh
            total = total + mm_nt(g_pad[at:at + 288, :], weight[dh])
        by_shift[8:296, :] = total
        j = iota((288, channels), 0) & 15
        centre = by_shift[8:296, channels:2 * channels]
        centre = centre + jnp.where(j == 15, 0.0, by_shift[9:297, 0:channels])
        centre = centre + jnp.where(j == 0, 0.0, by_shift[7:295, 2 * channels:])
        centre = centre.astype(BF)
        sides = jnp.where(j == 0, by_shift[8:296, 0:channels], by_shift[8:296, 2 * channels:])
        sides = jnp.where((j == 0) | (j == 15), sides, 0.0)
        leaving[0:288, :] = sides.astype(BF)
        leaving[288:304, :] = centre[0:16]
        leaving[304:320, :] = centre[272:288]
        out[...] = mm(q_back[...], leaving[...]).astype(BF)
        return centre[16:272]

    def grad_sends(layer):
        out, got, send, recv = layer[5:9]
        copies = []
        for side in range(2):
            copies.append(remote(out.at[16 * side:16 * side + 16],
                                 got.at[pl.ds(pl.multiple_of(16 * seen[side], 16), 16)],
                                 send.at[side], recv.at[seen[side]], vert[side]))
        copies.append(remote(out.at[32:48], got.at[32:48], send.at[2], recv.at[2], west))
        copies.append(remote(out.at[48:64], got.at[48:64], send.at[3], recv.at[3], east))
        for i, (target_at, slot) in enumerate(diagonal):
            copies.append(remote(out.at[64 + 16 * i:80 + 16 * i],
                                 got.at[pl.ds(pl.multiple_of(64 + 16 * slot, 16), 16)],
                                 send.at[4 + i], recv.at[4 + slot], target_at))
        for copy in copies:
            copy.start()
        return copies

    def grad_waits(layer):
        out, got, send, recv = layer[5:9]
        for i in range(8):
            remote(out.at[0:16], got.at[16 * i:16 * i + 16], send.at[i], recv.at[i], west).wait_recv()

    def weight_grad(block, spots):
        block = block.astype(BF)
        units = block.shape[0] // 16
        for h in range(2):
            values = block[:, 128 * h:128 * h + 128].reshape(units, 16, 128)
            for first, count, red, to in spots:
                red.halves[h, to:to + count] = values[first:first + count]

    edge_waits()
    pad_tile(layer1, feat_ref[...], mm(q_fwd[...], edges[1][...]), C1)
    sent += patch_sends()
    loads[4].wait()
    pre1 = convolve(layer1, w1)
    cdf1 = normal_cdf(pre1)
    act1 = (pre1 * cdf1).astype(BF)
    slope1[...] = gelu_slope(pre1, cdf1)
    for dh in range(3):
        windows[dh] = layer1[1][16 * dh:16 * dh + 256, :].T
    r, c = iota((256, 64), 0), iota((256, 64), 1)
    spread = hot(c == 8 * (r >> 5) + ((r & 15) >> 1), 0.25).astype(BF)
    loads[5].wait()
    cot = mm(spread, cot_ref[...])
    loads[6].wait()

    patch_waits()
    patches = patch_refs[3]
    halo_pre = mm(patches[:, 0:384], w1[0])
    for dh in (1, 2):
        halo_pre = halo_pre + mm(patches[:, 384 * dh:384 * dh + 384], w1[dh])
    halo_cdf = normal_cdf(halo_pre)
    halo_act = (halo_pre * halo_cdf).astype(BF)
    pad_tile(layer2, act1, mm(q_act[...], halo_act), C2)
    second_pre = convolve(layer2, w2)
    cdf2 = normal_cdf(second_pre)
    grad2 = (cot * gelu_slope(second_pre, cdf2)).astype(BF)
    layer2[2][32:288, :] = grad2
    for dh in range(3):
        spots = [(0, 48, red2, 48 * dh)] if dh < 2 else [(0, 32, red2, 96), (32, 16, red1, FIRST_UNITS)]
        weight_grad(mm_tn(layer2[1][16 * dh:16 * dh + 256, :], grad2), spots)
        red2.core_send(48 * dh, spots[0][1])
    centre2 = input_side(layer2, w2, C2)
    sent += grad_sends(layer2)

    own = (centre2.astype(F32) * slope1[...]).astype(BF)
    leaving = (layer2[5][...].astype(F32) * gelu_slope(halo_pre, halo_cdf)).astype(BF)
    for dh in range(3):
        block = mm(windows[dh], own) + mm_tn(patches[:, 384 * dh:384 * dh + 384], leaving)
        weight_grad(block, [(0, 24, red1, 24 * dh)])
    red1.core_send(0, B_UNITS)
    red2.core_add()
    red1.core_add()
    pre2[...] = second_pre * cdf2

    r, c = iota((64, 256), 0), iota((64, 256), 1)
    gather_cells = hot(r == 8 * (c >> 5) + ((c & 15) >> 1), 0.25).astype(BF)
    act2 = pre2[...]
    high = act2.astype(BF)
    low = (act2 - high.astype(F32)).astype(BF)
    pooled_ref[...] = (mm(gather_cells, high) + mm(gather_cells, low)).astype(BF)

    red2.first_add()
    red1.first_add()

    grad_waits(layer2)
    first_grad = centre2.astype(F32) + mm(place_grads, layer2[6][...])
    layer1[2][32:288, :] = (first_grad * slope1[...]).astype(BF)
    centre1 = input_side(layer1, w1, C1)
    sent += grad_sends(layer1)

    red2.second_add()
    red1.second_add()
    red2.near_add()
    red1.near_add()

    grad_waits(layer1)
    grad_ref[...] = (centre1.astype(F32) + mm(place_grads, layer1[6][...])).astype(BF)

    for copy in sent + rule_copies:
        copy.wait_send()
    red2.flush()
    red1.flush()
    red2.far_add()
    red1.far_add()
    red2.gather_second()
    red1.gather_second()
    for red in (red2, red1):
        red.far_flush()
        red.near_flush()
    red2.gather_first()
    red1.gather_first()
    red2.gather_core()
    red1.gather_core()
    list(red2.gather_done())
    red2.flush()
    squares = jnp.zeros((16, 128), F32)
    for h in range(2):
        squares = sum_squares(second_out, h, 0, A_UNITS // 8, squares)
    squares = sum_squares(first_out, core, 0, B_UNITS // 8, squares)
    for part, at in red1.gather_done():
        squares = sum_squares(first_out, 1 - core, at, red1.m[part] // 2, squares)
    square_ref[...] = squares
    red1.flush()


def sum_squares(ref, half, at, steps, total):
    def body(i, total):
        values = ref[half, pl.ds(at + i * 8, 8)].astype(F32)
        return total + jnp.sum(values * values, axis=0)

    return lax.fori_loop(0, steps, body, total)


def finish_kernel(pooled_ref, grad_ref, first_ref, second_ref, square_ref, pooled_out, grad_out, first_out, second_out,
                  first_rows, second_rows, sems):
    copies = [pltpu.make_async_copy(pooled_ref, pooled_out, sems.at[0]),
              pltpu.make_async_copy(grad_ref, grad_out, sems.at[1])]
    for copy in copies:
        copy.start()

    squared = jnp.sum(jnp.sum(square_ref[...], axis=0, keepdims=True), axis=1, keepdims=True)
    target_norm = math.sqrt(9.0 * (C1 + C2) * C2)
    scale = jnp.broadcast_to(target_norm / jnp.sqrt(squared + 1e-06), (16, 128))

    def write(ref, at, to, count, out):
        def body(i, carry):
            for h in range(2):
                values = ref[h, pl.ds(at + i * 8, 8)].astype(F32) * scale
                rows = pl.ds(pl.multiple_of((to + i * 8) * 16, 128), 128)
                out[rows, 128 * h:128 * h + 128] = values.astype(BF).reshape(128, 128)
            return carry

        lax.fori_loop(0, count // 8, body, 0)

    jobs = [(second_ref, n * 64, n * 64, 64, second_rows, second_out) for n in range(2)]
    jobs.append((first_ref, 0, 0, FIRST_UNITS, first_rows, first_out))
    jobs.append((first_ref, FIRST_UNITS, A_UNITS, LAST_UNITS, second_rows, second_out))
    for n, (ref, at, to, count, rows, out) in enumerate(jobs):
        write(ref, at, to, count, rows)
        span = pl.ds(16 * to, 16 * count)
        copies.append(pltpu.make_async_copy(rows.at[span], out.at[span], sems.at[2 + n]))
        copies[-1].start()
    for copy in copies:
        copy.wait()


def on_device(features, conv_first, conv_second, cotangent, edge_pick, edge_flip, corner_rule):
    vmem = pl.BlockSpec(memory_space=pltpu.VMEM)
    hbm = pl.BlockSpec(memory_space=pltpu.HBM)
    pooled, input_grad, first, second, square = pl.pallas_call(
        step_kernel,
        out_shape=(
            jax.ShapeDtypeStruct((64, C2), BF),
            jax.ShapeDtypeStruct((256, C1), BF),
            jax.ShapeDtypeStruct((2, B_UNITS, 16, 128), BF),
            jax.ShapeDtypeStruct((2, A_UNITS, 16, 128), BF),
            jax.ShapeDtypeStruct((16, 128), F32),
        ),
        in_specs=[hbm] * 7,
        out_specs=[vmem] * 5,
        scratch_shapes=(
            edge_scratch(C1)
            + patch_scratch()
            + layer_scratch(C1)
            + layer_scratch(C2)
            + reduce_scratch(*MA)
            + reduce_scratch(*MB)
            + [
                pltpu.VMEM((256, C1), BF),
                pltpu.VMEM((3, 3 * C1, C2), BF),
                pltpu.VMEM((3, 3 * C2, C2), BF),
                pltpu.VMEM((64, C2), BF),
                pltpu.SMEM((1, 1, 2), jnp.int32),
                pltpu.SMEM((1, 1, 2), jnp.int32),
                pltpu.SMEM((1, 1, 4), jnp.int32),
                pltpu.SemaphoreType.DMA((7,)),
                pltpu.VMEM((8, 128), jnp.int32),
                pltpu.VMEM((4, 8, 128), jnp.int32),
                pltpu.SemaphoreType.DMA((4,)),
                pltpu.SemaphoreType.DMA((4,)),
                pltpu.VMEM((320, 256), BF),
                pltpu.VMEM((128, 384), BF),
                pltpu.VMEM((320, 128), BF),
                pltpu.VMEM((256, C2), F32),
                pltpu.VMEM((256, C2), F32),
                pltpu.VMEM((3, 3 * C1, 256), BF),
            ]
        ),
        compiler_params=pltpu.CompilerParams(
            collective_id=0, has_side_effects=True, vmem_limit_bytes=32 * 1024 * 1024
        ),
        name="level_step",
    )(*(
        pltpu.with_memory_space_constraint(value, pltpu.HBM)
        for value in (
            features.reshape(256, C1),
            conv_first.reshape(3, 3 * C1, C2),
            conv_second.reshape(3, 3 * C2, C2),
            cotangent.reshape(64, C2),
            edge_pick,
            edge_flip,
            corner_rule,
        )
    ))
    pooled, input_grad, first, second = pl.pallas_call(
        finish_kernel,
        out_shape=(
            jax.ShapeDtypeStruct((64, C2), BF),
            jax.ShapeDtypeStruct((256, C1), BF),
            jax.ShapeDtypeStruct((9 * C1, C2), BF),
            jax.ShapeDtypeStruct((9 * C2, C2), BF),
        ),
        in_specs=[vmem] * 5,
        out_specs=[hbm] * 4,
        scratch_shapes=[
            pltpu.VMEM((9 * C1, C2), BF),
            pltpu.VMEM((9 * C2, C2), BF),
            pltpu.SemaphoreType.DMA((6,)),
        ],
        compiler_params=pltpu.CompilerParams(vmem_limit_bytes=16 * 1024 * 1024),
        name="scale_outputs",
    )(pooled, input_grad, first, second, square)
    return (
        pooled.reshape(1, 1, 8, 8, C2),
        input_grad.reshape(1, 1, 16, 16, C1),
        first.reshape(3, 3, C1, C2),
        second.reshape(3, 3, C2, C2),
    )


def solution(mesh):
    return jax.shard_map(
        on_device,
        mesh=mesh,
        in_specs=(
            P("lon", "lat", None, None, None),
            P(),
            P(),
            P("lon", "lat", None, None, None),
            P("lon", "lat", None),
            P("lon", "lat", None),
            P("lon", "lat", None),
        ),
        out_specs=(P("lon", "lat", None, None, None), P("lon", "lat", None, None, None), P(), P()),
        check_vma=False,
    )
```

```python
import math

import jax
import jax.numpy as jnp
from jax import lax
from jax.experimental import pallas as pl
from jax.experimental.pallas import tpu as pltpu
from jax.sharding import PartitionSpec as P

MESH = pl.DeviceIdType.MESH
BF = jnp.bfloat16
F32 = jnp.float32
NX, NY, NZ = 4, 4, 16
LON, LAT = 2 * NY * NZ, 4
C1, C2 = 128, 256


def normal_cdf(values):
    return 0.5 * (1.0 + lax.erf(values * (1.0 / math.sqrt(2.0))))


def gelu_slope(values, cdf):
    return cdf + values * jnp.exp(-0.5 * values * values) * (1.0 / math.sqrt(2.0 * math.pi))


def iota(shape, dim):
    return lax.broadcasted_iota(jnp.int32, shape, dim)


def hot(cond, value=1.0):
    return jnp.where(cond, jnp.float32(value), jnp.float32(0.0))


def wide(row, count):
    return jnp.concatenate([row] * count, axis=1)


def edge_cell(edge, flip, position):
    at = jnp.where(flip == 1, 15 - position, position)
    return jnp.where(edge == 0, at, jnp.where(edge == 1, 240 + at, jnp.where(edge == 2, 16 * at, 16 * at + 15)))


def mm(a, b):
    return jnp.dot(a, b, preferred_element_type=F32)


def mm_nt(a, b):
    return lax.dot_general(a, b, (((1,), (1,)), ((), ())), preferred_element_type=F32)


def mm_tn(a, b):
    return lax.dot_general(a, b, (((0,), (0,)), ((), ())), preferred_element_type=F32)


def remote(src, dst, send_sem, recv_sem, device):
    return pltpu.make_async_remote_copy(
        src_ref=src, dst_ref=dst, send_sem=send_sem, recv_sem=recv_sem,
        device_id=device, device_id_type=MESH,
    )


def corner_slot(edge, at_end):
    return jnp.where(
        edge == 0, at_end, jnp.where(edge == 1, 2 + at_end, jnp.where(edge == 2, 2 * at_end, 1 + 2 * at_end))
    )


class Reduce:
    def __init__(self, m, refs, place):
        self.m = m
        self.total = m[0] + m[1]
        self.start = (0, 16 * m[0])
        (self.halves, self.r0, self.a1, r1a, r1b, a2a, a2b, r2a, r2b, self.a3, self.n3, self.f3, self.out,
         self.s_send, self.s_recv, self.g_send, self.g_recv) = refs
        self.r1, self.a2, self.r2 = (r1a, r1b), (a2a, a2b), (r2a, r2b)
        self.x, self.y, self.z, self.core, self.device = place
        self.near, self.far = lax.rem(self.z, 4), lax.div(self.z, 4)
        self.pending = []
        self.pieces = []
        self.waited = 0

    def other_core(self):
        return self.device(self.x, self.y, self.z, 1 - self.core)

    def peer(self, axis, d):
        x = lax.rem(self.x + d, NX) if axis == "x" else self.x
        y = lax.rem(self.y + d, NY) if axis == "y" else self.y
        return self.device(x, y, self.z, self.core)

    def axes(self, part):
        return ("x", "y") if part == 0 else ("y", "x")

    def coords(self, part):
        return (self.x, self.y) if part == 0 else (self.y, self.x)

    def send(self, copy):
        copy.start()
        self.pending.append(copy)

    def received(self, ref, sem):
        remote(ref, ref, self.s_send.at[0], sem, self.other_core()).wait_recv()

    def flush(self):
        for copy in self.pending:
            copy.wait_send()
        self.pending = []

    def far_flush(self):
        @pl.when(self.near < self.total // 2)
        def _():
            for copy in self.far_copies():
                copy.wait_send()

    def near_flush(self):
        @pl.when(self.near < self.total // 2)
        def _():
            for copy in self.near_copies():
                copy.wait_send()

    def core_send(self, at, count):
        k = len(self.pieces)
        self.pieces.append((at, count))
        self.send(remote(self.halves.at[1 - self.core, at:at + count], self.r0.at[at:at + count],
                         self.s_send.at[k], self.s_recv.at[k], self.other_core()))

    def core_add(self):
        for k, (at, count) in enumerate(self.pieces):
            self.received(self.r0.at[at:at + count], self.s_recv.at[k])
        for e in (2, 1, 3, 0):
            for part in range(2):
                m = self.m[part]
                ca, cb = self.coords(part)
                block = lax.rem(cb + e, 4)
                for d in (2, 1, 3):
                    at = pl.ds(self.start[part] + (lax.rem(ca + d, 4) * 4 + block) * m, m)
                    self.a1[at] = (self.halves[self.core, at].astype(F32) + self.r0[at].astype(F32)).astype(BF)
                    self.send(remote(self.a1.at[at], self.r1[part].at[d - 1, pl.ds(block * m, m)],
                                     self.s_send.at[3 + 12 * part + 3 * e + d - 1], self.s_recv.at[3 + 4 * part + e],
                                     self.peer(self.axes(part)[0], d)))

    def first_add(self):
        for e in (2, 1, 3, 0):
            for part in range(2):
                m = self.m[part]
                r1, a2, r2 = self.r1[part], self.a2[part], self.r2[part]
                ca, cb = self.coords(part)
                self.received(r2, self.s_recv.at[3 + 4 * part + e])
                block = lax.rem(cb + e, 4)
                at = pl.ds(block * m, m)
                own = pl.ds(self.start[part] + (ca * 4 + block) * m, m)
                total = self.halves[self.core, own].astype(F32) + self.r0[own].astype(F32)
                for d in range(3):
                    total = total + r1[d, at].astype(F32)
                a2[at] = total.astype(BF)
                if e:
                    self.send(remote(a2.at[at], r2.at[e - 1], self.s_send.at[27 + 3 * part + e - 1],
                                     self.s_recv.at[11 + part], self.peer(self.axes(part)[1], e)))

    def second_add(self):
        for part in range(2):
            m = self.m[part]
            a2, r2 = self.a2[part], self.r2[part]
            cb = self.coords(part)[1]
            self.received(r2, self.s_recv.at[11 + part])
            total = a2[pl.ds(cb * m, m)].astype(F32)
            for e in range(3):
                total = total + r2[e].astype(F32)
            self.a3[part * self.m[0]:part * self.m[0] + m] = total.astype(BF)
        for d in (2, 1, 3):
            owner = lax.rem(self.near + d, 4)
            self.send(remote(self.a3.at[pl.ds(2 * owner, 2)], self.n3.at[d - 1], self.s_send.at[32 + d],
                             self.s_recv.at[13], self.device(self.x, self.y, 4 * self.far + owner, self.core)))

    def near_add(self):
        self.received(self.n3, self.s_recv.at[13])
        total = self.a3[pl.ds(2 * self.near, 2)].astype(F32)
        for e in range(3):
            total = total + self.n3[e].astype(F32)
        self.f3[self.far] = total.astype(BF)

        @pl.when(self.near < self.total // 2)
        def _():
            for copy in self.far_copies():
                copy.start()

    def far_copies(self):
        return [
            remote(self.f3.at[self.far], self.f3.at[self.far], self.s_send.at[35 + d], self.s_recv.at[14],
                   self.device(self.x, self.y, 4 * lax.rem(self.far + d, 4) + self.near, self.core))
            for d in (2, 1, 3)
        ]

    def unit_at(self, u):
        ma, mb = self.m
        first = (self.x * 4 + self.y) * ma + u
        second = self.start[1] + (self.y * 4 + self.x) * mb + u - ma
        return jnp.where(u < ma, first, second)

    def near_copies(self):
        at = pl.ds(self.unit_at(2 * self.near), 2)
        return [
            remote(self.out.at[self.core, at], self.out.at[self.core, at], self.g_send.at[19 + d], self.g_recv.at[19 + d],
                   self.device(self.x, self.y, 4 * self.far + lax.rem(self.near + d, 4), self.core))
            for d in (2, 1, 3)
        ]

    def far_add(self):
        @pl.when(self.near < self.total // 2)
        def _():
            self.received(self.f3.at[0:3], self.s_recv.at[14])
            total = self.f3[0].astype(F32)
            for e in range(1, 4):
                total = total + self.f3[e].astype(F32)
            self.out[self.core, pl.ds(self.unit_at(2 * self.near), 2)] = total.astype(BF)
            for copy in self.near_copies():
                copy.start()

    def gather_second(self):
        for d in (1, 3, 2):
            owner = lax.rem(self.near + 4 - d, 4)

            @pl.when(owner < self.total // 2)
            def _():
                self.received(self.out.at[self.core, pl.ds(self.unit_at(2 * owner), 2)], self.g_recv.at[19 + d])

        for part in range(2):
            m = self.m[part]
            ca, cb = self.coords(part)
            at = pl.ds(self.start[part] + (ca * 4 + cb) * m, m)
            for d in (2, 1, 3):
                k = part * 3 + d - 1
                self.send(remote(self.out.at[self.core, at], self.out.at[self.core, at], self.g_send.at[k],
                                 self.g_recv.at[k], self.peer(self.axes(part)[1], d)))
        for part in range(2):
            self.forward(part, 0)

    def forward(self, part, e):
        m = self.m[part]
        ca, cb = self.coords(part)
        at = pl.ds(self.start[part] + (ca * 4 + lax.rem(cb + 4 - e, 4)) * m, m)
        for d in (2, 1, 3):
            self.send(remote(self.out.at[self.core, at], self.out.at[self.core, at],
                             self.g_send.at[23 + 12 * part + 3 * e + d - 1], self.g_recv.at[6 + part * 3 + d - 1],
                             self.peer(self.axes(part)[0], d)))

    def gather_first(self):
        for e in (1, 3, 2):
            for part in range(2):
                m = self.m[part]
                ca, cb = self.coords(part)
                at = pl.ds(self.start[part] + (ca * 4 + lax.rem(cb + 4 - e, 4)) * m, m)
                self.received(self.out.at[self.core, at], self.g_recv.at[part * 3 + e - 1])
                self.forward(part, e)
        for part in range(2):
            n = 4 * self.m[part]
            self.to_core(part, 0, pl.ds(self.start[part] + self.coords(part)[0] * n, n))

    def to_core(self, part, d, at):
        k = 12 + part * 4 + d
        self.send(remote(self.out.at[self.core, at], self.out.at[self.core, at], self.g_send.at[k],
                         self.g_recv.at[k], self.other_core()))

    def block_of(self, part, d):
        n = 4 * self.m[part]
        return pl.ds(self.start[part] + lax.rem(self.coords(part)[0] + 4 - d, 4) * n, n)

    def gather_core(self):
        for d in (1, 3, 2):
            for part in range(2):
                at = self.block_of(part, d)
                self.received(self.out.at[self.core, at], self.g_recv.at[6 + part * 3 + d - 1])
                self.to_core(part, d, at)

    def gather_done(self):
        for d in (0, 1, 3, 2):
            for part in range(2):
                at = self.block_of(part, d)
                self.received(self.out.at[1 - self.core, at], self.g_recv.at[12 + part * 4 + d])
                yield part, at.start


def reduce_scratch(ma, mb):
    units = 16 * (ma + mb)
    return [
        pltpu.VMEM((2, units, 16, 128), BF),
        pltpu.VMEM((units, 16, 128), BF),
        pltpu.VMEM((units, 16, 128), BF),
        pltpu.VMEM((3, 4 * ma, 16, 128), BF),
        pltpu.VMEM((3, 4 * mb, 16, 128), BF),
        pltpu.VMEM((4 * ma, 16, 128), BF),
        pltpu.VMEM((4 * mb, 16, 128), BF),
        pltpu.VMEM((3, ma, 16, 128), BF),
        pltpu.VMEM((3, mb, 16, 128), BF),
        pltpu.VMEM((8, 16, 128), BF),
        pltpu.VMEM((3, 2, 16, 128), BF),
        pltpu.VMEM((4, 2, 16, 128), BF),
        pltpu.SemaphoreType.DMA((39,)),
        pltpu.SemaphoreType.DMA((15,)),
        pltpu.SemaphoreType.DMA((47,)),
        pltpu.SemaphoreType.DMA((23,)),
    ]


N_REDUCE = 16
MA, MB = (4, 4), (4, 2)
A_UNITS, B_UNITS, FIRST_UNITS, LAST_UNITS = 128, 96, 72, 16


def edge_scratch(channels):
    return [
        pltpu.VMEM((80, channels), BF),
        pltpu.VMEM((256, channels), BF),
        pltpu.SemaphoreType.DMA((8,)),
        pltpu.SemaphoreType.DMA((8,)),
    ]


def patch_scratch():
    return [
        pltpu.VMEM((32, 9 * C1), BF),
        pltpu.VMEM((2, 32, 3 * C1), BF),
        pltpu.VMEM((4, 16, C1), BF),
        pltpu.VMEM((128, 9 * C1), BF),
        pltpu.VMEM((2, 32, 3 * C1), BF),
        pltpu.VMEM((4, 16, C1), BF),
        pltpu.SemaphoreType.DMA((8,)),
        pltpu.SemaphoreType.DMA((8,)),
    ]


def layer_scratch(channels):
    return [
        pltpu.VMEM((304, channels), F32),
        pltpu.VMEM((384, 3 * channels), BF),
        pltpu.VMEM((416, C2), BF),
        pltpu.VMEM((304, 3 * channels), F32),
        pltpu.VMEM((384, channels), BF),
        pltpu.VMEM((128, channels), BF),
        pltpu.VMEM((128, channels), BF),
        pltpu.SemaphoreType.DMA((8,)),
        pltpu.SemaphoreType.DMA((8,)),
    ]


N_EDGE, N_PATCH, N_LAYER = 4, 8, 9


def step_kernel(*refs):
    (feat_hbm, w1_hbm, w2_hbm, cot_hbm, pick_hbm, flip_hbm, rule_hbm,
     pooled_ref, grad_ref, first_out, second_out, square_ref) = refs[:12]
    refs = refs[12:]
    edges, refs = refs[:N_EDGE], refs[N_EDGE:]
    patch_refs, refs = refs[:N_PATCH], refs[N_PATCH:]
    layer1, refs = refs[:N_LAYER], refs[N_LAYER:]
    layer2, refs = refs[:N_LAYER], refs[N_LAYER:]
    red2_refs, refs = refs[:N_REDUCE], refs[N_REDUCE:]
    red1_refs, refs = refs[:N_REDUCE], refs[N_REDUCE:]
    (feat_ref, w1, w2, cot_ref, pick_ref, flip_ref, rule_ref, load_sem,
     rules_out, rules_in, rule_send, rule_recv, q_fwd, q_back, q_act, slope1, pre2,
     windows) = refs
    red2_refs = red2_refs[:12] + (second_out,) + red2_refs[12:]
    red1_refs = red1_refs[:12] + (first_out,) + red1_refs[12:]

    lon, lat = lax.axis_index("lon"), lax.axis_index("lat")
    y = lax.div(lon, 2 * NZ)
    z = lax.div(lax.rem(lon, 2 * NZ), 2)
    x = lax.rem(lon, 2) * 2 + lax.div(lat, 2)
    core = lax.rem(lat, 2)

    def device(x_at, y_at, z_at, core_at):
        return (y_at * (2 * NZ) + z_at * 2 + lax.div(x_at, 2), lax.rem(x_at, 2) * 2 + core_at)

    across = lax.rem(lon + LON // 2, LON)
    below, above = lat == 0, lat == LAT - 1
    vert = (
        (jnp.where(below, across, lon), jnp.where(below, lat, lat - 1)),
        (jnp.where(above, across, lon), jnp.where(above, lat, lat + 1)),
    )
    seen = (jnp.where(below, 0, 1), jnp.where(above, 1, 0))

    def west_of(at):
        return (lax.rem(at[0] + LON - 1, LON), at[1])

    def east_of(at):
        return (lax.rem(at[0] + 1, LON), at[1])

    here = (lon, lat)
    west, east = west_of(here), east_of(here)
    diagonal = [
        (west_of(vert[0]), 2 * seen[0] + 1),
        (east_of(vert[0]), 2 * seen[0]),
        (west_of(vert[1]), 2 * seen[1] + 1),
        (east_of(vert[1]), 2 * seen[1]),
    ]

    barrier = pltpu.get_barrier_semaphore()
    partners = [device(x, y, lax.rem(z + 4 * d, NZ), core) for d in (2, 1, 3)]
    partners += [d[0] for d in diagonal] + [west, east, vert[0], vert[1]]
    for d in (2, 1, 3):
        partners.append(device(x, y, 4 * lax.div(z, 4) + lax.rem(z + d, 4), core))
        partners.append(device(lax.rem(x + d, NX), y, z, core))
        partners.append(device(x, lax.rem(y + d, NY), z, core))
    partners.append(device(x, y, z, 1 - core))
    for partner in partners:
        pl.semaphore_signal(barrier, inc=1, device_id=partner, device_id_type=MESH)

    loads = [
        pltpu.make_async_copy(src, dst, load_sem.at[n])
        for n, (src, dst) in enumerate((
            (pick_hbm, pick_ref), (flip_hbm, flip_ref), (rule_hbm, rule_ref), (feat_hbm, feat_ref),
            (w1_hbm, w1), (cot_hbm, cot_ref), (w2_hbm, w2),
        ))
    ]
    for load in loads:
        load.start()

    for load in loads[:3]:
        load.wait()
    picks = [pick_ref[0, 0, s] for s in range(2)]
    flips = [flip_ref[0, 0, s] for s in range(2)]
    rules = [rule_ref[0, 0, k] for k in range(4)]

    row8 = iota((8, 128), 0)
    rules_out[...] = jnp.where(
        row8 == 0, picks[0], jnp.where(row8 == 1, flips[0], jnp.where(row8 == 2, picks[1], flips[1]))
    )

    p, cell = iota((80, 256), 0), iota((80, 256), 1)
    k = p & 15
    want = jnp.where(
        p < 16, k, jnp.where(p < 32, 240 + k, jnp.where(p < 48, 16 * k, jnp.where(p < 64, 16 * k + 15, (
            jnp.where(k == 0, 0, jnp.where(k == 1, 15, jnp.where(k == 2, 240, jnp.where(k == 3, 255, -1))))
        ))))
    )
    take_edges = hot(cell == want).astype(BF)

    loads[3].wait()
    edges[0][...] = mm(take_edges, feat_ref[...]).astype(BF)
    edges[1][224:256, :] = jnp.zeros((32, C1), BF)
    layer1[1][288:384, :] = jnp.zeros((96, 3 * C1), BF)

    pl.semaphore_wait(barrier, len(partners))

    def edge_sends():
        out, got, send, recv = edges
        copies = []
        for i, (target, slot) in enumerate(diagonal):
            copies.append(remote(out.at[64:80], got.at[pl.ds(pl.multiple_of(160 + 16 * slot, 16), 16)],
                                 send.at[4 + i], recv.at[4 + slot], target))
        for side in range(2):
            copies.append(remote(out.at[0:64], got.at[pl.ds(pl.multiple_of(64 * seen[side], 64), 64)],
                                 send.at[side], recv.at[seen[side]], vert[side]))
        copies.append(remote(out.at[32:48], got.at[144:160], send.at[2], recv.at[3], west))
        copies.append(remote(out.at[48:64], got.at[128:144], send.at[3], recv.at[2], east))
        for copy in copies:
            copy.start()
        return copies

    def edge_waits():
        out, got, send, recv = edges
        spots = [(0, 64), (64, 64), (128, 16), (144, 16), (160, 16), (176, 16), (192, 16), (208, 16)]
        for i, (at, size) in enumerate(spots):
            remote(out.at[0:size], got.at[at:at + size], send.at[i], recv.at[i], west).wait_recv()

    sent = edge_sends()
    rule_copies = []
    for i, (target, slot) in enumerate(((vert[0], seen[0]), (vert[1], seen[1]), (west, 3), (east, 2))):
        rule_copies.append(remote(rules_out, rules_in.at[slot], rule_send.at[i], rule_recv.at[slot], target))
    for copy in rule_copies:
        copy.start()

    r, c = iota((288, 256), 0), iota((288, 256), 1)
    j, i = r & 15, r >> 4
    want = jnp.where(j == 0, 127 + i, jnp.where(j == 15, 143 + i, -1))
    q_fwd[0:288, :] = hot(c == want).astype(BF)
    r, c = iota((32, 256), 0), iota((32, 256), 1)
    k, north = r & 15, r >= 16
    flip = jnp.where(north, flips[1], flips[0])
    pick = jnp.where(north, picks[1], picks[0])
    want = jnp.where(north, 64, 0) + 16 * pick + jnp.where(flip == 1, 15 - k, k)
    q_fwd[288:320, :] = hot(c == want).astype(BF)

    def halo_cells(p, q):
        block, k = p >> 4, p & 15
        low, high = k == 0, k == 15
        corner_at = (0, 15, 272, 287)
        want = jnp.where(block == 0, 288 + k, jnp.where(block == 1, 304 + k, jnp.where(
            block == 2, 16 * k + 16, jnp.where(block == 3, 16 * k + 31, -1))))
        half = jnp.full_like(want, -1)
        ends = ((0, 1), (2, 3), (0, 2), (1, 3))
        for b in range(4):
            first, second = ends[b]
            half = jnp.where((block == b) & low & (rules[first] == 1), corner_at[first], half)
            half = jnp.where((block == b) & high & (rules[second] == 1), corner_at[second], half)
            want = jnp.where((block == 4 + b) & low & (rules[b] != 1), corner_at[b], want)
        return (hot(q == want) + hot(q == half, 0.5)).astype(BF)

    q_back[...] = halo_cells(iota((128, 384), 0), iota((128, 384), 1))
    q_act[...] = halo_cells(iota((320, 128), 1), iota((320, 128), 0))

    for layer in (layer1, layer2):
        g_pad = layer[2]
        g_pad[0:32, :] = jnp.zeros((32, C2), BF)
        g_pad[288:416, :] = jnp.zeros((128, C2), BF)
        layer[4][320:384, :] = jnp.zeros((64, layer[4].shape[1]), BF)

    red2 = Reduce(MA, red2_refs, (x, y, z, core, device))
    red1 = Reduce(MB, red1_refs, (x, y, z, core, device))
    used = FIRST_UNITS + LAST_UNITS
    red1.halves[:, used:B_UNITS] = jnp.zeros((2, B_UNITS - used, 16, 128), BF)
    red1.a3[6:8] = jnp.zeros((2, 16, 128), BF)

    for slot in range(4):
        remote(rules_out, rules_in.at[slot], rule_send.at[slot], rule_recv.at[slot], west).wait_recv()

    r, c = iota((16, 256), 0), iota((16, 256), 1)
    for side in range(2):
        def source(position):
            return 64 * side + 16 * picks[side] + jnp.where(flips[side] == 1, 15 - position, position)

        rows = 2 * side
        w_pick, w_flip = wide(rules_in[2, rows:rows + 1, :], 2), wide(rules_in[2, rows + 1:rows + 2, :], 2)
        e_pick, e_flip = wide(rules_in[3, rows:rows + 1, :], 2), wide(rules_in[3, rows + 1:rows + 2, :], 2)
        w_at = 160 + 32 * side + corner_slot(w_pick, jnp.where(w_flip == 1, 0, 1))
        e_at = 176 + 32 * side + corner_slot(e_pick, jnp.where(e_flip == 1, 1, 0))
        w_rule, e_rule = rules[2 * side] == 1, rules[2 * side + 1] == 1
        shape = (16, 256)
        w_main = jnp.where(w_rule, jnp.full(shape, -1), jnp.broadcast_to(w_at, shape))
        e_main = jnp.where(e_rule, jnp.full(shape, -1), jnp.broadcast_to(e_at, shape))
        w_a, w_c = jnp.where(w_rule, source(0), -1), jnp.where(w_rule, 128 + 15 * side, -1)
        e_a, e_c = jnp.where(e_rule, source(15), -1), jnp.where(e_rule, 144 + 15 * side, -1)
        w_row = hot(c == w_main) + hot(c == w_a, 0.5) + hot(c == w_c, 0.5)
        e_row = hot(c == e_main) + hot(c == e_a, 0.5) + hot(c == e_c, 0.5)
        values = jnp.where(r == 0, w_row, jnp.where(r == 15, e_row, 0.0))
        q_fwd[272 * side:272 * side + 16, :] = values.astype(BF)

    face = (jnp.where(below, 0, 1), jnp.where(above, 1, 0))
    facing = []
    for side in range(2):
        south = face[side] == 0
        facing.append((
            jnp.where(south, rules_in[side, 0:1, 0:128], rules_in[side, 2:3, 0:128]),
            jnp.where(south, rules_in[side, 1:2, 0:128], rules_in[side, 3:4, 0:128]),
        ))
    p = iota((1, 128), 1)
    block, k = p >> 4, p & 15
    on_north = (block == 1) | (block >= 6)
    pick = jnp.where(on_north, facing[1][0], facing[0][0])
    flip = jnp.where(on_north, facing[1][1], facing[0][1])
    position = jnp.where(block < 2, k, jnp.where((block & 1) == 1, 15, 0))
    target = edge_cell(pick, flip, position)
    target = jnp.where(block == 2, 16 * k + 15, jnp.where(block == 3, 16 * k, target))
    target = jnp.where((block >= 4) & (k != 0), -1, target)
    place_grads = hot(iota((256, 128), 0) == target).astype(BF)

    r, c = iota((32, 256), 0), iota((32, 256), 1)
    pick = jnp.where(r < 16, wide(facing[0][0], 2), wide(facing[1][0], 2))
    flip = jnp.where(r < 16, wide(facing[0][1], 2), wide(facing[1][1], 2))
    take_cells = hot(c == edge_cell(pick, flip, r & 15)).astype(BF)
    r, c = iota((64, 384), 0), iota((64, 384), 1)
    row = r & 31
    take_strips = hot((row < 18) & (c == 16 * row + jnp.where(r < 32, 15, 0))).astype(BF)
    tap, which = r & 15, r >> 4
    tap_row = (tap * 11) >> 5
    pick = jnp.where(which < 2, wide(facing[0][0], 3), wide(facing[1][0], 3))
    flip = jnp.where(which < 2, wide(facing[0][1], 3), wide(facing[1][1], 3))
    at = 16 * tap_row + edge_cell(pick, flip, jnp.where((which & 1) == 1, 15, 0))
    take_corners = [
        hot((tap < 9) & (tap - 3 * tap_row == dw) & (c == at)).astype(BF) for dw in range(3)
    ]

    def patch_sends():
        cells, strips, corners, got_cells, got_strips, got_corners, send, recv = patch_refs
        padded = layer1[1]
        values = mm(take_corners[0], padded[:, 0:C1])
        for dw in (1, 2):
            values = values + mm(take_corners[dw], padded[:, dw * C1:(dw + 1) * C1])
        corners[...] = values.astype(BF).reshape(4, 16, C1)
        copies = []
        for i, (target_at, slot) in enumerate(diagonal):
            copies.append(remote(corners.at[i], got_corners.at[slot], send.at[4 + i], recv.at[4 + slot], target_at))
            copies[-1].start()
        strips[...] = mm(take_strips, padded[...]).astype(BF).reshape(2, 32, 3 * C1)
        copies.append(remote(strips.at[0], got_strips.at[0], send.at[2], recv.at[2], east))
        copies.append(remote(strips.at[1], got_strips.at[1], send.at[3], recv.at[3], west))
        for copy in copies[-2:]:
            copy.start()
        for dh in range(3):
            cells[:, 384 * dh:384 * dh + 384] = mm(take_cells, padded[16 * dh:16 * dh + 256, :]).astype(BF)
        for side in range(2):
            copies.append(remote(cells.at[16 * side:16 * side + 16],
                                 got_cells.at[pl.ds(pl.multiple_of(16 * seen[side], 16), 16)],
                                 send.at[side], recv.at[seen[side]], vert[side]))
            copies[-1].start()
        return copies

    def patch_waits():
        cells, strips, corners, got_cells, got_strips, got_corners, send, recv = patch_refs
        for i in range(2):
            remote(cells.at[0:16], got_cells.at[16 * i:16 * i + 16], send.at[i], recv.at[i], west).wait_recv()
            remote(strips.at[i], got_strips.at[i], send.at[2 + i], recv.at[2 + i], west).wait_recv()
        r, c = iota((32, 64), 0), iota((32, 64), 1)
        both = got_strips[...].reshape(64, 3 * C1)
        for dh in range(3):
            spread_rows = hot(c == jnp.where(r < 16, r, r + 16) + dh).astype(BF)
            got_cells[32:64, 384 * dh:384 * dh + 384] = mm(spread_rows, both).astype(BF)
        for i in range(4):
            remote(corners.at[i], got_corners.at[i], send.at[4 + i], recv.at[4 + i], west).wait_recv()
        r, c = iota((64, 64), 0), iota((64, 64), 1)
        taps = got_corners[...].reshape(64, C1)
        for tap in range(9):
            first_row = hot(((r & 15) == 0) & (c == r + tap)).astype(BF)
            got_cells[64:128, C1 * tap:C1 * tap + C1] = mm(first_row, taps).astype(BF)

    def pad_tile(layer, tile, cells, channels):
        ext, padded = layer[:2]
        south, north = cells[288:304], cells[304:320]
        ext[8:24, :] = south
        ext[24:280, :] = tile.astype(F32)
        ext[280:296, :] = north
        j = iota((288, channels), 0) & 15
        padded[0:288, 0:channels] = jnp.where(j == 0, cells[0:288], ext[7:295, :]).astype(BF)
        padded[0:288, channels:2 * channels] = ext[8:296, :].astype(BF)
        padded[0:288, 2 * channels:] = jnp.where(j == 15, cells[0:288], ext[9:297, :]).astype(BF)

    def convolve(layer, weight):
        padded = layer[1]
        total = mm(padded[0:256, :], weight[0])
        for dh in (1, 2):
            total = total + mm(padded[16 * dh:16 * dh + 256, :], weight[dh])
        return total

    def input_side(layer, weight, channels):
        g_pad, by_shift, leaving, out = layer[2:6]
        total = mm_nt(g_pad[32:320, :], weight[0])
        for dh in (1, 2):
            at = 32 - 16 * dh
            total = total + mm_nt(g_pad[at:at + 288, :], weight[dh])
        by_shift[8:296, :] = total
        j = iota((288, channels), 0) & 15
        centre = by_shift[8:296, channels:2 * channels]
        centre = centre + jnp.where(j == 15, 0.0, by_shift[9:297, 0:channels])
        centre = centre + jnp.where(j == 0, 0.0, by_shift[7:295, 2 * channels:])
        centre = centre.astype(BF)
        sides = jnp.where(j == 0, by_shift[8:296, 0:channels], by_shift[8:296, 2 * channels:])
        sides = jnp.where((j == 0) | (j == 15), sides, 0.0)
        leaving[0:288, :] = sides.astype(BF)
        leaving[288:304, :] = centre[0:16]
        leaving[304:320, :] = centre[272:288]
        out[...] = mm(q_back[...], leaving[...]).astype(BF)
        return centre[16:272]

    def grad_sends(layer):
        out, got, send, recv = layer[5:9]
        copies = []
        for side in range(2):
            copies.append(remote(out.at[16 * side:16 * side + 16],
                                 got.at[pl.ds(pl.multiple_of(16 * seen[side], 16), 16)],
                                 send.at[side], recv.at[seen[side]], vert[side]))
        copies.append(remote(out.at[32:48], got.at[32:48], send.at[2], recv.at[2], west))
        copies.append(remote(out.at[48:64], got.at[48:64], send.at[3], recv.at[3], east))
        for i, (target_at, slot) in enumerate(diagonal):
            copies.append(remote(out.at[64 + 16 * i:80 + 16 * i],
                                 got.at[pl.ds(pl.multiple_of(64 + 16 * slot, 16), 16)],
                                 send.at[4 + i], recv.at[4 + slot], target_at))
        for copy in copies:
            copy.start()
        return copies

    def grad_waits(layer):
        out, got, send, recv = layer[5:9]
        for i in range(8):
            remote(out.at[0:16], got.at[16 * i:16 * i + 16], send.at[i], recv.at[i], west).wait_recv()

    def weight_grad(block, spots):
        block = block.astype(BF)
        units = block.shape[0] // 16
        for h in range(2):
            values = block[:, 128 * h:128 * h + 128].reshape(units, 16, 128)
            for first, count, red, to in spots:
                red.halves[h, to:to + count] = values[first:first + count]

    edge_waits()
    pad_tile(layer1, feat_ref[...], mm(q_fwd[...], edges[1][...]), C1)
    sent += patch_sends()
    loads[4].wait()
    pre1 = convolve(layer1, w1)
    cdf1 = normal_cdf(pre1)
    act1 = (pre1 * cdf1).astype(BF)
    slope1[...] = gelu_slope(pre1, cdf1)
    for dh in range(3):
        windows[dh] = layer1[1][16 * dh:16 * dh + 256, :].T
    r, c = iota((256, 64), 0), iota((256, 64), 1)
    spread = hot(c == 8 * (r >> 5) + ((r & 15) >> 1), 0.25).astype(BF)
    loads[5].wait()
    cot = mm(spread, cot_ref[...])
    loads[6].wait()

    patch_waits()
    patches = patch_refs[3]
    halo_pre = mm(patches[:, 0:384], w1[0])
    for dh in (1, 2):
        halo_pre = halo_pre + mm(patches[:, 384 * dh:384 * dh + 384], w1[dh])
    halo_cdf = normal_cdf(halo_pre)
    halo_act = (halo_pre * halo_cdf).astype(BF)
    pad_tile(layer2, act1, mm(q_act[...], halo_act), C2)
    second_pre = convolve(layer2, w2)
    cdf2 = normal_cdf(second_pre)
    grad2 = (cot * gelu_slope(second_pre, cdf2)).astype(BF)
    layer2[2][32:288, :] = grad2
    for dh in range(3):
        spots = [(0, 48, red2, 48 * dh)] if dh < 2 else [(0, 32, red2, 96), (32, 16, red1, FIRST_UNITS)]
        weight_grad(mm_tn(layer2[1][16 * dh:16 * dh + 256, :], grad2), spots)
        red2.core_send(48 * dh, spots[0][1])
    centre2 = input_side(layer2, w2, C2)
    sent += grad_sends(layer2)

    own = (centre2.astype(F32) * slope1[...]).astype(BF)
    leaving = (layer2[5][...].astype(F32) * gelu_slope(halo_pre, halo_cdf)).astype(BF)
    for dh in range(3):
        block = mm(windows[dh], own) + mm_tn(patches[:, 384 * dh:384 * dh + 384], leaving)
        weight_grad(block, [(0, 24, red1, 24 * dh)])
    red1.core_send(0, B_UNITS)
    red2.core_add()
    red1.core_add()
    pre2[...] = second_pre * cdf2

    r, c = iota((64, 256), 0), iota((64, 256), 1)
    gather_cells = hot(r == 8 * (c >> 5) + ((c & 15) >> 1), 0.25).astype(BF)
    act2 = pre2[...]
    high = act2.astype(BF)
    low = (act2 - high.astype(F32)).astype(BF)
    pooled_ref[...] = (mm(gather_cells, high) + mm(gather_cells, low)).astype(BF)

    red2.first_add()
    red1.first_add()

    grad_waits(layer2)
    first_grad = centre2.astype(F32) + mm(place_grads, layer2[6][...])
    layer1[2][32:288, :] = (first_grad * slope1[...]).astype(BF)
    centre1 = input_side(layer1, w1, C1)
    sent += grad_sends(layer1)

    red2.second_add()
    red1.second_add()
    red2.near_add()
    red1.near_add()

    grad_waits(layer1)
    grad_ref[...] = (centre1.astype(F32) + mm(place_grads, layer1[6][...])).astype(BF)

    for copy in sent + rule_copies:
        copy.wait_send()
    red2.flush()
    red1.flush()
    red2.far_add()
    red1.far_add()
    red2.gather_second()
    red1.gather_second()
    for red in (red2, red1):
        red.far_flush()
        red.near_flush()
    red2.gather_first()
    red1.gather_first()
    red2.gather_core()
    red1.gather_core()
    list(red2.gather_done())
    red2.flush()
    squares = jnp.zeros((16, 128), F32)
    for h in range(2):
        squares = sum_squares(second_out, h, 0, A_UNITS // 8, squares)
    squares = sum_squares(first_out, core, 0, B_UNITS // 8, squares)
    for part, at in red1.gather_done():
        squares = sum_squares(first_out, 1 - core, at, red1.m[part] // 2, squares)
    square_ref[...] = squares
    red1.flush()


def sum_squares(ref, half, at, steps, total):
    def body(i, total):
        values = ref[half, pl.ds(at + i * 8, 8)].astype(F32)
        return total + jnp.sum(values * values, axis=0)

    return lax.fori_loop(0, steps, body, total)


def finish_kernel(pooled_ref, grad_ref, first_ref, second_ref, square_ref, pooled_out, grad_out, first_out, second_out,
                  first_rows, second_rows, sems):
    copies = [pltpu.make_async_copy(pooled_ref, pooled_out, sems.at[0]),
              pltpu.make_async_copy(grad_ref, grad_out, sems.at[1])]
    for copy in copies:
        copy.start()

    squared = jnp.sum(jnp.sum(square_ref[...], axis=0, keepdims=True), axis=1, keepdims=True)
    target_norm = math.sqrt(9.0 * (C1 + C2) * C2)
    scale = jnp.broadcast_to(target_norm / jnp.sqrt(squared + 1e-06), (16, 128))

    def write(ref, at, to, count, out):
        def body(i, carry):
            for h in range(2):
                values = ref[h, pl.ds(at + i * 8, 8)].astype(F32) * scale
                rows = pl.ds(pl.multiple_of((to + i * 8) * 16, 128), 128)
                out[rows, 128 * h:128 * h + 128] = values.astype(BF).reshape(128, 128)
            return carry

        lax.fori_loop(0, count // 8, body, 0)

    jobs = [(second_ref, n * 64, n * 64, 64, second_rows, second_out) for n in range(2)]
    jobs.append((first_ref, 0, 0, FIRST_UNITS, first_rows, first_out))
    jobs.append((first_ref, FIRST_UNITS, A_UNITS, LAST_UNITS, second_rows, second_out))
    for n, (ref, at, to, count, rows, out) in enumerate(jobs):
        write(ref, at, to, count, rows)
        span = pl.ds(16 * to, 16 * count)
        copies.append(pltpu.make_async_copy(rows.at[span], out.at[span], sems.at[2 + n]))
        copies[-1].start()
    for copy in copies:
        copy.wait()


def on_device(features, conv_first, conv_second, cotangent, edge_pick, edge_flip, corner_rule):
    vmem = pl.BlockSpec(memory_space=pltpu.VMEM)
    hbm = pl.BlockSpec(memory_space=pltpu.HBM)
    pooled, input_grad, first, second, square = pl.pallas_call(
        step_kernel,
        out_shape=(
            jax.ShapeDtypeStruct((64, C2), BF),
            jax.ShapeDtypeStruct((256, C1), BF),
            jax.ShapeDtypeStruct((2, B_UNITS, 16, 128), BF),
            jax.ShapeDtypeStruct((2, A_UNITS, 16, 128), BF),
            jax.ShapeDtypeStruct((16, 128), F32),
        ),
        in_specs=[hbm] * 7,
        out_specs=[vmem] * 5,
        scratch_shapes=(
            edge_scratch(C1)
            + patch_scratch()
            + layer_scratch(C1)
            + layer_scratch(C2)
            + reduce_scratch(*MA)
            + reduce_scratch(*MB)
            + [
                pltpu.VMEM((256, C1), BF),
                pltpu.VMEM((3, 3 * C1, C2), BF),
                pltpu.VMEM((3, 3 * C2, C2), BF),
                pltpu.VMEM((64, C2), BF),
                pltpu.SMEM((1, 1, 2), jnp.int32),
                pltpu.SMEM((1, 1, 2), jnp.int32),
                pltpu.SMEM((1, 1, 4), jnp.int32),
                pltpu.SemaphoreType.DMA((7,)),
                pltpu.VMEM((8, 128), jnp.int32),
                pltpu.VMEM((4, 8, 128), jnp.int32),
                pltpu.SemaphoreType.DMA((4,)),
                pltpu.SemaphoreType.DMA((4,)),
                pltpu.VMEM((320, 256), BF),
                pltpu.VMEM((128, 384), BF),
                pltpu.VMEM((320, 128), BF),
                pltpu.VMEM((256, C2), F32),
                pltpu.VMEM((256, C2), F32),
                pltpu.VMEM((3, 3 * C1, 256), BF),
            ]
        ),
        compiler_params=pltpu.CompilerParams(
            collective_id=0, has_side_effects=True, vmem_limit_bytes=32 * 1024 * 1024
        ),
        name="level_step",
    )(*(
        pltpu.with_memory_space_constraint(value, pltpu.HBM)
        for value in (
            features.reshape(256, C1),
            conv_first.reshape(3, 3 * C1, C2),
            conv_second.reshape(3, 3 * C2, C2),
            cotangent.reshape(64, C2),
            edge_pick,
            edge_flip,
            corner_rule,
        )
    ))
    pooled, input_grad, first, second = pl.pallas_call(
        finish_kernel,
        out_shape=(
            jax.ShapeDtypeStruct((64, C2), BF),
            jax.ShapeDtypeStruct((256, C1), BF),
            jax.ShapeDtypeStruct((9 * C1, C2), BF),
            jax.ShapeDtypeStruct((9 * C2, C2), BF),
        ),
        in_specs=[vmem] * 5,
        out_specs=[hbm] * 4,
        scratch_shapes=[
            pltpu.VMEM((9 * C1, C2), BF),
            pltpu.VMEM((9 * C2, C2), BF),
            pltpu.SemaphoreType.DMA((6,)),
        ],
        compiler_params=pltpu.CompilerParams(vmem_limit_bytes=16 * 1024 * 1024),
        name="scale_outputs",
    )(pooled, input_grad, first, second, square)
    return (
        pooled.reshape(1, 1, 8, 8, C2),
        input_grad.reshape(1, 1, 16, 16, C1),
        first.reshape(3, 3, C1, C2),
        second.reshape(3, 3, C2, C2),
    )


def solution(mesh):
    return jax.shard_map(
        on_device,
        mesh=mesh,
        in_specs=(
            P("lon", "lat", None, None, None),
            P(),
            P(),
            P("lon", "lat", None, None, None),
            P("lon", "lat", None),
            P("lon", "lat", None),
            P("lon", "lat", None),
        ),
        out_specs=(P("lon", "lat", None, None, None), P("lon", "lat", None, None, None), P(), P()),
        check_vma=False,
    )
```

```python
import math

import jax
import jax.numpy as jnp
from jax import lax
from jax.experimental import pallas as pl
from jax.experimental.pallas import tpu as pltpu
from jax.sharding import PartitionSpec as P

MESH = pl.DeviceIdType.MESH
BF = jnp.bfloat16
F32 = jnp.float32
NX, NY, NZ = 4, 4, 16
LON, LAT = 2 * NY * NZ, 4
C1, C2 = 128, 256


def normal_cdf(values):
    return 0.5 * (1.0 + lax.erf(values * (1.0 / math.sqrt(2.0))))


def gelu_slope(values, cdf):
    return cdf + values * jnp.exp(-0.5 * values * values) * (1.0 / math.sqrt(2.0 * math.pi))


def iota(shape, dim):
    return lax.broadcasted_iota(jnp.int32, shape, dim)


def hot(cond, value=1.0):
    return jnp.where(cond, jnp.float32(value), jnp.float32(0.0))


def wide(row, count):
    return jnp.concatenate([row] * count, axis=1)


def edge_cell(edge, flip, position):
    at = jnp.where(flip == 1, 15 - position, position)
    return jnp.where(edge == 0, at, jnp.where(edge == 1, 240 + at, jnp.where(edge == 2, 16 * at, 16 * at + 15)))


def mm(a, b):
    return jnp.dot(a, b, preferred_element_type=F32)


def mm_nt(a, b):
    return lax.dot_general(a, b, (((1,), (1,)), ((), ())), preferred_element_type=F32)


def mm_tn(a, b):
    return lax.dot_general(a, b, (((0,), (0,)), ((), ())), preferred_element_type=F32)


def remote(src, dst, send_sem, recv_sem, device):
    return pltpu.make_async_remote_copy(
        src_ref=src, dst_ref=dst, send_sem=send_sem, recv_sem=recv_sem,
        device_id=device, device_id_type=MESH,
    )


def corner_slot(edge, at_end):
    return jnp.where(
        edge == 0, at_end, jnp.where(edge == 1, 2 + at_end, jnp.where(edge == 2, 2 * at_end, 1 + 2 * at_end))
    )


class Reduce:
    def __init__(self, m, refs, place):
        self.m = m
        self.total = m[0] + m[1]
        self.start = (0, 16 * m[0])
        (self.halves, self.r0, self.a1, r1a, r1b, a2a, a2b, r2a, r2b, self.a3, self.n3, self.f3, self.out,
         self.s_send, self.s_recv, self.g_send, self.g_recv) = refs
        self.r1, self.a2, self.r2 = (r1a, r1b), (a2a, a2b), (r2a, r2b)
        self.x, self.y, self.z, self.core, self.device = place
        self.near, self.far = lax.rem(self.z, 4), lax.div(self.z, 4)
        self.pending = []
        self.pieces = []
        self.waited = 0

    def other_core(self):
        return self.device(self.x, self.y, self.z, 1 - self.core)

    def peer(self, axis, d):
        x = lax.rem(self.x + d, NX) if axis == "x" else self.x
        y = lax.rem(self.y + d, NY) if axis == "y" else self.y
        return self.device(x, y, self.z, self.core)

    def axes(self, part):
        return ("x", "y") if part == 0 else ("y", "x")

    def coords(self, part):
        return (self.x, self.y) if part == 0 else (self.y, self.x)

    def send(self, copy):
        copy.start()
        self.pending.append(copy)

    def received(self, ref, sem):
        remote(ref, ref, self.s_send.at[0], sem, self.other_core()).wait_recv()

    def flush(self):
        for copy in self.pending:
            copy.wait_send()
        self.pending = []

    def far_flush(self):
        @pl.when(self.near < self.total // 2)
        def _():
            for copy in self.far_copies():
                copy.wait_send()

    def near_flush(self):
        @pl.when(self.near < self.total // 2)
        def _():
            for copy in self.near_copies():
                copy.wait_send()

    def core_send(self, at, count):
        k = len(self.pieces)
        self.pieces.append((at, count))
        self.send(remote(self.halves.at[1 - self.core, at:at + count], self.r0.at[at:at + count],
                         self.s_send.at[k], self.s_recv.at[k], self.other_core()))

    def core_add(self):
        for part in range(2):
            n = 4 * self.m[part]
            mine = self.coords(part)[0]
            while self.waited < len(self.pieces) and self.pieces[self.waited][0] < self.start[part] + 4 * n:
                at, count = self.pieces[self.waited]
                self.received(self.r0.at[at:at + count], self.s_recv.at[self.waited])
                self.waited += 1
            k = 3 + part
            for d in (2, 1, 3, 0):
                at = pl.ds(self.start[part] + lax.rem(mine + d, 4) * n, n)
                self.a1[at] = (self.halves[self.core, at].astype(F32) + self.r0[at].astype(F32)).astype(BF)
                if d:
                    self.send(remote(self.a1.at[at], self.r1[part].at[d - 1],
                                     self.s_send.at[3 * k - 7 + d], self.s_recv.at[k],
                                     self.peer(self.axes(part)[0], d)))

    def first_add(self):
        for part in range(2):
            m = self.m[part]
            r1, a2, r2 = self.r1[part], self.a2[part], self.r2[part]
            ca, cb = self.coords(part)
            self.received(r1, self.s_recv.at[3 + part])
            k = 5 + part
            for d in (2, 1, 3, 0):
                block = lax.rem(cb + d, 4)
                at = pl.ds(block * m, m)
                total = self.a1[pl.ds(self.start[part] + (ca * 4 + block) * m, m)].astype(F32)
                for e in range(3):
                    total = total + r1[e, at].astype(F32)
                a2[at] = total.astype(BF)
                if d:
                    self.send(remote(a2.at[at], r2.at[d - 1],
                                     self.s_send.at[3 * k - 7 + d], self.s_recv.at[k],
                                     self.peer(self.axes(part)[1], d)))

    def second_add(self):
        for part in range(2):
            m = self.m[part]
            a2, r2 = self.a2[part], self.r2[part]
            cb = self.coords(part)[1]
            self.received(r2, self.s_recv.at[5 + part])
            total = a2[pl.ds(cb * m, m)].astype(F32)
            for e in range(3):
                total = total + r2[e].astype(F32)
            self.a3[part * self.m[0]:part * self.m[0] + m] = total.astype(BF)
        for d in (2, 1, 3):
            owner = lax.rem(self.near + d, 4)
            self.send(remote(self.a3.at[pl.ds(2 * owner, 2)], self.n3.at[d - 1], self.s_send.at[14 + d],
                             self.s_recv.at[7], self.device(self.x, self.y, 4 * self.far + owner, self.core)))

    def near_add(self):
        self.received(self.n3, self.s_recv.at[7])
        total = self.a3[pl.ds(2 * self.near, 2)].astype(F32)
        for e in range(3):
            total = total + self.n3[e].astype(F32)
        self.f3[self.far] = total.astype(BF)

        @pl.when(self.near < self.total // 2)
        def _():
            for copy in self.far_copies():
                copy.start()

    def far_copies(self):
        return [
            remote(self.f3.at[self.far], self.f3.at[self.far], self.s_send.at[17 + d], self.s_recv.at[8],
                   self.device(self.x, self.y, 4 * lax.rem(self.far + d, 4) + self.near, self.core))
            for d in (2, 1, 3)
        ]

    def unit_at(self, u):
        ma, mb = self.m
        first = (self.x * 4 + self.y) * ma + u
        second = self.start[1] + (self.y * 4 + self.x) * mb + u - ma
        return jnp.where(u < ma, first, second)

    def near_copies(self):
        copies = []
        for d in (2, 1, 3):
            for q in range(2):
                at = self.unit_at(2 * self.near + q)
                copies.append(remote(
                    self.out.at[self.core, at], self.out.at[self.core, at], self.g_send.at[19 + 2 * d + q - 1],
                    self.g_recv.at[19 + d], self.device(self.x, self.y, 4 * self.far + lax.rem(self.near + d, 4), self.core)
                ))
        return copies

    def far_add(self):
        @pl.when(self.near < self.total // 2)
        def _():
            self.received(self.f3.at[0:3], self.s_recv.at[8])
            total = self.f3[0].astype(F32)
            for e in range(1, 4):
                total = total + self.f3[e].astype(F32)
            total = total.astype(BF)
            for q in range(2):
                self.out[self.core, self.unit_at(2 * self.near + q)] = total[q]
            for copy in self.near_copies():
                copy.start()

    def gather_second(self):
        for d in (1, 3, 2):
            owner = lax.rem(self.near + 4 - d, 4)

            @pl.when(owner < self.total // 2)
            def _():
                self.received(self.f3.at[0], self.g_recv.at[19 + d])

        for part in range(2):
            m = self.m[part]
            ca, cb = self.coords(part)
            at = pl.ds(self.start[part] + (ca * 4 + cb) * m, m)
            for d in (2, 1, 3):
                self.send(remote(self.out.at[self.core, at], self.out.at[self.core, at], self.g_send.at[part * 3 + d - 1],
                                 self.g_recv.at[part], self.peer(self.axes(part)[1], d)))

    def gather_first(self):
        for part in range(2):
            m = self.m[part]
            ca = self.coords(part)[0]
            self.received(self.r2[part], self.g_recv.at[part])
            at = pl.ds(self.start[part] + ca * 4 * m, 4 * m)
            for d in (2, 1, 3):
                k = 6 + part * 3 + d - 1
                self.send(remote(self.out.at[self.core, at], self.out.at[self.core, at], self.g_send.at[k],
                                 self.g_recv.at[k], self.peer(self.axes(part)[0], d)))
            self.to_core(part, 0, at)

    def to_core(self, part, d, at):
        k = 12 + part * 4 + d
        self.send(remote(self.out.at[self.core, at], self.out.at[self.core, at], self.g_send.at[k],
                         self.g_recv.at[k], self.other_core()))

    def block_of(self, part, d):
        n = 4 * self.m[part]
        return pl.ds(self.start[part] + lax.rem(self.coords(part)[0] + 4 - d, 4) * n, n)

    def gather_core(self):
        for d in (1, 3, 2):
            for part in range(2):
                at = self.block_of(part, d)
                self.received(self.out.at[self.core, at], self.g_recv.at[6 + part * 3 + d - 1])
                self.to_core(part, d, at)

    def gather_done(self):
        for d in (0, 1, 3, 2):
            for part in range(2):
                at = self.block_of(part, d)
                self.received(self.out.at[1 - self.core, at], self.g_recv.at[12 + part * 4 + d])
                yield part, at.start


def reduce_scratch(ma, mb):
    units = 16 * (ma + mb)
    return [
        pltpu.VMEM((2, units, 16, 128), BF),
        pltpu.VMEM((units, 16, 128), BF),
        pltpu.VMEM((units, 16, 128), BF),
        pltpu.VMEM((3, 4 * ma, 16, 128), BF),
        pltpu.VMEM((3, 4 * mb, 16, 128), BF),
        pltpu.VMEM((4 * ma, 16, 128), BF),
        pltpu.VMEM((4 * mb, 16, 128), BF),
        pltpu.VMEM((3, ma, 16, 128), BF),
        pltpu.VMEM((3, mb, 16, 128), BF),
        pltpu.VMEM((8, 16, 128), BF),
        pltpu.VMEM((3, 2, 16, 128), BF),
        pltpu.VMEM((4, 2, 16, 128), BF),
        pltpu.SemaphoreType.DMA((21,)),
        pltpu.SemaphoreType.DMA((21,)),
        pltpu.SemaphoreType.DMA((27,)),
        pltpu.SemaphoreType.DMA((23,)),
    ]


N_REDUCE = 16
MA, MB = (4, 4), (3, 3)
A_UNITS, B_UNITS, FIRST_UNITS, LAST_UNITS = 128, 96, 72, 16


def edge_scratch(channels):
    return [
        pltpu.VMEM((80, channels), BF),
        pltpu.VMEM((256, channels), BF),
        pltpu.SemaphoreType.DMA((8,)),
        pltpu.SemaphoreType.DMA((8,)),
    ]


def patch_scratch():
    return [
        pltpu.VMEM((32, 9 * C1), BF),
        pltpu.VMEM((2, 32, 3 * C1), BF),
        pltpu.VMEM((4, 16, C1), BF),
        pltpu.VMEM((128, 9 * C1), BF),
        pltpu.VMEM((2, 32, 3 * C1), BF),
        pltpu.VMEM((4, 16, C1), BF),
        pltpu.SemaphoreType.DMA((8,)),
        pltpu.SemaphoreType.DMA((8,)),
    ]


def layer_scratch(channels):
    return [
        pltpu.VMEM((304, channels), F32),
        pltpu.VMEM((384, 3 * channels), BF),
        pltpu.VMEM((416, C2), BF),
        pltpu.VMEM((304, 3 * channels), F32),
        pltpu.VMEM((384, channels), BF),
        pltpu.VMEM((128, channels), BF),
        pltpu.VMEM((128, channels), BF),
        pltpu.SemaphoreType.DMA((8,)),
        pltpu.SemaphoreType.DMA((8,)),
    ]


N_EDGE, N_PATCH, N_LAYER = 4, 8, 9


def step_kernel(*refs):
    (feat_hbm, w1_hbm, w2_hbm, cot_hbm, pick_hbm, flip_hbm, rule_hbm,
     pooled_ref, grad_ref, first_out, second_out, square_ref) = refs[:12]
    refs = refs[12:]
    edges, refs = refs[:N_EDGE], refs[N_EDGE:]
    patch_refs, refs = refs[:N_PATCH], refs[N_PATCH:]
    layer1, refs = refs[:N_LAYER], refs[N_LAYER:]
    layer2, refs = refs[:N_LAYER], refs[N_LAYER:]
    red2_refs, refs = refs[:N_REDUCE], refs[N_REDUCE:]
    red1_refs, refs = refs[:N_REDUCE], refs[N_REDUCE:]
    (feat_ref, w1, w2, cot_ref, pick_ref, flip_ref, rule_ref, load_sem,
     rules_out, rules_in, rule_send, rule_recv, q_fwd, q_back, q_act, slope1, pre2,
     windows) = refs
    red2_refs = red2_refs[:12] + (second_out,) + red2_refs[12:]
    red1_refs = red1_refs[:12] + (first_out,) + red1_refs[12:]

    lon, lat = lax.axis_index("lon"), lax.axis_index("lat")
    y = lax.div(lon, 2 * NZ)
    z = lax.div(lax.rem(lon, 2 * NZ), 2)
    x = lax.rem(lon, 2) * 2 + lax.div(lat, 2)
    core = lax.rem(lat, 2)

    def device(x_at, y_at, z_at, core_at):
        return (y_at * (2 * NZ) + z_at * 2 + lax.div(x_at, 2), lax.rem(x_at, 2) * 2 + core_at)

    across = lax.rem(lon + LON // 2, LON)
    below, above = lat == 0, lat == LAT - 1
    vert = (
        (jnp.where(below, across, lon), jnp.where(below, lat, lat - 1)),
        (jnp.where(above, across, lon), jnp.where(above, lat, lat + 1)),
    )
    seen = (jnp.where(below, 0, 1), jnp.where(above, 1, 0))

    def west_of(at):
        return (lax.rem(at[0] + LON - 1, LON), at[1])

    def east_of(at):
        return (lax.rem(at[0] + 1, LON), at[1])

    here = (lon, lat)
    west, east = west_of(here), east_of(here)
    diagonal = [
        (west_of(vert[0]), 2 * seen[0] + 1),
        (east_of(vert[0]), 2 * seen[0]),
        (west_of(vert[1]), 2 * seen[1] + 1),
        (east_of(vert[1]), 2 * seen[1]),
    ]

    barrier = pltpu.get_barrier_semaphore()
    partners = [device(x, y, lax.rem(z + 4 * d, NZ), core) for d in (2, 1, 3)]
    partners += [d[0] for d in diagonal] + [west, east, vert[0], vert[1]]
    for d in (2, 1, 3):
        partners.append(device(x, y, 4 * lax.div(z, 4) + lax.rem(z + d, 4), core))
        partners.append(device(lax.rem(x + d, NX), y, z, core))
        partners.append(device(x, lax.rem(y + d, NY), z, core))
    partners.append(device(x, y, z, 1 - core))
    for partner in partners:
        pl.semaphore_signal(barrier, inc=1, device_id=partner, device_id_type=MESH)

    loads = [
        pltpu.make_async_copy(src, dst, load_sem.at[n])
        for n, (src, dst) in enumerate((
            (pick_hbm, pick_ref), (flip_hbm, flip_ref), (rule_hbm, rule_ref), (feat_hbm, feat_ref),
            (w1_hbm, w1), (cot_hbm, cot_ref), (w2_hbm, w2),
        ))
    ]
    for load in loads:
        load.start()

    for load in loads[:3]:
        load.wait()
    picks = [pick_ref[0, 0, s] for s in range(2)]
    flips = [flip_ref[0, 0, s] for s in range(2)]
    rules = [rule_ref[0, 0, k] for k in range(4)]

    row8 = iota((8, 128), 0)
    rules_out[...] = jnp.where(
        row8 == 0, picks[0], jnp.where(row8 == 1, flips[0], jnp.where(row8 == 2, picks[1], flips[1]))
    )

    p, cell = iota((80, 256), 0), iota((80, 256), 1)
    k = p & 15
    want = jnp.where(
        p < 16, k, jnp.where(p < 32, 240 + k, jnp.where(p < 48, 16 * k, jnp.where(p < 64, 16 * k + 15, (
            jnp.where(k == 0, 0, jnp.where(k == 1, 15, jnp.where(k == 2, 240, jnp.where(k == 3, 255, -1))))
        ))))
    )
    take_edges = hot(cell == want).astype(BF)

    loads[3].wait()
    edges[0][...] = mm(take_edges, feat_ref[...]).astype(BF)
    edges[1][224:256, :] = jnp.zeros((32, C1), BF)
    layer1[1][288:384, :] = jnp.zeros((96, 3 * C1), BF)

    pl.semaphore_wait(barrier, len(partners))

    def edge_sends():
        out, got, send, recv = edges
        copies = []
        for i, (target, slot) in enumerate(diagonal):
            copies.append(remote(out.at[64:80], got.at[pl.ds(pl.multiple_of(160 + 16 * slot, 16), 16)],
                                 send.at[4 + i], recv.at[4 + slot], target))
        for side in range(2):
            copies.append(remote(out.at[0:64], got.at[pl.ds(pl.multiple_of(64 * seen[side], 64), 64)],
                                 send.at[side], recv.at[seen[side]], vert[side]))
        copies.append(remote(out.at[32:48], got.at[144:160], send.at[2], recv.at[3], west))
        copies.append(remote(out.at[48:64], got.at[128:144], send.at[3], recv.at[2], east))
        for copy in copies:
            copy.start()
        return copies

    def edge_waits():
        out, got, send, recv = edges
        spots = [(0, 64), (64, 64), (128, 16), (144, 16), (160, 16), (176, 16), (192, 16), (208, 16)]
        for i, (at, size) in enumerate(spots):
            remote(out.at[0:size], got.at[at:at + size], send.at[i], recv.at[i], west).wait_recv()

    sent = edge_sends()
    rule_copies = []
    for i, (target, slot) in enumerate(((vert[0], seen[0]), (vert[1], seen[1]), (west, 3), (east, 2))):
        rule_copies.append(remote(rules_out, rules_in.at[slot], rule_send.at[i], rule_recv.at[slot], target))
    for copy in rule_copies:
        copy.start()

    r, c = iota((288, 256), 0), iota((288, 256), 1)
    j, i = r & 15, r >> 4
    want = jnp.where(j == 0, 127 + i, jnp.where(j == 15, 143 + i, -1))
    q_fwd[0:288, :] = hot(c == want).astype(BF)
    r, c = iota((32, 256), 0), iota((32, 256), 1)
    k, north = r & 15, r >= 16
    flip = jnp.where(north, flips[1], flips[0])
    pick = jnp.where(north, picks[1], picks[0])
    want = jnp.where(north, 64, 0) + 16 * pick + jnp.where(flip == 1, 15 - k, k)
    q_fwd[288:320, :] = hot(c == want).astype(BF)

    def halo_cells(p, q):
        block, k = p >> 4, p & 15
        low, high = k == 0, k == 15
        corner_at = (0, 15, 272, 287)
        want = jnp.where(block == 0, 288 + k, jnp.where(block == 1, 304 + k, jnp.where(
            block == 2, 16 * k + 16, jnp.where(block == 3, 16 * k + 31, -1))))
        half = jnp.full_like(want, -1)
        ends = ((0, 1), (2, 3), (0, 2), (1, 3))
        for b in range(4):
            first, second = ends[b]
            half = jnp.where((block == b) & low & (rules[first] == 1), corner_at[first], half)
            half = jnp.where((block == b) & high & (rules[second] == 1), corner_at[second], half)
            want = jnp.where((block == 4 + b) & low & (rules[b] != 1), corner_at[b], want)
        return (hot(q == want) + hot(q == half, 0.5)).astype(BF)

    q_back[...] = halo_cells(iota((128, 384), 0), iota((128, 384), 1))
    q_act[...] = halo_cells(iota((320, 128), 1), iota((320, 128), 0))

    for layer in (layer1, layer2):
        g_pad = layer[2]
        g_pad[0:32, :] = jnp.zeros((32, C2), BF)
        g_pad[288:416, :] = jnp.zeros((128, C2), BF)
        layer[4][320:384, :] = jnp.zeros((64, layer[4].shape[1]), BF)

    red2 = Reduce(MA, red2_refs, (x, y, z, core, device))
    red1 = Reduce(MB, red1_refs, (x, y, z, core, device))
    used = FIRST_UNITS + LAST_UNITS
    red1.halves[:, used:B_UNITS] = jnp.zeros((2, B_UNITS - used, 16, 128), BF)
    red1.a3[6:8] = jnp.zeros((2, 16, 128), BF)

    for slot in range(4):
        remote(rules_out, rules_in.at[slot], rule_send.at[slot], rule_recv.at[slot], west).wait_recv()

    r, c = iota((16, 256), 0), iota((16, 256), 1)
    for side in range(2):
        def source(position):
            return 64 * side + 16 * picks[side] + jnp.where(flips[side] == 1, 15 - position, position)

        rows = 2 * side
        w_pick, w_flip = wide(rules_in[2, rows:rows + 1, :], 2), wide(rules_in[2, rows + 1:rows + 2, :], 2)
        e_pick, e_flip = wide(rules_in[3, rows:rows + 1, :], 2), wide(rules_in[3, rows + 1:rows + 2, :], 2)
        w_at = 160 + 32 * side + corner_slot(w_pick, jnp.where(w_flip == 1, 0, 1))
        e_at = 176 + 32 * side + corner_slot(e_pick, jnp.where(e_flip == 1, 1, 0))
        w_rule, e_rule = rules[2 * side] == 1, rules[2 * side + 1] == 1
        shape = (16, 256)
        w_main = jnp.where(w_rule, jnp.full(shape, -1), jnp.broadcast_to(w_at, shape))
        e_main = jnp.where(e_rule, jnp.full(shape, -1), jnp.broadcast_to(e_at, shape))
        w_a, w_c = jnp.where(w_rule, source(0), -1), jnp.where(w_rule, 128 + 15 * side, -1)
        e_a, e_c = jnp.where(e_rule, source(15), -1), jnp.where(e_rule, 144 + 15 * side, -1)
        w_row = hot(c == w_main) + hot(c == w_a, 0.5) + hot(c == w_c, 0.5)
        e_row = hot(c == e_main) + hot(c == e_a, 0.5) + hot(c == e_c, 0.5)
        values = jnp.where(r == 0, w_row, jnp.where(r == 15, e_row, 0.0))
        q_fwd[272 * side:272 * side + 16, :] = values.astype(BF)

    face = (jnp.where(below, 0, 1), jnp.where(above, 1, 0))
    facing = []
    for side in range(2):
        south = face[side] == 0
        facing.append((
            jnp.where(south, rules_in[side, 0:1, 0:128], rules_in[side, 2:3, 0:128]),
            jnp.where(south, rules_in[side, 1:2, 0:128], rules_in[side, 3:4, 0:128]),
        ))
    p = iota((1, 128), 1)
    block, k = p >> 4, p & 15
    on_north = (block == 1) | (block >= 6)
    pick = jnp.where(on_north, facing[1][0], facing[0][0])
    flip = jnp.where(on_north, facing[1][1], facing[0][1])
    position = jnp.where(block < 2, k, jnp.where((block & 1) == 1, 15, 0))
    target = edge_cell(pick, flip, position)
    target = jnp.where(block == 2, 16 * k + 15, jnp.where(block == 3, 16 * k, target))
    target = jnp.where((block >= 4) & (k != 0), -1, target)
    place_grads = hot(iota((256, 128), 0) == target).astype(BF)

    r, c = iota((32, 256), 0), iota((32, 256), 1)
    pick = jnp.where(r < 16, wide(facing[0][0], 2), wide(facing[1][0], 2))
    flip = jnp.where(r < 16, wide(facing[0][1], 2), wide(facing[1][1], 2))
    take_cells = hot(c == edge_cell(pick, flip, r & 15)).astype(BF)
    r, c = iota((64, 384), 0), iota((64, 384), 1)
    row = r & 31
    take_strips = hot((row < 18) & (c == 16 * row + jnp.where(r < 32, 15, 0))).astype(BF)
    tap, which = r & 15, r >> 4
    tap_row = (tap * 11) >> 5
    pick = jnp.where(which < 2, wide(facing[0][0], 3), wide(facing[1][0], 3))
    flip = jnp.where(which < 2, wide(facing[0][1], 3), wide(facing[1][1], 3))
    at = 16 * tap_row + edge_cell(pick, flip, jnp.where((which & 1) == 1, 15, 0))
    take_corners = [
        hot((tap < 9) & (tap - 3 * tap_row == dw) & (c == at)).astype(BF) for dw in range(3)
    ]

    def patch_sends():
        cells, strips, corners, got_cells, got_strips, got_corners, send, recv = patch_refs
        padded = layer1[1]
        values = mm(take_corners[0], padded[:, 0:C1])
        for dw in (1, 2):
            values = values + mm(take_corners[dw], padded[:, dw * C1:(dw + 1) * C1])
        corners[...] = values.astype(BF).reshape(4, 16, C1)
        copies = []
        for i, (target_at, slot) in enumerate(diagonal):
            copies.append(remote(corners.at[i], got_corners.at[slot], send.at[4 + i], recv.at[4 + slot], target_at))
            copies[-1].start()
        strips[...] = mm(take_strips, padded[...]).astype(BF).reshape(2, 32, 3 * C1)
        copies.append(remote(strips.at[0], got_strips.at[0], send.at[2], recv.at[2], east))
        copies.append(remote(strips.at[1], got_strips.at[1], send.at[3], recv.at[3], west))
        for copy in copies[-2:]:
            copy.start()
        for dh in range(3):
            cells[:, 384 * dh:384 * dh + 384] = mm(take_cells, padded[16 * dh:16 * dh + 256, :]).astype(BF)
        for side in range(2):
            copies.append(remote(cells.at[16 * side:16 * side + 16],
                                 got_cells.at[pl.ds(pl.multiple_of(16 * seen[side], 16), 16)],
                                 send.at[side], recv.at[seen[side]], vert[side]))
            copies[-1].start()
        return copies

    def patch_waits():
        cells, strips, corners, got_cells, got_strips, got_corners, send, recv = patch_refs
        for i in range(2):
            remote(cells.at[0:16], got_cells.at[16 * i:16 * i + 16], send.at[i], recv.at[i], west).wait_recv()
            remote(strips.at[i], got_strips.at[i], send.at[2 + i], recv.at[2 + i], west).wait_recv()
        r, c = iota((32, 64), 0), iota((32, 64), 1)
        both = got_strips[...].reshape(64, 3 * C1)
        for dh in range(3):
            spread_rows = hot(c == jnp.where(r < 16, r, r + 16) + dh).astype(BF)
            got_cells[32:64, 384 * dh:384 * dh + 384] = mm(spread_rows, both).astype(BF)
        for i in range(4):
            remote(corners.at[i], got_corners.at[i], send.at[4 + i], recv.at[4 + i], west).wait_recv()
        r, c = iota((64, 64), 0), iota((64, 64), 1)
        taps = got_corners[...].reshape(64, C1)
        for tap in range(9):
            first_row = hot(((r & 15) == 0) & (c == r + tap)).astype(BF)
            got_cells[64:128, C1 * tap:C1 * tap + C1] = mm(first_row, taps).astype(BF)

    def pad_tile(layer, tile, cells, channels):
        ext, padded = layer[:2]
        south, north = cells[288:304], cells[304:320]
        ext[8:24, :] = south
        ext[24:280, :] = tile.astype(F32)
        ext[280:296, :] = north
        j = iota((288, channels), 0) & 15
        padded[0:288, 0:channels] = jnp.where(j == 0, cells[0:288], ext[7:295, :]).astype(BF)
        padded[0:288, channels:2 * channels] = ext[8:296, :].astype(BF)
        padded[0:288, 2 * channels:] = jnp.where(j == 15, cells[0:288], ext[9:297, :]).astype(BF)

    def convolve(layer, weight):
        padded = layer[1]
        total = mm(padded[0:256, :], weight[0])
        for dh in (1, 2):
            total = total + mm(padded[16 * dh:16 * dh + 256, :], weight[dh])
        return total

    def input_side(layer, weight, channels):
        g_pad, by_shift, leaving, out = layer[2:6]
        total = mm_nt(g_pad[32:320, :], weight[0])
        for dh in (1, 2):
            at = 32 - 16 * dh
            total = total + mm_nt(g_pad[at:at + 288, :], weight[dh])
        by_shift[8:296, :] = total
        j = iota((288, channels), 0) & 15
        centre = by_shift[8:296, channels:2 * channels]
        centre = centre + jnp.where(j == 15, 0.0, by_shift[9:297, 0:channels])
        centre = centre + jnp.where(j == 0, 0.0, by_shift[7:295, 2 * channels:])
        centre = centre.astype(BF)
        sides = jnp.where(j == 0, by_shift[8:296, 0:channels], by_shift[8:296, 2 * channels:])
        sides = jnp.where((j == 0) | (j == 15), sides, 0.0)
        leaving[0:288, :] = sides.astype(BF)
        leaving[288:304, :] = centre[0:16]
        leaving[304:320, :] = centre[272:288]
        out[...] = mm(q_back[...], leaving[...]).astype(BF)
        return centre[16:272]

    def grad_sends(layer):
        out, got, send, recv = layer[5:9]
        copies = []
        for side in range(2):
            copies.append(remote(out.at[16 * side:16 * side + 16],
                                 got.at[pl.ds(pl.multiple_of(16 * seen[side], 16), 16)],
                                 send.at[side], recv.at[seen[side]], vert[side]))
        copies.append(remote(out.at[32:48], got.at[32:48], send.at[2], recv.at[2], west))
        copies.append(remote(out.at[48:64], got.at[48:64], send.at[3], recv.at[3], east))
        for i, (target_at, slot) in enumerate(diagonal):
            copies.append(remote(out.at[64 + 16 * i:80 + 16 * i],
                                 got.at[pl.ds(pl.multiple_of(64 + 16 * slot, 16), 16)],
                                 send.at[4 + i], recv.at[4 + slot], target_at))
        for copy in copies:
            copy.start()
        return copies

    def grad_waits(layer):
        out, got, send, recv = layer[5:9]
        for i in range(8):
            remote(out.at[0:16], got.at[16 * i:16 * i + 16], send.at[i], recv.at[i], west).wait_recv()

    def weight_grad(block, spots):
        block = block.astype(BF)
        units = block.shape[0] // 16
        for h in range(2):
            values = block[:, 128 * h:128 * h + 128].reshape(units, 16, 128)
            for first, count, red, to in spots:
                red.halves[h, to:to + count] = values[first:first + count]

    edge_waits()
    pad_tile(layer1, feat_ref[...], mm(q_fwd[...], edges[1][...]), C1)
    sent += patch_sends()
    loads[4].wait()
    pre1 = convolve(layer1, w1)
    cdf1 = normal_cdf(pre1)
    act1 = (pre1 * cdf1).astype(BF)
    slope1[...] = gelu_slope(pre1, cdf1)
    for dh in range(3):
        windows[dh] = layer1[1][16 * dh:16 * dh + 256, :].T
    r, c = iota((256, 64), 0), iota((256, 64), 1)
    spread = hot(c == 8 * (r >> 5) + ((r & 15) >> 1), 0.25).astype(BF)
    loads[5].wait()
    cot = mm(spread, cot_ref[...])
    loads[6].wait()

    patch_waits()
    patches = patch_refs[3]
    halo_pre = mm(patches[:, 0:384], w1[0])
    for dh in (1, 2):
        halo_pre = halo_pre + mm(patches[:, 384 * dh:384 * dh + 384], w1[dh])
    halo_cdf = normal_cdf(halo_pre)
    halo_act = (halo_pre * halo_cdf).astype(BF)
    pad_tile(layer2, act1, mm(q_act[...], halo_act), C2)
    second_pre = convolve(layer2, w2)
    cdf2 = normal_cdf(second_pre)
    grad2 = (cot * gelu_slope(second_pre, cdf2)).astype(BF)
    layer2[2][32:288, :] = grad2
    for dh in range(3):
        spots = [(0, 48, red2, 48 * dh)] if dh < 2 else [(0, 32, red2, 96), (32, 16, red1, FIRST_UNITS)]
        weight_grad(mm_tn(layer2[1][16 * dh:16 * dh + 256, :], grad2), spots)
        red2.core_send(48 * dh, spots[0][1])
    centre2 = input_side(layer2, w2, C2)
    sent += grad_sends(layer2)

    own = (centre2.astype(F32) * slope1[...]).astype(BF)
    leaving = (layer2[5][...].astype(F32) * gelu_slope(halo_pre, halo_cdf)).astype(BF)
    for dh in range(3):
        block = mm(windows[dh], own) + mm_tn(patches[:, 384 * dh:384 * dh + 384], leaving)
        weight_grad(block, [(0, 24, red1, 24 * dh)])
    red1.core_send(0, B_UNITS)
    red2.core_add()
    red1.core_add()
    pre2[...] = second_pre * cdf2

    r, c = iota((64, 256), 0), iota((64, 256), 1)
    gather_cells = hot(r == 8 * (c >> 5) + ((c & 15) >> 1), 0.25).astype(BF)
    act2 = pre2[...]
    high = act2.astype(BF)
    low = (act2 - high.astype(F32)).astype(BF)
    pooled_ref[...] = (mm(gather_cells, high) + mm(gather_cells, low)).astype(BF)

    red2.first_add()
    red1.first_add()

    grad_waits(layer2)
    first_grad = centre2.astype(F32) + mm(place_grads, layer2[6][...])
    layer1[2][32:288, :] = (first_grad * slope1[...]).astype(BF)
    centre1 = input_side(layer1, w1, C1)
    sent += grad_sends(layer1)

    red2.second_add()
    red1.second_add()
    red2.near_add()
    red1.near_add()

    grad_waits(layer1)
    grad_ref[...] = (centre1.astype(F32) + mm(place_grads, layer1[6][...])).astype(BF)

    for copy in sent + rule_copies:
        copy.wait_send()
    red2.flush()
    red1.flush()
    red2.far_add()
    red1.far_add()
    red2.gather_second()
    red1.gather_second()
    for red in (red2, red1):
        red.far_flush()
        red.near_flush()
    red2.gather_first()
    red1.gather_first()
    red2.gather_core()
    red1.gather_core()
    list(red2.gather_done())
    red2.flush()
    squares = jnp.zeros((16, 128), F32)
    for h in range(2):
        squares = sum_squares(second_out, h, 0, A_UNITS // 4, squares)
    squares = sum_squares(first_out, core, 0, B_UNITS // 4, squares)
    for part, at in red1.gather_done():
        squares = sum_squares(first_out, 1 - core, at, red1.m[part], squares)
    square_ref[...] = squares
    red1.flush()


def sum_squares(ref, half, at, steps, total):
    def body(i, total):
        values = ref[half, pl.ds(at + i * 4, 4)].astype(F32)
        return total + jnp.sum(values * values, axis=0)

    return lax.fori_loop(0, steps, body, total)


def finish_kernel(pooled_ref, grad_ref, first_ref, second_ref, square_ref, pooled_out, grad_out, first_out, second_out,
                  first_rows, second_rows, sems):
    copies = [pltpu.make_async_copy(pooled_ref, pooled_out, sems.at[0]),
              pltpu.make_async_copy(grad_ref, grad_out, sems.at[1])]
    for copy in copies:
        copy.start()

    squared = jnp.sum(jnp.sum(square_ref[...], axis=0, keepdims=True), axis=1, keepdims=True)
    target_norm = math.sqrt(9.0 * (C1 + C2) * C2)
    scale = jnp.broadcast_to(target_norm / jnp.sqrt(squared + 1e-06), (16, 128))

    def write(ref, at, to, count, out):
        def body(i, carry):
            for h in range(2):
                values = ref[h, pl.ds(at + i * 8, 8)].astype(F32) * scale
                rows = pl.ds(pl.multiple_of((to + i * 8) * 16, 128), 128)
                out[rows, 128 * h:128 * h + 128] = values.astype(BF).reshape(128, 128)
            return carry

        lax.fori_loop(0, count // 8, body, 0)

    jobs = [(second_ref, n * 64, n * 64, 64, second_rows, second_out) for n in range(2)]
    jobs.append((first_ref, 0, 0, FIRST_UNITS, first_rows, first_out))
    jobs.append((first_ref, FIRST_UNITS, A_UNITS, LAST_UNITS, second_rows, second_out))
    for n, (ref, at, to, count, rows, out) in enumerate(jobs):
        write(ref, at, to, count, rows)
        span = pl.ds(16 * to, 16 * count)
        copies.append(pltpu.make_async_copy(rows.at[span], out.at[span], sems.at[2 + n]))
        copies[-1].start()
    for copy in copies:
        copy.wait()


def on_device(features, conv_first, conv_second, cotangent, edge_pick, edge_flip, corner_rule):
    vmem = pl.BlockSpec(memory_space=pltpu.VMEM)
    hbm = pl.BlockSpec(memory_space=pltpu.HBM)
    pooled, input_grad, first, second, square = pl.pallas_call(
        step_kernel,
        out_shape=(
            jax.ShapeDtypeStruct((64, C2), BF),
            jax.ShapeDtypeStruct((256, C1), BF),
            jax.ShapeDtypeStruct((2, B_UNITS, 16, 128), BF),
            jax.ShapeDtypeStruct((2, A_UNITS, 16, 128), BF),
            jax.ShapeDtypeStruct((16, 128), F32),
        ),
        in_specs=[hbm] * 7,
        out_specs=[vmem] * 5,
        scratch_shapes=(
            edge_scratch(C1)
            + patch_scratch()
            + layer_scratch(C1)
            + layer_scratch(C2)
            + reduce_scratch(*MA)
            + reduce_scratch(*MB)
            + [
                pltpu.VMEM((256, C1), BF),
                pltpu.VMEM((3, 3 * C1, C2), BF),
                pltpu.VMEM((3, 3 * C2, C2), BF),
                pltpu.VMEM((64, C2), BF),
                pltpu.SMEM((1, 1, 2), jnp.int32),
                pltpu.SMEM((1, 1, 2), jnp.int32),
                pltpu.SMEM((1, 1, 4), jnp.int32),
                pltpu.SemaphoreType.DMA((7,)),
                pltpu.VMEM((8, 128), jnp.int32),
                pltpu.VMEM((4, 8, 128), jnp.int32),
                pltpu.SemaphoreType.DMA((4,)),
                pltpu.SemaphoreType.DMA((4,)),
                pltpu.VMEM((320, 256), BF),
                pltpu.VMEM((128, 384), BF),
                pltpu.VMEM((320, 128), BF),
                pltpu.VMEM((256, C2), F32),
                pltpu.VMEM((256, C2), F32),
                pltpu.VMEM((3, 3 * C1, 256), BF),
            ]
        ),
        compiler_params=pltpu.CompilerParams(
            collective_id=0, has_side_effects=True, vmem_limit_bytes=32 * 1024 * 1024
        ),
        name="level_step",
    )(*(
        pltpu.with_memory_space_constraint(value, pltpu.HBM)
        for value in (
            features.reshape(256, C1),
            conv_first.reshape(3, 3 * C1, C2),
            conv_second.reshape(3, 3 * C2, C2),
            cotangent.reshape(64, C2),
            edge_pick,
            edge_flip,
            corner_rule,
        )
    ))
    pooled, input_grad, first, second = pl.pallas_call(
        finish_kernel,
        out_shape=(
            jax.ShapeDtypeStruct((64, C2), BF),
            jax.ShapeDtypeStruct((256, C1), BF),
            jax.ShapeDtypeStruct((9 * C1, C2), BF),
            jax.ShapeDtypeStruct((9 * C2, C2), BF),
        ),
        in_specs=[vmem] * 5,
        out_specs=[hbm] * 4,
        scratch_shapes=[
            pltpu.VMEM((9 * C1, C2), BF),
            pltpu.VMEM((9 * C2, C2), BF),
            pltpu.SemaphoreType.DMA((6,)),
        ],
        compiler_params=pltpu.CompilerParams(vmem_limit_bytes=16 * 1024 * 1024),
        name="scale_outputs",
    )(pooled, input_grad, first, second, square)
    return (
        pooled.reshape(1, 1, 8, 8, C2),
        input_grad.reshape(1, 1, 16, 16, C1),
        first.reshape(3, 3, C1, C2),
        second.reshape(3, 3, C2, C2),
    )


def solution(mesh):
    return jax.shard_map(
        on_device,
        mesh=mesh,
        in_specs=(
            P("lon", "lat", None, None, None),
            P(),
            P(),
            P("lon", "lat", None, None, None),
            P("lon", "lat", None),
            P("lon", "lat", None),
            P("lon", "lat", None),
        ),
        out_specs=(P("lon", "lat", None, None, None), P("lon", "lat", None, None, None), P(), P()),
        check_vma=False,
    )
```

```python
import math

import jax
import jax.numpy as jnp
from jax import lax
from jax.experimental import pallas as pl
from jax.experimental.pallas import tpu as pltpu
from jax.sharding import PartitionSpec as P

MESH = pl.DeviceIdType.MESH
BF = jnp.bfloat16
F32 = jnp.float32
NX, NY, NZ = 4, 4, 16
LON, LAT = 2 * NY * NZ, 4
C1, C2 = 128, 256


def normal_cdf(values):
    return 0.5 * (1.0 + lax.erf(values * (1.0 / math.sqrt(2.0))))


def gelu_slope(values, cdf):
    return cdf + values * jnp.exp(-0.5 * values * values) * (1.0 / math.sqrt(2.0 * math.pi))


def iota(shape, dim):
    return lax.broadcasted_iota(jnp.int32, shape, dim)


def hot(cond, value=1.0):
    return jnp.where(cond, jnp.float32(value), jnp.float32(0.0))


def wide(row, count):
    return jnp.concatenate([row] * count, axis=1)


def edge_cell(edge, flip, position):
    at = jnp.where(flip == 1, 15 - position, position)
    return jnp.where(edge == 0, at, jnp.where(edge == 1, 240 + at, jnp.where(edge == 2, 16 * at, 16 * at + 15)))


def mm(a, b):
    return jnp.dot(a, b, preferred_element_type=F32)


def mm_nt(a, b):
    return lax.dot_general(a, b, (((1,), (1,)), ((), ())), preferred_element_type=F32)


def mm_tn(a, b):
    return lax.dot_general(a, b, (((0,), (0,)), ((), ())), preferred_element_type=F32)


def remote(src, dst, send_sem, recv_sem, device):
    return pltpu.make_async_remote_copy(
        src_ref=src, dst_ref=dst, send_sem=send_sem, recv_sem=recv_sem,
        device_id=device, device_id_type=MESH,
    )


def corner_slot(edge, at_end):
    return jnp.where(
        edge == 0, at_end, jnp.where(edge == 1, 2 + at_end, jnp.where(edge == 2, 2 * at_end, 1 + 2 * at_end))
    )


class Reduce:
    def __init__(self, m, refs, place):
        self.m = m
        self.total = m[0] + m[1]
        self.start = (0, 16 * m[0])
        (self.halves, self.r0, self.a1, r1a, r1b, a2a, a2b, r2a, r2b, self.f3, self.out,
         self.s_send, self.s_recv, self.g_send, self.g_recv) = refs
        self.r1, self.a2, self.r2 = (r1a, r1b), (a2a, a2b), (r2a, r2b)
        self.x, self.y, self.z, self.core, self.device = place
        self.near, self.far = lax.rem(self.z, 4), lax.div(self.z, 4)
        self.pending = []
        self.guarded = []
        self.pieces = []
        self.waited = 0

    def other_core(self):
        return self.device(self.x, self.y, self.z, 1 - self.core)

    def peer(self, axis, d):
        x = lax.rem(self.x + d, NX) if axis == "x" else self.x
        y = lax.rem(self.y + d, NY) if axis == "y" else self.y
        return self.device(x, y, self.z, self.core)

    def axes(self, part):
        return ("x", "y") if part == 0 else ("y", "x")

    def coords(self, part):
        return (self.x, self.y) if part == 0 else (self.y, self.x)

    def send(self, copy):
        copy.start()
        self.pending.append(copy)

    def received(self, ref, sem):
        remote(ref, ref, self.s_send.at[0], sem, self.other_core()).wait_recv()

    def flush(self):
        for copy in self.pending:
            copy.wait_send()
        for wanted, copy in self.guarded:
            pl.when(wanted)(copy.wait_send)
        self.pending, self.guarded = [], []

    def send_if(self, wanted, copy):
        pl.when(wanted)(copy.start)
        self.guarded.append((wanted, copy))

    def plane(self, part):
        for db in (2, 1, 3, 0):
            for dz in (2, 3, 1, 0):
                if db or dz:
                    x, y = self.x, self.y
                    if part == 0:
                        y = lax.rem(y + db, 4)
                    else:
                        x = lax.rem(x + db, 4)
                    near = lax.rem(self.near + dz, 4)
                    yield 4 * db + dz - 1, (y if part == 0 else x), near, self.device(x, y, 4 * self.far + near, self.core)

    def core_send(self, at, count):
        k = len(self.pieces)
        self.pieces.append((at, count))
        self.send(remote(self.halves.at[1 - self.core, at:at + count], self.r0.at[at:at + count],
                         self.s_send.at[k], self.s_recv.at[k], self.other_core()))

    def core_add(self):
        for part in range(2):
            n = 4 * self.m[part]
            mine = self.coords(part)[0]
            while self.waited < len(self.pieces) and self.pieces[self.waited][0] < self.start[part] + 4 * n:
                at, count = self.pieces[self.waited]
                self.received(self.r0.at[at:at + count], self.s_recv.at[self.waited])
                self.waited += 1
            k = 3 + part
            for d in (2, 1, 3, 0):
                at = pl.ds(self.start[part] + lax.rem(mine + d, 4) * n, n)
                self.a1[at] = (self.halves[self.core, at].astype(F32) + self.r0[at].astype(F32)).astype(BF)
                if d:
                    self.send(remote(self.a1.at[at], self.r1[part].at[d - 1],
                                     self.s_send.at[3 * k - 7 + d], self.s_recv.at[k],
                                     self.peer(self.axes(part)[0], d)))

    def first_add(self):
        for part in range(2):
            m = self.m[part]
            r1, a2, r2 = self.r1[part], self.a2[part], self.r2[part]
            ca = self.coords(part)[0]
            self.received(r1, self.s_recv.at[3 + part])
            total = self.a1[pl.ds(self.start[part] + ca * 4 * m, 4 * m)].astype(F32)
            for e in range(3):
                total = total + r1[e].astype(F32)
            a2[...] = total.astype(BF)
            for slot, b_at, near, target in self.plane(part):
                self.send_if(near < m, remote(
                    a2.at[b_at * m + lax.rem(near, m)], r2.at[slot], self.s_send.at[9 + 15 * part + slot],
                    self.s_recv.at[5 + part], target))

    def second_add(self):
        for part in range(2):
            m = self.m[part]
            cb = self.coords(part)[1]

            @pl.when(self.near < m)
            def _():
                self.received(self.r2[part], self.s_recv.at[5 + part])
                total = self.a2[part][cb * m + lax.rem(self.near, m)].astype(F32)
                for e in range(15):
                    total = total + self.r2[part][e].astype(F32)
                self.f3[self.far, part] = total.astype(BF)

        for d in (2, 1, 3):
            self.send(remote(self.f3.at[self.far], self.f3.at[self.far], self.s_send.at[39 + d - 1], self.s_recv.at[8],
                             self.device(self.x, self.y, 4 * lax.rem(self.far + d, 4) + self.near, self.core)))

    def far_add(self):
        self.received(self.f3.at[0:3], self.s_recv.at[8])
        for part in range(2):
            m = self.m[part]
            ca, cb = self.coords(part)
            total = self.f3[0, part].astype(F32)
            for e in range(1, 4):
                total = total + self.f3[e, part].astype(F32)
            at = self.start[part] + (ca * 4 + cb) * m + lax.rem(self.near, m)

            @pl.when(self.near < m)
            def _():
                self.out[self.core, at] = total.astype(BF)

            for slot, _, _, target in self.plane(part):
                self.send_if(self.near < m, remote(
                    self.out.at[self.core, at], self.out.at[self.core, at], self.g_send.at[15 * part + slot],
                    self.g_recv.at[part], target))

    def gather_second(self):
        for part in range(2):
            m = self.m[part]
            ca = self.coords(part)[0]
            owns = self.near < m

            @pl.when(owns)
            def _():
                self.received(self.a1.at[0:4 * m - 1], self.g_recv.at[part])

            @pl.when(jnp.logical_not(owns))
            def _():
                self.received(self.a1.at[0:4 * m], self.g_recv.at[part])

            at = pl.ds(self.start[part] + ca * 4 * m, 4 * m)
            for d in (2, 1, 3):
                k = part * 3 + d - 1
                self.send(remote(self.out.at[self.core, at], self.out.at[self.core, at], self.g_send.at[30 + k],
                                 self.g_recv.at[6 + k], self.peer(self.axes(part)[0], d)))
            self.to_core(part, 0, at)

    def to_core(self, part, d, at):
        k = 12 + part * 4 + d
        self.send(remote(self.out.at[self.core, at], self.out.at[self.core, at], self.g_send.at[24 + k],
                         self.g_recv.at[k], self.other_core()))

    def block_of(self, part, d):
        n = 4 * self.m[part]
        return pl.ds(self.start[part] + lax.rem(self.coords(part)[0] + 4 - d, 4) * n, n)

    def gather_core(self):
        for d in (1, 3, 2):
            for part in range(2):
                at = self.block_of(part, d)
                self.received(self.out.at[self.core, at], self.g_recv.at[6 + part * 3 + d - 1])
                self.to_core(part, d, at)

    def gather_done(self):
        for d in (0, 1, 3, 2):
            for part in range(2):
                at = self.block_of(part, d)
                self.received(self.out.at[1 - self.core, at], self.g_recv.at[12 + part * 4 + d])
                yield part, at.start


def reduce_scratch(ma, mb):
    units = 16 * (ma + mb)
    return [
        pltpu.VMEM((2, units, 16, 128), BF),
        pltpu.VMEM((units, 16, 128), BF),
        pltpu.VMEM((units, 16, 128), BF),
        pltpu.VMEM((3, 4 * ma, 16, 128), BF),
        pltpu.VMEM((3, 4 * mb, 16, 128), BF),
        pltpu.VMEM((4 * ma, 16, 128), BF),
        pltpu.VMEM((4 * mb, 16, 128), BF),
        pltpu.VMEM((15, 16, 128), BF),
        pltpu.VMEM((15, 16, 128), BF),
        pltpu.VMEM((4, 2, 16, 128), BF),
        pltpu.SemaphoreType.DMA((42,)),
        pltpu.SemaphoreType.DMA((9,)),
        pltpu.SemaphoreType.DMA((44,)),
        pltpu.SemaphoreType.DMA((20,)),
    ]


N_REDUCE = 14
MA, MB = (4, 4), (4, 2)
A_UNITS, B_UNITS, FIRST_UNITS, LAST_UNITS = 128, 96, 72, 16


def edge_scratch(channels):
    return [
        pltpu.VMEM((80, channels), BF),
        pltpu.VMEM((256, channels), BF),
        pltpu.SemaphoreType.DMA((8,)),
        pltpu.SemaphoreType.DMA((8,)),
    ]


def patch_scratch():
    return [
        pltpu.VMEM((32, 9 * C1), BF),
        pltpu.VMEM((2, 32, 3 * C1), BF),
        pltpu.VMEM((4, 16, C1), BF),
        pltpu.VMEM((128, 9 * C1), BF),
        pltpu.VMEM((2, 32, 3 * C1), BF),
        pltpu.VMEM((4, 16, C1), BF),
        pltpu.SemaphoreType.DMA((8,)),
        pltpu.SemaphoreType.DMA((8,)),
    ]


def layer_scratch(channels):
    return [
        pltpu.VMEM((304, channels), F32),
        pltpu.VMEM((384, 3 * channels), BF),
        pltpu.VMEM((416, C2), BF),
        pltpu.VMEM((304, 3 * channels), F32),
        pltpu.VMEM((384, channels), BF),
        pltpu.VMEM((128, channels), BF),
        pltpu.VMEM((128, channels), BF),
        pltpu.SemaphoreType.DMA((8,)),
        pltpu.SemaphoreType.DMA((8,)),
    ]


N_EDGE, N_PATCH, N_LAYER = 4, 8, 9


def step_kernel(*refs):
    (feat_hbm, w1_hbm, w2_hbm, cot_hbm, pick_hbm, flip_hbm, rule_hbm,
     pooled_ref, grad_ref, first_out, second_out, square_ref) = refs[:12]
    refs = refs[12:]
    edges, refs = refs[:N_EDGE], refs[N_EDGE:]
    patch_refs, refs = refs[:N_PATCH], refs[N_PATCH:]
    layer1, refs = refs[:N_LAYER], refs[N_LAYER:]
    layer2, refs = refs[:N_LAYER], refs[N_LAYER:]
    red2_refs, refs = refs[:N_REDUCE], refs[N_REDUCE:]
    red1_refs, refs = refs[:N_REDUCE], refs[N_REDUCE:]
    (feat_ref, w1, w2, cot_ref, pick_ref, flip_ref, rule_ref, load_sem,
     rules_out, rules_in, rule_send, rule_recv, q_fwd, q_back, q_act, slope1, pre2,
     windows) = refs
    red2_refs = red2_refs[:10] + (second_out,) + red2_refs[10:]
    red1_refs = red1_refs[:10] + (first_out,) + red1_refs[10:]

    lon, lat = lax.axis_index("lon"), lax.axis_index("lat")
    y = lax.div(lon, 2 * NZ)
    z = lax.div(lax.rem(lon, 2 * NZ), 2)
    x = lax.rem(lon, 2) * 2 + lax.div(lat, 2)
    core = lax.rem(lat, 2)

    def device(x_at, y_at, z_at, core_at):
        return (y_at * (2 * NZ) + z_at * 2 + lax.div(x_at, 2), lax.rem(x_at, 2) * 2 + core_at)

    across = lax.rem(lon + LON // 2, LON)
    below, above = lat == 0, lat == LAT - 1
    vert = (
        (jnp.where(below, across, lon), jnp.where(below, lat, lat - 1)),
        (jnp.where(above, across, lon), jnp.where(above, lat, lat + 1)),
    )
    seen = (jnp.where(below, 0, 1), jnp.where(above, 1, 0))

    def west_of(at):
        return (lax.rem(at[0] + LON - 1, LON), at[1])

    def east_of(at):
        return (lax.rem(at[0] + 1, LON), at[1])

    here = (lon, lat)
    west, east = west_of(here), east_of(here)
    diagonal = [
        (west_of(vert[0]), 2 * seen[0] + 1),
        (east_of(vert[0]), 2 * seen[0]),
        (west_of(vert[1]), 2 * seen[1] + 1),
        (east_of(vert[1]), 2 * seen[1]),
    ]

    barrier = pltpu.get_barrier_semaphore()
    partners = [device(x, y, lax.rem(z + 4 * d, NZ), core) for d in (2, 1, 3)]
    partners += [d[0] for d in diagonal] + [west, east, vert[0], vert[1]]
    for d in (2, 1, 3):
        for dz in (2, 1, 3, 0):
            z_at = 4 * lax.div(z, 4) + lax.rem(z + dz, 4)
            partners.append(device(lax.rem(x + d, NX), y, z_at, core))
            partners.append(device(x, lax.rem(y + d, NY), z_at, core))
        partners.append(device(x, y, 4 * lax.div(z, 4) + lax.rem(z + d, 4), core))
    partners.append(device(x, y, z, 1 - core))
    for partner in partners:
        pl.semaphore_signal(barrier, inc=1, device_id=partner, device_id_type=MESH)

    loads = [
        pltpu.make_async_copy(src, dst, load_sem.at[n])
        for n, (src, dst) in enumerate((
            (pick_hbm, pick_ref), (flip_hbm, flip_ref), (rule_hbm, rule_ref), (feat_hbm, feat_ref),
            (w1_hbm, w1), (cot_hbm, cot_ref), (w2_hbm, w2),
        ))
    ]
    for load in loads:
        load.start()

    for load in loads[:3]:
        load.wait()
    picks = [pick_ref[0, 0, s] for s in range(2)]
    flips = [flip_ref[0, 0, s] for s in range(2)]
    rules = [rule_ref[0, 0, k] for k in range(4)]

    row8 = iota((8, 128), 0)
    rules_out[...] = jnp.where(
        row8 == 0, picks[0], jnp.where(row8 == 1, flips[0], jnp.where(row8 == 2, picks[1], flips[1]))
    )

    p, cell = iota((80, 256), 0), iota((80, 256), 1)
    k = p & 15
    want = jnp.where(
        p < 16, k, jnp.where(p < 32, 240 + k, jnp.where(p < 48, 16 * k, jnp.where(p < 64, 16 * k + 15, (
            jnp.where(k == 0, 0, jnp.where(k == 1, 15, jnp.where(k == 2, 240, jnp.where(k == 3, 255, -1))))
        ))))
    )
    take_edges = hot(cell == want).astype(BF)

    loads[3].wait()
    edges[0][...] = mm(take_edges, feat_ref[...]).astype(BF)
    edges[1][224:256, :] = jnp.zeros((32, C1), BF)
    layer1[1][288:384, :] = jnp.zeros((96, 3 * C1), BF)

    pl.semaphore_wait(barrier, len(partners))

    def edge_sends():
        out, got, send, recv = edges
        copies = []
        for i, (target, slot) in enumerate(diagonal):
            copies.append(remote(out.at[64:80], got.at[pl.ds(pl.multiple_of(160 + 16 * slot, 16), 16)],
                                 send.at[4 + i], recv.at[4 + slot], target))
        for side in range(2):
            copies.append(remote(out.at[0:64], got.at[pl.ds(pl.multiple_of(64 * seen[side], 64), 64)],
                                 send.at[side], recv.at[seen[side]], vert[side]))
        copies.append(remote(out.at[32:48], got.at[144:160], send.at[2], recv.at[3], west))
        copies.append(remote(out.at[48:64], got.at[128:144], send.at[3], recv.at[2], east))
        for copy in copies:
            copy.start()
        return copies

    def edge_waits():
        out, got, send, recv = edges
        spots = [(0, 64), (64, 64), (128, 16), (144, 16), (160, 16), (176, 16), (192, 16), (208, 16)]
        for i, (at, size) in enumerate(spots):
            remote(out.at[0:size], got.at[at:at + size], send.at[i], recv.at[i], west).wait_recv()

    sent = edge_sends()
    rule_copies = []
    for i, (target, slot) in enumerate(((vert[0], seen[0]), (vert[1], seen[1]), (west, 3), (east, 2))):
        rule_copies.append(remote(rules_out, rules_in.at[slot], rule_send.at[i], rule_recv.at[slot], target))
    for copy in rule_copies:
        copy.start()

    r, c = iota((288, 256), 0), iota((288, 256), 1)
    j, i = r & 15, r >> 4
    want = jnp.where(j == 0, 127 + i, jnp.where(j == 15, 143 + i, -1))
    q_fwd[0:288, :] = hot(c == want).astype(BF)
    r, c = iota((32, 256), 0), iota((32, 256), 1)
    k, north = r & 15, r >= 16
    flip = jnp.where(north, flips[1], flips[0])
    pick = jnp.where(north, picks[1], picks[0])
    want = jnp.where(north, 64, 0) + 16 * pick + jnp.where(flip == 1, 15 - k, k)
    q_fwd[288:320, :] = hot(c == want).astype(BF)

    def halo_cells(p, q):
        block, k = p >> 4, p & 15
        low, high = k == 0, k == 15
        corner_at = (0, 15, 272, 287)
        want = jnp.where(block == 0, 288 + k, jnp.where(block == 1, 304 + k, jnp.where(
            block == 2, 16 * k + 16, jnp.where(block == 3, 16 * k + 31, -1))))
        half = jnp.full_like(want, -1)
        ends = ((0, 1), (2, 3), (0, 2), (1, 3))
        for b in range(4):
            first, second = ends[b]
            half = jnp.where((block == b) & low & (rules[first] == 1), corner_at[first], half)
            half = jnp.where((block == b) & high & (rules[second] == 1), corner_at[second], half)
            want = jnp.where((block == 4 + b) & low & (rules[b] != 1), corner_at[b], want)
        return (hot(q == want) + hot(q == half, 0.5)).astype(BF)

    q_back[...] = halo_cells(iota((128, 384), 0), iota((128, 384), 1))
    q_act[...] = halo_cells(iota((320, 128), 1), iota((320, 128), 0))

    for layer in (layer1, layer2):
        g_pad = layer[2]
        g_pad[0:32, :] = jnp.zeros((32, C2), BF)
        g_pad[288:416, :] = jnp.zeros((128, C2), BF)
        layer[4][320:384, :] = jnp.zeros((64, layer[4].shape[1]), BF)

    red2 = Reduce(MA, red2_refs, (x, y, z, core, device))
    red1 = Reduce(MB, red1_refs, (x, y, z, core, device))
    used = FIRST_UNITS + LAST_UNITS
    red1.halves[:, used:B_UNITS] = jnp.zeros((2, B_UNITS - used, 16, 128), BF)
    red1.f3[red1.far] = jnp.zeros((2, 16, 128), BF)

    for slot in range(4):
        remote(rules_out, rules_in.at[slot], rule_send.at[slot], rule_recv.at[slot], west).wait_recv()

    r, c = iota((16, 256), 0), iota((16, 256), 1)
    for side in range(2):
        def source(position):
            return 64 * side + 16 * picks[side] + jnp.where(flips[side] == 1, 15 - position, position)

        rows = 2 * side
        w_pick, w_flip = wide(rules_in[2, rows:rows + 1, :], 2), wide(rules_in[2, rows + 1:rows + 2, :], 2)
        e_pick, e_flip = wide(rules_in[3, rows:rows + 1, :], 2), wide(rules_in[3, rows + 1:rows + 2, :], 2)
        w_at = 160 + 32 * side + corner_slot(w_pick, jnp.where(w_flip == 1, 0, 1))
        e_at = 176 + 32 * side + corner_slot(e_pick, jnp.where(e_flip == 1, 1, 0))
        w_rule, e_rule = rules[2 * side] == 1, rules[2 * side + 1] == 1
        shape = (16, 256)
        w_main = jnp.where(w_rule, jnp.full(shape, -1), jnp.broadcast_to(w_at, shape))
        e_main = jnp.where(e_rule, jnp.full(shape, -1), jnp.broadcast_to(e_at, shape))
        w_a, w_c = jnp.where(w_rule, source(0), -1), jnp.where(w_rule, 128 + 15 * side, -1)
        e_a, e_c = jnp.where(e_rule, source(15), -1), jnp.where(e_rule, 144 + 15 * side, -1)
        w_row = hot(c == w_main) + hot(c == w_a, 0.5) + hot(c == w_c, 0.5)
        e_row = hot(c == e_main) + hot(c == e_a, 0.5) + hot(c == e_c, 0.5)
        values = jnp.where(r == 0, w_row, jnp.where(r == 15, e_row, 0.0))
        q_fwd[272 * side:272 * side + 16, :] = values.astype(BF)

    face = (jnp.where(below, 0, 1), jnp.where(above, 1, 0))
    facing = []
    for side in range(2):
        south = face[side] == 0
        facing.append((
            jnp.where(south, rules_in[side, 0:1, 0:128], rules_in[side, 2:3, 0:128]),
            jnp.where(south, rules_in[side, 1:2, 0:128], rules_in[side, 3:4, 0:128]),
        ))
    p = iota((1, 128), 1)
    block, k = p >> 4, p & 15
    on_north = (block == 1) | (block >= 6)
    pick = jnp.where(on_north, facing[1][0], facing[0][0])
    flip = jnp.where(on_north, facing[1][1], facing[0][1])
    position = jnp.where(block < 2, k, jnp.where((block & 1) == 1, 15, 0))
    target = edge_cell(pick, flip, position)
    target = jnp.where(block == 2, 16 * k + 15, jnp.where(block == 3, 16 * k, target))
    target = jnp.where((block >= 4) & (k != 0), -1, target)
    place_grads = hot(iota((256, 128), 0) == target).astype(BF)

    r, c = iota((32, 256), 0), iota((32, 256), 1)
    pick = jnp.where(r < 16, wide(facing[0][0], 2), wide(facing[1][0], 2))
    flip = jnp.where(r < 16, wide(facing[0][1], 2), wide(facing[1][1], 2))
    take_cells = hot(c == edge_cell(pick, flip, r & 15)).astype(BF)
    r, c = iota((64, 384), 0), iota((64, 384), 1)
    row = r & 31
    take_strips = hot((row < 18) & (c == 16 * row + jnp.where(r < 32, 15, 0))).astype(BF)
    tap, which = r & 15, r >> 4
    tap_row = (tap * 11) >> 5
    pick = jnp.where(which < 2, wide(facing[0][0], 3), wide(facing[1][0], 3))
    flip = jnp.where(which < 2, wide(facing[0][1], 3), wide(facing[1][1], 3))
    at = 16 * tap_row + edge_cell(pick, flip, jnp.where((which & 1) == 1, 15, 0))
    take_corners = [
        hot((tap < 9) & (tap - 3 * tap_row == dw) & (c == at)).astype(BF) for dw in range(3)
    ]

    def patch_sends():
        cells, strips, corners, got_cells, got_strips, got_corners, send, recv = patch_refs
        padded = layer1[1]
        values = mm(take_corners[0], padded[:, 0:C1])
        for dw in (1, 2):
            values = values + mm(take_corners[dw], padded[:, dw * C1:(dw + 1) * C1])
        corners[...] = values.astype(BF).reshape(4, 16, C1)
        copies = []
        for i, (target_at, slot) in enumerate(diagonal):
            copies.append(remote(corners.at[i], got_corners.at[slot], send.at[4 + i], recv.at[4 + slot], target_at))
            copies[-1].start()
        strips[...] = mm(take_strips, padded[...]).astype(BF).reshape(2, 32, 3 * C1)
        copies.append(remote(strips.at[0], got_strips.at[0], send.at[2], recv.at[2], east))
        copies.append(remote(strips.at[1], got_strips.at[1], send.at[3], recv.at[3], west))
        for copy in copies[-2:]:
            copy.start()
        for dh in range(3):
            cells[:, 384 * dh:384 * dh + 384] = mm(take_cells, padded[16 * dh:16 * dh + 256, :]).astype(BF)
        for side in range(2):
            copies.append(remote(cells.at[16 * side:16 * side + 16],
                                 got_cells.at[pl.ds(pl.multiple_of(16 * seen[side], 16), 16)],
                                 send.at[side], recv.at[seen[side]], vert[side]))
            copies[-1].start()
        return copies

    def patch_waits():
        cells, strips, corners, got_cells, got_strips, got_corners, send, recv = patch_refs
        for i in range(2):
            remote(cells.at[0:16], got_cells.at[16 * i:16 * i + 16], send.at[i], recv.at[i], west).wait_recv()
            remote(strips.at[i], got_strips.at[i], send.at[2 + i], recv.at[2 + i], west).wait_recv()
        r, c = iota((32, 64), 0), iota((32, 64), 1)
        both = got_strips[...].reshape(64, 3 * C1)
        for dh in range(3):
            spread_rows = hot(c == jnp.where(r < 16, r, r + 16) + dh).astype(BF)
            got_cells[32:64, 384 * dh:384 * dh + 384] = mm(spread_rows, both).astype(BF)
        for i in range(4):
            remote(corners.at[i], got_corners.at[i], send.at[4 + i], recv.at[4 + i], west).wait_recv()
        r, c = iota((64, 64), 0), iota((64, 64), 1)
        taps = got_corners[...].reshape(64, C1)
        for tap in range(9):
            first_row = hot(((r & 15) == 0) & (c == r + tap)).astype(BF)
            got_cells[64:128, C1 * tap:C1 * tap + C1] = mm(first_row, taps).astype(BF)

    def pad_tile(layer, tile, cells, channels):
        ext, padded = layer[:2]
        south, north = cells[288:304], cells[304:320]
        ext[8:24, :] = south
        ext[24:280, :] = tile.astype(F32)
        ext[280:296, :] = north
        j = iota((288, channels), 0) & 15
        padded[0:288, 0:channels] = jnp.where(j == 0, cells[0:288], ext[7:295, :]).astype(BF)
        padded[0:288, channels:2 * channels] = ext[8:296, :].astype(BF)
        padded[0:288, 2 * channels:] = jnp.where(j == 15, cells[0:288], ext[9:297, :]).astype(BF)

    def convolve(layer, weight):
        padded = layer[1]
        total = mm(padded[0:256, :], weight[0])
        for dh in (1, 2):
            total = total + mm(padded[16 * dh:16 * dh + 256, :], weight[dh])
        return total

    def input_side(layer, weight, channels):
        g_pad, by_shift, leaving, out = layer[2:6]
        total = mm_nt(g_pad[32:320, :], weight[0])
        for dh in (1, 2):
            at = 32 - 16 * dh
            total = total + mm_nt(g_pad[at:at + 288, :], weight[dh])
        by_shift[8:296, :] = total
        j = iota((288, channels), 0) & 15
        centre = by_shift[8:296, channels:2 * channels]
        centre = centre + jnp.where(j == 15, 0.0, by_shift[9:297, 0:channels])
        centre = centre + jnp.where(j == 0, 0.0, by_shift[7:295, 2 * channels:])
        centre = centre.astype(BF)
        sides = jnp.where(j == 0, by_shift[8:296, 0:channels], by_shift[8:296, 2 * channels:])
        sides = jnp.where((j == 0) | (j == 15), sides, 0.0)
        leaving[0:288, :] = sides.astype(BF)
        leaving[288:304, :] = centre[0:16]
        leaving[304:320, :] = centre[272:288]
        out[...] = mm(q_back[...], leaving[...]).astype(BF)
        return centre[16:272]

    def grad_sends(layer):
        out, got, send, recv = layer[5:9]
        copies = []
        for side in range(2):
            copies.append(remote(out.at[16 * side:16 * side + 16],
                                 got.at[pl.ds(pl.multiple_of(16 * seen[side], 16), 16)],
                                 send.at[side], recv.at[seen[side]], vert[side]))
        copies.append(remote(out.at[32:48], got.at[32:48], send.at[2], recv.at[2], west))
        copies.append(remote(out.at[48:64], got.at[48:64], send.at[3], recv.at[3], east))
        for i, (target_at, slot) in enumerate(diagonal):
            copies.append(remote(out.at[64 + 16 * i:80 + 16 * i],
                                 got.at[pl.ds(pl.multiple_of(64 + 16 * slot, 16), 16)],
                                 send.at[4 + i], recv.at[4 + slot], target_at))
        for copy in copies:
            copy.start()
        return copies

    def grad_waits(layer):
        out, got, send, recv = layer[5:9]
        for i in range(8):
            remote(out.at[0:16], got.at[16 * i:16 * i + 16], send.at[i], recv.at[i], west).wait_recv()

    def weight_grad(block, spots):
        block = block.astype(BF)
        units = block.shape[0] // 16
        for h in range(2):
            values = block[:, 128 * h:128 * h + 128].reshape(units, 16, 128)
            for first, count, red, to in spots:
                red.halves[h, to:to + count] = values[first:first + count]

    edge_waits()
    pad_tile(layer1, feat_ref[...], mm(q_fwd[...], edges[1][...]), C1)
    sent += patch_sends()
    loads[4].wait()
    pre1 = convolve(layer1, w1)
    cdf1 = normal_cdf(pre1)
    act1 = (pre1 * cdf1).astype(BF)
    slope1[...] = gelu_slope(pre1, cdf1)
    for dh in range(3):
        windows[dh] = layer1[1][16 * dh:16 * dh + 256, :].T
    r, c = iota((256, 64), 0), iota((256, 64), 1)
    spread = hot(c == 8 * (r >> 5) + ((r & 15) >> 1), 0.25).astype(BF)
    loads[5].wait()
    cot = mm(spread, cot_ref[...])
    loads[6].wait()

    patch_waits()
    patches = patch_refs[3]
    halo_pre = mm(patches[:, 0:384], w1[0])
    for dh in (1, 2):
        halo_pre = halo_pre + mm(patches[:, 384 * dh:384 * dh + 384], w1[dh])
    halo_cdf = normal_cdf(halo_pre)
    halo_act = (halo_pre * halo_cdf).astype(BF)
    pad_tile(layer2, act1, mm(q_act[...], halo_act), C2)
    second_pre = convolve(layer2, w2)
    cdf2 = normal_cdf(second_pre)
    grad2 = (cot * gelu_slope(second_pre, cdf2)).astype(BF)
    layer2[2][32:288, :] = grad2
    for dh in range(3):
        spots = [(0, 48, red2, 48 * dh)] if dh < 2 else [(0, 32, red2, 96), (32, 16, red1, FIRST_UNITS)]
        weight_grad(mm_tn(layer2[1][16 * dh:16 * dh + 256, :], grad2), spots)
        red2.core_send(48 * dh, spots[0][1])
    centre2 = input_side(layer2, w2, C2)
    sent += grad_sends(layer2)

    own = (centre2.astype(F32) * slope1[...]).astype(BF)
    leaving = (layer2[5][...].astype(F32) * gelu_slope(halo_pre, halo_cdf)).astype(BF)
    for dh in range(3):
        block = mm(windows[dh], own) + mm_tn(patches[:, 384 * dh:384 * dh + 384], leaving)
        weight_grad(block, [(0, 24, red1, 24 * dh)])
    red1.core_send(0, B_UNITS)
    red2.core_add()
    red1.core_add()
    pre2[...] = second_pre * cdf2

    r, c = iota((64, 256), 0), iota((64, 256), 1)
    gather_cells = hot(r == 8 * (c >> 5) + ((c & 15) >> 1), 0.25).astype(BF)
    act2 = pre2[...]
    high = act2.astype(BF)
    low = (act2 - high.astype(F32)).astype(BF)
    pooled_ref[...] = (mm(gather_cells, high) + mm(gather_cells, low)).astype(BF)

    red2.first_add()
    red1.first_add()

    grad_waits(layer2)
    first_grad = centre2.astype(F32) + mm(place_grads, layer2[6][...])
    layer1[2][32:288, :] = (first_grad * slope1[...]).astype(BF)
    centre1 = input_side(layer1, w1, C1)
    sent += grad_sends(layer1)

    red2.second_add()
    red1.second_add()

    grad_waits(layer1)
    grad_ref[...] = (centre1.astype(F32) + mm(place_grads, layer1[6][...])).astype(BF)

    for copy in sent + rule_copies:
        copy.wait_send()
    red2.flush()
    red1.flush()
    red2.far_add()
    red1.far_add()
    red2.gather_second()
    red1.gather_second()
    red2.gather_core()
    red1.gather_core()
    list(red2.gather_done())
    red2.flush()
    squares = jnp.zeros((16, 128), F32)
    for h in range(2):
        squares = sum_squares(second_out, h, 0, A_UNITS // 8, squares)
    squares = sum_squares(first_out, core, 0, B_UNITS // 8, squares)
    for part, at in red1.gather_done():
        squares = sum_squares(first_out, 1 - core, at, red1.m[part] // 2, squares)
    square_ref[...] = squares
    red1.flush()


def sum_squares(ref, half, at, steps, total):
    def body(i, total):
        values = ref[half, pl.ds(at + i * 8, 8)].astype(F32)
        return total + jnp.sum(values * values, axis=0)

    return lax.fori_loop(0, steps, body, total)


def finish_kernel(pooled_ref, grad_ref, first_ref, second_ref, square_ref, pooled_out, grad_out, first_out, second_out,
                  first_rows, second_rows, sems):
    copies = [pltpu.make_async_copy(pooled_ref, pooled_out, sems.at[0]),
              pltpu.make_async_copy(grad_ref, grad_out, sems.at[1])]
    for copy in copies:
        copy.start()

    squared = jnp.sum(jnp.sum(square_ref[...], axis=0, keepdims=True), axis=1, keepdims=True)
    target_norm = math.sqrt(9.0 * (C1 + C2) * C2)
    scale = jnp.broadcast_to(target_norm / jnp.sqrt(squared + 1e-06), (16, 128))

    def write(ref, at, to, count, out):
        def body(i, carry):
            for h in range(2):
                values = ref[h, pl.ds(at + i * 8, 8)].astype(F32) * scale
                rows = pl.ds(pl.multiple_of((to + i * 8) * 16, 128), 128)
                out[rows, 128 * h:128 * h + 128] = values.astype(BF).reshape(128, 128)
            return carry

        lax.fori_loop(0, count // 8, body, 0)

    jobs = [(second_ref, n * 64, n * 64, 64, second_rows, second_out) for n in range(2)]
    jobs.append((first_ref, 0, 0, FIRST_UNITS, first_rows, first_out))
    jobs.append((first_ref, FIRST_UNITS, A_UNITS, LAST_UNITS, second_rows, second_out))
    for n, (ref, at, to, count, rows, out) in enumerate(jobs):
        write(ref, at, to, count, rows)
        span = pl.ds(16 * to, 16 * count)
        copies.append(pltpu.make_async_copy(rows.at[span], out.at[span], sems.at[2 + n]))
        copies[-1].start()
    for copy in copies:
        copy.wait()


def on_device(features, conv_first, conv_second, cotangent, edge_pick, edge_flip, corner_rule):
    vmem = pl.BlockSpec(memory_space=pltpu.VMEM)
    hbm = pl.BlockSpec(memory_space=pltpu.HBM)
    pooled, input_grad, first, second, square = pl.pallas_call(
        step_kernel,
        out_shape=(
            jax.ShapeDtypeStruct((64, C2), BF),
            jax.ShapeDtypeStruct((256, C1), BF),
            jax.ShapeDtypeStruct((2, B_UNITS, 16, 128), BF),
            jax.ShapeDtypeStruct((2, A_UNITS, 16, 128), BF),
            jax.ShapeDtypeStruct((16, 128), F32),
        ),
        in_specs=[hbm] * 7,
        out_specs=[vmem] * 5,
        scratch_shapes=(
            edge_scratch(C1)
            + patch_scratch()
            + layer_scratch(C1)
            + layer_scratch(C2)
            + reduce_scratch(*MA)
            + reduce_scratch(*MB)
            + [
                pltpu.VMEM((256, C1), BF),
                pltpu.VMEM((3, 3 * C1, C2), BF),
                pltpu.VMEM((3, 3 * C2, C2), BF),
                pltpu.VMEM((64, C2), BF),
                pltpu.SMEM((1, 1, 2), jnp.int32),
                pltpu.SMEM((1, 1, 2), jnp.int32),
                pltpu.SMEM((1, 1, 4), jnp.int32),
                pltpu.SemaphoreType.DMA((7,)),
                pltpu.VMEM((8, 128), jnp.int32),
                pltpu.VMEM((4, 8, 128), jnp.int32),
                pltpu.SemaphoreType.DMA((4,)),
                pltpu.SemaphoreType.DMA((4,)),
                pltpu.VMEM((320, 256), BF),
                pltpu.VMEM((128, 384), BF),
                pltpu.VMEM((320, 128), BF),
                pltpu.VMEM((256, C2), F32),
                pltpu.VMEM((256, C2), F32),
                pltpu.VMEM((3, 3 * C1, 256), BF),
            ]
        ),
        compiler_params=pltpu.CompilerParams(
            collective_id=0, has_side_effects=True, vmem_limit_bytes=32 * 1024 * 1024
        ),
        name="level_step",
    )(*(
        pltpu.with_memory_space_constraint(value, pltpu.HBM)
        for value in (
            features.reshape(256, C1),
            conv_first.reshape(3, 3 * C1, C2),
            conv_second.reshape(3, 3 * C2, C2),
            cotangent.reshape(64, C2),
            edge_pick,
            edge_flip,
            corner_rule,
        )
    ))
    pooled, input_grad, first, second = pl.pallas_call(
        finish_kernel,
        out_shape=(
            jax.ShapeDtypeStruct((64, C2), BF),
            jax.ShapeDtypeStruct((256, C1), BF),
            jax.ShapeDtypeStruct((9 * C1, C2), BF),
            jax.ShapeDtypeStruct((9 * C2, C2), BF),
        ),
        in_specs=[vmem] * 5,
        out_specs=[hbm] * 4,
        scratch_shapes=[
            pltpu.VMEM((9 * C1, C2), BF),
            pltpu.VMEM((9 * C2, C2), BF),
            pltpu.SemaphoreType.DMA((6,)),
        ],
        compiler_params=pltpu.CompilerParams(vmem_limit_bytes=16 * 1024 * 1024),
        name="scale_outputs",
    )(pooled, input_grad, first, second, square)
    return (
        pooled.reshape(1, 1, 8, 8, C2),
        input_grad.reshape(1, 1, 16, 16, C1),
        first.reshape(3, 3, C1, C2),
        second.reshape(3, 3, C2, C2),
    )


def solution(mesh):
    return jax.shard_map(
        on_device,
        mesh=mesh,
        in_specs=(
            P("lon", "lat", None, None, None),
            P(),
            P(),
            P("lon", "lat", None, None, None),
            P("lon", "lat", None),
            P("lon", "lat", None),
            P("lon", "lat", None),
        ),
        out_specs=(P("lon", "lat", None, None, None), P("lon", "lat", None, None, None), P(), P()),
        check_vma=False,
    )
```

```python
import math

import jax
import jax.numpy as jnp
from jax import lax
from jax.experimental import pallas as pl
from jax.experimental.pallas import tpu as pltpu
from jax.sharding import PartitionSpec as P

MESH = pl.DeviceIdType.MESH
BF = jnp.bfloat16
F32 = jnp.float32
NX, NY, NZ = 4, 4, 16
LON, LAT = 2 * NY * NZ, 4
C1, C2 = 128, 256


def normal_cdf(values):
    return 0.5 * (1.0 + lax.erf(values * (1.0 / math.sqrt(2.0))))


def gelu_slope(values, cdf):
    return cdf + values * jnp.exp(-0.5 * values * values) * (1.0 / math.sqrt(2.0 * math.pi))


def iota(shape, dim):
    return lax.broadcasted_iota(jnp.int32, shape, dim)


def hot(cond, value=1.0):
    return jnp.where(cond, jnp.float32(value), jnp.float32(0.0))


def wide(row, count):
    return jnp.concatenate([row] * count, axis=1)


def edge_cell(edge, flip, position):
    at = jnp.where(flip == 1, 15 - position, position)
    return jnp.where(edge == 0, at, jnp.where(edge == 1, 240 + at, jnp.where(edge == 2, 16 * at, 16 * at + 15)))


def mm(a, b):
    return jnp.dot(a, b, preferred_element_type=F32)


def mm_nt(a, b):
    return lax.dot_general(a, b, (((1,), (1,)), ((), ())), preferred_element_type=F32)


def mm_tn(a, b):
    return lax.dot_general(a, b, (((0,), (0,)), ((), ())), preferred_element_type=F32)


def remote(src, dst, send_sem, recv_sem, device):
    return pltpu.make_async_remote_copy(
        src_ref=src, dst_ref=dst, send_sem=send_sem, recv_sem=recv_sem,
        device_id=device, device_id_type=MESH,
    )


def corner_slot(edge, at_end):
    return jnp.where(
        edge == 0, at_end, jnp.where(edge == 1, 2 + at_end, jnp.where(edge == 2, 2 * at_end, 1 + 2 * at_end))
    )


class Reduce:
    def __init__(self, m, refs, place):
        self.m = m
        self.total = m[0] + m[1]
        self.start = (0, 16 * m[0])
        (self.halves, self.r0, self.a1, r1a, r1b, a2a, a2b, r2a, r2b, self.f3, self.out,
         self.s_send, self.s_recv, self.g_send, self.g_recv) = refs
        self.r1, self.a2, self.r2 = (r1a, r1b), (a2a, a2b), (r2a, r2b)
        self.x, self.y, self.z, self.core, self.device = place
        self.near, self.far = lax.rem(self.z, 4), lax.div(self.z, 4)
        self.pending = []
        self.guarded = []
        self.pieces = []
        self.waited = 0

    def other_core(self):
        return self.device(self.x, self.y, self.z, 1 - self.core)

    def peer(self, axis, d):
        x = lax.rem(self.x + d, NX) if axis == "x" else self.x
        y = lax.rem(self.y + d, NY) if axis == "y" else self.y
        return self.device(x, y, self.z, self.core)

    def axes(self, part):
        return ("x", "y") if part == 0 else ("y", "x")

    def coords(self, part):
        return (self.x, self.y) if part == 0 else (self.y, self.x)

    def send(self, copy):
        copy.start()
        self.pending.append(copy)

    def received(self, ref, sem):
        remote(ref, ref, self.s_send.at[0], sem, self.other_core()).wait_recv()

    def flush(self, keep=0):
        done = len(self.pending) - keep
        for copy in self.pending[:done]:
            copy.wait_send()
        for wanted, copy in self.guarded:
            pl.when(wanted)(copy.wait_send)
        self.pending, self.guarded = self.pending[done:], []

    def send_if(self, wanted, copy):
        pl.when(wanted)(copy.start)
        self.guarded.append((wanted, copy))

    def plane(self, part):
        for db in (2, 1, 3, 0):
            for dz in (2, 3, 1, 0):
                if db or dz:
                    x, y = self.x, self.y
                    if part == 0:
                        y = lax.rem(y + db, 4)
                    else:
                        x = lax.rem(x + db, 4)
                    near = lax.rem(self.near + dz, 4)
                    yield 4 * db + dz - 1, (y if part == 0 else x), near, self.device(x, y, 4 * self.far + near, self.core)

    def core_send(self, at, count):
        k = len(self.pieces)
        self.pieces.append((at, count))
        self.send(remote(self.halves.at[1 - self.core, at:at + count], self.r0.at[at:at + count],
                         self.s_send.at[k], self.s_recv.at[k], self.other_core()))

    def core_add(self):
        for part in range(2):
            n = 4 * self.m[part]
            mine = self.coords(part)[0]
            while self.waited < len(self.pieces) and self.pieces[self.waited][0] < self.start[part] + 4 * n:
                at, count = self.pieces[self.waited]
                self.received(self.r0.at[at:at + count], self.s_recv.at[self.waited])
                self.waited += 1
            k = 3 + part
            for d in (2, 1, 3, 0):
                at = pl.ds(self.start[part] + lax.rem(mine + d, 4) * n, n)
                self.a1[at] = (self.halves[self.core, at].astype(F32) + self.r0[at].astype(F32)).astype(BF)
                if d:
                    self.send(remote(self.a1.at[at], self.r1[part].at[d - 1],
                                     self.s_send.at[3 * k - 7 + d], self.s_recv.at[k],
                                     self.peer(self.axes(part)[0], d)))

    def first_add(self):
        for part in range(2):
            m = self.m[part]
            r1, a2, r2 = self.r1[part], self.a2[part], self.r2[part]
            ca = self.coords(part)[0]
            self.received(r1, self.s_recv.at[3 + part])
            total = self.a1[pl.ds(self.start[part] + ca * 4 * m, 4 * m)].astype(F32)
            for e in range(3):
                total = total + r1[e].astype(F32)
            a2[...] = total.astype(BF)
            for slot, b_at, near, target in self.plane(part):
                self.send_if(near < m, remote(
                    a2.at[b_at * m + lax.rem(near, m)], r2.at[slot], self.s_send.at[9 + 15 * part + slot],
                    self.s_recv.at[5 + part], target))

    def second_add(self):
        for part in range(2):
            m = self.m[part]
            cb = self.coords(part)[1]

            @pl.when(self.near < m)
            def _():
                self.received(self.r2[part], self.s_recv.at[5 + part])
                total = self.a2[part][cb * m + lax.rem(self.near, m)].astype(F32)
                for e in range(15):
                    total = total + self.r2[part][e].astype(F32)
                self.f3[self.far, part] = total.astype(BF)

        for d in (2, 1, 3):
            self.send(remote(self.f3.at[self.far], self.f3.at[self.far], self.s_send.at[39 + d - 1], self.s_recv.at[8],
                             self.device(self.x, self.y, 4 * lax.rem(self.far + d, 4) + self.near, self.core)))

    def far_add(self):
        self.received(self.f3.at[0:3], self.s_recv.at[8])
        for part in range(2):
            m = self.m[part]
            ca, cb = self.coords(part)
            total = self.f3[0, part].astype(F32)
            for e in range(1, 4):
                total = total + self.f3[e, part].astype(F32)
            at = self.start[part] + (ca * 4 + cb) * m + lax.rem(self.near, m)

            @pl.when(self.near < m)
            def _():
                self.out[self.core, at] = total.astype(BF)

            for slot, _, _, target in self.plane(part):
                self.send_if(self.near < m, remote(
                    self.out.at[self.core, at], self.out.at[self.core, at], self.g_send.at[15 * part + slot],
                    self.g_recv.at[part], target))

    def gather_second(self):
        for part in range(2):
            m = self.m[part]
            ca = self.coords(part)[0]
            owns = self.near < m

            @pl.when(owns)
            def _():
                self.received(self.a1.at[0:4 * m - 1], self.g_recv.at[part])

            @pl.when(jnp.logical_not(owns))
            def _():
                self.received(self.a1.at[0:4 * m], self.g_recv.at[part])

            at = pl.ds(self.start[part] + ca * 4 * m, 4 * m)
            for d in (2, 1, 3):
                k = part * 3 + d - 1
                self.send(remote(self.out.at[self.core, at], self.out.at[self.core, at], self.g_send.at[30 + k],
                                 self.g_recv.at[6 + k], self.peer(self.axes(part)[0], d)))
            self.to_core(part, 0, at)

    def to_core(self, part, d, at):
        k = 12 + part * 4 + d
        self.send(remote(self.out.at[self.core, at], self.out.at[self.core, at], self.g_send.at[24 + k],
                         self.g_recv.at[k], self.other_core()))

    def block_of(self, part, d):
        n = 4 * self.m[part]
        return pl.ds(self.start[part] + lax.rem(self.coords(part)[0] + 4 - d, 4) * n, n)

    def gather_core(self):
        for d in (1, 3, 2):
            for part in range(2):
                at = self.block_of(part, d)
                self.received(self.out.at[self.core, at], self.g_recv.at[6 + part * 3 + d - 1])
                self.to_core(part, d, at)

    def gather_done(self):
        for d in (0, 1, 3, 2):
            for part in range(2):
                at = self.block_of(part, d)
                self.received(self.out.at[1 - self.core, at], self.g_recv.at[12 + part * 4 + d])
                yield part, at.start


def reduce_scratch(ma, mb):
    units = 16 * (ma + mb)
    return [
        pltpu.VMEM((2, units, 16, 128), BF),
        pltpu.VMEM((units, 16, 128), BF),
        pltpu.VMEM((units, 16, 128), BF),
        pltpu.VMEM((3, 4 * ma, 16, 128), BF),
        pltpu.VMEM((3, 4 * mb, 16, 128), BF),
        pltpu.VMEM((4 * ma, 16, 128), BF),
        pltpu.VMEM((4 * mb, 16, 128), BF),
        pltpu.VMEM((15, 16, 128), BF),
        pltpu.VMEM((15, 16, 128), BF),
        pltpu.VMEM((4, 2, 16, 128), BF),
        pltpu.SemaphoreType.DMA((42,)),
        pltpu.SemaphoreType.DMA((9,)),
        pltpu.SemaphoreType.DMA((44,)),
        pltpu.SemaphoreType.DMA((20,)),
    ]


N_REDUCE = 14
MA, MB = (4, 4), (4, 2)
A_UNITS, B_UNITS, FIRST_UNITS, LAST_UNITS = 128, 96, 72, 16


def edge_scratch(channels):
    return [
        pltpu.VMEM((80, channels), BF),
        pltpu.VMEM((256, channels), BF),
        pltpu.SemaphoreType.DMA((8,)),
        pltpu.SemaphoreType.DMA((8,)),
    ]


def patch_scratch():
    return [
        pltpu.VMEM((32, 9 * C1), BF),
        pltpu.VMEM((2, 32, 3 * C1), BF),
        pltpu.VMEM((4, 16, C1), BF),
        pltpu.VMEM((128, 9 * C1), BF),
        pltpu.VMEM((2, 32, 3 * C1), BF),
        pltpu.VMEM((4, 16, C1), BF),
        pltpu.SemaphoreType.DMA((8,)),
        pltpu.SemaphoreType.DMA((8,)),
    ]


def layer_scratch(channels):
    return [
        pltpu.VMEM((304, channels), F32),
        pltpu.VMEM((384, 3 * channels), BF),
        pltpu.VMEM((416, C2), BF),
        pltpu.VMEM((304, 3 * channels), F32),
        pltpu.VMEM((384, channels), BF),
        pltpu.VMEM((128, channels), BF),
        pltpu.VMEM((128, channels), BF),
        pltpu.SemaphoreType.DMA((8,)),
        pltpu.SemaphoreType.DMA((8,)),
    ]


N_EDGE, N_PATCH, N_LAYER = 4, 8, 9


def step_kernel(*refs):
    (feat_hbm, w1_hbm, w2_hbm, cot_hbm, pick_hbm, flip_hbm, rule_hbm,
     pooled_ref, grad_ref, first_out, second_out, square_ref) = refs[:12]
    refs = refs[12:]
    edges, refs = refs[:N_EDGE], refs[N_EDGE:]
    patch_refs, refs = refs[:N_PATCH], refs[N_PATCH:]
    layer1, refs = refs[:N_LAYER], refs[N_LAYER:]
    layer2, refs = refs[:N_LAYER], refs[N_LAYER:]
    red2_refs, refs = refs[:N_REDUCE], refs[N_REDUCE:]
    red1_refs, refs = refs[:N_REDUCE], refs[N_REDUCE:]
    (feat_ref, w1, w2, cot_ref, pick_ref, flip_ref, rule_ref, load_sem,
     rules_out, rules_in, rule_send, rule_recv, q_fwd, q_back, q_act, slope1, pre2,
     windows) = refs
    red2_refs = red2_refs[:10] + (second_out,) + red2_refs[10:]
    red1_refs = red1_refs[:10] + (first_out,) + red1_refs[10:]

    lon, lat = lax.axis_index("lon"), lax.axis_index("lat")
    y = lax.div(lon, 2 * NZ)
    z = lax.div(lax.rem(lon, 2 * NZ), 2)
    x = lax.rem(lon, 2) * 2 + lax.div(lat, 2)
    core = lax.rem(lat, 2)

    def device(x_at, y_at, z_at, core_at):
        return (y_at * (2 * NZ) + z_at * 2 + lax.div(x_at, 2), lax.rem(x_at, 2) * 2 + core_at)

    across = lax.rem(lon + LON // 2, LON)
    below, above = lat == 0, lat == LAT - 1
    vert = (
        (jnp.where(below, across, lon), jnp.where(below, lat, lat - 1)),
        (jnp.where(above, across, lon), jnp.where(above, lat, lat + 1)),
    )
    seen = (jnp.where(below, 0, 1), jnp.where(above, 1, 0))

    def west_of(at):
        return (lax.rem(at[0] + LON - 1, LON), at[1])

    def east_of(at):
        return (lax.rem(at[0] + 1, LON), at[1])

    here = (lon, lat)
    west, east = west_of(here), east_of(here)
    diagonal = [
        (west_of(vert[0]), 2 * seen[0] + 1),
        (east_of(vert[0]), 2 * seen[0]),
        (west_of(vert[1]), 2 * seen[1] + 1),
        (east_of(vert[1]), 2 * seen[1]),
    ]

    barrier = pltpu.get_barrier_semaphore()
    partners = [device(x, y, lax.rem(z + 4 * d, NZ), core) for d in (2, 1, 3)]
    partners += [d[0] for d in diagonal] + [west, east, vert[0], vert[1]]
    for d in (2, 1, 3):
        for dz in (2, 1, 3, 0):
            z_at = 4 * lax.div(z, 4) + lax.rem(z + dz, 4)
            partners.append(device(lax.rem(x + d, NX), y, z_at, core))
            partners.append(device(x, lax.rem(y + d, NY), z_at, core))
        partners.append(device(x, y, 4 * lax.div(z, 4) + lax.rem(z + d, 4), core))
    partners.append(device(x, y, z, 1 - core))
    for partner in partners:
        pl.semaphore_signal(barrier, inc=1, device_id=partner, device_id_type=MESH)

    loads = [
        pltpu.make_async_copy(src, dst, load_sem.at[n])
        for n, (src, dst) in enumerate((
            (pick_hbm, pick_ref), (flip_hbm, flip_ref), (rule_hbm, rule_ref), (feat_hbm, feat_ref),
            (w1_hbm, w1), (cot_hbm, cot_ref), (w2_hbm, w2),
        ))
    ]
    for load in loads:
        load.start()

    for load in loads[:3]:
        load.wait()
    picks = [pick_ref[0, 0, s] for s in range(2)]
    flips = [flip_ref[0, 0, s] for s in range(2)]
    rules = [rule_ref[0, 0, k] for k in range(4)]

    row8 = iota((8, 128), 0)
    rules_out[...] = jnp.where(
        row8 == 0, picks[0], jnp.where(row8 == 1, flips[0], jnp.where(row8 == 2, picks[1], flips[1]))
    )

    p, cell = iota((80, 256), 0), iota((80, 256), 1)
    k = p & 15
    want = jnp.where(
        p < 16, k, jnp.where(p < 32, 240 + k, jnp.where(p < 48, 16 * k, jnp.where(p < 64, 16 * k + 15, (
            jnp.where(k == 0, 0, jnp.where(k == 1, 15, jnp.where(k == 2, 240, jnp.where(k == 3, 255, -1))))
        ))))
    )
    take_edges = hot(cell == want).astype(BF)

    loads[3].wait()
    edges[0][...] = mm(take_edges, feat_ref[...]).astype(BF)
    edges[1][224:256, :] = jnp.zeros((32, C1), BF)
    layer1[1][288:384, :] = jnp.zeros((96, 3 * C1), BF)

    pl.semaphore_wait(barrier, len(partners))

    def edge_sends():
        out, got, send, recv = edges
        copies = []
        for i, (target, slot) in enumerate(diagonal):
            copies.append(remote(out.at[64:80], got.at[pl.ds(pl.multiple_of(160 + 16 * slot, 16), 16)],
                                 send.at[4 + i], recv.at[4 + slot], target))
        for side in range(2):
            copies.append(remote(out.at[0:64], got.at[pl.ds(pl.multiple_of(64 * seen[side], 64), 64)],
                                 send.at[side], recv.at[seen[side]], vert[side]))
        copies.append(remote(out.at[32:48], got.at[144:160], send.at[2], recv.at[3], west))
        copies.append(remote(out.at[48:64], got.at[128:144], send.at[3], recv.at[2], east))
        for copy in copies:
            copy.start()
        return copies

    def edge_waits():
        out, got, send, recv = edges
        spots = [(0, 64), (64, 64), (128, 16), (144, 16), (160, 16), (176, 16), (192, 16), (208, 16)]
        for i, (at, size) in enumerate(spots):
            remote(out.at[0:size], got.at[at:at + size], send.at[i], recv.at[i], west).wait_recv()

    sent = edge_sends()
    rule_copies = []
    for i, (target, slot) in enumerate(((vert[0], seen[0]), (vert[1], seen[1]), (west, 3), (east, 2))):
        rule_copies.append(remote(rules_out, rules_in.at[slot], rule_send.at[i], rule_recv.at[slot], target))
    for copy in rule_copies:
        copy.start()

    r, c = iota((288, 256), 0), iota((288, 256), 1)
    j, i = r & 15, r >> 4
    want = jnp.where(j == 0, 127 + i, jnp.where(j == 15, 143 + i, -1))
    q_fwd[0:288, :] = hot(c == want).astype(BF)
    r, c = iota((32, 256), 0), iota((32, 256), 1)
    k, north = r & 15, r >= 16
    flip = jnp.where(north, flips[1], flips[0])
    pick = jnp.where(north, picks[1], picks[0])
    want = jnp.where(north, 64, 0) + 16 * pick + jnp.where(flip == 1, 15 - k, k)
    q_fwd[288:320, :] = hot(c == want).astype(BF)

    def halo_cells(p, q):
        block, k = p >> 4, p & 15
        low, high = k == 0, k == 15
        corner_at = (0, 15, 272, 287)
        want = jnp.where(block == 0, 288 + k, jnp.where(block == 1, 304 + k, jnp.where(
            block == 2, 16 * k + 16, jnp.where(block == 3, 16 * k + 31, -1))))
        half = jnp.full_like(want, -1)
        ends = ((0, 1), (2, 3), (0, 2), (1, 3))
        for b in range(4):
            first, second = ends[b]
            half = jnp.where((block == b) & low & (rules[first] == 1), corner_at[first], half)
            half = jnp.where((block == b) & high & (rules[second] == 1), corner_at[second], half)
            want = jnp.where((block == 4 + b) & low & (rules[b] != 1), corner_at[b], want)
        return (hot(q == want) + hot(q == half, 0.5)).astype(BF)

    q_back[...] = halo_cells(iota((128, 384), 0), iota((128, 384), 1))
    q_act[...] = halo_cells(iota((320, 128), 1), iota((320, 128), 0))

    for layer in (layer1, layer2):
        g_pad = layer[2]
        g_pad[0:32, :] = jnp.zeros((32, C2), BF)
        g_pad[288:416, :] = jnp.zeros((128, C2), BF)
        layer[4][320:384, :] = jnp.zeros((64, layer[4].shape[1]), BF)

    red2 = Reduce(MA, red2_refs, (x, y, z, core, device))
    red1 = Reduce(MB, red1_refs, (x, y, z, core, device))
    used = FIRST_UNITS + LAST_UNITS
    red1.halves[:, used:B_UNITS] = jnp.zeros((2, B_UNITS - used, 16, 128), BF)
    red1.f3[red1.far] = jnp.zeros((2, 16, 128), BF)

    for slot in range(4):
        remote(rules_out, rules_in.at[slot], rule_send.at[slot], rule_recv.at[slot], west).wait_recv()

    r, c = iota((16, 256), 0), iota((16, 256), 1)
    for side in range(2):
        def source(position):
            return 64 * side + 16 * picks[side] + jnp.where(flips[side] == 1, 15 - position, position)

        rows = 2 * side
        w_pick, w_flip = wide(rules_in[2, rows:rows + 1, :], 2), wide(rules_in[2, rows + 1:rows + 2, :], 2)
        e_pick, e_flip = wide(rules_in[3, rows:rows + 1, :], 2), wide(rules_in[3, rows + 1:rows + 2, :], 2)
        w_at = 160 + 32 * side + corner_slot(w_pick, jnp.where(w_flip == 1, 0, 1))
        e_at = 176 + 32 * side + corner_slot(e_pick, jnp.where(e_flip == 1, 1, 0))
        w_rule, e_rule = rules[2 * side] == 1, rules[2 * side + 1] == 1
        shape = (16, 256)
        w_main = jnp.where(w_rule, jnp.full(shape, -1), jnp.broadcast_to(w_at, shape))
        e_main = jnp.where(e_rule, jnp.full(shape, -1), jnp.broadcast_to(e_at, shape))
        w_a, w_c = jnp.where(w_rule, source(0), -1), jnp.where(w_rule, 128 + 15 * side, -1)
        e_a, e_c = jnp.where(e_rule, source(15), -1), jnp.where(e_rule, 144 + 15 * side, -1)
        w_row = hot(c == w_main) + hot(c == w_a, 0.5) + hot(c == w_c, 0.5)
        e_row = hot(c == e_main) + hot(c == e_a, 0.5) + hot(c == e_c, 0.5)
        values = jnp.where(r == 0, w_row, jnp.where(r == 15, e_row, 0.0))
        q_fwd[272 * side:272 * side + 16, :] = values.astype(BF)

    face = (jnp.where(below, 0, 1), jnp.where(above, 1, 0))
    facing = []
    for side in range(2):
        south = face[side] == 0
        facing.append((
            jnp.where(south, rules_in[side, 0:1, 0:128], rules_in[side, 2:3, 0:128]),
            jnp.where(south, rules_in[side, 1:2, 0:128], rules_in[side, 3:4, 0:128]),
        ))
    p = iota((1, 128), 1)
    block, k = p >> 4, p & 15
    on_north = (block == 1) | (block >= 6)
    pick = jnp.where(on_north, facing[1][0], facing[0][0])
    flip = jnp.where(on_north, facing[1][1], facing[0][1])
    position = jnp.where(block < 2, k, jnp.where((block & 1) == 1, 15, 0))
    target = edge_cell(pick, flip, position)
    target = jnp.where(block == 2, 16 * k + 15, jnp.where(block == 3, 16 * k, target))
    target = jnp.where((block >= 4) & (k != 0), -1, target)
    place_grads = hot(iota((256, 128), 0) == target).astype(BF)

    r, c = iota((32, 256), 0), iota((32, 256), 1)
    pick = jnp.where(r < 16, wide(facing[0][0], 2), wide(facing[1][0], 2))
    flip = jnp.where(r < 16, wide(facing[0][1], 2), wide(facing[1][1], 2))
    take_cells = hot(c == edge_cell(pick, flip, r & 15)).astype(BF)
    r, c = iota((64, 384), 0), iota((64, 384), 1)
    row = r & 31
    take_strips = hot((row < 18) & (c == 16 * row + jnp.where(r < 32, 15, 0))).astype(BF)
    tap, which = r & 15, r >> 4
    tap_row = (tap * 11) >> 5
    pick = jnp.where(which < 2, wide(facing[0][0], 3), wide(facing[1][0], 3))
    flip = jnp.where(which < 2, wide(facing[0][1], 3), wide(facing[1][1], 3))
    at = 16 * tap_row + edge_cell(pick, flip, jnp.where((which & 1) == 1, 15, 0))
    take_corners = [
        hot((tap < 9) & (tap - 3 * tap_row == dw) & (c == at)).astype(BF) for dw in range(3)
    ]

    def patch_sends():
        cells, strips, corners, got_cells, got_strips, got_corners, send, recv = patch_refs
        padded = layer1[1]
        values = mm(take_corners[0], padded[:, 0:C1])
        for dw in (1, 2):
            values = values + mm(take_corners[dw], padded[:, dw * C1:(dw + 1) * C1])
        corners[...] = values.astype(BF).reshape(4, 16, C1)
        copies = []
        for i, (target_at, slot) in enumerate(diagonal):
            copies.append(remote(corners.at[i], got_corners.at[slot], send.at[4 + i], recv.at[4 + slot], target_at))
            copies[-1].start()
        strips[...] = mm(take_strips, padded[...]).astype(BF).reshape(2, 32, 3 * C1)
        copies.append(remote(strips.at[0], got_strips.at[0], send.at[2], recv.at[2], east))
        copies.append(remote(strips.at[1], got_strips.at[1], send.at[3], recv.at[3], west))
        for copy in copies[-2:]:
            copy.start()
        for dh in range(3):
            cells[:, 384 * dh:384 * dh + 384] = mm(take_cells, padded[16 * dh:16 * dh + 256, :]).astype(BF)
        for side in range(2):
            copies.append(remote(cells.at[16 * side:16 * side + 16],
                                 got_cells.at[pl.ds(pl.multiple_of(16 * seen[side], 16), 16)],
                                 send.at[side], recv.at[seen[side]], vert[side]))
            copies[-1].start()
        return copies

    def patch_waits():
        cells, strips, corners, got_cells, got_strips, got_corners, send, recv = patch_refs
        for i in range(2):
            remote(cells.at[0:16], got_cells.at[16 * i:16 * i + 16], send.at[i], recv.at[i], west).wait_recv()
            remote(strips.at[i], got_strips.at[i], send.at[2 + i], recv.at[2 + i], west).wait_recv()
        r, c = iota((32, 64), 0), iota((32, 64), 1)
        both = got_strips[...].reshape(64, 3 * C1)
        for dh in range(3):
            spread_rows = hot(c == jnp.where(r < 16, r, r + 16) + dh).astype(BF)
            got_cells[32:64, 384 * dh:384 * dh + 384] = mm(spread_rows, both).astype(BF)
        for i in range(4):
            remote(corners.at[i], got_corners.at[i], send.at[4 + i], recv.at[4 + i], west).wait_recv()
        r, c = iota((64, 64), 0), iota((64, 64), 1)
        taps = got_corners[...].reshape(64, C1)
        for tap in range(9):
            first_row = hot(((r & 15) == 0) & (c == r + tap)).astype(BF)
            got_cells[64:128, C1 * tap:C1 * tap + C1] = mm(first_row, taps).astype(BF)

    def pad_tile(layer, tile, cells, channels):
        ext, padded = layer[:2]
        south, north = cells[288:304], cells[304:320]
        ext[8:24, :] = south
        ext[24:280, :] = tile.astype(F32)
        ext[280:296, :] = north
        j = iota((288, channels), 0) & 15
        padded[0:288, 0:channels] = jnp.where(j == 0, cells[0:288], ext[7:295, :]).astype(BF)
        padded[0:288, channels:2 * channels] = ext[8:296, :].astype(BF)
        padded[0:288, 2 * channels:] = jnp.where(j == 15, cells[0:288], ext[9:297, :]).astype(BF)

    def convolve(layer, weight):
        padded = layer[1]
        total = mm(padded[0:256, :], weight[0])
        for dh in (1, 2):
            total = total + mm(padded[16 * dh:16 * dh + 256, :], weight[dh])
        return total

    def input_side(layer, weight, channels):
        g_pad, by_shift, leaving, out = layer[2:6]
        total = mm_nt(g_pad[32:320, :], weight[0])
        for dh in (1, 2):
            at = 32 - 16 * dh
            total = total + mm_nt(g_pad[at:at + 288, :], weight[dh])
        by_shift[8:296, :] = total
        j = iota((288, channels), 0) & 15
        centre = by_shift[8:296, channels:2 * channels]
        centre = centre + jnp.where(j == 15, 0.0, by_shift[9:297, 0:channels])
        centre = centre + jnp.where(j == 0, 0.0, by_shift[7:295, 2 * channels:])
        centre = centre.astype(BF)
        sides = jnp.where(j == 0, by_shift[8:296, 0:channels], by_shift[8:296, 2 * channels:])
        sides = jnp.where((j == 0) | (j == 15), sides, 0.0)
        leaving[0:288, :] = sides.astype(BF)
        leaving[288:304, :] = centre[0:16]
        leaving[304:320, :] = centre[272:288]
        out[...] = mm(q_back[...], leaving[...]).astype(BF)
        return centre[16:272]

    def grad_sends(layer):
        out, got, send, recv = layer[5:9]
        copies = []
        for side in range(2):
            copies.append(remote(out.at[16 * side:16 * side + 16],
                                 got.at[pl.ds(pl.multiple_of(16 * seen[side], 16), 16)],
                                 send.at[side], recv.at[seen[side]], vert[side]))
        copies.append(remote(out.at[32:48], got.at[32:48], send.at[2], recv.at[2], west))
        copies.append(remote(out.at[48:64], got.at[48:64], send.at[3], recv.at[3], east))
        for i, (target_at, slot) in enumerate(diagonal):
            copies.append(remote(out.at[64 + 16 * i:80 + 16 * i],
                                 got.at[pl.ds(pl.multiple_of(64 + 16 * slot, 16), 16)],
                                 send.at[4 + i], recv.at[4 + slot], target_at))
        for copy in copies:
            copy.start()
        return copies

    def grad_waits(layer):
        out, got, send, recv = layer[5:9]
        for i in range(8):
            remote(out.at[0:16], got.at[16 * i:16 * i + 16], send.at[i], recv.at[i], west).wait_recv()

    def weight_grad(block, spots):
        block = block.astype(BF)
        units = block.shape[0] // 16
        for h in range(2):
            values = block[:, 128 * h:128 * h + 128].reshape(units, 16, 128)
            for first, count, red, to in spots:
                red.halves[h, to:to + count] = values[first:first + count]

    edge_waits()
    pad_tile(layer1, feat_ref[...], mm(q_fwd[...], edges[1][...]), C1)
    sent += patch_sends()
    loads[4].wait()
    pre1 = convolve(layer1, w1)
    cdf1 = normal_cdf(pre1)
    act1 = (pre1 * cdf1).astype(BF)
    slope1[...] = gelu_slope(pre1, cdf1)
    for dh in range(3):
        windows[dh] = layer1[1][16 * dh:16 * dh + 256, :].T
    r, c = iota((256, 64), 0), iota((256, 64), 1)
    spread = hot(c == 8 * (r >> 5) + ((r & 15) >> 1), 0.25).astype(BF)
    loads[5].wait()
    cot = mm(spread, cot_ref[...])
    loads[6].wait()

    patch_waits()
    patches = patch_refs[3]
    halo_pre = mm(patches[:, 0:384], w1[0])
    for dh in (1, 2):
        halo_pre = halo_pre + mm(patches[:, 384 * dh:384 * dh + 384], w1[dh])
    halo_cdf = normal_cdf(halo_pre)
    halo_act = (halo_pre * halo_cdf).astype(BF)
    pad_tile(layer2, act1, mm(q_act[...], halo_act), C2)
    second_pre = convolve(layer2, w2)
    cdf2 = normal_cdf(second_pre)
    grad2 = (cot * gelu_slope(second_pre, cdf2)).astype(BF)
    layer2[2][32:288, :] = grad2
    for dh in range(3):
        spots = [(0, 48, red2, 48 * dh)] if dh < 2 else [(0, 32, red2, 96), (32, 16, red1, FIRST_UNITS)]
        weight_grad(mm_tn(layer2[1][16 * dh:16 * dh + 256, :], grad2), spots)
        red2.core_send(48 * dh, spots[0][1])
    centre2 = input_side(layer2, w2, C2)
    sent += grad_sends(layer2)

    own = (centre2.astype(F32) * slope1[...]).astype(BF)
    leaving = (layer2[5][...].astype(F32) * gelu_slope(halo_pre, halo_cdf)).astype(BF)
    for dh in range(3):
        block = mm(windows[dh], own) + mm_tn(patches[:, 384 * dh:384 * dh + 384], leaving)
        weight_grad(block, [(0, 24, red1, 24 * dh)])
    red1.core_send(0, B_UNITS)
    red2.core_add()
    red1.core_add()
    pre2[...] = second_pre * cdf2

    r, c = iota((64, 256), 0), iota((64, 256), 1)
    gather_cells = hot(r == 8 * (c >> 5) + ((c & 15) >> 1), 0.25).astype(BF)
    act2 = pre2[...]
    high = act2.astype(BF)
    low = (act2 - high.astype(F32)).astype(BF)
    pooled_ref[...] = (mm(gather_cells, high) + mm(gather_cells, low)).astype(BF)

    red2.first_add()
    red1.first_add()

    grad_waits(layer2)
    first_grad = centre2.astype(F32) + mm(place_grads, layer2[6][...])
    layer1[2][32:288, :] = (first_grad * slope1[...]).astype(BF)
    centre1 = input_side(layer1, w1, C1)
    sent += grad_sends(layer1)

    red2.second_add()
    red1.second_add()

    grad_waits(layer1)
    grad_ref[...] = (centre1.astype(F32) + mm(place_grads, layer1[6][...])).astype(BF)

    for copy in sent + rule_copies:
        copy.wait_send()
    red2.flush(3)
    red1.flush(3)
    red2.far_add()
    red1.far_add()
    red2.gather_second()
    red1.gather_second()
    red2.gather_core()
    red1.gather_core()
    list(red2.gather_done())
    red2.flush()
    squares = jnp.zeros((16, 128), F32)
    for h in range(2):
        squares = sum_squares(second_out, h, 0, A_UNITS // 8, squares)
    squares = sum_squares(first_out, core, 0, B_UNITS // 8, squares)
    for part, at in red1.gather_done():
        squares = sum_squares(first_out, 1 - core, at, red1.m[part] // 2, squares)
    square_ref[...] = squares
    red1.flush()


def sum_squares(ref, half, at, steps, total):
    def body(i, total):
        values = ref[half, pl.ds(at + i * 8, 8)].astype(F32)
        return total + jnp.sum(values * values, axis=0)

    return lax.fori_loop(0, steps, body, total)


def finish_kernel(pooled_ref, grad_ref, first_ref, second_ref, square_ref, pooled_out, grad_out, first_out, second_out,
                  first_rows, second_rows, sems):
    copies = [pltpu.make_async_copy(pooled_ref, pooled_out, sems.at[0]),
              pltpu.make_async_copy(grad_ref, grad_out, sems.at[1])]
    for copy in copies:
        copy.start()

    squared = jnp.sum(jnp.sum(square_ref[...], axis=0, keepdims=True), axis=1, keepdims=True)
    target_norm = math.sqrt(9.0 * (C1 + C2) * C2)
    scale = jnp.broadcast_to(target_norm / jnp.sqrt(squared + 1e-06), (16, 128))

    def write(ref, at, to, count, out):
        def body(i, carry):
            for h in range(2):
                values = ref[h, pl.ds(at + i * 8, 8)].astype(F32) * scale
                rows = pl.ds(pl.multiple_of((to + i * 8) * 16, 128), 128)
                out[rows, 128 * h:128 * h + 128] = values.astype(BF).reshape(128, 128)
            return carry

        lax.fori_loop(0, count // 8, body, 0)

    jobs = [(second_ref, n * 64, n * 64, 64, second_rows, second_out) for n in range(2)]
    jobs.append((first_ref, 0, 0, FIRST_UNITS, first_rows, first_out))
    jobs.append((first_ref, FIRST_UNITS, A_UNITS, LAST_UNITS, second_rows, second_out))
    for n, (ref, at, to, count, rows, out) in enumerate(jobs):
        write(ref, at, to, count, rows)
        span = pl.ds(16 * to, 16 * count)
        copies.append(pltpu.make_async_copy(rows.at[span], out.at[span], sems.at[2 + n]))
        copies[-1].start()
    for copy in copies:
        copy.wait()


def on_device(features, conv_first, conv_second, cotangent, edge_pick, edge_flip, corner_rule):
    vmem = pl.BlockSpec(memory_space=pltpu.VMEM)
    hbm = pl.BlockSpec(memory_space=pltpu.HBM)
    pooled, input_grad, first, second, square = pl.pallas_call(
        step_kernel,
        out_shape=(
            jax.ShapeDtypeStruct((64, C2), BF),
            jax.ShapeDtypeStruct((256, C1), BF),
            jax.ShapeDtypeStruct((2, B_UNITS, 16, 128), BF),
            jax.ShapeDtypeStruct((2, A_UNITS, 16, 128), BF),
            jax.ShapeDtypeStruct((16, 128), F32),
        ),
        in_specs=[hbm] * 7,
        out_specs=[vmem] * 5,
        scratch_shapes=(
            edge_scratch(C1)
            + patch_scratch()
            + layer_scratch(C1)
            + layer_scratch(C2)
            + reduce_scratch(*MA)
            + reduce_scratch(*MB)
            + [
                pltpu.VMEM((256, C1), BF),
                pltpu.VMEM((3, 3 * C1, C2), BF),
                pltpu.VMEM((3, 3 * C2, C2), BF),
                pltpu.VMEM((64, C2), BF),
                pltpu.SMEM((1, 1, 2), jnp.int32),
                pltpu.SMEM((1, 1, 2), jnp.int32),
                pltpu.SMEM((1, 1, 4), jnp.int32),
                pltpu.SemaphoreType.DMA((7,)),
                pltpu.VMEM((8, 128), jnp.int32),
                pltpu.VMEM((4, 8, 128), jnp.int32),
                pltpu.SemaphoreType.DMA((4,)),
                pltpu.SemaphoreType.DMA((4,)),
                pltpu.VMEM((320, 256), BF),
                pltpu.VMEM((128, 384), BF),
                pltpu.VMEM((320, 128), BF),
                pltpu.VMEM((256, C2), F32),
                pltpu.VMEM((256, C2), F32),
                pltpu.VMEM((3, 3 * C1, 256), BF),
            ]
        ),
        compiler_params=pltpu.CompilerParams(
            collective_id=0, has_side_effects=True, vmem_limit_bytes=32 * 1024 * 1024
        ),
        name="level_step",
    )(*(
        pltpu.with_memory_space_constraint(value, pltpu.HBM)
        for value in (
            features.reshape(256, C1),
            conv_first.reshape(3, 3 * C1, C2),
            conv_second.reshape(3, 3 * C2, C2),
            cotangent.reshape(64, C2),
            edge_pick,
            edge_flip,
            corner_rule,
        )
    ))
    pooled, input_grad, first, second = pl.pallas_call(
        finish_kernel,
        out_shape=(
            jax.ShapeDtypeStruct((64, C2), BF),
            jax.ShapeDtypeStruct((256, C1), BF),
            jax.ShapeDtypeStruct((9 * C1, C2), BF),
            jax.ShapeDtypeStruct((9 * C2, C2), BF),
        ),
        in_specs=[vmem] * 5,
        out_specs=[hbm] * 4,
        scratch_shapes=[
            pltpu.VMEM((9 * C1, C2), BF),
            pltpu.VMEM((9 * C2, C2), BF),
            pltpu.SemaphoreType.DMA((6,)),
        ],
        compiler_params=pltpu.CompilerParams(vmem_limit_bytes=16 * 1024 * 1024),
        name="scale_outputs",
    )(pooled, input_grad, first, second, square)
    return (
        pooled.reshape(1, 1, 8, 8, C2),
        input_grad.reshape(1, 1, 16, 16, C1),
        first.reshape(3, 3, C1, C2),
        second.reshape(3, 3, C2, C2),
    )


def solution(mesh):
    return jax.shard_map(
        on_device,
        mesh=mesh,
        in_specs=(
            P("lon", "lat", None, None, None),
            P(),
            P(),
            P("lon", "lat", None, None, None),
            P("lon", "lat", None),
            P("lon", "lat", None),
            P("lon", "lat", None),
        ),
        out_specs=(P("lon", "lat", None, None, None), P("lon", "lat", None, None, None), P(), P()),
        check_vma=False,
    )
```
